32 devices in a mesh: scene: 8 (over z, y), seq: 2 (over core), head: 2 (over x).
Axes of the slice: x: 2, y: 2, z: 4, core: 2. Of those that a mesh axis runs over, the one named last changes fastest.
Arguments:
- tokens: bfloat16 [16384, 1024], P(('scene', 'seq')), may hold values from -6 to 6
- counts: int32 [8], P('scene'), may hold values from 1024 to 2048, as said below
- w_qkv: bfloat16 [3, 1024, 1024], P(None, ('scene', 'seq'), 'head'), may hold values from -0.1875 to 0.1875
- w_out: bfloat16 [1024, 1024], P('head', ('scene', 'seq')), may hold values from -4 to 4
- w_up: bfloat16 [1024, 4096], P(('scene', 'seq'), 'head'), may hold values from -0.1875 to 0.1875
- w_down: bfloat16 [4096, 1024], P('head', ('scene', 'seq')), may hold values from -0.09375 to 0.09375
- gain_one: bfloat16 [1024], P(('scene', 'seq')), may hold values from 0.099609375 to 1.8984375
- shift_one: bfloat16 [1024], P(('scene', 'seq')), may hold values from -3 to 3
- gain_two: bfloat16 [1024], P(('scene', 'seq')), may hold values from 0.099609375 to 1.8984375
- shift_two: bfloat16 [1024], P(('scene', 'seq')), may hold values from -3 to 3
- cotangent: bfloat16 [16384, 1024], P(('scene', 'seq')), may hold values from -6 to 6
Outputs:
- output: float32 [16384, 1024], P(('scene', 'seq'))
- tokens_grad: float32 [16384, 1024], P(('scene', 'seq'))
- w_qkv_grad: float32 [3, 1024, 1024], P(None, ('scene', 'seq'), 'head')
- w_out_grad: float32 [1024, 1024], P('head', ('scene', 'seq'))
- w_up_grad: float32 [1024, 4096], P(('scene', 'seq'), 'head')
- w_down_grad: float32 [4096, 1024], P('head', ('scene', 'seq'))
- gain_one_grad: float32 [1024], P(('scene', 'seq'))
- shift_one_grad: float32 [1024], P(('scene', 'seq'))
- gain_two_grad: float32 [1024], P(('scene', 'seq'))
- shift_two_grad: float32 [1024], P(('scene', 'seq'))
The draws below stay inside these ranges and needn't reach their ends.
Inputs may be any that keep to these rules, and one draw needn't show every extreme that they name: Slots 0 to counts - 1 of a scene hold its tokens, the others are padding; in every draw some scene has all 2048 slots valid and some exactly 1024.
All inputs are finite; a program needn't handle non-finite values.
Results may differ from the reference program's by a relative error of at most 0.022.
Values may be sent and summed in bfloat16 or wider, within the bound.
A program may use at most 448 MiB of HBM per device.

```python
import jax
import jax.numpy as jnp
from jax import lax

D = 1024
H = 16
FF = 4096
SEQ = 2048
SCENES = 8
ROWS = 16384


def draw_counts(key, part):
    first_key, second_key = jax.random.split(jax.random.fold_in(key, 17))
    drawn = jax.random.randint(first_key, (SCENES,), SEQ // 2, SEQ + 1)
    order = jax.random.permutation(second_key, SCENES)
    drawn = drawn.at[order[0]].set(SEQ)
    drawn = drawn.at[order[1]].set(SEQ // 2)
    return drawn.astype(jnp.int32)


def with_spikes(values, rng, source, target, parts, factor):
    def block_of(dim):
        return (jnp.arange(values.shape[dim]) // (values.shape[dim] // parts)).reshape((-1,) + (1,) * (values.ndim - 1 - dim))

    near = jax.random.permutation(rng, parts)[block_of(target)]
    other_side = (block_of(target) + parts // 2) % parts
    return jnp.where((block_of(source) == near) | (block_of(source) == other_side), factor * values, values)


def shard_levels(rng, dims, cuts, least, high):
    loudness = 1.0
    for axis_at, shards_of in cuts:
        heights = jax.random.uniform(jax.random.fold_in(jax.random.fold_in(rng, 6), axis_at), (shards_of,), jnp.float32, least / len(cuts), high / len(cuts))
        loudness = loudness * jnp.repeat(jnp.exp(heights), dims[axis_at] // shards_of).reshape((-1,) + (1,) * (len(dims) - 1 - axis_at))
    return loudness


def noise(own_key, shape, width, bound, cuts=(), held_as=jnp.bfloat16):
    values = width * jax.random.normal(own_key, shape, jnp.float32)
    if cuts:
        values = values * shard_levels(own_key, shape, cuts, -0.22, 0.18)
    return jnp.clip(values, -bound, bound).astype(held_as)


def bell_draw_with(key, shape, scale, most, cuts, heavy, held_as=jnp.bfloat16):
    array = scale * jax.random.normal(key, shape, jnp.float32)
    if cuts:
        array = array * shard_levels(key, shape, cuts, -0.22, 0.18)
    return jnp.clip(with_spikes(array, jax.random.fold_in(key, 3), *heavy), -most, most).astype(held_as)


def setup_inputs(seed: int = 0) -> dict:
    arg_keys = jax.random.split(jax.random.key(seed), 12)
    tokens = bell_draw_with(arg_keys[0], (ROWS, D), 1.0, 6.0, ((0, 16),), (0, 1, 16, 2.0))
    counts = draw_counts(jax.random.fold_in(arg_keys[11], 71), 0)
    w_qkv = noise(arg_keys[2], (3, D, D), D ** -0.5, 0.1875, ((1, 16), (2, 2)))
    w_out = noise(arg_keys[3], (D, D), (max(1, D * 4 // SEQ)) ** -0.5, 4.0, ((0, 2), (1, 16)))
    w_up = noise(arg_keys[4], (D, FF), D ** -0.5, 0.1875, ((0, 16), (1, 2)))
    w_down = noise(arg_keys[5], (FF, D), FF ** -0.5, 0.09375, ((0, 2), (1, 16)))
    gain_one = jnp.clip(1.0 + 0.18 * jax.random.normal(arg_keys[6], (D,), jnp.float32), 0.099609375, 1.8984375).astype(jnp.bfloat16)
    shift_one = noise(arg_keys[7], (D,), 0.5, 3.0, ((0, 16),))
    gain_two = jnp.clip(1.0 + 0.18 * jax.random.normal(arg_keys[8], (D,), jnp.float32), 0.099609375, 1.8984375).astype(jnp.bfloat16)
    shift_two = noise(arg_keys[9], (D,), 0.5, 3.0, ((0, 16),))
    cotangent = bell_draw_with(arg_keys[10], (ROWS, D), 1.0, 6.0, ((0, 16),), (0, 1, 16, 2.0))
    return {"tokens": tokens, "counts": counts, "w_qkv": w_qkv, "w_out": w_out, "w_up": w_up, "w_down": w_down, "gain_one": gain_one, "shift_one": shift_one, "gain_two": gain_two, "shift_two": shift_two, "cotangent": cotangent}


@jax.custom_vjp
def low(v):
    return lax.optimization_barrier(v.astype(jnp.bfloat16)).astype(jnp.float32)

@jax.custom_vjp
def low_back(v):
    return v

def low_keep(v):
    return (low(v), None)

def low_pass(kept, grad):
    return (grad,)

def back_keep(v):
    return (v, None)

def back_low(kept, grad):
    return (low(grad),)
low.defvjp(low_keep, low_pass)
low_back.defvjp(back_keep, back_low)

def normed(values, gain, shift):
    centre = values - lax.optimization_barrier(jnp.mean(values, axis=-1, keepdims=True))
    spread = lax.optimization_barrier(jnp.mean(centre * centre, axis=-1, keepdims=True))
    return centre * lax.rsqrt(spread + 1e-05) * gain + shift

def layer(values, proj_qkv, proj_out, proj_up, proj_down, gain_a, shift_a, gain_b, shift_b, valid_count):
    head_size = D // H
    scale = head_size ** (-0.5)
    highest = lax.Precision.HIGHEST
    normed_one = low(normed(values, gain_a, shift_a))
    projected = low(low_back(jnp.einsum('td,cdf->ctf', normed_one, proj_qkv, precision=highest)))
    queries = projected[0].reshape(SEQ, H, head_size)
    key_heads = projected[1].reshape(SEQ, H, head_size)
    value_heads = projected[2].reshape(SEQ, H, head_size)
    valid = jnp.arange(SEQ, dtype=jnp.int32) < valid_count
    block = min(512, SEQ)
    query_blocks = queries.reshape(SEQ // block, block, H, head_size)

    def attend(query_block):
        raw = low_back(jnp.einsum('qhe,khe->hqk', query_block, key_heads, precision=highest) * scale)
        masked = jnp.where(valid[None, None, :], raw, -1e+30)
        probs = low(jax.nn.softmax(masked, axis=-1))
        return jnp.einsum('hqk,khe->qhe', probs, value_heads, precision=highest)
    context = lax.map(jax.checkpoint(attend), query_blocks).reshape(SEQ, D)
    context = low(low_back(context))
    residual = values + low_back(jnp.dot(context, proj_out, precision=highest))
    normed_two = low(normed(residual, gain_b, shift_b))
    up_proj = low_back(jnp.dot(normed_two, proj_up, precision=highest))
    activated = low(jax.nn.gelu(up_proj, approximate=False))
    return residual + low_back(jnp.dot(activated, proj_down, precision=highest))

def reference(tokens, counts, w_qkv, w_out, w_up, w_down, gain_one, shift_one, gain_two, shift_two, cotangent):
    weights = tuple((item.astype(jnp.float32) for item in (w_qkv, w_out, w_up, w_down, gain_one, shift_one, gain_two, shift_two)))
    inputs = tokens.astype(jnp.float32).reshape(SCENES, SEQ, D)
    grads_in = cotangent.astype(jnp.float32).reshape(SCENES, SEQ, D)

    def scene_step(carry, pieces):
        scene_in, scene_count, scene_grad = pieces

        def closed(values, *params):
            return layer(values, *params, scene_count)
        result, pull = jax.vjp(closed, scene_in, *weights)
        grads = pull(scene_grad)
        carry = tuple((total + grad for total, grad in zip(carry, grads[1:])))
        return (carry, (result, grads[0]))
    init = tuple((jnp.zeros(item.shape, jnp.float32) for item in weights))
    totals, (results, input_grads) = lax.scan(scene_step, init, (inputs, counts, grads_in))
    return (results.reshape(ROWS, D), input_grads.reshape(ROWS, D), totals[0], totals[1], totals[2], totals[3], totals[4], totals[5], totals[6], totals[7])
```

```python
from functools import partial

import jax
import jax.numpy as jnp
from jax import lax
from jax.experimental import pallas as pl
from jax.experimental.pallas import tpu as pltpu
from jax.sharding import PartitionSpec as P

MESH = pl.DeviceIdType.MESH
ZS = 4


def place(ny):
    scene = lax.axis_index("scene")
    return scene // ny, scene % ny, lax.axis_index("seq")


def remote(src, dst, send_sem, recv_sem, device):
    return pltpu.make_async_remote_copy(
        src_ref=src, dst_ref=dst, send_sem=send_sem, recv_sem=recv_sem,
        device_id=device, device_id_type=MESH,
    )


def greet(ny):
    z, y, core = place(ny)
    barrier = pltpu.get_barrier_semaphore()
    for step in range(1, ZS):
        pl.semaphore_signal(barrier, 1, device_id={"scene": (z + step) % ZS * ny + y}, device_id_type=MESH)
    for step in range(1, ny):
        pl.semaphore_signal(barrier, 1, device_id={"scene": z * ny + (y + step) % ny}, device_id_type=MESH)
    pl.semaphore_signal(barrier, 1, device_id={"seq": 1 - core}, device_id_type=MESH)
    pl.semaphore_wait(barrier, ZS + ny - 1)


def gather_kernel(ny, groups, shard, full, zsend, zrecv, ysend, yrecv, csend, crecv, own_sem):
    z, y, core = place(ny)
    own = pltpu.make_async_copy(shard, full.at[z, y, core], own_sem)
    own.start()
    greet(ny)

    def z_copy(g, step):
        cols = groups[g]
        return remote(shard.at[:, cols], full.at[z, y, core, :, cols], zsend.at[g, step - 1], zrecv.at[g, step - 1],
                      {"scene": (z + step) % ZS * ny + y})

    def y_copy(g, zi, step):
        cols = groups[g]
        zz = (z + ZS - zi) % ZS
        src = shard.at[:, cols] if zi == 0 else full.at[zz, y, core, :, cols]
        return remote(src, full.at[zz, y, core, :, cols], ysend.at[g, zi, step - 1], yrecv.at[g, zi, step - 1],
                      {"scene": z * ny + (y + step) % ny})

    def c_copy(g, zi, step):
        cols = groups[g]
        zz = (z + ZS - zi) % ZS
        yy = (y + ny - step) % ny
        src = shard.at[:, cols] if zi == 0 and step == 0 else full.at[zz, yy, core, :, cols]
        return remote(src, full.at[zz, yy, core, :, cols], csend.at[g, zi, step], crecv.at[g, zi, step], {"seq": 1 - core})

    for g in range(len(groups)):
        for step in range(1, ZS):
            z_copy(g, step).start()
    for g in range(len(groups)):
        for step in range(1, ny):
            y_copy(g, 0, step).start()
        c_copy(g, 0, 0).start()
    for g in range(len(groups)):
        for zi in range(1, ZS):
            z_copy(g, zi).wait_recv()
            for step in range(1, ny):
                y_copy(g, zi, step).start()
            c_copy(g, zi, 0).start()
        for zi in range(ZS):
            for step in range(1, ny):
                y_copy(g, zi, step).wait_recv()
                c_copy(g, zi, step).start()
    own.wait()
    for g in range(len(groups)):
        for zi in range(ZS):
            if zi:
                z_copy(g, zi).wait_send()
            for step in range(1, ny):
                y_copy(g, zi, step).wait_send()
            for step in range(ny):
                c_copy(g, zi, step).wait()


def gather_all(shard, scenes, groups):
    ny = scenes // ZS
    rows, cols = shard.shape
    n = len(groups)
    sem = pltpu.SemaphoreType.DMA
    full = pl.pallas_call(
        partial(gather_kernel, ny, groups),
        out_shape=jax.ShapeDtypeStruct((ZS, ny, 2, rows, cols), shard.dtype),
        in_specs=[pl.BlockSpec(memory_space=pl.ANY)],
        out_specs=pl.BlockSpec(memory_space=pl.ANY),
        scratch_shapes=[sem((n, ZS - 1)), sem((n, ZS - 1)), sem((n, ZS, max(ny - 1, 1))), sem((n, ZS, max(ny - 1, 1))),
                        sem((n, ZS, ny)), sem((n, ZS, ny)), sem],
        compiler_params=pltpu.CompilerParams(collective_id=0, has_side_effects=True),
        name="gather_weights",
    )(shard)
    return full.reshape(scenes * 2 * rows, cols)


def scatter_kernel(ny, groups, parts, out, own, from_core, sum_one, from_y, sum_two, from_z,
                   own_sem, csend, crecv, ysend, yrecv, zsend, zrecv):
    z, y, core = place(ny)
    greet(ny)

    def load(g):
        cols = groups[g]
        return pltpu.make_async_copy(parts.at[:, :, core, :, cols], own.at[:, :, :, cols], own_sem.at[g])

    def c_copy(g):
        cols = groups[g]
        return remote(parts.at[:, :, 1 - core, :, cols], from_core.at[:, :, :, cols], csend.at[g], crecv.at[g], {"seq": 1 - core})

    def y_copy(g, step):
        cols = groups[g]
        yy = (y + step) % ny
        return remote(sum_one.at[:, yy, :, cols], from_y.at[step - 1, :, :, cols], ysend.at[g, step - 1], yrecv.at[g, step - 1],
                      {"scene": z * ny + yy})

    def z_copy(g, step):
        cols = groups[g]
        zz = (z + step) % ZS
        return remote(sum_two.at[zz, :, cols], from_z.at[step - 1, :, cols], zsend.at[g, step - 1], zrecv.at[g, step - 1],
                      {"scene": zz * ny + y})

    n = len(groups)
    for g in range(n):
        load(g).start()
        c_copy(g).start()
    f32 = jnp.float32

    def stage_two(g):
        cols = groups[g]
        for step in range(1, ny):
            y_copy(g, step).wait_recv()
        for zz in range(ZS):
            total = sum_one[zz, y, :, cols].astype(f32)
            for step in range(1, ny):
                total += from_y[step - 1, zz, :, cols].astype(f32)
            sum_two[zz, :, cols] = total.astype(sum_two.dtype)
        for step in range(1, ZS):
            z_copy(g, step).start()

    for g in range(n):
        cols = groups[g]
        load(g).wait()
        c_copy(g).wait_recv()
        for zz in range(ZS):
            for yy in range(ny):
                sum_one[zz, yy, :, cols] = (
                    own[zz, yy, :, cols].astype(f32) + from_core[zz, yy, :, cols].astype(f32)
                ).astype(sum_one.dtype)
        for step in range(1, ny):
            y_copy(g, step).start()
        if g >= 1:
            stage_two(g - 1)
    stage_two(n - 1)
    for g in range(n):
        cols = groups[g]
        for step in range(1, ZS):
            z_copy(g, step).wait_recv()
        total = sum_two[z, :, cols].astype(f32)
        for step in range(1, ZS):
            total += from_z[step - 1, :, cols].astype(f32)
        out[:, cols] = total
    for g in range(n):
        c_copy(g).wait_send()
        for step in range(1, ny):
            y_copy(g, step).wait_send()
        for step in range(1, ZS):
            z_copy(g, step).wait_send()


def scatter_all(parts, scenes, groups):
    ny = scenes // ZS
    cols = parts.shape[1]
    rows = parts.shape[0] // (scenes * 2)
    n = len(groups)
    sem = pltpu.SemaphoreType.DMA
    low = parts.dtype
    return pl.pallas_call(
        partial(scatter_kernel, ny, groups),
        out_shape=jax.ShapeDtypeStruct((rows, cols), jnp.float32),
        in_specs=[pl.BlockSpec(memory_space=pl.ANY)],
        out_specs=pl.BlockSpec(memory_space=pltpu.VMEM),
        scratch_shapes=[
            pltpu.VMEM((ZS, ny, rows, cols), low), pltpu.VMEM((ZS, ny, rows, cols), low), pltpu.VMEM((ZS, ny, rows, cols), low),
            pltpu.VMEM((max(ny - 1, 1), ZS, rows, cols), low), pltpu.VMEM((ZS, rows, cols), low),
            pltpu.VMEM((ZS - 1, rows, cols), low),
            sem((n,)), sem((n,)), sem((n,)), sem((n, max(ny - 1, 1))), sem((n, max(ny - 1, 1))), sem((n, ZS - 1)), sem((n, ZS - 1))],
        compiler_params=pltpu.CompilerParams(collective_id=1, has_side_effects=True, vmem_limit_bytes=48 * 2**20),
        name="scatter_grads",
    )(parts.reshape(ZS, ny, 2, rows, cols))


def exchange(part, heads):
    low = part.astype(jnp.bfloat16)
    total = part
    for step in range(1, heads):
        moved = lax.ppermute(low, "head", [(i, (i + step) % heads) for i in range(heads)])
        total = total + moved.astype(jnp.float32)
    return total


def pack_weights(w_qkv, w_out, w_up, w_down, *norms):
    columns = jnp.pad(jnp.stack(norms, axis=1), ((0, 0), (0, 124)))
    return jnp.concatenate([columns, w_qkv[0], w_qkv[1], w_qkv[2], w_out.T, w_up, w_down.T], axis=1)


def column_groups(width, hidden):
    edges = [0, 128 + 3 * width, 128 + 4 * width + hidden // 2, 128 + 4 * width + hidden, 128 + 4 * width + 2 * hidden]
    return [pl.ds(a, b - a) for a, b in zip(edges, edges[1:])]


def split_columns(full, width, hidden):
    at, out = 0, []
    for size in (128, width, width, width, width, hidden, hidden):
        out.append(full[:, at:at + size])
        at += size
    return out


D = 1024
H = 16


def normed(values, gain, shift):
    centre = values - jnp.mean(values, axis=-1, keepdims=True)
    spread = jnp.mean(centre * centre, axis=-1, keepdims=True)
    return centre * lax.rsqrt(spread + 1e-05) * gain + shift


def masked_scores(queries, keys_all, valid_count, scale):
    length = keys_all.shape[0]
    key_heads = keys_all.reshape(length, queries.shape[1], queries.shape[2])
    raw = jnp.einsum("qhe,khe->hqk", queries, key_heads, preferred_element_type=jnp.float32) * scale
    valid = lax.iota(jnp.int32, length) < valid_count
    return (jnp.where(valid[None, None, :], raw, -1e30), key_heads)


def attend_forward(scale, inputs):
    queries, keys_all, values_all, valid_count = inputs
    masked, key_heads = masked_scores(queries, keys_all, valid_count, scale)
    value_heads = values_all.reshape(key_heads.shape)
    top = jnp.max(masked, axis=-1, keepdims=True)
    expo = jnp.exp(masked - top)
    total = jnp.sum(expo, axis=-1, keepdims=True)
    probs = (expo / total).astype(jnp.bfloat16)
    context = jnp.einsum("hqk,khe->qhe", probs, value_heads, preferred_element_type=jnp.float32)
    return (context.reshape(queries.shape[0], -1), (top + jnp.log(total))[..., 0])


def attend_backward(scale, inputs):
    queries, keys_all, values_all, valid_count, log_total, grad_context = inputs
    masked, key_heads = masked_scores(queries, keys_all, valid_count, scale)
    value_heads = values_all.reshape(key_heads.shape)
    probs = jnp.exp(masked - log_total[..., None])
    probs_low = probs.astype(jnp.bfloat16)
    grad_heads = grad_context.reshape(queries.shape)
    grad_probs = jnp.einsum(
        "qhe,khe->hqk", grad_heads, value_heads, preferred_element_type=jnp.float32
    )
    inner = jnp.sum(probs * grad_probs, axis=-1, keepdims=True)
    grad_scores = (probs * (grad_probs - inner)).astype(jnp.bfloat16)
    grad_query = (
        jnp.einsum("hqk,khe->qhe", grad_scores, key_heads, preferred_element_type=jnp.float32)
        * scale
    )
    grad_key = (
        jnp.einsum("hqk,qhe->khe", grad_scores, queries, preferred_element_type=jnp.float32) * scale
    )
    grad_value = jnp.einsum(
        "hqk,qhe->khe", probs_low, grad_heads, preferred_element_type=jnp.float32
    )
    length = keys_all.shape[0]
    return (
        grad_query.reshape(queries.shape[0], -1),
        grad_key.reshape(length, -1),
        grad_value.reshape(length, -1),
    )


def on_device(
    n_scene, n_head, tokens, counts, w_qkv, w_out, w_up, w_down, gain_one, shift_one, gain_two, shift_two, cotangent
):
    scenes = counts.shape[0]
    exchange_heads = partial(exchange, heads=n_head)
    tok_rows = tokens.shape[0]
    per_scene = tok_rows // scenes
    head_size = D // H
    scale = head_size ** (-0.5)
    width, hidden = w_qkv.shape[2], w_up.shape[1]
    shard = pack_weights(w_qkv, w_out, w_up, w_down, gain_one, shift_one, gain_two, shift_two)
    groups = column_groups(width, hidden)
    full = gather_all(shard, n_scene, groups)
    norms, full_q, full_k, full_v, full_out_t, full_up, full_down_t = split_columns(full, width, hidden)
    full_qkv = jnp.stack([full_q, full_k, full_v])
    full_out, full_down = full_out_t.T, full_down_t.T
    gain_a, shift_a, gain_b, shift_b = list(norms[:, :4].T.astype(jnp.float32))
    inputs_f = tokens.astype(jnp.float32)
    normed_one_low = normed(inputs_f, gain_a, shift_a).astype(jnp.bfloat16)
    projected = jnp.einsum(
        "td,cdf->ctf", normed_one_low, full_qkv, preferred_element_type=jnp.float32
    ).astype(jnp.bfloat16)
    width_local = projected.shape[2]
    heads_local = width_local // head_size
    queries = projected[0].reshape(scenes, per_scene, heads_local, head_size)
    keys_local = projected[1].reshape(scenes, per_scene, width_local)
    values_local = projected[2].reshape(scenes, per_scene, width_local)
    keys_all, values_all = (
        lax.all_gather(keys_local, "seq", axis=1, tiled=True),
        lax.all_gather(values_local, "seq", axis=1, tiled=True),
    )
    context, log_total = lax.map(
        partial(attend_forward, scale), (queries, keys_all, values_all, counts)
    )
    context_low = context.reshape(tok_rows, width_local).astype(jnp.bfloat16)
    attn_part = jnp.dot(context_low, full_out, preferred_element_type=jnp.float32)
    residual = inputs_f + exchange_heads(attn_part)
    normed_two_low = normed(residual, gain_b, shift_b).astype(jnp.bfloat16)
    up_proj = jnp.dot(normed_two_low, full_up, preferred_element_type=jnp.float32)
    activated = jax.nn.gelu(up_proj, approximate=False).astype(jnp.bfloat16)
    mlp_part = jnp.dot(activated, full_down, preferred_element_type=jnp.float32)
    output = residual + exchange_heads(mlp_part)
    grad_output = cotangent.astype(jnp.float32)
    grad_down = jnp.einsum("tf,td->fd", activated, cotangent, preferred_element_type=jnp.float32)
    grad_act = jnp.einsum("td,fd->tf", cotangent, full_down, preferred_element_type=jnp.float32)
    _, gelu_pull = jax.vjp(partial(jax.nn.gelu, approximate=False), up_proj)
    grad_up_low = gelu_pull(grad_act)[0].astype(jnp.bfloat16)
    grad_up = jnp.einsum(
        "td,tf->df", normed_two_low, grad_up_low, preferred_element_type=jnp.float32
    )
    norm_two_part = jnp.einsum(
        "tf,df->td", grad_up_low, full_up, preferred_element_type=jnp.float32
    )
    _, pull_two = jax.vjp(normed, residual, gain_b, shift_b)
    resid_piece, grad_gain_two, grad_shift_two = pull_two(exchange_heads(norm_two_part))
    grad_resid = grad_output + resid_piece
    grad_resid_low = grad_resid.astype(jnp.bfloat16)
    grad_outproj = jnp.einsum(
        "tf,td->fd", context_low, grad_resid_low, preferred_element_type=jnp.float32
    )
    grad_context = jnp.einsum(
        "td,fd->tf", grad_resid_low, full_out, preferred_element_type=jnp.float32
    )
    grad_context = grad_context.astype(jnp.bfloat16).reshape(scenes, per_scene, width_local)
    grad_query, key_terms, value_terms = lax.map(
        partial(attend_backward, scale),
        (queries, keys_all, values_all, counts, log_total, grad_context),
    )
    key_grad, value_grad = (
        lax.psum_scatter(
            key_terms.astype(jnp.bfloat16), "seq", scatter_dimension=1, tiled=True
        ).astype(jnp.float32),
        lax.psum_scatter(
            value_terms.astype(jnp.bfloat16), "seq", scatter_dimension=1, tiled=True
        ).astype(jnp.float32),
    )
    grad_proj = jnp.stack(
        [
            grad_query.reshape(tok_rows, width_local),
            key_grad.reshape(tok_rows, width_local),
            value_grad.reshape(tok_rows, width_local),
        ]
    ).astype(jnp.bfloat16)
    grad_qkv = jnp.einsum(
        "td,ctf->cdf", normed_one_low, grad_proj, preferred_element_type=jnp.float32
    )
    norm_one_part = jnp.einsum(
        "ctf,cdf->td", grad_proj, full_qkv, preferred_element_type=jnp.float32
    )
    _, pull_one = jax.vjp(normed, inputs_f, gain_a, shift_a)
    input_piece, grad_gain_one, grad_shift_one = pull_one(exchange_heads(norm_one_part))
    tokens_grad = grad_resid + input_piece
    low = jnp.bfloat16
    norm_grads = jnp.stack([grad_gain_one, grad_shift_one, grad_gain_two, grad_shift_two], axis=1)
    norm_grads = jnp.pad(norm_grads, ((0, 0), (0, 124)))
    parts = jnp.concatenate(
        [norm_grads.astype(low), grad_qkv[0].astype(low), grad_qkv[1].astype(low), grad_qkv[2].astype(low),
         grad_outproj.T.astype(low), grad_up.astype(low), grad_down.T.astype(low)], axis=1)
    mine = scatter_all(parts, n_scene, groups)
    norms, mine_q, mine_k, mine_v, mine_out, mine_up, mine_down = split_columns(mine, width, hidden)
    return (output, tokens_grad, jnp.stack([mine_q, mine_k, mine_v]), mine_out.T, mine_up, mine_down.T,
            norms[:, 0], norms[:, 1], norms[:, 2], norms[:, 3])


def solution(mesh):
    in_specs = (
        P(("scene", "seq"), None),
        P("scene"),
        P(None, ("scene", "seq"), "head"),
        P("head", ("scene", "seq")),
        P(("scene", "seq"), "head"),
        P("head", ("scene", "seq")),
        P(("scene", "seq")),
        P(("scene", "seq")),
        P(("scene", "seq")),
        P(("scene", "seq")),
        P(("scene", "seq"), None),
    )
    out_specs = (
        P(("scene", "seq"), None),
        P(("scene", "seq"), None),
        P(None, ("scene", "seq"), "head"),
        P("head", ("scene", "seq")),
        P(("scene", "seq"), "head"),
        P("head", ("scene", "seq")),
        P(("scene", "seq")),
        P(("scene", "seq")),
        P(("scene", "seq")),
        P(("scene", "seq")),
    )
    return jax.shard_map(
        partial(on_device, mesh.shape["scene"], mesh.shape["head"]), mesh=mesh, in_specs=in_specs, out_specs=out_specs, check_vma=False
    )
```

```python
from functools import partial

import jax
import jax.numpy as jnp
from jax import lax
from jax.experimental import pallas as pl
from jax.experimental.pallas import tpu as pltpu
from jax.sharding import PartitionSpec as P

MESH = pl.DeviceIdType.MESH
ZS = 4


def place(ny):
    scene = lax.axis_index("scene")
    return scene // ny, scene % ny, lax.axis_index("seq")


def remote(src, dst, send_sem, recv_sem, device):
    return pltpu.make_async_remote_copy(
        src_ref=src, dst_ref=dst, send_sem=send_sem, recv_sem=recv_sem,
        device_id=device, device_id_type=MESH,
    )


def greet(ny):
    z, y, core = place(ny)
    barrier = pltpu.get_barrier_semaphore()
    for step in range(1, ZS):
        pl.semaphore_signal(barrier, 1, device_id={"scene": (z + step) % ZS * ny + y}, device_id_type=MESH)
    for step in range(1, ny):
        pl.semaphore_signal(barrier, 1, device_id={"scene": z * ny + (y + step) % ny}, device_id_type=MESH)
    pl.semaphore_signal(barrier, 1, device_id={"seq": 1 - core}, device_id_type=MESH)
    pl.semaphore_wait(barrier, ZS + ny - 1)


def scatter_kernel(ny, groups, parts, out, own, from_core, sum_one, from_y, sum_two, from_z,
                   own_sem, csend, crecv, ysend, yrecv, zsend, zrecv):
    z, y, core = place(ny)
    greet(ny)

    def load(g):
        cols = groups[g]
        return pltpu.make_async_copy(parts.at[:, :, core, :, cols], own.at[:, :, :, cols], own_sem.at[g])

    def c_copy(g):
        cols = groups[g]
        return remote(parts.at[:, :, 1 - core, :, cols], from_core.at[:, :, :, cols], csend.at[g], crecv.at[g], {"seq": 1 - core})

    def y_copy(g, step):
        cols = groups[g]
        yy = (y + step) % ny
        return remote(sum_one.at[:, yy, :, cols], from_y.at[step - 1, :, :, cols], ysend.at[g, step - 1], yrecv.at[g, step - 1],
                      {"scene": z * ny + yy})

    def z_copy(g, step):
        cols = groups[g]
        zz = (z + step) % ZS
        return remote(sum_two.at[zz, :, cols], from_z.at[step - 1, :, cols], zsend.at[g, step - 1], zrecv.at[g, step - 1],
                      {"scene": zz * ny + y})

    n = len(groups)
    for g in range(n):
        load(g).start()
        c_copy(g).start()
    f32 = jnp.float32

    def stage_two(g):
        cols = groups[g]
        for step in range(1, ny):
            y_copy(g, step).wait_recv()
        for zz in range(ZS):
            total = sum_one[zz, y, :, cols].astype(f32)
            for step in range(1, ny):
                total += from_y[step - 1, zz, :, cols].astype(f32)
            sum_two[zz, :, cols] = total.astype(sum_two.dtype)
        for step in range(1, ZS):
            z_copy(g, step).start()

    for g in range(n):
        cols = groups[g]
        load(g).wait()
        c_copy(g).wait_recv()
        for zz in range(ZS):
            for yy in range(ny):
                sum_one[zz, yy, :, cols] = (
                    own[zz, yy, :, cols].astype(f32) + from_core[zz, yy, :, cols].astype(f32)
                ).astype(sum_one.dtype)
        for step in range(1, ny):
            y_copy(g, step).start()
        if g >= 1:
            stage_two(g - 1)
    stage_two(n - 1)
    for g in range(n):
        cols = groups[g]
        for step in range(1, ZS):
            z_copy(g, step).wait_recv()
        total = sum_two[z, :, cols].astype(f32)
        for step in range(1, ZS):
            total += from_z[step - 1, :, cols].astype(f32)
        out[:, cols] = total
    for g in range(n):
        c_copy(g).wait_send()
        for step in range(1, ny):
            y_copy(g, step).wait_send()
        for step in range(1, ZS):
            z_copy(g, step).wait_send()


def scatter_all(parts, scenes, groups):
    ny = scenes // ZS
    cols = parts.shape[1]
    rows = parts.shape[0] // (scenes * 2)
    n = len(groups)
    sem = pltpu.SemaphoreType.DMA
    low = parts.dtype
    return pl.pallas_call(
        partial(scatter_kernel, ny, groups),
        out_shape=jax.ShapeDtypeStruct((rows, cols), jnp.float32),
        in_specs=[pl.BlockSpec(memory_space=pl.ANY)],
        out_specs=pl.BlockSpec(memory_space=pltpu.VMEM),
        scratch_shapes=[
            pltpu.VMEM((ZS, ny, rows, cols), low), pltpu.VMEM((ZS, ny, rows, cols), low), pltpu.VMEM((ZS, ny, rows, cols), low),
            pltpu.VMEM((max(ny - 1, 1), ZS, rows, cols), low), pltpu.VMEM((ZS, rows, cols), low),
            pltpu.VMEM((ZS - 1, rows, cols), low),
            sem((n,)), sem((n,)), sem((n,)), sem((n, max(ny - 1, 1))), sem((n, max(ny - 1, 1))), sem((n, ZS - 1)), sem((n, ZS - 1))],
        compiler_params=pltpu.CompilerParams(collective_id=1, has_side_effects=True, vmem_limit_bytes=48 * 2**20),
        name="scatter_grads",
    )(parts.reshape(ZS, ny, 2, rows, cols))


def exchange(part, heads):
    low = part.astype(jnp.bfloat16)
    total = part
    for step in range(1, heads):
        moved = lax.ppermute(low, "head", [(i, (i + step) % heads) for i in range(heads)])
        total = total + moved.astype(jnp.float32)
    return total


def column_groups(width, hidden):
    edges = [0, 128 + 3 * width, 128 + 4 * width + hidden // 2, 128 + 4 * width + hidden, 128 + 4 * width + 2 * hidden]
    return [pl.ds(a, b - a) for a, b in zip(edges, edges[1:])]


def split_columns(full, width, hidden):
    at, out = 0, []
    for size in (128, width, width, width, width, hidden, hidden):
        out.append(full[:, at:at + size])
        at += size
    return out


F32 = jnp.float32
LOW = jnp.bfloat16


def dot(a, b, ca, cb):
    return lax.dot_general(a, b, (((ca,), (cb,)), ((), ())), preferred_element_type=F32)


def only_head(x, h, size):
    lane = lax.broadcasted_iota(jnp.int32, x.shape, 1)
    return jnp.where(lane // size == h, x, jnp.zeros_like(x))


class Gather:
    def __init__(self, ny, source, full, cols, sems):
        self.ny, self.source, self.full, self.cols = ny, source, full, cols
        self.rsend, self.rrecv, self.lsend, self.lrecv, self.ysend, self.yrecv, self.csend, self.crecv = sems
        self.z, self.y, self.core = place(ny)

    def at(self, zz, yy):
        return self.full.at[zz, yy, self.core, :, self.cols]

    def right(self, k):
        src = self.source() if k == 0 else self.at(self.z - k, self.y)
        dst = self.at(self.z - k, self.y)
        return remote(src, dst, self.rsend.at[k], self.rrecv.at[k], {"scene": (self.z + 1) * self.ny + self.y})

    def left(self, k):
        src = self.source() if k == 0 else self.at(self.z + k, self.y)
        dst = self.at(self.z + k, self.y)
        return remote(src, dst, self.lsend.at[k], self.lrecv.at[k], {"scene": (self.z - 1) * self.ny + self.y})

    def across(self, zz, step, own=False):
        src = self.source() if own else self.at(zz, self.y)
        peer = self.z * self.ny + (self.y + step) % self.ny
        return remote(src, self.at(zz, self.y), self.ysend.at[zz, step - 1], self.yrecv.at[zz, step - 1], {"scene": peer})

    def arrival(self, zz, step):
        yy = (self.y + self.ny - step) % self.ny
        return remote(self.at(zz, yy), self.at(zz, yy), self.ysend.at[zz, step - 1], self.yrecv.at[zz, step - 1],
                      {"scene": self.z * self.ny + yy})

    def twin(self, zz, step, own=False):
        src = self.source() if own else self.at(zz, (self.y + self.ny - step) % self.ny)
        dst = self.at(zz, (self.y + self.ny - step) % self.ny)
        return remote(src, dst, self.csend.at[zz, step], self.crecv.at[zz, step], {"seq": 1 - self.core})

    def begin(self):
        @pl.when(self.z < ZS - 1)
        def _():
            self.right(0).start()

        @pl.when(self.z > 0)
        def _():
            self.left(0).start()

        for step in range(1, self.ny):
            self.across(self.z, step, True).start()
        self.twin(self.z, 0, True).start()

    def hop(self, k):
        @pl.when(self.z >= k)
        def _():
            self.right(k - 1).wait_recv()
            if k < ZS - 1:
                @pl.when(self.z < ZS - 1)
                def _():
                    self.right(k).start()
            for step in range(1, self.ny):
                self.across(self.z - k, step).start()
            self.twin(self.z - k, 0).start()

        @pl.when(self.z + k < ZS)
        def _():
            self.left(k - 1).wait_recv()
            if k < ZS - 1:
                @pl.when(self.z > 0)
                def _():
                    self.left(k).start()
            for step in range(1, self.ny):
                self.across(self.z + k, step).start()
            self.twin(self.z + k, 0).start()

    def spread(self):
        for step in range(1, self.ny):
            for zz in range(ZS):
                self.arrival(zz, step).wait_recv()
                self.twin(zz, step).start()

    def finish(self):
        for k in range(ZS - 1):
            @pl.when((self.z < ZS - 1) & (self.z >= k))
            def _():
                self.right(k).wait_send()

            @pl.when((self.z > 0) & (self.z + k < ZS))
            def _():
                self.left(k).wait_send()
        for zz in range(ZS):
            for step in range(1, self.ny):
                self.arrival(zz, step).wait_send()
            for step in range(self.ny):
                self.twin(zz, step).wait()


def gather_sems(ny):
    sem = pltpu.SemaphoreType.DMA
    return [sem((ZS - 1,)), sem((ZS - 1,)), sem((ZS - 1,)), sem((ZS - 1,)), sem((ZS, max(ny - 1, 1))), sem((ZS, max(ny - 1, 1))),
            sem((ZS, ny)), sem((ZS, ny))]


def greet_all(ny, heads):
    z, y, core = place(ny)
    head = lax.axis_index("head")
    barrier = pltpu.get_barrier_semaphore()

    def signal(device):
        pl.semaphore_signal(barrier, 1, device_id=device, device_id_type=MESH)

    for step in range(1, ZS):
        signal({"scene": (z + step) % ZS * ny + y})
    for step in range(1, ny):
        signal({"scene": z * ny + (y + step) % ny})
    for step in range(1, heads):
        signal({"head": (head + step) % heads})
    signal({"seq": 1 - core})
    pl.semaphore_wait(barrier, ZS + ny - 1 + heads - 1)


def split_cols(total, parts):
    size = total // parts
    return [pl.ds(i * size, size) for i in range(parts)]


def forward_kernel(dims, limits, shard_qkv, shard_out, shard_up, shard_down, tokens,
                   n1_out, q_out, k_out, v_out, full_qkv, full_out, full_up, full_down, probs, context, context_all, inverse,
                   w0, hat, n1, q_s, k_s, v_s, bias, ctx_s, local_sem, kv_send, kv_recv, xw_send, xw_recv, xc_send, xc_recv, *sems):
    ny, heads, rows, width, size, block, pairs, steps_q, halves = dims
    pair, part = pl.program_id(0), pl.program_id(1)
    step = pair * steps_q + part
    z, y, core = place(ny)
    head = lax.axis_index("head")
    d_model = tokens.shape[1]
    per = 8
    own_cols = pl.ds(pl.multiple_of(head * width, width), width)

    def of(i):
        return sems[i * per:(i + 1) * per]

    first = Gather(ny, lambda: shard_qkv, w0, slice(None), of(0))
    others = [Gather(ny, lambda: full_out.at[z, y, core], full_out, slice(None), of(1))]
    for n, (shard, full) in enumerate(((shard_up, full_up), (shard_down, full_down))):
        for i, cols in enumerate(split_cols(full_up.shape[-1], halves)):
            others.append(Gather(ny, partial(lambda s, c: s.at[:, c], shard, cols), full, cols, of(2 + n * halves + i)))

    def local(src, dst, i):
        return pltpu.make_async_copy(src, dst, local_sem.at[i])

    def out_copy(step):
        return remote(shard_out, full_out.at[z, y, core, :, own_cols], xw_send.at[step - 1], xw_recv.at[step - 1],
                      {"head": (head + step) % heads})

    def kv_copy(i):
        src = (k_s, v_s)[i]
        return remote(src.at[pl.ds(0, rows)], src.at[pl.ds(rows, rows)], kv_send.at[i], kv_recv.at[i], {"seq": 1 - core})

    def ctx_copy(p, step):
        cols = pl.ds(pl.multiple_of(p * 2 * size, 2 * size), 2 * size)
        wide = pl.ds(pl.multiple_of(head * width + p * 2 * size, 2 * size), 2 * size)
        return remote(ctx_s.at[:, cols], context_all.at[:, wide], xc_send.at[p, step - 1], xc_recv.at[p, step - 1],
                      {"head": (head + step) % heads})

    own_blocks = [(shard_qkv, w0.at[z, y, core], 0), (shard_out, full_out.at[z, y, core, :, own_cols], 1),
                  (shard_up, full_up.at[z, y, core], 2), (shard_down, full_down.at[z, y, core], 3)]
    results = [(w0, full_qkv, 4), (n1, n1_out, 5), (q_s, q_out, 6), (k_s, k_out, 7), (v_s, v_out, 8)]
    ctx_local = (ctx_s, context_all.at[:, own_cols], 9)

    @pl.when(step == 0)
    def _():
        for item in own_blocks:
            local(*item).start()
        greet_all(ny, heads)
        first.begin()
        for i in range(1, heads):
            out_copy(i).start()
        tile = min(128, rows)

        @pl.loop(0, rows // tile)
        def _(i):
            at = pl.ds(pl.multiple_of(i * tile, tile), tile)
            x = tokens[at].astype(F32)
            centre = x - jnp.mean(x, axis=1, keepdims=True)
            spread = jnp.mean(centre * centre, axis=1, keepdims=True)
            hat[at] = centre * lax.rsqrt(spread + 1e-05)

        low_rows = lax.broadcasted_iota(jnp.int32, bias.shape, 0)
        lane = lax.broadcasted_iota(jnp.int32, bias.shape, 1)
        limit = jnp.where(low_rows < rows, limits[0], limits[1] + rows)
        bias[...] = jnp.where((low_rows >= limit) & (lane == 0), -1e30, 0.0).astype(LOW)
        first.hop(1)
        first.hop(2)
        first.hop(3)
        local(*own_blocks[1]).wait()
        for i in range(1, heads):
            out_copy(i).wait_recv()
        others[0].begin()
        others[1].begin()
        first.spread()
        for item in (own_blocks[0], own_blocks[2], own_blocks[3]):
            local(*item).wait()
        first.finish()
        local(*results[0]).start()
        norms = w0[:, :, :, :, :128].reshape(d_model, 128).astype(F32).T
        gain, shift = norms[0:1], norms[1:2]
        tile = min(256, rows)

        @pl.loop(0, rows // tile)
        def _(i):
            at = pl.ds(pl.multiple_of(i * tile, tile), tile)
            n1[at] = (hat[at] * gain + shift).astype(LOW)

        for c, dst in ((1, k_s), (2, v_s), (0, q_s)):
            @pl.loop(0, rows // tile)
            def _(i):
                at = pl.ds(pl.multiple_of(i * tile, tile), tile)
                w = w0[:, :, :, :, 128 + c * width:128 + (c + 1) * width].reshape(d_model, width)
                value = dot(n1[at], w, 1, 0).astype(LOW)
                dst[at] = value * LOW(size ** -0.5) if c == 0 else value

            if c:
                kv_copy(c - 1).start()
        for item in results[1:3]:
            local(*item).start()
        kv_copy(0).wait()
        kv_copy(1).wait()
        for item in results[3:]:
            local(*item).start()

    total = pairs * steps_q
    slots = 2 * total
    events = []
    n = len(others)
    for g in range(n):
        events += [(1.0 + g * 2.6, others[g], 1), (2.0 + g * 2.6, others[g], 2), (3.0 + g * 2.6, others[g], 3), (4.6 + g * 2.6, others[g], 4)]
        if g + 2 < n:
            events.append((1.5 + g * 2.6, others[g + 2], 0))
    events.sort(key=lambda item: item[0])
    last = max(item[0] for item in events) + 1

    def run(slot_in_step):
        for when, gather, what in events:
            slot = min(int(when * min(1.0, slots / 16)), slots - 1)
            if slot % 2 != slot_in_step:
                continue

            @pl.when(step == slot // 2)
            def _():
                if what == 0:
                    gather.begin()
                elif what < 4:
                    gather.hop(what)
                else:
                    gather.spread()

    queries = q_s[pl.ds(pl.multiple_of(part * block, block), block), pl.ds(pl.multiple_of(pair * 2 * size, 2 * size), 2 * size)]
    cols = pl.ds(pl.multiple_of(pair * 2 * size, 2 * size), 2 * size)
    keys = jnp.concatenate([k_s[:, cols], bias[...]], axis=1)
    values_t = v_s[:, cols].T
    ones = (lax.broadcasted_iota(jnp.int32, (block, bias.shape[1]), 1) == 0).astype(LOW)
    pieces = []
    for h in range(2):
        run(h)
        scores = dot(keys, jnp.concatenate([only_head(queries, h, size), ones], axis=1), 1, 1)
        top = jnp.max(scores, axis=0, keepdims=True)
        expo = jnp.exp(scores - top)
        over = 1.0 / jnp.sum(expo, axis=0, keepdims=True)
        low = expo.astype(LOW)
        probs[h] = low
        pieces.append(dot(values_t, low, 1, 0)[h * size:(h + 1) * size] * over)
        inverse[0, h:h + 1] = over
    here = jnp.concatenate(pieces, axis=0).T.astype(LOW)
    context[...] = here
    ctx_s[pl.ds(pl.multiple_of(part * block, block), block), cols] = here

    @pl.when(part == steps_q - 1)
    def _():
        for i in range(1, heads):
            ctx_copy(pair, i).start()

    @pl.when(step == total - 1)
    def _():
        local(*ctx_local).start()
        for gather in others:
            gather.finish()
        for item in results:
            local(*item).wait()
        local(*ctx_local).wait()
        for i in range(1, heads):
            out_copy(i).wait_send()
            for p in range(pairs):
                ctx_copy(p, i).wait()


def forward(limits, shard_qkv, shard_out, shard_up, shard_down, tokens, scenes, heads, size):
    ny = scenes // ZS
    rows, d_model = tokens.shape
    rl, width = shard_out.shape
    hidden = shard_up.shape[1]
    pairs = width // (2 * size)
    block = min(512, rows)
    steps_q = rows // block
    halves = 2
    sem = pltpu.SemaphoreType.DMA
    any_space = pl.BlockSpec(memory_space=pl.ANY)
    shape = jax.ShapeDtypeStruct
    wide = shard_qkv.shape[1]
    outs = [shape((rows, d_model), LOW), shape((rows, width), LOW), shape((2 * rows, width), LOW), shape((2 * rows, width), LOW),
            shape((ZS, ny, 2, rl, wide), LOW), shape((ZS, ny, 2, rl, d_model), LOW), shape((ZS, ny, 2, rl, hidden), LOW),
            shape((ZS, ny, 2, rl, hidden), LOW), shape((2 * pairs, 2 * rows, rows), LOW), shape((rows, width), LOW),
            shape((rows, d_model), LOW), shape((pairs, 8, rows), F32)]
    out_specs = [any_space] * 8 + [
        pl.BlockSpec((2, 2 * rows, block), lambda p, i: (p, 0, i)), pl.BlockSpec((block, 2 * size), lambda p, i: (i, p)),
        any_space, pl.BlockSpec((1, 8, block), lambda p, i: (p, 0, i))]
    scratch = [pltpu.VMEM((ZS, ny, 2, rl, wide), LOW), pltpu.VMEM((rows, d_model), F32), pltpu.VMEM((rows, d_model), LOW),
               pltpu.VMEM((rows, width), LOW), pltpu.VMEM((2 * rows, width), LOW), pltpu.VMEM((2 * rows, width), LOW),
               pltpu.VMEM((2 * rows, 128), LOW), pltpu.VMEM((rows, width), LOW), sem((10,)), sem((2,)), sem((2,)),
               sem((max(heads - 1, 1),)), sem((max(heads - 1, 1),)), sem((pairs, max(heads - 1, 1))), sem((pairs, max(heads - 1, 1)))]
    for _ in range(2 + 2 * halves):
        scratch += gather_sems(ny)
    dims = (ny, heads, rows, width, size, block, pairs, steps_q, halves)
    flops = 2 * rows * d_model * 3 * width + 8 * rows * rows * width
    results = pl.pallas_call(
        partial(forward_kernel, dims),
        grid=(pairs, steps_q),
        out_shape=outs,
        in_specs=[pl.BlockSpec(memory_space=pltpu.SMEM)] + [any_space] * 4 + [pl.BlockSpec(memory_space=pltpu.VMEM)],
        out_specs=out_specs,
        scratch_shapes=scratch,
        compiler_params=pltpu.CompilerParams(collective_id=0, has_side_effects=True, vmem_limit_bytes=60 * 2**20),
        cost_estimate=pl.CostEstimate(flops=flops, bytes_accessed=60 * 2**20, transcendentals=0),
        name="forward_attention",
    )(limits, shard_qkv, shard_out, shard_up, shard_down, tokens)
    n1, q, k, v, full_qkv, full_out, full_up, full_down, probs, context, context_all, inverse = results
    flat = lambda a: a.reshape(d_model, a.shape[-1])
    return n1, q, k, v, flat(full_qkv), flat(full_out), flat(full_up), flat(full_down), probs, context, context_all, inverse


def backward_kernel(size, probs, queries, keys, values, grad, context, inverse, dq, dk, dv, dk_acc, dv_acc):
    part = pl.program_id(1)
    block = grad.shape[0]

    @pl.when(part == 0)
    def _():
        dk_acc[...] = jnp.zeros_like(dk_acc)
        dv_acc[...] = jnp.zeros_like(dv_acc)

    upper = grad[...].astype(F32)
    inner = (upper * context[...].astype(F32)).T
    upper_t = upper.T
    row = lax.broadcasted_iota(jnp.int32, upper_t.shape, 0)
    keys_t = keys[...].T
    pieces = []
    for h in range(2):
        over = inverse[0, h:h + 1]
        shift = jnp.sum(inner[h * size:(h + 1) * size], axis=0, keepdims=True) * over
        scaled = jnp.where(row // size == h, upper_t * over, 0.0)
        dp = dot(values[...], scaled.astype(LOW), 1, 0) - shift
        low = probs[h]
        ds = (low.astype(F32) * dp).astype(LOW)
        dv_acc[...] += dot(low, scaled.T.astype(LOW), 1, 0)
        dk_acc[...] += dot(ds, only_head(queries[...], h, size), 1, 0)
        pieces.append(dot(keys_t, ds, 1, 0)[h * size:(h + 1) * size])
    dq[...] = (jnp.concatenate(pieces, axis=0) * size ** -0.5).T.astype(LOW)

    @pl.when(part == pl.num_programs(1) - 1)
    def _():
        dk[...] = dk_acc[...].astype(LOW)
        dv[...] = dv_acc[...].astype(LOW)


def backward(probs, q, k, v, grad, context, inverse, size):
    rows, width = q.shape
    pairs = width // (2 * size)
    block = min(512, rows)
    spec = pl.BlockSpec
    q_spec = spec((block, 2 * size), lambda p, i: (i, p))
    k_spec = spec((2 * rows, 2 * size), lambda p, i: (0, p))
    shape = jax.ShapeDtypeStruct
    return pl.pallas_call(
        partial(backward_kernel, size),
        grid=(pairs, rows // block),
        out_shape=[shape((rows, width), LOW), shape((2 * rows, width), LOW), shape((2 * rows, width), LOW)],
        in_specs=[spec((2, 2 * rows, block), lambda p, i: (p, 0, i)), q_spec, k_spec, k_spec, q_spec, q_spec,
                  spec((1, 8, block), lambda p, i: (p, 0, i))],
        out_specs=[q_spec, k_spec, k_spec],
        scratch_shapes=[pltpu.VMEM((2 * rows, 2 * size), F32), pltpu.VMEM((2 * rows, 2 * size), F32)],
        compiler_params=pltpu.CompilerParams(vmem_limit_bytes=60 * 2**20),
        cost_estimate=pl.CostEstimate(flops=16 * rows * rows * width, bytes_accessed=50 * 2**20, transcendentals=0),
        name="backward_attention",
    )(probs, q, k, v, grad, context, inverse)


def normed(values, gain, shift):
    centre = values - jnp.mean(values, axis=-1, keepdims=True)
    spread = jnp.mean(centre * centre, axis=-1, keepdims=True)
    return centre * lax.rsqrt(spread + 1e-05) * gain + shift


def mm(spec, a, b):
    return jnp.einsum(spec, a, b, preferred_element_type=F32)


def on_device(n_scene, n_head, tokens, counts, w_qkv, w_out, w_up, w_down, gain_one, shift_one, gain_two, shift_two, cotangent):
    rows, d_model = tokens.shape
    width, hidden = w_qkv.shape[2], w_up.shape[1]
    size = 64
    core, head = lax.axis_index("seq"), lax.axis_index("head")
    limits = jnp.stack([counts[0] - core * rows, counts[0] - (1 - core) * rows]).astype(jnp.int32)
    columns = jnp.pad(jnp.stack([gain_one, shift_one, gain_two, shift_two], axis=1), ((0, 0), (0, 124)))
    shard_qkv = jnp.concatenate([columns, w_qkv[0], w_qkv[1], w_qkv[2]], axis=1)
    n1, q, k, v, full_qkv, full_out, full_up, full_down, probs, context, context_all, inverse = forward(
        limits, shard_qkv, w_out.T, w_up, w_down.T, tokens, n_scene, n_head, size)
    gain_a, shift_a, gain_b, shift_b = list(full_qkv[:, :4].T.astype(F32))
    full_q, full_k, full_v = [full_qkv[:, 128 + i * width:128 + (i + 1) * width] for i in range(3)]
    inputs_f = tokens.astype(F32)
    residual = inputs_f + mm("tf,df->td", context_all, full_out)
    n2 = normed(residual, gain_b, shift_b).astype(LOW)
    up_proj = mm("td,df->tf", n2, full_up)
    activated = jax.nn.gelu(up_proj, approximate=False).astype(LOW)
    output = residual + exchange(mm("tf,df->td", activated, full_down), n_head)
    grad_act = mm("td,df->tf", cotangent, full_down)
    _, gelu_pull = jax.vjp(partial(jax.nn.gelu, approximate=False), up_proj)
    grad_up_low = gelu_pull(grad_act)[0].astype(LOW)
    norm_two_part = mm("tf,df->td", grad_up_low, full_up)
    grad_up = mm("td,tf->df", n2, grad_up_low)
    grad_down = mm("td,tf->df", cotangent, activated)
    _, pull_two = jax.vjp(normed, residual, gain_b, shift_b)
    resid_piece, grad_gain_two, grad_shift_two = pull_two(exchange(norm_two_part, n_head))
    grad_resid = cotangent.astype(F32) + resid_piece
    grad_resid_low = grad_resid.astype(LOW)
    own_out = lax.dynamic_slice(full_out, (0, head * width), (d_model, width))
    grad_outproj = mm("td,tf->df", grad_resid_low, context)
    grad_context = mm("td,df->tf", grad_resid_low, own_out).astype(LOW)
    dq, dk, dv = backward(probs, q, k, v, grad_context, context, inverse, size)
    other = lax.ppermute(jnp.stack([dk[rows:], dv[rows:]]), "seq", [(0, 1), (1, 0)])
    gk = (dk[:rows].astype(F32) + other[0].astype(F32)).astype(LOW)
    gv = (dv[:rows].astype(F32) + other[1].astype(F32)).astype(LOW)
    norm_one_part = mm("tf,df->td", dq, full_q) + mm("tf,df->td", gk, full_k) + mm("tf,df->td", gv, full_v)
    grad_q, grad_k, grad_v = [mm("td,tf->df", n1, g).astype(LOW) for g in (dq, gk, gv)]
    _, pull_one = jax.vjp(normed, inputs_f, gain_a, shift_a)
    input_piece, grad_gain_one, grad_shift_one = pull_one(exchange(norm_one_part, n_head))
    tokens_grad = grad_resid + input_piece
    norm_grads = jnp.pad(jnp.stack([grad_gain_one, grad_shift_one, grad_gain_two, grad_shift_two], axis=1), ((0, 0), (0, 124)))
    parts = jnp.concatenate([norm_grads.astype(LOW), grad_q, grad_k, grad_v, grad_outproj.astype(LOW), grad_up.astype(LOW),
                             grad_down.astype(LOW)], axis=1)
    mine = scatter_all(parts, n_scene, column_groups(width, hidden))
    norms, mine_q, mine_k, mine_v, mine_out, mine_up, mine_down = split_columns(mine, width, hidden)
    return (output, tokens_grad, jnp.stack([mine_q, mine_k, mine_v]), mine_out.T, mine_up, mine_down.T,
            norms[:, 0], norms[:, 1], norms[:, 2], norms[:, 3])


def solution(mesh):
    rows, both = ("scene", "seq"), P(("scene", "seq"))
    weights = (P(None, rows, "head"), P("head", rows), P(rows, "head"), P("head", rows), both, both, both, both)
    return jax.shard_map(
        partial(on_device, mesh.shape["scene"], mesh.shape["head"]), mesh=mesh,
        in_specs=(P(rows, None), P("scene"), *weights, P(rows, None)),
        out_specs=(P(rows, None), P(rows, None), *weights),
        check_vma=False,
    )
```

```python
from functools import partial

import jax
import jax.numpy as jnp
from jax import lax
from jax.experimental import pallas as pl
from jax.experimental.pallas import tpu as pltpu
from jax.sharding import PartitionSpec as P

MESH = pl.DeviceIdType.MESH
ZS = 4


def place(ny):
    scene = lax.axis_index("scene")
    return scene // ny, scene % ny, lax.axis_index("seq")


def remote(src, dst, send_sem, recv_sem, device):
    return pltpu.make_async_remote_copy(
        src_ref=src, dst_ref=dst, send_sem=send_sem, recv_sem=recv_sem,
        device_id=device, device_id_type=MESH,
    )


def exchange(part, heads):
    low = part.astype(jnp.bfloat16)
    total = part
    for step in range(1, heads):
        moved = lax.ppermute(low, "head", [(i, (i + step) % heads) for i in range(heads)])
        total = total + moved.astype(jnp.float32)
    return total


F32 = jnp.float32
LOW = jnp.bfloat16


def dot(a, b, ca, cb):
    return lax.dot_general(a, b, (((ca,), (cb,)), ((), ())), preferred_element_type=F32)


def only_head(x, h, size):
    lane = lax.broadcasted_iota(jnp.int32, x.shape, 1)
    return jnp.where(lane // size == h, x, jnp.zeros_like(x))


class Gather:
    def __init__(self, ny, source, full, cols, sems):
        self.ny, self.source, self.full, self.cols = ny, source, full, cols
        self.rsend, self.rrecv, self.lsend, self.lrecv, self.ysend, self.yrecv, self.csend, self.crecv = sems
        self.z, self.y, self.core = place(ny)

    def at(self, zz, yy):
        return self.full.at[zz, yy, self.core, :, self.cols]

    def right(self, k):
        src = self.source() if k == 0 else self.at(self.z - k, self.y)
        dst = self.at(self.z - k, self.y)
        return remote(src, dst, self.rsend.at[k], self.rrecv.at[k], {"scene": (self.z + 1) * self.ny + self.y})

    def left(self, k):
        src = self.source() if k == 0 else self.at(self.z + k, self.y)
        dst = self.at(self.z + k, self.y)
        return remote(src, dst, self.lsend.at[k], self.lrecv.at[k], {"scene": (self.z - 1) * self.ny + self.y})

    def across(self, zz, step, own=False):
        src = self.source() if own else self.at(zz, self.y)
        peer = self.z * self.ny + (self.y + step) % self.ny
        return remote(src, self.at(zz, self.y), self.ysend.at[zz, step - 1], self.yrecv.at[zz, step - 1], {"scene": peer})

    def arrival(self, zz, step):
        yy = (self.y + self.ny - step) % self.ny
        return remote(self.at(zz, yy), self.at(zz, yy), self.ysend.at[zz, step - 1], self.yrecv.at[zz, step - 1],
                      {"scene": self.z * self.ny + yy})

    def twin(self, zz, step, own=False):
        src = self.source() if own else self.at(zz, (self.y + self.ny - step) % self.ny)
        dst = self.at(zz, (self.y + self.ny - step) % self.ny)
        return remote(src, dst, self.csend.at[zz, step], self.crecv.at[zz, step], {"seq": 1 - self.core})

    def begin(self):
        @pl.when(self.z < ZS - 1)
        def _():
            self.right(0).start()

        @pl.when(self.z > 0)
        def _():
            self.left(0).start()

        for step in range(1, self.ny):
            self.across(self.z, step, True).start()
        self.twin(self.z, 0, True).start()

    def hop(self, k):
        @pl.when(self.z >= k)
        def _():
            self.right(k - 1).wait_recv()
            if k < ZS - 1:
                @pl.when(self.z < ZS - 1)
                def _():
                    self.right(k).start()
            for step in range(1, self.ny):
                self.across(self.z - k, step).start()
            self.twin(self.z - k, 0).start()

        @pl.when(self.z + k < ZS)
        def _():
            self.left(k - 1).wait_recv()
            if k < ZS - 1:
                @pl.when(self.z > 0)
                def _():
                    self.left(k).start()
            for step in range(1, self.ny):
                self.across(self.z + k, step).start()
            self.twin(self.z + k, 0).start()

    def spread(self):
        for step in range(1, self.ny):
            for zz in range(ZS):
                self.arrival(zz, step).wait_recv()
                self.twin(zz, step).start()

    def finish(self):
        for k in range(ZS - 1):
            @pl.when((self.z < ZS - 1) & (self.z >= k))
            def _():
                self.right(k).wait_send()

            @pl.when((self.z > 0) & (self.z + k < ZS))
            def _():
                self.left(k).wait_send()
        for zz in range(ZS):
            for step in range(1, self.ny):
                self.arrival(zz, step).wait_send()
            for step in range(self.ny):
                self.twin(zz, step).wait()


def gather_sems(ny):
    sem = pltpu.SemaphoreType.DMA
    return [sem((ZS - 1,)), sem((ZS - 1,)), sem((ZS - 1,)), sem((ZS - 1,)), sem((ZS, max(ny - 1, 1))), sem((ZS, max(ny - 1, 1))),
            sem((ZS, ny)), sem((ZS, ny))]


def greet_all(ny, heads):
    z, y, core = place(ny)
    head = lax.axis_index("head")
    barrier = pltpu.get_barrier_semaphore()

    def signal(device):
        pl.semaphore_signal(barrier, 1, device_id=device, device_id_type=MESH)

    for step in range(1, ZS):
        signal({"scene": (z + step) % ZS * ny + y})
    for step in range(1, ny):
        signal({"scene": z * ny + (y + step) % ny})
    for step in range(1, heads):
        signal({"head": (head + step) % heads})
    signal({"seq": 1 - core})
    pl.semaphore_wait(barrier, ZS + ny - 1 + heads - 1)


def split_cols(total, parts):
    size = total // parts
    return [pl.ds(i * size, size) for i in range(parts)]


def forward_kernel(dims, limits, shard_qkv, shard_out, shard_up, shard_down, tokens,
                   n1_out, q_out, k_out, v_out, full_qkv, full_out, full_up, full_down, probs, context, context_all, inverse,
                   w0, hat, n1, q_s, k_s, v_s, bias, ctx_s, local_sem, kv_send, kv_recv, xw_send, xw_recv, xc_send, xc_recv, *sems):
    ny, heads, rows, width, size, block, pairs, steps_q, halves = dims
    pair, part = pl.program_id(0), pl.program_id(1)
    step = pair * steps_q + part
    z, y, core = place(ny)
    head = lax.axis_index("head")
    d_model = tokens.shape[1]
    per = 8
    own_cols = pl.ds(pl.multiple_of(head * width, width), width)

    def of(i):
        return sems[i * per:(i + 1) * per]

    first = Gather(ny, lambda: shard_qkv, w0, slice(None), of(0))
    others = [Gather(ny, lambda: full_out.at[z, y, core], full_out, slice(None), of(1))]
    for n, (shard, full) in enumerate(((shard_up, full_up), (shard_down, full_down))):
        for i, cols in enumerate(split_cols(full_up.shape[-1], halves)):
            others.append(Gather(ny, partial(lambda s, c: s.at[:, c], shard, cols), full, cols, of(2 + n * halves + i)))

    def local(src, dst, i):
        return pltpu.make_async_copy(src, dst, local_sem.at[i])

    def out_copy(step):
        return remote(shard_out, full_out.at[z, y, core, :, own_cols], xw_send.at[step - 1], xw_recv.at[step - 1],
                      {"head": (head + step) % heads})

    def kv_copy(i):
        src = (k_s, v_s)[i]
        return remote(src.at[pl.ds(0, rows)], src.at[pl.ds(rows, rows)], kv_send.at[i], kv_recv.at[i], {"seq": 1 - core})

    def ctx_copy(p, step):
        cols = pl.ds(pl.multiple_of(p * 2 * size, 2 * size), 2 * size)
        wide = pl.ds(pl.multiple_of(head * width + p * 2 * size, 2 * size), 2 * size)
        return remote(ctx_s.at[:, cols], context_all.at[:, wide], xc_send.at[p, step - 1], xc_recv.at[p, step - 1],
                      {"head": (head + step) % heads})

    own_blocks = [(shard_qkv, w0.at[z, y, core], 0), (shard_out, full_out.at[z, y, core, :, own_cols], 1),
                  (shard_up, full_up.at[z, y, core], 2), (shard_down, full_down.at[z, y, core], 3)]
    results = [(w0, full_qkv, 4), (n1, n1_out, 5), (q_s, q_out, 6), (k_s, k_out, 7), (v_s, v_out, 8)]
    ctx_local = (ctx_s, context_all.at[:, own_cols], 9)

    @pl.when(step == 0)
    def _():
        for item in own_blocks:
            local(*item).start()
        greet_all(ny, heads)
        first.begin()
        for i in range(1, heads):
            out_copy(i).start()
        tile = min(128, rows)

        @pl.loop(0, rows // tile)
        def _(i):
            at = pl.ds(pl.multiple_of(i * tile, tile), tile)
            x = tokens[at].astype(F32)
            centre = x - jnp.mean(x, axis=1, keepdims=True)
            spread = jnp.mean(centre * centre, axis=1, keepdims=True)
            hat[at] = centre * lax.rsqrt(spread + 1e-05)

        low_rows = lax.broadcasted_iota(jnp.int32, bias.shape, 0)
        lane = lax.broadcasted_iota(jnp.int32, bias.shape, 1)
        limit = jnp.where(low_rows < rows, limits[0], limits[1] + rows)
        bias[...] = jnp.where((low_rows >= limit) & (lane == 0), -1e30, 0.0).astype(LOW)
        first.hop(1)
        first.hop(2)
        first.hop(3)
        local(*own_blocks[1]).wait()
        for i in range(1, heads):
            out_copy(i).wait_recv()
        others[0].begin()
        others[1].begin()
        first.spread()
        for item in (own_blocks[0], own_blocks[2], own_blocks[3]):
            local(*item).wait()
        first.finish()
        local(*results[0]).start()
        norms = w0[:, :, :, :, :128].reshape(d_model, 128).astype(F32).T
        gain, shift = norms[0:1], norms[1:2]
        tile = min(256, rows)

        @pl.loop(0, rows // tile)
        def _(i):
            at = pl.ds(pl.multiple_of(i * tile, tile), tile)
            n1[at] = (hat[at] * gain + shift).astype(LOW)

        for c, dst in ((1, k_s), (2, v_s), (0, q_s)):
            @pl.loop(0, rows // tile)
            def _(i):
                at = pl.ds(pl.multiple_of(i * tile, tile), tile)
                w = w0[:, :, :, :, 128 + c * width:128 + (c + 1) * width].reshape(d_model, width)
                value = dot(n1[at], w, 1, 0).astype(LOW)
                dst[at] = value * LOW(size ** -0.5) if c == 0 else value

            if c:
                kv_copy(c - 1).start()
        for item in results[1:3]:
            local(*item).start()
        kv_copy(0).wait()
        kv_copy(1).wait()
        for item in results[3:]:
            local(*item).start()

    total = pairs * steps_q
    slots = 2 * total
    events = []
    n = len(others)
    for g in range(n):
        events += [(1.0 + g * 2.6, others[g], 1), (2.0 + g * 2.6, others[g], 2), (3.0 + g * 2.6, others[g], 3), (4.6 + g * 2.6, others[g], 4)]
        if g + 2 < n:
            events.append((1.5 + g * 2.6, others[g + 2], 0))
    events.sort(key=lambda item: item[0])
    last = max(item[0] for item in events) + 1

    def run(slot_in_step):
        for when, gather, what in events:
            slot = min(int(when * min(1.0, slots / 16)), slots - 1)
            if slot % 2 != slot_in_step:
                continue

            @pl.when(step == slot // 2)
            def _():
                if what == 0:
                    gather.begin()
                elif what < 4:
                    gather.hop(what)
                else:
                    gather.spread()

    queries = q_s[pl.ds(pl.multiple_of(part * block, block), block), pl.ds(pl.multiple_of(pair * 2 * size, 2 * size), 2 * size)]
    cols = pl.ds(pl.multiple_of(pair * 2 * size, 2 * size), 2 * size)
    keys = jnp.concatenate([k_s[:, cols], bias[...]], axis=1)
    values_t = v_s[:, cols].T
    ones = (lax.broadcasted_iota(jnp.int32, (block, bias.shape[1]), 1) == 0).astype(LOW)
    pieces = []
    for h in range(2):
        run(h)
        scores = dot(keys, jnp.concatenate([only_head(queries, h, size), ones], axis=1), 1, 1)
        top = jnp.max(scores, axis=0, keepdims=True)
        expo = jnp.exp(scores - top)
        over = 1.0 / jnp.sum(expo, axis=0, keepdims=True)
        low = expo.astype(LOW)
        probs[h] = low
        pieces.append(dot(values_t, low, 1, 0)[h * size:(h + 1) * size] * over)
        inverse[0, h:h + 1] = over
    here = jnp.concatenate(pieces, axis=0).T.astype(LOW)
    context[...] = here
    ctx_s[pl.ds(pl.multiple_of(part * block, block), block), cols] = here

    @pl.when(part == steps_q - 1)
    def _():
        for i in range(1, heads):
            ctx_copy(pair, i).start()

    @pl.when(step == total - 1)
    def _():
        local(*ctx_local).start()
        for gather in others:
            gather.finish()
        for item in results:
            local(*item).wait()
        local(*ctx_local).wait()
        for i in range(1, heads):
            out_copy(i).wait_send()
            for p in range(pairs):
                ctx_copy(p, i).wait()


def forward(limits, shard_qkv, shard_out, shard_up, shard_down, tokens, scenes, heads, size):
    ny = scenes // ZS
    rows, d_model = tokens.shape
    rl, width = shard_out.shape
    hidden = shard_up.shape[1]
    pairs = width // (2 * size)
    block = min(512, rows)
    steps_q = rows // block
    halves = 2
    sem = pltpu.SemaphoreType.DMA
    any_space = pl.BlockSpec(memory_space=pl.ANY)
    shape = jax.ShapeDtypeStruct
    wide = shard_qkv.shape[1]
    outs = [shape((rows, d_model), LOW), shape((rows, width), LOW), shape((2 * rows, width), LOW), shape((2 * rows, width), LOW),
            shape((ZS, ny, 2, rl, wide), LOW), shape((ZS, ny, 2, rl, d_model), LOW), shape((ZS, ny, 2, rl, hidden), LOW),
            shape((ZS, ny, 2, rl, hidden), LOW), shape((2 * pairs, 2 * rows, rows), LOW), shape((rows, width), LOW),
            shape((rows, d_model), LOW), shape((pairs, 8, rows), F32)]
    out_specs = [any_space] * 8 + [
        pl.BlockSpec((2, 2 * rows, block), lambda p, i: (p, 0, i)), pl.BlockSpec((block, 2 * size), lambda p, i: (i, p)),
        any_space, pl.BlockSpec((1, 8, block), lambda p, i: (p, 0, i))]
    scratch = [pltpu.VMEM((ZS, ny, 2, rl, wide), LOW), pltpu.VMEM((rows, d_model), F32), pltpu.VMEM((rows, d_model), LOW),
               pltpu.VMEM((rows, width), LOW), pltpu.VMEM((2 * rows, width), LOW), pltpu.VMEM((2 * rows, width), LOW),
               pltpu.VMEM((2 * rows, 128), LOW), pltpu.VMEM((rows, width), LOW), sem((10,)), sem((2,)), sem((2,)),
               sem((max(heads - 1, 1),)), sem((max(heads - 1, 1),)), sem((pairs, max(heads - 1, 1))), sem((pairs, max(heads - 1, 1)))]
    for _ in range(2 + 2 * halves):
        scratch += gather_sems(ny)
    dims = (ny, heads, rows, width, size, block, pairs, steps_q, halves)
    flops = 2 * rows * d_model * 3 * width + 8 * rows * rows * width
    results = pl.pallas_call(
        partial(forward_kernel, dims),
        grid=(pairs, steps_q),
        out_shape=outs,
        in_specs=[pl.BlockSpec(memory_space=pltpu.SMEM)] + [any_space] * 4 + [pl.BlockSpec(memory_space=pltpu.VMEM)],
        out_specs=out_specs,
        scratch_shapes=scratch,
        compiler_params=pltpu.CompilerParams(collective_id=0, has_side_effects=True, vmem_limit_bytes=60 * 2**20),
        cost_estimate=pl.CostEstimate(flops=flops, bytes_accessed=60 * 2**20, transcendentals=0),
        name="forward_attention",
    )(limits, shard_qkv, shard_out, shard_up, shard_down, tokens)
    n1, q, k, v, full_qkv, full_out, full_up, full_down, probs, context, context_all, inverse = results
    flat = lambda a: a.reshape(d_model, a.shape[-1])
    return n1, q, k, v, flat(full_qkv), flat(full_out), flat(full_up), flat(full_down), probs, context, context_all, inverse


class Scatter:
    def __init__(self, ny, parts, cols, bufs, sems):
        self.ny, self.parts, self.cols = ny, parts, cols
        self.own, self.from_core, self.from_y, self.sum_two, self.from_z = bufs
        self.load_sem, self.csend, self.crecv, self.ysend, self.yrecv, self.zsend, self.zrecv = sems
        self.z, self.y, self.core = place(ny)

    def load(self):
        return pltpu.make_async_copy(self.parts.at[:, :, self.core, :, self.cols], self.own, self.load_sem.at[0])

    def to_core(self):
        return remote(self.parts.at[:, :, 1 - self.core, :, self.cols], self.from_core, self.csend.at[0], self.crecv.at[0],
                      {"seq": 1 - self.core})

    def to_y(self, step):
        yy = (self.y + step) % self.ny
        return remote(self.own.at[:, yy], self.from_y.at[step - 1], self.ysend.at[step - 1], self.yrecv.at[step - 1],
                      {"scene": self.z * self.ny + yy})

    def to_z(self, step):
        zz = (self.z + step) % ZS
        return remote(self.sum_two.at[zz], self.from_z.at[step - 1], self.zsend.at[step - 1], self.zrecv.at[step - 1],
                      {"scene": zz * self.ny + self.y})

    def begin(self):
        self.load().start()
        self.to_core().start()

    def one(self):
        self.load().wait()
        self.to_core().wait_recv()
        for zz in range(ZS):
            for yy in range(self.ny):
                self.own[zz, yy] = (self.own[zz, yy].astype(F32) + self.from_core[zz, yy].astype(F32)).astype(LOW)
        for step in range(1, self.ny):
            self.to_y(step).start()

    def two(self):
        for step in range(1, self.ny):
            self.to_y(step).wait_recv()
        for zz in range(ZS):
            total = self.own[zz, self.y].astype(F32)
            for step in range(1, self.ny):
                total += self.from_y[step - 1, zz].astype(F32)
            self.sum_two[zz] = total.astype(LOW)
        for step in range(1, ZS):
            self.to_z(step).start()

    def three(self, out):
        for step in range(1, ZS):
            self.to_z(step).wait_recv()
        total = self.sum_two[self.z].astype(F32)
        for step in range(1, ZS):
            total += self.from_z[step - 1].astype(F32)
        out[:, self.cols] = total

    def finish(self):
        self.to_core().wait_send()
        for step in range(1, self.ny):
            self.to_y(step).wait_send()
        for step in range(1, ZS):
            self.to_z(step).wait_send()


SCATTER_BUFS, SCATTER_SEMS = 5, 7


def scatter_scratch(ny, rl, cols):
    sem = pltpu.SemaphoreType.DMA
    other = max(ny - 1, 1)
    return [pltpu.VMEM((ZS, ny, rl, cols), LOW), pltpu.VMEM((ZS, ny, rl, cols), LOW), pltpu.VMEM((other, ZS, rl, cols), LOW),
            pltpu.VMEM((ZS, rl, cols), LOW), pltpu.VMEM((ZS - 1, rl, cols), LOW),
            sem((1,)), sem((1,)), sem((1,)), sem((other,)), sem((other,)), sem((ZS - 1,)), sem((ZS - 1,))]


def make_scatters(ny, plan, scratch):
    n = SCATTER_BUFS + SCATTER_SEMS
    result = []
    for i, (parts, cols) in enumerate(plan):
        mine = scratch[i * n:(i + 1) * n]
        result.append(Scatter(ny, parts, cols, mine[:SCATTER_BUFS], mine[SCATTER_BUFS:]))
    return result


def backward_kernel(dims, probs, queries, keys, values, grad, context, inverse, parts_out, parts_up,
                    dq, gk, gv, mine_out, mine_up,
                    dk_acc, dv_acc, kept, stage, landed, kv_send, kv_recv, *scratch):
    ny, heads, rows, size, pairs, steps_q, halves = dims
    pair, part = pl.program_id(0), pl.program_id(1)
    step = pair * steps_q + part
    total = pairs * steps_q
    block = grad.shape[0]
    z, y, core = place(ny)
    width = parts_out.shape[-1]
    plan = [(parts_out, pl.ds(0, width))] + [(parts_up, cols) for cols in split_cols(parts_up.shape[-1], halves)]
    scatters = make_scatters(ny, plan, scratch)
    targets = [mine_out] + [mine_up] * halves

    def kv_copy(p, i):
        return remote(stage.at[p, i], landed.at[p, i], kv_send.at[p, i], kv_recv.at[p, i], {"seq": 1 - core})

    @pl.when(step == 0)
    def _():
        greet_all(ny, 1)
        for item in scatters:
            item.begin()

    slots = 2 * total
    events = []
    for i in range(len(scatters)):
        events += [(1.2 + i * 2.5, i, 1), (4.0 + i * 4.0, i, 2), (8.0 + i * 4.0, i, 3)]
    events.sort()

    def run(slot_in_step):
        for when, i, what in events:
            slot = min(int(when * min(1.0, slots / 16)), slots)
            if slot == slots or slot % 2 != slot_in_step:
                continue

            @pl.when(step == slot // 2)
            def _():
                if what == 1:
                    scatters[i].one()
                elif what == 2:
                    scatters[i].two()
                else:
                    scatters[i].three(targets[i])

    @pl.when(part == 0)
    def _():
        dk_acc[...] = jnp.zeros_like(dk_acc)
        dv_acc[...] = jnp.zeros_like(dv_acc)

    upper = grad[...].astype(F32)
    inner = (upper * context[...].astype(F32)).T
    upper_t = upper.T
    row = lax.broadcasted_iota(jnp.int32, upper_t.shape, 0)
    keys_t = keys[...].T
    pieces = []
    for h in range(2):
        run(h)
        over = inverse[0, h:h + 1]
        shift = jnp.sum(inner[h * size:(h + 1) * size], axis=0, keepdims=True) * over
        scaled = jnp.where(row // size == h, upper_t * over, 0.0)
        dp = dot(values[...], scaled.astype(LOW), 1, 0) - shift
        low = probs[h]
        ds = (low.astype(F32) * dp).astype(LOW)
        dv_acc[...] += dot(low, scaled.T.astype(LOW), 1, 0)
        dk_acc[...] += dot(ds, only_head(queries[...], h, size), 1, 0)
        pieces.append(dot(keys_t, ds, 1, 0)[h * size:(h + 1) * size])
    dq[...] = (jnp.concatenate(pieces, axis=0) * size ** -0.5).T.astype(LOW)

    @pl.when(part == steps_q - 1)
    def _():
        for i, acc in enumerate((dk_acc, dv_acc)):
            stage[pair, i] = acc[rows:].astype(LOW)
            kv_copy(pair, i).start()
            kept[pair, i] = acc[:rows]

    @pl.when(step == total - 1)
    def _():
        for when, i, what in events:
            if min(int(when * min(1.0, slots / 16)), slots) == slots:
                if what == 1:
                    scatters[i].one()
                elif what == 2:
                    scatters[i].two()
                else:
                    scatters[i].three(targets[i])
        for item in scatters:
            item.finish()
        for p in range(pairs):
            for i, dst in enumerate((gk, gv)):
                kv_copy(p, i).wait()
                dst[:, p * 2 * size:(p + 1) * 2 * size] = (kept[p, i] + landed[p, i].astype(F32)).astype(LOW)


def backward(probs, q, k, v, grad, context, inverse, parts_out, parts_up, scenes, size):
    ny = scenes // ZS
    rows, width = q.shape
    pairs = width // (2 * size)
    block = min(512, rows)
    d_model, hidden = parts_up.shape
    rl = d_model // (2 * scenes)
    halves = 2
    spec = pl.BlockSpec
    q_spec = spec((block, 2 * size), lambda p, i: (i, p))
    k_spec = spec((2 * rows, 2 * size), lambda p, i: (0, p))
    any_space = spec(memory_space=pl.ANY)
    whole = spec(memory_space=pltpu.VMEM)
    shape = jax.ShapeDtypeStruct
    sem = pltpu.SemaphoreType.DMA
    pair_buf = (pairs, 2, rows, 2 * size)
    scratch = [pltpu.VMEM((2 * rows, 2 * size), F32), pltpu.VMEM((2 * rows, 2 * size), F32), pltpu.VMEM(pair_buf, F32),
               pltpu.VMEM(pair_buf, LOW), pltpu.VMEM(pair_buf, LOW), sem((pairs, 2)), sem((pairs, 2))]
    scratch += scatter_scratch(ny, rl, width)
    for _ in range(halves):
        scratch += scatter_scratch(ny, rl, hidden // halves)
    return pl.pallas_call(
        partial(backward_kernel, (ny, 1, rows, size, pairs, rows // block, halves)),
        grid=(pairs, rows // block),
        out_shape=[shape((rows, width), LOW), shape((rows, width), LOW), shape((rows, width), LOW), shape((rl, width), F32),
                   shape((rl, hidden), F32)],
        in_specs=[spec((2, 2 * rows, block), lambda p, i: (p, 0, i)), q_spec, k_spec, k_spec, q_spec, q_spec,
                  spec((1, 8, block), lambda p, i: (p, 0, i)), any_space, any_space],
        out_specs=[q_spec, whole, whole, whole, whole],
        scratch_shapes=scratch,
        compiler_params=pltpu.CompilerParams(collective_id=1, has_side_effects=True, vmem_limit_bytes=60 * 2**20),
        cost_estimate=pl.CostEstimate(flops=16 * rows * rows * width, bytes_accessed=50 * 2**20, transcendentals=0),
        name="backward_attention",
    )(probs, q, k, v, grad, context, inverse, parts_out.reshape(ZS, ny, 2, rl, width), parts_up.reshape(ZS, ny, 2, rl, hidden))


def last_kernel(dims, gq, gk, gv, n1, tokens, resid, full_qkv, norm_two, parts_down,
                tokens_grad, mine_qkv, mine_down,
                part_one, part_low, arrived, parts_qkv, norm_land, norm_own, out_v, x_send, x_recv, n_send, n_recv, out_sem, *scratch):
    ny, heads, rows, d_model, width, tile, halves = dims
    z, y, core = place(ny)
    head = lax.axis_index("head")
    hidden = parts_down.shape[-1]
    wide = full_qkv.shape[1]
    rl = mine_qkv.shape[0]
    plan = [(parts_down, cols) for cols in split_cols(hidden, halves)] + [(parts_qkv, pl.ds(0, wide))]
    scatters = make_scatters(ny, plan, scratch)
    targets = [mine_down] * halves + [mine_qkv]
    chunks = rows // tile

    def x_copy(i, step):
        at = pl.ds(i * tile, tile)
        return remote(part_low.at[at], arrived.at[step - 1, at], x_send.at[i, step - 1], x_recv.at[i, step - 1],
                      {"head": (head + step) % heads})

    def n_copy(step):
        return remote(norm_own, norm_land.at[step - 1], n_send.at[step - 1], n_recv.at[step - 1], {"head": (head + step) % heads})

    def out_copy(i):
        at = pl.ds(i * tile, tile)
        return pltpu.make_async_copy(out_v.at[at], tokens_grad.at[at], out_sem.at[i])

    greet_all(ny, heads)
    for item in scatters[:halves]:
        item.begin()
    for i in range(chunks):
        at = pl.ds(i * tile, tile)
        total = jnp.zeros((tile, d_model), F32)
        for c, g in enumerate((gq, gk, gv)):
            total += dot(g[at], full_qkv[:, 128 + c * width:128 + (c + 1) * width], 1, 1)
        part_one[at] = total
        part_low[at] = total.astype(LOW)
        for step in range(1, heads):
            x_copy(i, step).start()
    for item in scatters[:halves]:
        item.one()
    gain = full_qkv[:, :128].astype(F32).T[0:1]

    def hat_of(at):
        x = tokens[at].astype(F32)
        centre = x - jnp.mean(x, axis=1, keepdims=True)
        spread = lax.rsqrt(jnp.mean(centre * centre, axis=1, keepdims=True) + 1e-05)
        return centre * spread, spread

    gain_sum = jnp.zeros((1, d_model), F32)
    shift_sum = jnp.zeros((1, d_model), F32)
    for i in range(chunks):
        at = pl.ds(i * tile, tile)
        hat, _ = hat_of(at)
        gain_sum += jnp.sum(part_one[at] * hat, axis=0, keepdims=True)
        shift_sum += jnp.sum(part_one[at], axis=0, keepdims=True)
    sums = jnp.concatenate([gain_sum, shift_sum, norm_two[...], jnp.zeros((4, d_model), F32)], axis=0)
    sums = jnp.concatenate([sums, jnp.zeros((120, d_model), F32)], axis=0).T.astype(LOW)
    parts_qkv[:, :, :, :, :128] = sums.reshape(ZS, ny, 2, rl, 128)
    per_z = d_model // ZS
    for zz in range(ZS):
        cols = n1[:, zz * per_z:(zz + 1) * per_z]
        for c, g in enumerate((gq, gk, gv)):
            value = dot(cols, g[...], 0, 0).astype(LOW)
            parts_qkv[zz, :, :, :, 128 + c * width:128 + (c + 1) * width] = value.reshape(ny, 2, rl, width)
    scatters[halves].begin()
    scatters[0].two()
    scatters[halves].one()
    scatters[1].two()

    def receive(i):
        at = pl.ds(i * tile, tile)
        total = part_one[at]
        for step in range(1, heads):
            x_copy(i, step).wait_recv()
            total += arrived[step - 1, at].astype(F32)
        hat, spread = hat_of(at)
        scaled = total * gain
        inner = scaled - jnp.mean(scaled, axis=1, keepdims=True) - hat * jnp.mean(scaled * hat, axis=1, keepdims=True)
        out_v[at] = resid[at] + inner * spread
        out_copy(i).start()

    half = chunks // 2
    for i in range(half):
        receive(i)
    scatters[0].three(targets[0])
    scatters[1].three(targets[1])
    scatters[halves].two()
    for i in range(half, chunks - 1):
        receive(i)
    scatters[halves].three(targets[halves])
    norm_own[...] = mine_qkv[:, :128]
    for step in range(1, heads):
        n_copy(step).start()
    receive(chunks - 1)
    total = mine_qkv[:, :128]
    for step in range(1, heads):
        n_copy(step).wait()
        total += norm_land[step - 1]
    mine_qkv[:, :128] = total
    for item in scatters:
        item.finish()
    for i in range(chunks):
        out_copy(i).wait()
        for step in range(1, heads):
            x_copy(i, step).wait_send()


def last_stage(gq, gk, gv, n1, tokens, resid, full_qkv, norm_two, parts_down, scenes, heads):
    ny = scenes // ZS
    rows, d_model = tokens.shape
    width, hidden = gq.shape[1], parts_down.shape[1]
    rl = d_model // (2 * scenes)
    wide = full_qkv.shape[1]
    tile = min(128, rows)
    chunks = rows // tile
    halves = 2
    others = max(heads - 1, 1)
    sem = pltpu.SemaphoreType.DMA
    shape = jax.ShapeDtypeStruct
    any_space, whole = pl.BlockSpec(memory_space=pl.ANY), pl.BlockSpec(memory_space=pltpu.VMEM)
    scratch = [pltpu.VMEM((rows, d_model), F32), pltpu.VMEM((rows, d_model), LOW), pltpu.VMEM((others, rows, d_model), LOW),
               pltpu.VMEM((ZS, ny, 2, rl, wide), LOW), pltpu.VMEM((others, rl, 128), F32), pltpu.VMEM((rl, 128), F32),
               pltpu.VMEM((rows, d_model), F32), sem((chunks, others)), sem((chunks, others)), sem((others,)), sem((others,)),
               sem((chunks,))]
    for _ in range(halves):
        scratch += scatter_scratch(ny, rl, hidden // halves)
    scratch += scatter_scratch(ny, rl, wide)
    return pl.pallas_call(
        partial(last_kernel, (ny, heads, rows, d_model, width, tile, halves)),
        out_shape=[shape((rows, d_model), F32), shape((rl, wide), F32), shape((rl, hidden), F32)],
        in_specs=[whole] * 8 + [any_space],
        out_specs=[any_space, whole, whole],
        scratch_shapes=scratch,
        compiler_params=pltpu.CompilerParams(collective_id=2, has_side_effects=True, vmem_limit_bytes=62 * 2**20),
        cost_estimate=pl.CostEstimate(flops=12 * rows * d_model * width, bytes_accessed=30 * 2**20, transcendentals=0),
        name="last_stage",
    )(gq, gk, gv, n1, tokens, resid, full_qkv, norm_two, parts_down.reshape(ZS, ny, 2, rl, hidden))


def normed(values, gain, shift):
    centre = values - jnp.mean(values, axis=-1, keepdims=True)
    spread = jnp.mean(centre * centre, axis=-1, keepdims=True)
    return centre * lax.rsqrt(spread + 1e-05) * gain + shift


def mm(spec, a, b):
    return jnp.einsum(spec, a, b, preferred_element_type=F32)


def on_device(n_scene, n_head, tokens, counts, w_qkv, w_out, w_up, w_down, gain_one, shift_one, gain_two, shift_two, cotangent):
    rows, d_model = tokens.shape
    width, hidden = w_qkv.shape[2], w_up.shape[1]
    size = 64
    core, head = lax.axis_index("seq"), lax.axis_index("head")
    limits = jnp.stack([counts[0] - core * rows, counts[0] - (1 - core) * rows]).astype(jnp.int32)
    columns = jnp.pad(jnp.stack([gain_one, shift_one, gain_two, shift_two], axis=1), ((0, 0), (0, 124)))
    shard_qkv = jnp.concatenate([columns, w_qkv[0], w_qkv[1], w_qkv[2]], axis=1)
    n1, q, k, v, full_qkv, full_out, full_up, full_down, probs, context, context_all, inverse = forward(
        limits, shard_qkv, w_out.T, w_up, w_down.T, tokens, n_scene, n_head, size)
    gain_a, shift_a, gain_b, shift_b = list(full_qkv[:, :4].T.astype(F32))
    inputs_f = tokens.astype(F32)
    residual = inputs_f + mm("tf,df->td", context_all, full_out)
    n2 = normed(residual, gain_b, shift_b).astype(LOW)
    up_proj = mm("td,df->tf", n2, full_up)
    activated = jax.nn.gelu(up_proj, approximate=False).astype(LOW)
    grad_act = mm("td,df->tf", cotangent, full_down)
    _, gelu_pull = jax.vjp(partial(jax.nn.gelu, approximate=False), up_proj)
    grad_up_low = gelu_pull(grad_act)[0].astype(LOW)
    norm_two_part = mm("tf,df->td", grad_up_low, full_up)
    norm_two_sum = exchange(norm_two_part, n_head)
    grad_up = mm("td,tf->df", n2, grad_up_low).astype(LOW)
    grad_down = mm("td,tf->df", cotangent, activated).astype(LOW)
    _, pull_two = jax.vjp(normed, residual, gain_b, shift_b)
    _, grad_gain_two, grad_shift_two = pull_two(norm_two_part)
    resid_piece, _, _ = pull_two(norm_two_sum)
    grad_resid = cotangent.astype(F32) + resid_piece
    grad_resid_low = grad_resid.astype(LOW)
    own_out = lax.dynamic_slice(full_out, (0, head * width), (d_model, width))
    grad_outproj = mm("td,tf->df", grad_resid_low, context).astype(LOW)
    grad_context = mm("td,df->tf", grad_resid_low, own_out).astype(LOW)
    activated, grad_context = lax.optimization_barrier((activated, grad_context))
    output = residual + exchange(mm("tf,df->td", activated, full_down), n_head)
    gq, gk, gv, mine_out, mine_up = backward(probs, q, k, v, grad_context, context, inverse, grad_outproj, grad_up, n_scene, size)
    norm_two = jnp.stack([grad_gain_two, grad_shift_two])
    tokens_grad, mine_qkv, mine_down = last_stage(
        gq, gk, gv, n1, tokens, grad_resid, full_qkv, norm_two, grad_down, n_scene, n_head)
    mine = [mine_qkv[:, 128 + i * width:128 + (i + 1) * width] for i in range(3)]
    return (output, tokens_grad, jnp.stack(mine), mine_out.T, mine_up, mine_down.T,
            mine_qkv[:, 0], mine_qkv[:, 1], mine_qkv[:, 2], mine_qkv[:, 3])


def solution(mesh):
    rows, both = ("scene", "seq"), P(("scene", "seq"))
    weights = (P(None, rows, "head"), P("head", rows), P(rows, "head"), P("head", rows), both, both, both, both)
    return jax.shard_map(
        partial(on_device, mesh.shape["scene"], mesh.shape["head"]), mesh=mesh,
        in_specs=(P(rows, None), P("scene"), *weights, P(rows, None)),
        out_specs=(P(rows, None), P(rows, None), *weights),
        check_vma=False,
    )
```

```python
from functools import partial

import jax
import jax.numpy as jnp
from jax import lax
from jax.experimental import pallas as pl
from jax.experimental.pallas import tpu as pltpu
from jax.sharding import PartitionSpec as P

MESH = pl.DeviceIdType.MESH
ZS = 4


def place(ny):
    scene = lax.axis_index("scene")
    return scene // ny, scene % ny, lax.axis_index("seq")


def remote(src, dst, send_sem, recv_sem, device):
    return pltpu.make_async_remote_copy(
        src_ref=src, dst_ref=dst, send_sem=send_sem, recv_sem=recv_sem,
        device_id=device, device_id_type=MESH,
    )


def exchange(total, low, heads):
    for step in range(1, heads):
        moved = lax.ppermute(low, "head", [(i, (i + step) % heads) for i in range(heads)])
        total = total + moved.astype(jnp.float32)
    return total


F32 = jnp.float32
LOW = jnp.bfloat16


def dot(a, b, ca, cb):
    return lax.dot_general(a, b, (((ca,), (cb,)), ((), ())), preferred_element_type=F32)


def only_head(x, h, size):
    lane = lax.broadcasted_iota(jnp.int32, x.shape, 1)
    return jnp.where(lane // size == h, x, jnp.zeros_like(x))


class Gather:
    def __init__(self, ny, source, full, cols, sems):
        self.ny, self.source, self.full, self.cols = ny, source, full, cols
        self.rsend, self.rrecv, self.lsend, self.lrecv, self.ysend, self.yrecv, self.csend, self.crecv = sems
        self.z, self.y, self.core = place(ny)

    def at(self, zz, yy):
        return self.full.at[zz, yy, self.core, :, self.cols]

    def right(self, k):
        src = self.source() if k == 0 else self.at(self.z - k, self.y)
        dst = self.at(self.z - k, self.y)
        return remote(src, dst, self.rsend.at[k], self.rrecv.at[k], {"scene": (self.z + 1) * self.ny + self.y})

    def left(self, k):
        src = self.source() if k == 0 else self.at(self.z + k, self.y)
        dst = self.at(self.z + k, self.y)
        return remote(src, dst, self.lsend.at[k], self.lrecv.at[k], {"scene": (self.z - 1) * self.ny + self.y})

    def across(self, zz, step, own=False):
        src = self.source() if own else self.at(zz, self.y)
        peer = self.z * self.ny + (self.y + step) % self.ny
        return remote(src, self.at(zz, self.y), self.ysend.at[zz, step - 1], self.yrecv.at[zz, step - 1], {"scene": peer})

    def arrival(self, zz, step):
        yy = (self.y + self.ny - step) % self.ny
        return remote(self.at(zz, yy), self.at(zz, yy), self.ysend.at[zz, step - 1], self.yrecv.at[zz, step - 1],
                      {"scene": self.z * self.ny + yy})

    def twin(self, zz, step, own=False):
        src = self.source() if own else self.at(zz, (self.y + self.ny - step) % self.ny)
        dst = self.at(zz, (self.y + self.ny - step) % self.ny)
        return remote(src, dst, self.csend.at[zz, step], self.crecv.at[zz, step], {"seq": 1 - self.core})

    def begin(self):
        @pl.when(self.z < ZS - 1)
        def _():
            self.right(0).start()

        @pl.when(self.z > 0)
        def _():
            self.left(0).start()

        for step in range(1, self.ny):
            self.across(self.z, step, True).start()
        self.twin(self.z, 0, True).start()

    def hop(self, k):
        @pl.when(self.z >= k)
        def _():
            self.right(k - 1).wait_recv()
            if k < ZS - 1:
                @pl.when(self.z < ZS - 1)
                def _():
                    self.right(k).start()
            for step in range(1, self.ny):
                self.across(self.z - k, step).start()
            self.twin(self.z - k, 0).start()

        @pl.when(self.z + k < ZS)
        def _():
            self.left(k - 1).wait_recv()
            if k < ZS - 1:
                @pl.when(self.z > 0)
                def _():
                    self.left(k).start()
            for step in range(1, self.ny):
                self.across(self.z + k, step).start()
            self.twin(self.z + k, 0).start()

    def spread(self):
        for step in range(1, self.ny):
            for zz in range(ZS):
                self.arrival(zz, step).wait_recv()
                self.twin(zz, step).start()

    def finish(self):
        for k in range(ZS - 1):
            @pl.when((self.z < ZS - 1) & (self.z >= k))
            def _():
                self.right(k).wait_send()

            @pl.when((self.z > 0) & (self.z + k < ZS))
            def _():
                self.left(k).wait_send()
        for zz in range(ZS):
            for step in range(1, self.ny):
                self.arrival(zz, step).wait_send()
            for step in range(self.ny):
                self.twin(zz, step).wait()


def gather_sems(ny):
    sem = pltpu.SemaphoreType.DMA
    return [sem((ZS - 1,)), sem((ZS - 1,)), sem((ZS - 1,)), sem((ZS - 1,)), sem((ZS, max(ny - 1, 1))), sem((ZS, max(ny - 1, 1))),
            sem((ZS, ny)), sem((ZS, ny))]


def greet_all(ny, heads):
    z, y, core = place(ny)
    head = lax.axis_index("head")
    barrier = pltpu.get_barrier_semaphore()

    def signal(device):
        pl.semaphore_signal(barrier, 1, device_id=device, device_id_type=MESH)

    for step in range(1, ZS):
        signal({"scene": (z + step) % ZS * ny + y})
    for step in range(1, ny):
        signal({"scene": z * ny + (y + step) % ny})
    for step in range(1, heads):
        signal({"head": (head + step) % heads})
    signal({"seq": 1 - core})
    pl.semaphore_wait(barrier, ZS + ny - 1 + heads - 1)


def split_cols(total, parts):
    size = total // parts
    return [pl.ds(i * size, size) for i in range(parts)]


def forward_kernel(dims, limits, shard_qkv, shard_out, shard_up, shard_down, tokens,
                   n1_out, q_out, k_out, v_out, full_qkv, full_out, full_up, full_down, probs, context, context_all, inverse,
                   w0, hat, n1, q_s, k_s, v_s, bias, ctx_s, local_sem, kv_send, kv_recv, xw_send, xw_recv, xc_send, xc_recv, *sems):
    ny, heads, rows, width, size, block, pairs, steps_q, halves = dims
    pair, part = pl.program_id(0), pl.program_id(1)
    step = pair * steps_q + part
    z, y, core = place(ny)
    head = lax.axis_index("head")
    d_model = tokens.shape[1]
    per = 8
    own_cols = pl.ds(pl.multiple_of(head * width, width), width)

    def of(i):
        return sems[i * per:(i + 1) * per]

    first = Gather(ny, lambda: shard_qkv, w0, slice(None), of(0))
    others = [Gather(ny, lambda: full_out.at[z, y, core], full_out, slice(None), of(1))]
    for n, (shard, full) in enumerate(((shard_up, full_up), (shard_down, full_down))):
        for i, cols in enumerate(split_cols(full_up.shape[-1], halves)):
            others.append(Gather(ny, partial(lambda s, c: s.at[:, c], shard, cols), full, cols, of(2 + n * halves + i)))

    def local(src, dst, i):
        return pltpu.make_async_copy(src, dst, local_sem.at[i])

    def out_copy(step):
        return remote(shard_out, full_out.at[z, y, core, :, own_cols], xw_send.at[step - 1], xw_recv.at[step - 1],
                      {"head": (head + step) % heads})

    def kv_copy(i):
        src = (k_s, v_s)[i]
        return remote(src.at[pl.ds(0, rows)], src.at[pl.ds(rows, rows)], kv_send.at[i], kv_recv.at[i], {"seq": 1 - core})

    def ctx_copy(p, step):
        cols = pl.ds(pl.multiple_of(p * 2 * size, 2 * size), 2 * size)
        wide = pl.ds(pl.multiple_of(head * width + p * 2 * size, 2 * size), 2 * size)
        return remote(ctx_s.at[:, cols], context_all.at[:, wide], xc_send.at[p, step - 1], xc_recv.at[p, step - 1],
                      {"head": (head + step) % heads})

    own_blocks = [(shard_qkv, w0.at[z, y, core], 0), (shard_out, full_out.at[z, y, core, :, own_cols], 1),
                  (shard_up, full_up.at[z, y, core], 2), (shard_down, full_down.at[z, y, core], 3)]
    results = [(w0, full_qkv, 4), (n1, n1_out, 5), (q_s, q_out, 6), (k_s, k_out, 7), (v_s, v_out, 8)]
    ctx_local = (ctx_s, context_all.at[:, own_cols], 9)

    @pl.when(step == 0)
    def _():
        for item in own_blocks:
            local(*item).start()
        greet_all(ny, heads)
        first.begin()
        for i in range(1, heads):
            out_copy(i).start()
        tile = min(128, rows)

        @pl.loop(0, rows // tile)
        def _(i):
            at = pl.ds(pl.multiple_of(i * tile, tile), tile)
            x = tokens[at].astype(F32)
            centre = x - jnp.mean(x, axis=1, keepdims=True)
            spread = jnp.mean(centre * centre, axis=1, keepdims=True)
            hat[at] = centre * lax.rsqrt(spread + 1e-05)

        low_rows = lax.broadcasted_iota(jnp.int32, bias.shape, 0)
        lane = lax.broadcasted_iota(jnp.int32, bias.shape, 1)
        limit = jnp.where(low_rows < rows, limits[0], limits[1] + rows)
        bias[...] = jnp.where((low_rows >= limit) & (lane == 0), -1e30, 0.0).astype(LOW)
        first.hop(1)
        first.hop(2)
        first.hop(3)
        local(*own_blocks[1]).wait()
        for i in range(1, heads):
            out_copy(i).wait_recv()
        others[0].begin()
        others[1].begin()
        first.spread()
        for item in (own_blocks[0], own_blocks[2], own_blocks[3]):
            local(*item).wait()
        first.finish()
        local(*results[0]).start()
        norms = w0[:, :, :, :, :128].reshape(d_model, 128).astype(F32).T
        gain, shift = norms[0:1], norms[1:2]
        tile = min(256, rows)

        @pl.loop(0, rows // tile)
        def _(i):
            at = pl.ds(pl.multiple_of(i * tile, tile), tile)
            n1[at] = (hat[at] * gain + shift).astype(LOW)

        for c, dst in ((1, k_s), (2, v_s), (0, q_s)):
            @pl.loop(0, rows // tile)
            def _(i):
                at = pl.ds(pl.multiple_of(i * tile, tile), tile)
                w = w0[:, :, :, :, 128 + c * width:128 + (c + 1) * width].reshape(d_model, width)
                value = dot(n1[at], w, 1, 0).astype(LOW)
                dst[at] = value * LOW(size ** -0.5) if c == 0 else value

            if c:
                kv_copy(c - 1).start()
        for item in results[1:3]:
            local(*item).start()
        kv_copy(0).wait()
        kv_copy(1).wait()
        for item in results[3:]:
            local(*item).start()

    total = pairs * steps_q
    slots = 2 * total
    events = []
    n = len(others)
    for g in range(n):
        events += [(1.0 + g * 2.6, others[g], 1), (2.0 + g * 2.6, others[g], 2), (3.0 + g * 2.6, others[g], 3), (4.6 + g * 2.6, others[g], 4)]
        if g + 2 < n:
            events.append((1.5 + g * 2.6, others[g + 2], 0))
    events.sort(key=lambda item: item[0])
    last = max(item[0] for item in events) + 1

    def run(slot_in_step):
        for when, gather, what in events:
            slot = min(int(when * min(1.0, slots / 16)), slots - 1)
            if slot % 2 != slot_in_step:
                continue

            @pl.when(step == slot // 2)
            def _():
                if what == 0:
                    gather.begin()
                elif what < 4:
                    gather.hop(what)
                else:
                    gather.spread()

    queries = q_s[pl.ds(pl.multiple_of(part * block, block), block), pl.ds(pl.multiple_of(pair * 2 * size, 2 * size), 2 * size)]
    cols = pl.ds(pl.multiple_of(pair * 2 * size, 2 * size), 2 * size)
    keys = jnp.concatenate([k_s[:, cols], bias[...]], axis=1)
    values_t = v_s[:, cols].T
    ones = (lax.broadcasted_iota(jnp.int32, (block, bias.shape[1]), 1) == 0).astype(LOW)
    pieces = []
    for h in range(2):
        run(h)
        scores = dot(keys, jnp.concatenate([only_head(queries, h, size), ones], axis=1), 1, 1)
        top = jnp.max(scores, axis=0, keepdims=True)
        expo = jnp.exp(scores - top)
        over = 1.0 / jnp.sum(expo, axis=0, keepdims=True)
        low = expo.astype(LOW)
        probs[h] = low
        pieces.append(dot(values_t, low, 1, 0)[h * size:(h + 1) * size] * over)
        inverse[0, h:h + 1] = over
    here = jnp.concatenate(pieces, axis=0).T.astype(LOW)
    context[...] = here
    ctx_s[pl.ds(pl.multiple_of(part * block, block), block), cols] = here

    @pl.when(part == steps_q - 1)
    def _():
        for i in range(1, heads):
            ctx_copy(pair, i).start()

    @pl.when(step == total - 1)
    def _():
        local(*ctx_local).start()
        for gather in others:
            gather.finish()
        for item in results:
            local(*item).wait()
        local(*ctx_local).wait()
        for i in range(1, heads):
            out_copy(i).wait_send()
            for p in range(pairs):
                ctx_copy(p, i).wait()


def forward(limits, shard_qkv, shard_out, shard_up, shard_down, tokens, scenes, heads, size):
    ny = scenes // ZS
    rows, d_model = tokens.shape
    rl, width = shard_out.shape
    hidden = shard_up.shape[1]
    pairs = width // (2 * size)
    block = min(512, rows)
    steps_q = rows // block
    halves = 2
    sem = pltpu.SemaphoreType.DMA
    any_space = pl.BlockSpec(memory_space=pl.ANY)
    shape = jax.ShapeDtypeStruct
    wide = shard_qkv.shape[1]
    outs = [shape((rows, d_model), LOW), shape((rows, width), LOW), shape((2 * rows, width), LOW), shape((2 * rows, width), LOW),
            shape((ZS, ny, 2, rl, wide), LOW), shape((ZS, ny, 2, rl, d_model), LOW), shape((ZS, ny, 2, rl, hidden), LOW),
            shape((ZS, ny, 2, rl, hidden), LOW), shape((2 * pairs, 2 * rows, rows), LOW), shape((rows, width), LOW),
            shape((rows, d_model), LOW), shape((pairs, 8, rows), F32)]
    out_specs = [any_space] * 8 + [
        pl.BlockSpec((2, 2 * rows, block), lambda p, i: (p, 0, i)), pl.BlockSpec((block, 2 * size), lambda p, i: (i, p)),
        any_space, pl.BlockSpec((1, 8, block), lambda p, i: (p, 0, i))]
    scratch = [pltpu.VMEM((ZS, ny, 2, rl, wide), LOW), pltpu.VMEM((rows, d_model), F32), pltpu.VMEM((rows, d_model), LOW),
               pltpu.VMEM((rows, width), LOW), pltpu.VMEM((2 * rows, width), LOW), pltpu.VMEM((2 * rows, width), LOW),
               pltpu.VMEM((2 * rows, 128), LOW), pltpu.VMEM((rows, width), LOW), sem((10,)), sem((2,)), sem((2,)),
               sem((max(heads - 1, 1),)), sem((max(heads - 1, 1),)), sem((pairs, max(heads - 1, 1))), sem((pairs, max(heads - 1, 1)))]
    for _ in range(2 + 2 * halves):
        scratch += gather_sems(ny)
    dims = (ny, heads, rows, width, size, block, pairs, steps_q, halves)
    flops = 2 * rows * d_model * 3 * width + 8 * rows * rows * width
    results = pl.pallas_call(
        partial(forward_kernel, dims),
        grid=(pairs, steps_q),
        out_shape=outs,
        in_specs=[pl.BlockSpec(memory_space=pltpu.SMEM)] + [any_space] * 4 + [pl.BlockSpec(memory_space=pltpu.VMEM)],
        out_specs=out_specs,
        scratch_shapes=scratch,
        compiler_params=pltpu.CompilerParams(collective_id=0, has_side_effects=True, vmem_limit_bytes=60 * 2**20),
        cost_estimate=pl.CostEstimate(flops=flops, bytes_accessed=60 * 2**20, transcendentals=0),
        name="forward_attention",
    )(limits, shard_qkv, shard_out, shard_up, shard_down, tokens)
    n1, q, k, v, full_qkv, full_out, full_up, full_down, probs, context, context_all, inverse = results
    flat = lambda a: a.reshape(d_model, a.shape[-1])
    return n1, q, k, v, flat(full_qkv), flat(full_out), flat(full_up), flat(full_down), probs, context, context_all, inverse


def middle_kernel(dims, tokens, context_all, cotangent, full_qkv, full_out, full_up, full_down,
                  resid_grad, base, mlp_low, grad_context, norm_two, parts_out, parts_up, parts_down,
                  x_v, ctx_v, cot_v, norm_v, wo, wu, wd, n2, act, gu, resid, part, low, arrived, up_v, down_v, out_v, gctx_v,
                  base_v, mlp_v, in_sem, out_sem, slot_sem, x_send, x_recv):
    heads, rows, d_model, width, hidden, tile, size_d, size_f = dims
    head = lax.axis_index("head")
    chunks = rows // tile
    own_cols = pl.ds(pl.multiple_of(head * width, width), width)

    def load(src, dst, i):
        return pltpu.make_async_copy(src, dst, in_sem.at[i])

    loads = [load(context_all, ctx_v, 0), load(full_out, wo, 1), load(tokens, x_v, 2), load(full_qkv.at[:, pl.ds(0, 128)], norm_v, 3),
             load(full_up, wu, 4), load(cotangent, cot_v, 5), load(full_down, wd, 6)]
    for item in loads:
        item.start()

    def x_copy(i, step):
        at = pl.ds(pl.multiple_of(i * tile, tile), tile)
        return remote(low.at[at], arrived.at[step - 1, at], x_send.at[i, step - 1], x_recv.at[i, step - 1],
                      {"head": (head + step) % heads})

    barrier = pltpu.get_barrier_semaphore()
    for step in range(1, heads):
        pl.semaphore_signal(barrier, 1, device_id={"head": (head + step) % heads}, device_id_type=MESH)
    if heads > 1:
        pl.semaphore_wait(barrier, heads - 1)
    for item in loads[:4]:
        item.wait()
    norms = norm_v[...].astype(F32).T
    gain, shift = norms[2:3], norms[3:4]

    def hat_of(value):
        centre = value - jnp.mean(value, axis=1, keepdims=True)
        spread = lax.rsqrt(jnp.mean(centre * centre, axis=1, keepdims=True) + 1e-05)
        return centre * spread, spread

    @pl.loop(0, chunks)
    def _(i):
        at = pl.ds(pl.multiple_of(i * tile, tile), tile)
        value = x_v[at].astype(F32) + dot(ctx_v[at], wo[...], 1, 1)
        resid[at] = value
        n2[at] = (hat_of(value)[0] * gain + shift).astype(LOW)

    for item in loads[4:]:
        item.wait()
    norm_two[...] = jnp.zeros_like(norm_two)

    @pl.loop(0, chunks)
    def _(i):
        at = pl.ds(pl.multiple_of(i * tile, tile), tile)
        for f in range(hidden // size_f):
            cols = slice(f * size_f, (f + 1) * size_f)
            u = dot(n2[at], wu[:, cols], 1, 0)
            ga = dot(cot_v[at], wd[:, cols], 1, 0)
            phi = 0.5 + 0.5 * lax.erf(u * (0.5 ** 0.5))
            act[at, cols] = (u * phi).astype(LOW)
            gu[at, cols] = (ga * (phi + u * (jnp.exp(u * u * -0.5) * 0.3989422804014327))).astype(LOW)
        total = dot(gu[at], wu[...], 1, 1)
        part[at] = total
        low[at] = total.astype(LOW)
        for step in range(1, heads):
            x_copy(i, step).start()
        hat, _ = hat_of(resid[at])
        norm_two[0:1] += jnp.sum(total * hat, axis=0, keepdims=True)
        norm_two[1:2] += jnp.sum(total, axis=0, keepdims=True)

    for src, other, dst in ((n2, gu, up_v), (cot_v, act, down_v)):
        for f in range(hidden // size_f):
            cols = slice(f * size_f, (f + 1) * size_f)

            @pl.loop(0, d_model // size_d)
            def _(j):
                at = pl.ds(pl.multiple_of(j * size_d, size_d), size_d)
                dst[at, cols] = dot(src[:, at], other[:, cols], 0, 0).astype(LOW)

    stores = [pltpu.make_async_copy(up_v, parts_up, out_sem.at[0]), pltpu.make_async_copy(down_v, parts_down, out_sem.at[1])]
    for item in stores:
        item.start()

    def slot_copies(i):
        at = pl.ds(pl.multiple_of(i * tile, tile), tile)
        slot = i % 2
        return (pltpu.make_async_copy(base_v.at[slot], base.at[at], slot_sem.at[0, slot]),
                pltpu.make_async_copy(mlp_v.at[slot], mlp_low.at[at], slot_sem.at[1, slot]))

    @pl.loop(0, chunks)
    def _(i):
        at = pl.ds(pl.multiple_of(i * tile, tile), tile)
        value = dot(act[at], wd[...], 1, 1)

        @pl.when(i >= 2)
        def _():
            for item in slot_copies(i - 2):
                item.wait()

        base_v[i % 2] = resid[at] + value
        mlp_v[i % 2] = value.astype(LOW)
        for item in slot_copies(i):
            item.start()

    for i in range(max(0, chunks - 2), chunks):
        for item in slot_copies(i):
            item.wait()

    def chunk_stores(i):
        at = pl.ds(pl.multiple_of(i * tile, tile), tile)
        return (pltpu.make_async_copy(part.at[at], resid_grad.at[at], out_sem.at[3 + 2 * i]),
                pltpu.make_async_copy(gctx_v.at[at], grad_context.at[at], out_sem.at[4 + 2 * i]))

    @pl.loop(0, chunks)
    def _(i):
        at = pl.ds(pl.multiple_of(i * tile, tile), tile)
        total = part[at]
        for step in range(1, heads):
            x_copy(i, step).wait_recv()
            total += arrived[step - 1, at].astype(F32)
        hat, spread = hat_of(resid[at])
        scaled = total * gain
        inner = scaled - jnp.mean(scaled, axis=1, keepdims=True) - hat * jnp.mean(scaled * hat, axis=1, keepdims=True)
        total = cot_v[at].astype(F32) + inner * spread
        part[at] = total
        rounded = total.astype(LOW)
        n2[at] = rounded
        gctx_v[at] = dot(rounded, wo[:, own_cols], 1, 0).astype(LOW)
        for item in chunk_stores(i):
            item.start()

    @pl.loop(0, d_model // size_d)
    def _(j):
        at = pl.ds(pl.multiple_of(j * size_d, size_d), size_d)
        out_v[at] = dot(n2[:, at], ctx_v[:, own_cols], 0, 0).astype(LOW)

    store = pltpu.make_async_copy(out_v, parts_out, out_sem.at[2])
    store.start()
    for item in stores:
        item.wait()
    store.wait()
    for i in range(chunks):
        for item in chunk_stores(i):
            item.wait()
        for step in range(1, heads):
            x_copy(i, step).wait_send()


def middle(tokens, context_all, cotangent, full_qkv, full_out, full_up, full_down, heads):
    rows, d_model = tokens.shape
    hidden, width = full_up.shape[1], d_model // heads
    tile, size_d, size_f = min(256, rows), min(512, d_model), min(1024, hidden)
    chunks = rows // tile
    others = max(heads - 1, 1)
    sem = pltpu.SemaphoreType.DMA
    shape, vmem = jax.ShapeDtypeStruct, pltpu.VMEM
    any_space, whole = pl.BlockSpec(memory_space=pl.ANY), pl.BlockSpec(memory_space=pltpu.VMEM)
    big, wide = (rows, d_model), (rows, hidden)
    scratch = [vmem(big, LOW), vmem(big, LOW), vmem(big, LOW), vmem((d_model, 128), LOW), vmem((d_model, d_model), LOW),
               vmem((d_model, hidden), LOW), vmem((d_model, hidden), LOW), vmem(big, LOW), vmem(wide, LOW), vmem(wide, LOW),
               vmem(big, F32), vmem(big, F32), vmem(big, LOW), vmem((others, *big), LOW), vmem((d_model, hidden), LOW),
               vmem((d_model, hidden), LOW), vmem((d_model, width), LOW), vmem((rows, width), LOW), vmem((2, tile, d_model), F32),
               vmem((2, tile, d_model), LOW), sem((7,)), sem((3 + 2 * chunks,)), sem((2, 2)), sem((chunks, others)), sem((chunks, others))]
    return pl.pallas_call(
        partial(middle_kernel, (heads, rows, d_model, width, hidden, tile, size_d, size_f)),
        out_shape=[shape(big, F32), shape(big, F32), shape(big, LOW), shape((rows, width), LOW), shape((8, d_model), F32),
                   shape((d_model, width), LOW), shape((d_model, hidden), LOW), shape((d_model, hidden), LOW)],
        in_specs=[any_space] * 7,
        out_specs=[any_space] * 4 + [whole] + [any_space] * 3,
        scratch_shapes=scratch,
        compiler_params=pltpu.CompilerParams(collective_id=3, has_side_effects=True, vmem_limit_bytes=63 * 2**20),
        cost_estimate=pl.CostEstimate(flops=14 * rows * d_model * hidden, bytes_accessed=50 * 2**20, transcendentals=0),
        name="middle_stage",
    )(tokens, context_all, cotangent, full_qkv, full_out, full_up, full_down)


class Scatter:
    def __init__(self, ny, parts, cols, bufs, sems):
        self.ny, self.parts, self.cols = ny, parts, cols
        self.own, self.from_core, self.from_y, self.sum_two, self.from_z = bufs
        self.load_sem, self.csend, self.crecv, self.ysend, self.yrecv, self.zsend, self.zrecv = sems
        self.z, self.y, self.core = place(ny)

    def load(self):
        return pltpu.make_async_copy(self.parts.at[:, :, self.core, :, self.cols], self.own, self.load_sem.at[0])

    def to_core(self):
        return remote(self.parts.at[:, :, 1 - self.core, :, self.cols], self.from_core, self.csend.at[0], self.crecv.at[0],
                      {"seq": 1 - self.core})

    def to_y(self, step):
        yy = (self.y + step) % self.ny
        return remote(self.own.at[:, yy], self.from_y.at[step - 1], self.ysend.at[step - 1], self.yrecv.at[step - 1],
                      {"scene": self.z * self.ny + yy})

    def to_z(self, step):
        zz = (self.z + step) % ZS
        return remote(self.sum_two.at[zz], self.from_z.at[step - 1], self.zsend.at[step - 1], self.zrecv.at[step - 1],
                      {"scene": zz * self.ny + self.y})

    def begin(self):
        self.load().start()
        self.to_core().start()

    def one(self):
        self.load().wait()
        self.to_core().wait_recv()
        for zz in range(ZS):
            for yy in range(self.ny):
                self.own[zz, yy] = (self.own[zz, yy].astype(F32) + self.from_core[zz, yy].astype(F32)).astype(LOW)
        for step in range(1, self.ny):
            self.to_y(step).start()

    def two(self):
        for step in range(1, self.ny):
            self.to_y(step).wait_recv()
        for zz in range(ZS):
            total = self.own[zz, self.y].astype(F32)
            for step in range(1, self.ny):
                total += self.from_y[step - 1, zz].astype(F32)
            self.sum_two[zz] = total.astype(LOW)
        for step in range(1, ZS):
            self.to_z(step).start()

    def three(self, out, alone=False):
        for step in range(1, ZS):
            self.to_z(step).wait_recv()
        total = self.sum_two[self.z].astype(F32)
        for step in range(1, ZS):
            total += self.from_z[step - 1].astype(F32)
        if alone:
            out[...] = total
        else:
            out[:, self.cols] = total

    def finish(self):
        self.to_core().wait_send()
        for step in range(1, self.ny):
            self.to_y(step).wait_send()
        for step in range(1, ZS):
            self.to_z(step).wait_send()


SCATTER_BUFS, SCATTER_SEMS = 5, 7


def scatter_scratch(ny, rl, cols):
    sem = pltpu.SemaphoreType.DMA
    other = max(ny - 1, 1)
    return [pltpu.VMEM((ZS, ny, rl, cols), LOW), pltpu.VMEM((ZS, ny, rl, cols), LOW), pltpu.VMEM((other, ZS, rl, cols), LOW),
            pltpu.VMEM((ZS, rl, cols), LOW), pltpu.VMEM((ZS - 1, rl, cols), LOW),
            sem((1,)), sem((1,)), sem((1,)), sem((other,)), sem((other,)), sem((ZS - 1,)), sem((ZS - 1,))]


def make_scatters(ny, plan, scratch):
    n = SCATTER_BUFS + SCATTER_SEMS
    result = []
    for i, (parts, cols) in enumerate(plan):
        mine = scratch[i * n:(i + 1) * n]
        result.append(Scatter(ny, parts, cols, mine[:SCATTER_BUFS], mine[SCATTER_BUFS:]))
    return result


def backward_kernel(dims, probs, queries, keys, values, grad, context, inverse, parts_out, parts_up, parts_down,
                    dq, gk, gv, mine_out, mine_up, mine_down,
                    dk_acc, dv_acc, kept, stage, landed, kv_send, kv_recv, *scratch):
    ny, heads, rows, size, pairs, steps_q, halves = dims
    pair, part = pl.program_id(0), pl.program_id(1)
    step = pair * steps_q + part
    total = pairs * steps_q
    block = grad.shape[0]
    z, y, core = place(ny)
    width = parts_out.shape[-1]
    cols_of = split_cols(parts_up.shape[-1], halves)
    plan = [(parts_out, pl.ds(0, width))] + [(parts_up, cols) for cols in cols_of] + [(parts_down, cols_of[0])]
    scatters = make_scatters(ny, plan, scratch)
    targets = [mine_out] + [mine_up] * halves + [mine_down]

    def kv_copy(p, i):
        return remote(stage.at[p, i], landed.at[p, i], kv_send.at[p, i], kv_recv.at[p, i], {"seq": 1 - core})

    @pl.when(step == 0)
    def _():
        greet_all(ny, 1)
        for item in scatters:
            item.begin()

    slots = 2 * total
    events = []
    for i in range(len(scatters)):
        events += [(0.6 + i * 0.7, i, 1), (3.2 + i * 4.0, i, 2), (7.2 + i * 4.2, i, 3)]
    events.sort()

    def run(slot_in_step):
        for when, i, what in events:
            slot = min(int(when * min(1.0, slots / 16)), slots)
            if slot == slots or slot % 2 != slot_in_step:
                continue

            @pl.when(step == slot // 2)
            def _():
                if what == 1:
                    scatters[i].one()
                elif what == 2:
                    scatters[i].two()
                else:
                    scatters[i].three(targets[i])

    @pl.when(part == 0)
    def _():
        dk_acc[...] = jnp.zeros_like(dk_acc)
        dv_acc[...] = jnp.zeros_like(dv_acc)

    upper = grad[...].astype(F32)
    inner = (upper * context[...].astype(F32)).T
    upper_t = upper.T
    row = lax.broadcasted_iota(jnp.int32, upper_t.shape, 0)
    keys_t = keys[...].T
    pieces = []
    for h in range(2):
        run(h)
        over = inverse[0, h:h + 1]
        shift = jnp.sum(inner[h * size:(h + 1) * size], axis=0, keepdims=True) * over
        scaled = jnp.where(row // size == h, upper_t * over, 0.0)
        dp = dot(values[...], scaled.astype(LOW), 1, 0) - shift
        low = probs[h]
        ds = (low.astype(F32) * dp).astype(LOW)
        dv_acc[...] += dot(low, scaled.T.astype(LOW), 1, 0)
        dk_acc[...] += dot(ds, only_head(queries[...], h, size), 1, 0)
        pieces.append(dot(keys_t, ds, 1, 0)[h * size:(h + 1) * size])
    dq[...] = (jnp.concatenate(pieces, axis=0) * size ** -0.5).T.astype(LOW)

    @pl.when(part == steps_q - 1)
    def _():
        for i, acc in enumerate((dk_acc, dv_acc)):
            stage[pair, i] = acc[rows:].astype(LOW)
            kv_copy(pair, i).start()
            kept[pair, i] = acc[:rows]

    @pl.when(step == total - 1)
    def _():
        for when, i, what in events:
            if min(int(when * min(1.0, slots / 16)), slots) == slots:
                if what == 1:
                    scatters[i].one()
                elif what == 2:
                    scatters[i].two()
                else:
                    scatters[i].three(targets[i])
        for item in scatters:
            item.finish()
        for p in range(pairs):
            for i, dst in enumerate((gk, gv)):
                kv_copy(p, i).wait()
                dst[:, p * 2 * size:(p + 1) * 2 * size] = (kept[p, i] + landed[p, i].astype(F32)).astype(LOW)


def backward(probs, q, k, v, grad, context, inverse, parts_out, parts_up, parts_down, scenes, size):
    ny = scenes // ZS
    rows, width = q.shape
    pairs = width // (2 * size)
    block = min(512, rows)
    d_model, hidden = parts_up.shape
    rl = d_model // (2 * scenes)
    halves = 2
    spec = pl.BlockSpec
    q_spec = spec((block, 2 * size), lambda p, i: (i, p))
    k_spec = spec((2 * rows, 2 * size), lambda p, i: (0, p))
    any_space = spec(memory_space=pl.ANY)
    whole = spec(memory_space=pltpu.VMEM)
    shape = jax.ShapeDtypeStruct
    sem = pltpu.SemaphoreType.DMA
    pair_buf = (pairs, 2, rows, 2 * size)
    scratch = [pltpu.VMEM((2 * rows, 2 * size), F32), pltpu.VMEM((2 * rows, 2 * size), F32), pltpu.VMEM(pair_buf, F32),
               pltpu.VMEM(pair_buf, LOW), pltpu.VMEM(pair_buf, LOW), sem((pairs, 2)), sem((pairs, 2))]
    scratch += scatter_scratch(ny, rl, width)
    for _ in range(halves + 1):
        scratch += scatter_scratch(ny, rl, hidden // halves)
    return pl.pallas_call(
        partial(backward_kernel, (ny, 1, rows, size, pairs, rows // block, halves)),
        grid=(pairs, rows // block),
        out_shape=[shape((rows, width), LOW), shape((rows, width), LOW), shape((rows, width), LOW), shape((rl, width), F32),
                   shape((rl, hidden), F32), shape((rl, hidden // halves), F32)],
        in_specs=[spec((2, 2 * rows, block), lambda p, i: (p, 0, i)), q_spec, k_spec, k_spec, q_spec, q_spec,
                  spec((1, 8, block), lambda p, i: (p, 0, i)), any_space, any_space, any_space],
        out_specs=[q_spec, whole, whole, whole, whole, whole],
        scratch_shapes=scratch,
        compiler_params=pltpu.CompilerParams(collective_id=1, has_side_effects=True, vmem_limit_bytes=60 * 2**20),
        cost_estimate=pl.CostEstimate(flops=16 * rows * rows * width, bytes_accessed=50 * 2**20, transcendentals=0),
        name="backward_attention",
    )(probs, q, k, v, grad, context, inverse, parts_out.reshape(ZS, ny, 2, rl, width), parts_up.reshape(ZS, ny, 2, rl, hidden),
      parts_down.reshape(ZS, ny, 2, rl, hidden))


def last_kernel(dims, gq, gk, gv, n1, tokens, resid, full_qkv, norm_two, parts_down,
                tokens_grad, mine_qkv, mine_down,
                gq_v, gk_v, gv_v, n1_v, x_v, res_v, w_v, in_sem,
                part_one, part_low, arrived, parts_qkv, norm_land, norm_own, out_v, x_send, x_recv, n_send, n_recv, out_sem, *scratch):
    ny, heads, rows, d_model, width, tile, halves, split = dims
    z, y, core = place(ny)
    head = lax.axis_index("head")
    hidden = parts_down.shape[-1]
    wide = full_qkv.shape[1]
    rl = mine_qkv.shape[0]
    plan = [(parts_down, split_cols(hidden, halves)[-1]), (parts_qkv, pl.ds(0, split)), (parts_qkv, pl.ds(split, wide - split))]
    down, qkv_a, qkv_b = make_scatters(ny, plan, scratch)
    chunks = rows // tile
    loads = [pltpu.make_async_copy(src, dst, in_sem.at[i]) for i, (src, dst) in enumerate((
        (gq, gq_v), (full_qkv, w_v), (gk, gk_v), (gv, gv_v), (n1, n1_v), (tokens, x_v), (resid, res_v)))]
    for item in loads:
        item.start()

    def x_copy(i, step):
        at = pl.ds(i * tile, tile)
        return remote(part_low.at[at], arrived.at[step - 1, at], x_send.at[i, step - 1], x_recv.at[i, step - 1],
                      {"head": (head + step) % heads})

    def n_copy(step):
        return remote(norm_own, norm_land.at[step - 1], n_send.at[step - 1], n_recv.at[step - 1], {"head": (head + step) % heads})

    def out_copy(i):
        at = pl.ds(i * tile, tile)
        return pltpu.make_async_copy(out_v.at[at], tokens_grad.at[at], out_sem.at[i])

    greet_all(ny, heads)
    down.begin()
    for item in loads[:4]:
        item.wait()
    for i in range(chunks):
        at = pl.ds(i * tile, tile)
        total = jnp.zeros((tile, d_model), F32)
        for c, g in enumerate((gq_v, gk_v, gv_v)):
            total += dot(g[at], w_v[:, 128 + c * width:128 + (c + 1) * width], 1, 1)
        part_one[at] = total
        part_low[at] = total.astype(LOW)
        for step in range(1, heads):
            x_copy(i, step).start()
        if i == 0:
            down.one()
    for item in loads[4:]:
        item.wait()
    per_z = d_model // ZS
    for zz in range(ZS):
        cols = n1_v[:, zz * per_z:(zz + 1) * per_z]
        for c, g in enumerate((gq_v, gk_v, gv_v)):
            value = dot(cols, g[...], 0, 0).astype(LOW)
            parts_qkv[zz, :, :, :, 128 + c * width:128 + (c + 1) * width] = value.reshape(ny, 2, rl, width)
    qkv_b.begin()
    gain = w_v[:, :128].astype(F32).T[0:1]

    def hat_of(at):
        x = x_v[at].astype(F32)
        centre = x - jnp.mean(x, axis=1, keepdims=True)
        spread = lax.rsqrt(jnp.mean(centre * centre, axis=1, keepdims=True) + 1e-05)
        return centre * spread, spread

    gain_sum = jnp.zeros((1, d_model), F32)
    shift_sum = jnp.zeros((1, d_model), F32)
    for i in range(chunks):
        at = pl.ds(i * tile, tile)
        hat, _ = hat_of(at)
        gain_sum += jnp.sum(part_one[at] * hat, axis=0, keepdims=True)
        shift_sum += jnp.sum(part_one[at], axis=0, keepdims=True)
        if i == chunks // 2:
            qkv_b.one()
    sums = jnp.concatenate([gain_sum, shift_sum, norm_two[0:2], jnp.zeros((124, d_model), F32)], axis=0).T.astype(LOW)
    parts_qkv[:, :, :, :, :128] = sums.reshape(ZS, ny, 2, rl, 128)
    qkv_a.begin()

    def receive(i):
        at = pl.ds(i * tile, tile)
        total = part_one[at]
        for step in range(1, heads):
            x_copy(i, step).wait_recv()
            total += arrived[step - 1, at].astype(F32)
        hat, spread = hat_of(at)
        scaled = total * gain
        inner = scaled - jnp.mean(scaled, axis=1, keepdims=True) - hat * jnp.mean(scaled * hat, axis=1, keepdims=True)
        out_v[at] = res_v[at] + inner * spread
        out_copy(i).start()

    stages = [lambda: qkv_a.one(), lambda: down.two(), lambda: qkv_b.two(), lambda: down.three(mine_down, True), lambda: qkv_a.two(),
              lambda: qkv_b.three(mine_qkv), lambda: qkv_a.three(mine_qkv)]
    when = [0, 1, 3, 4, 5, 6, 7]
    for i in range(chunks):
        for at, stage in zip(when, stages):
            if at * chunks // 8 == i:
                stage()
        if i == chunks - 1:
            norm_own[...] = mine_qkv[:, :128]
            for step in range(1, heads):
                n_copy(step).start()
        receive(i)
    total = mine_qkv[:, :128]
    for step in range(1, heads):
        n_copy(step).wait()
        total += norm_land[step - 1]
    mine_qkv[:, :128] = total
    for item in (down, qkv_a, qkv_b):
        item.finish()
    for i in range(chunks):
        out_copy(i).wait()
        for step in range(1, heads):
            x_copy(i, step).wait_send()


def last_stage(gq, gk, gv, n1, tokens, resid, full_qkv, norm_two, parts_down, scenes, heads):
    ny = scenes // ZS
    rows, d_model = tokens.shape
    width, hidden = gq.shape[1], parts_down.shape[1]
    rl = d_model // (2 * scenes)
    wide = full_qkv.shape[1]
    tile = min(128, rows)
    chunks = rows // tile
    halves = 2
    split = (wide // 128 + 1) // 2 * 128
    others = max(heads - 1, 1)
    sem = pltpu.SemaphoreType.DMA
    shape, vmem = jax.ShapeDtypeStruct, pltpu.VMEM
    any_space, whole = pl.BlockSpec(memory_space=pl.ANY), pl.BlockSpec(memory_space=pltpu.VMEM)
    scratch = [vmem((rows, width), LOW), vmem((rows, width), LOW), vmem((rows, width), LOW), vmem((rows, d_model), LOW),
               vmem((rows, d_model), LOW), vmem((rows, d_model), F32), vmem((d_model, wide), LOW), sem((7,)),
               vmem((rows, d_model), F32), vmem((rows, d_model), LOW), vmem((others, rows, d_model), LOW),
               vmem((ZS, ny, 2, rl, wide), LOW), vmem((others, rl, 128), F32), vmem((rl, 128), F32),
               vmem((rows, d_model), F32), sem((chunks, others)), sem((chunks, others)), sem((others,)), sem((others,)),
               sem((chunks,))]
    for cols in (hidden // halves, split, wide - split):
        scratch += scatter_scratch(ny, rl, cols)
    return pl.pallas_call(
        partial(last_kernel, (ny, heads, rows, d_model, width, tile, halves, split)),
        out_shape=[shape((rows, d_model), F32), shape((rl, wide), F32), shape((rl, hidden // halves), F32)],
        in_specs=[any_space] * 7 + [whole, any_space],
        out_specs=[any_space, whole, whole],
        scratch_shapes=scratch,
        compiler_params=pltpu.CompilerParams(collective_id=2, has_side_effects=True, vmem_limit_bytes=63 * 2**20),
        cost_estimate=pl.CostEstimate(flops=12 * rows * d_model * width, bytes_accessed=30 * 2**20, transcendentals=0),
        name="last_stage",
    )(gq, gk, gv, n1, tokens, resid, full_qkv, norm_two, parts_down.reshape(ZS, ny, 2, rl, hidden))


def on_device(n_scene, n_head, tokens, counts, w_qkv, w_out, w_up, w_down, gain_one, shift_one, gain_two, shift_two, cotangent):
    rows, d_model = tokens.shape
    width, hidden = w_qkv.shape[2], w_up.shape[1]
    size = 64
    core = lax.axis_index("seq")
    limits = jnp.stack([counts[0] - core * rows, counts[0] - (1 - core) * rows]).astype(jnp.int32)
    columns = jnp.pad(jnp.stack([gain_one, shift_one, gain_two, shift_two], axis=1), ((0, 0), (0, 124)))
    shard_qkv = jnp.concatenate([columns, w_qkv[0], w_qkv[1], w_qkv[2]], axis=1)
    n1, q, k, v, full_qkv, full_out, full_up, full_down, probs, context, context_all, inverse = forward(
        limits, shard_qkv, w_out.T, w_up, w_down.T, tokens, n_scene, n_head, size)
    grad_resid, base, mlp_low, grad_context, norm_two, grad_outproj, grad_up, grad_down = middle(
        tokens, context_all, cotangent, full_qkv, full_out, full_up, full_down, n_head)
    output = exchange(base, mlp_low, n_head)
    gq, gk, gv, mine_out, mine_up, down_a = backward(
        probs, q, k, v, grad_context, context, inverse, grad_outproj, grad_up, grad_down, n_scene, size)
    tokens_grad, mine_qkv, down_b = last_stage(
        gq, gk, gv, n1, tokens, grad_resid, full_qkv, norm_two, grad_down, n_scene, n_head)
    mine_down = jnp.concatenate([down_a, down_b], axis=1)
    mine = [mine_qkv[:, 128 + i * width:128 + (i + 1) * width] for i in range(3)]
    return (output, tokens_grad, jnp.stack(mine), mine_out.T, mine_up, mine_down.T,
            mine_qkv[:, 0], mine_qkv[:, 1], mine_qkv[:, 2], mine_qkv[:, 3])


def solution(mesh):
    rows, both = ("scene", "seq"), P(("scene", "seq"))
    weights = (P(None, rows, "head"), P("head", rows), P(rows, "head"), P("head", rows), both, both, both, both)
    return jax.shard_map(
        partial(on_device, mesh.shape["scene"], mesh.shape["head"]), mesh=mesh,
        in_specs=(P(rows, None), P("scene"), *weights, P(rows, None)),
        out_specs=(P(rows, None), P(rows, None), *weights),
        check_vma=False,
    )
```

```python
from functools import partial

import jax
import jax.numpy as jnp
from jax import lax
from jax.experimental import pallas as pl
from jax.experimental.pallas import tpu as pltpu
from jax.sharding import PartitionSpec as P

MESH = pl.DeviceIdType.MESH
ZS = 4


def place(ny):
    scene = lax.axis_index("scene")
    return scene // ny, scene % ny, lax.axis_index("seq")


def remote(src, dst, send_sem, recv_sem, device):
    return pltpu.make_async_remote_copy(
        src_ref=src, dst_ref=dst, send_sem=send_sem, recv_sem=recv_sem,
        device_id=device, device_id_type=MESH,
    )


F32 = jnp.float32
LOW = jnp.bfloat16


def dot(a, b, ca, cb):
    return lax.dot_general(a, b, (((ca,), (cb,)), ((), ())), preferred_element_type=F32)


def only_head(x, h, size):
    lane = lax.broadcasted_iota(jnp.int32, x.shape, 1)
    return jnp.where(lane // size == h, x, jnp.zeros_like(x))


class Gather:
    def __init__(self, ny, source, full, cols, sems):
        self.ny, self.source, self.full, self.cols = ny, source, full, cols
        self.rsend, self.rrecv, self.lsend, self.lrecv, self.ysend, self.yrecv, self.csend, self.crecv = sems
        self.z, self.y, self.core = place(ny)

    def at(self, zz, yy):
        return self.full.at[zz, yy, self.core, :, self.cols]

    def right(self, k):
        src = self.source() if k == 0 else self.at(self.z - k, self.y)
        dst = self.at(self.z - k, self.y)
        return remote(src, dst, self.rsend.at[k], self.rrecv.at[k], {"scene": (self.z + 1) * self.ny + self.y})

    def left(self, k):
        src = self.source() if k == 0 else self.at(self.z + k, self.y)
        dst = self.at(self.z + k, self.y)
        return remote(src, dst, self.lsend.at[k], self.lrecv.at[k], {"scene": (self.z - 1) * self.ny + self.y})

    def across(self, zz, step, own=False):
        src = self.source() if own else self.at(zz, self.y)
        peer = self.z * self.ny + (self.y + step) % self.ny
        return remote(src, self.at(zz, self.y), self.ysend.at[zz, step - 1], self.yrecv.at[zz, step - 1], {"scene": peer})

    def arrival(self, zz, step):
        yy = (self.y + self.ny - step) % self.ny
        return remote(self.at(zz, yy), self.at(zz, yy), self.ysend.at[zz, step - 1], self.yrecv.at[zz, step - 1],
                      {"scene": self.z * self.ny + yy})

    def twin(self, zz, step, own=False):
        src = self.source() if own else self.at(zz, (self.y + self.ny - step) % self.ny)
        dst = self.at(zz, (self.y + self.ny - step) % self.ny)
        return remote(src, dst, self.csend.at[zz, step], self.crecv.at[zz, step], {"seq": 1 - self.core})

    def begin(self):
        @pl.when(self.z < ZS - 1)
        def _():
            self.right(0).start()

        @pl.when(self.z > 0)
        def _():
            self.left(0).start()

        for step in range(1, self.ny):
            self.across(self.z, step, True).start()
        self.twin(self.z, 0, True).start()

    def hop(self, k):
        @pl.when(self.z >= k)
        def _():
            self.right(k - 1).wait_recv()
            if k < ZS - 1:
                @pl.when(self.z < ZS - 1)
                def _():
                    self.right(k).start()
            for step in range(1, self.ny):
                self.across(self.z - k, step).start()
            self.twin(self.z - k, 0).start()

        @pl.when(self.z + k < ZS)
        def _():
            self.left(k - 1).wait_recv()
            if k < ZS - 1:
                @pl.when(self.z > 0)
                def _():
                    self.left(k).start()
            for step in range(1, self.ny):
                self.across(self.z + k, step).start()
            self.twin(self.z + k, 0).start()

    def spread(self):
        for step in range(1, self.ny):
            for zz in range(ZS):
                self.arrival(zz, step).wait_recv()
                self.twin(zz, step).start()

    def finish(self):
        for k in range(ZS - 1):
            @pl.when((self.z < ZS - 1) & (self.z >= k))
            def _():
                self.right(k).wait_send()

            @pl.when((self.z > 0) & (self.z + k < ZS))
            def _():
                self.left(k).wait_send()
        for zz in range(ZS):
            for step in range(1, self.ny):
                self.arrival(zz, step).wait_send()
            for step in range(self.ny):
                self.twin(zz, step).wait()


class PairGather(Gather):
    def row(self, zz):
        return self.full.at[zz, :, self.core, :, self.cols]

    def right(self, k):
        return remote(self.row(self.z - k), self.row(self.z - k), self.rsend.at[k], self.rrecv.at[k],
                      {"scene": (self.z + 1) * self.ny + self.y})

    def left(self, k):
        return remote(self.row(self.z + k), self.row(self.z + k), self.lsend.at[k], self.lrecv.at[k],
                      {"scene": (self.z - 1) * self.ny + self.y})

    def twin(self, zz):
        return remote(self.row(zz), self.row(zz), self.csend.at[zz, 0], self.crecv.at[zz, 0], {"seq": 1 - self.core})

    def begin(self):
        for step in range(1, self.ny):
            self.across(self.z, step, True).start()

    def pair(self):
        for step in range(1, self.ny):
            self.arrival(self.z, step).wait_recv()

        @pl.when(self.z < ZS - 1)
        def _():
            self.right(0).start()

        @pl.when(self.z > 0)
        def _():
            self.left(0).start()

        self.twin(self.z).start()

    def hop(self, k):
        @pl.when(self.z >= k)
        def _():
            self.right(k - 1).wait_recv()
            if k < ZS - 1:
                @pl.when(self.z < ZS - 1)
                def _():
                    self.right(k).start()
            self.twin(self.z - k).start()

        @pl.when(self.z + k < ZS)
        def _():
            self.left(k - 1).wait_recv()
            if k < ZS - 1:
                @pl.when(self.z > 0)
                def _():
                    self.left(k).start()
            self.twin(self.z + k).start()

    def finish(self):
        for k in range(ZS - 1):
            @pl.when((self.z < ZS - 1) & (self.z >= k))
            def _():
                self.right(k).wait_send()

            @pl.when((self.z > 0) & (self.z + k < ZS))
            def _():
                self.left(k).wait_send()
        for step in range(1, self.ny):
            self.across(self.z, step).wait_send()
        for zz in range(ZS):
            self.twin(zz).wait()


def gather_sems(ny):
    sem = pltpu.SemaphoreType.DMA
    return [sem((ZS - 1,)), sem((ZS - 1,)), sem((ZS - 1,)), sem((ZS - 1,)), sem((ZS, max(ny - 1, 1))), sem((ZS, max(ny - 1, 1))),
            sem((ZS, ny)), sem((ZS, ny))]


def greet_all(ny, heads):
    z, y, core = place(ny)
    head = lax.axis_index("head")
    barrier = pltpu.get_barrier_semaphore()

    def signal(device):
        pl.semaphore_signal(barrier, 1, device_id=device, device_id_type=MESH)

    for step in range(1, ZS):
        signal({"scene": (z + step) % ZS * ny + y})
    for step in range(1, ny):
        signal({"scene": z * ny + (y + step) % ny})
    for step in range(1, heads):
        signal({"head": (head + step) % heads})
    signal({"seq": 1 - core})
    pl.semaphore_wait(barrier, ZS + ny - 1 + heads - 1)


def split_cols(total, parts):
    size = total // parts
    return [pl.ds(i * size, size) for i in range(parts)]


def forward_kernel(dims, limits, shard_qkv, shard_out, shard_up, shard_down, tokens,
                   n1_out, q_out, k_out, v_out, full_qkv, full_out, full_up, full_down, probs, context, context_all, inverse,
                   w0, hat, n1, q_s, k_s, v_s, bias, ctx_s, local_sem, kv_send, kv_recv, xw_send, xw_recv, xt_send, xt_recv, xc_send, xc_recv, *sems):
    ny, heads, rows, width, size, block, pairs, steps_q, halves = dims
    pair, part = pl.program_id(0), pl.program_id(1)
    step = pair * steps_q + part
    z, y, core = place(ny)
    head = lax.axis_index("head")
    d_model = tokens.shape[1]
    per = 8
    own_cols = pl.ds(pl.multiple_of(head * width, width), width)

    def of(i):
        return sems[i * per:(i + 1) * per]

    first = Gather(ny, lambda: shard_qkv, w0, slice(None), of(0))
    outer = Gather(ny, lambda: shard_out, full_out, own_cols, of(1))
    thick = []
    for n, (shard, full) in enumerate(((shard_up, full_up), (shard_down, full_down))):
        for i, cols in enumerate(split_cols(full_up.shape[-1], halves)):
            kind = PairGather if n == 1 and i == halves - 1 else Gather
            thick.append(kind(ny, partial(lambda s, c: s.at[:, c], shard, cols), full, cols, of(2 + n * halves + i)))
    up_a, up_b, down_a, down_b = thick

    def local(src, dst, i):
        return pltpu.make_async_copy(src, dst, local_sem.at[i])

    def cols_of(step):
        return pl.ds(pl.multiple_of((head + heads - step) % heads * width, width), width)

    def out_copy(step):
        mine = full_out.at[:, :, core, :, own_cols]
        return remote(mine, mine, xw_send.at[step - 1], xw_recv.at[step - 1], {"head": (head + step) % heads})

    def out_twin(step):
        other = full_out.at[:, :, core, :, cols_of(step)]
        return remote(other, other, xt_send.at[step - 1], xt_recv.at[step - 1], {"seq": 1 - core})

    def kv_copy(i):
        src = (k_s, v_s)[i]
        return remote(src.at[pl.ds(0, rows)], src.at[pl.ds(rows, rows)], kv_send.at[i], kv_recv.at[i], {"seq": 1 - core})

    def ctx_copy(p, step):
        cols = pl.ds(pl.multiple_of(p * 2 * size, 2 * size), 2 * size)
        wide = pl.ds(pl.multiple_of(head * width + p * 2 * size, 2 * size), 2 * size)
        return remote(ctx_s.at[:, cols], context_all.at[:, wide], xc_send.at[p, step - 1], xc_recv.at[p, step - 1],
                      {"head": (head + step) % heads})

    own_blocks = [(shard_qkv, w0.at[z, y, core], 0), (shard_out, full_out.at[z, y, core, :, own_cols], 1),
                  (shard_up, full_up.at[z, y, core], 2), (shard_down, full_down.at[z, y, core], 3)]
    results = [(w0, full_qkv, 4), (n1, n1_out, 5), (q_s, q_out, 6), (k_s, k_out, 7), (v_s, v_out, 8)]
    ctx_local = (ctx_s, context_all.at[:, own_cols], 9)

    @pl.when(step == 0)
    def _():
        for item in own_blocks:
            local(*item).start()
        greet_all(ny, heads)
        first.begin()
        down_b.begin()
        tile = min(128, rows)

        @pl.loop(0, rows // tile)
        def _(i):
            at = pl.ds(pl.multiple_of(i * tile, tile), tile)
            x = tokens[at].astype(F32)
            centre = x - jnp.mean(x, axis=1, keepdims=True)
            spread = jnp.mean(centre * centre, axis=1, keepdims=True)
            hat[at] = centre * lax.rsqrt(spread + 1e-05)

        low_rows = lax.broadcasted_iota(jnp.int32, bias.shape, 0)
        lane = lax.broadcasted_iota(jnp.int32, bias.shape, 1)
        limit = jnp.where(low_rows < rows, limits[0], limits[1] + rows)
        bias[...] = jnp.where((low_rows >= limit) & (lane == 0), -1e30, 0.0).astype(LOW)
        first.hop(1)
        first.hop(2)
        outer.begin()
        first.hop(3)
        up_a.begin()
        first.spread()
        for item in own_blocks:
            local(*item).wait()
        first.finish()
        local(*results[0]).start()
        norms = w0[:, :, :, :, :128].reshape(d_model, 128).astype(F32).T
        gain, shift = norms[0:1], norms[1:2]
        tile = min(256, rows)

        @pl.loop(0, rows // tile)
        def _(i):
            at = pl.ds(pl.multiple_of(i * tile, tile), tile)
            n1[at] = (hat[at] * gain + shift).astype(LOW)

        for c, dst in ((1, k_s), (2, v_s), (0, q_s)):
            @pl.loop(0, rows // tile)
            def _(i):
                at = pl.ds(pl.multiple_of(i * tile, tile), tile)
                w = w0[:, :, :, :, 128 + c * width:128 + (c + 1) * width].reshape(d_model, width)
                value = dot(n1[at], w, 1, 0).astype(LOW)
                dst[at] = value * LOW(size ** -0.5) if c == 0 else value

            if c:
                kv_copy(c - 1).start()
            if c == 1:
                outer.hop(1)
                outer.hop(2)
            if c == 2:
                outer.hop(3)
                up_a.hop(1)
                up_b.begin()
        for item in results[1:3]:
            local(*item).start()
        kv_copy(0).wait()
        kv_copy(1).wait()
        for item in results[3:]:
            local(*item).start()

    total = pairs * steps_q
    slots = 2 * total

    def send_out():
        for i in range(1, heads):
            out_copy(i).start()

    def pass_out():
        for i in range(1, heads):
            out_copy(i).wait_recv()
            out_twin(i).start()

    events = [
        (0, lambda: up_a.hop(2)), (0, outer.spread), (0, send_out), (1, lambda: up_a.hop(3)), (1, down_a.begin),
        (2, lambda: up_b.hop(1)), (3, up_a.spread), (4, lambda: up_b.hop(2)), (4, pass_out), (5, lambda: up_b.hop(3)), (5, down_b.pair),
        (7, lambda: down_a.hop(1)), (8, up_b.spread), (9, lambda: down_a.hop(2)), (10, lambda: down_a.hop(3)),
        (12, lambda: down_b.hop(1)), (13, down_a.spread), (14, lambda: down_b.hop(2)), (15, lambda: down_b.hop(3))]

    def run(slot_in_step):
        for when, act in events:
            slot = min(int(when * min(1.0, slots / 16)), slots - 1)
            if slot % 2 == slot_in_step:
                pl.when(step == slot // 2)(act)

    queries = q_s[pl.ds(pl.multiple_of(part * block, block), block), pl.ds(pl.multiple_of(pair * 2 * size, 2 * size), 2 * size)]
    cols = pl.ds(pl.multiple_of(pair * 2 * size, 2 * size), 2 * size)
    keys = jnp.concatenate([k_s[:, cols], bias[...]], axis=1)
    values_t = v_s[:, cols].T
    ones = (lax.broadcasted_iota(jnp.int32, (block, bias.shape[1]), 1) == 0).astype(LOW)
    pieces = []
    for h in range(2):
        run(h)
        scores = dot(keys, jnp.concatenate([only_head(queries, h, size), ones], axis=1), 1, 1)
        top = jnp.max(scores, axis=0, keepdims=True)
        expo = jnp.exp(scores - top)
        over = 1.0 / jnp.sum(expo, axis=0, keepdims=True)
        low = expo.astype(LOW)
        probs[h] = low
        pieces.append(dot(values_t, low, 1, 0)[h * size:(h + 1) * size] * over)
        inverse[0, h:h + 1] = over
    here = jnp.concatenate(pieces, axis=0).T.astype(LOW)
    context[...] = here
    ctx_s[pl.ds(pl.multiple_of(part * block, block), block), cols] = here

    @pl.when(part == steps_q - 1)
    def _():
        for i in range(1, heads):
            ctx_copy(pair, i).start()

    @pl.when(step == total - 1)
    def _():
        local(*ctx_local).start()
        for gather in (outer, *thick):
            gather.finish()
        for item in results:
            local(*item).wait()
        local(*ctx_local).wait()
        for i in range(1, heads):
            out_copy(i).wait_send()
            out_twin(i).wait()
            for p in range(pairs):
                ctx_copy(p, i).wait()


def forward(limits, shard_qkv, shard_out, shard_up, shard_down, tokens, scenes, heads, size):
    ny = scenes // ZS
    rows, d_model = tokens.shape
    rl, width = shard_out.shape
    hidden = shard_up.shape[1]
    pairs = width // (2 * size)
    block = min(512, rows)
    steps_q = rows // block
    halves = 2
    sem = pltpu.SemaphoreType.DMA
    any_space = pl.BlockSpec(memory_space=pl.ANY)
    shape = jax.ShapeDtypeStruct
    wide = shard_qkv.shape[1]
    outs = [shape((rows, d_model), LOW), shape((rows, width), LOW), shape((2 * rows, width), LOW), shape((2 * rows, width), LOW),
            shape((ZS, ny, 2, rl, wide), LOW), shape((ZS, ny, 2, rl, d_model), LOW), shape((ZS, ny, 2, rl, hidden), LOW),
            shape((ZS, ny, 2, rl, hidden), LOW), shape((2 * pairs, 2 * rows, rows), LOW), shape((rows, width), LOW),
            shape((rows, d_model), LOW), shape((pairs, 8, rows), F32)]
    out_specs = [any_space] * 8 + [
        pl.BlockSpec((2, 2 * rows, block), lambda p, i: (p, 0, i)), pl.BlockSpec((block, 2 * size), lambda p, i: (i, p)),
        any_space, pl.BlockSpec((1, 8, block), lambda p, i: (p, 0, i))]
    scratch = [pltpu.VMEM((ZS, ny, 2, rl, wide), LOW), pltpu.VMEM((rows, d_model), F32), pltpu.VMEM((rows, d_model), LOW),
               pltpu.VMEM((rows, width), LOW), pltpu.VMEM((2 * rows, width), LOW), pltpu.VMEM((2 * rows, width), LOW),
               pltpu.VMEM((2 * rows, 128), LOW), pltpu.VMEM((rows, width), LOW), sem((10,)), sem((2,)), sem((2,)),
               sem((max(heads - 1, 1),)), sem((max(heads - 1, 1),)), sem((max(heads - 1, 1),)), sem((max(heads - 1, 1),)), sem((pairs, max(heads - 1, 1))), sem((pairs, max(heads - 1, 1)))]
    for _ in range(2 + 2 * halves):
        scratch += gather_sems(ny)
    dims = (ny, heads, rows, width, size, block, pairs, steps_q, halves)
    flops = 2 * rows * d_model * 3 * width + 8 * rows * rows * width
    results = pl.pallas_call(
        partial(forward_kernel, dims),
        grid=(pairs, steps_q),
        out_shape=outs,
        in_specs=[pl.BlockSpec(memory_space=pltpu.SMEM)] + [pl.BlockSpec(memory_space=pltpu.VMEM)] * 4 + [pl.BlockSpec(memory_space=pltpu.VMEM)],
        out_specs=out_specs,
        scratch_shapes=scratch,
        compiler_params=pltpu.CompilerParams(collective_id=0, has_side_effects=True, vmem_limit_bytes=60 * 2**20),
        cost_estimate=pl.CostEstimate(flops=flops, bytes_accessed=60 * 2**20, transcendentals=0),
        name="forward_attention",
    )(limits, shard_qkv, shard_out, shard_up, shard_down, tokens)
    n1, q, k, v, full_qkv, full_out, full_up, full_down, probs, context, context_all, inverse = results
    flat = lambda a: a.reshape(d_model, a.shape[-1])
    return n1, q, k, v, flat(full_qkv), flat(full_out), flat(full_up), flat(full_down), probs, context, context_all, inverse


class Scatter:
    def __init__(self, ny, parts, cols, bufs, sems):
        self.ny, self.parts, self.cols = ny, parts, cols
        self.own, self.from_core, self.from_y, self.sum_two, self.from_z = bufs
        self.load_sem, self.csend, self.crecv, self.ysend, self.yrecv, self.zsend, self.zrecv = sems
        self.z, self.y, self.core = place(ny)

    def load(self):
        return pltpu.make_async_copy(self.parts.at[:, :, self.core, :, self.cols], self.own, self.load_sem.at[0])

    def to_core(self):
        return remote(self.parts.at[:, :, 1 - self.core, :, self.cols], self.from_core, self.csend.at[0], self.crecv.at[0],
                      {"seq": 1 - self.core})

    def to_y(self, step):
        yy = (self.y + step) % self.ny
        return remote(self.own.at[:, yy], self.from_y.at[step - 1], self.ysend.at[step - 1], self.yrecv.at[step - 1],
                      {"scene": self.z * self.ny + yy})

    def to_z(self, step):
        zz = (self.z + step) % ZS
        return remote(self.sum_two.at[zz], self.from_z.at[step - 1], self.zsend.at[step - 1], self.zrecv.at[step - 1],
                      {"scene": zz * self.ny + self.y})

    def begin(self):
        self.load().start()
        self.to_core().start()

    def one(self):
        self.load().wait()
        self.to_core().wait_recv()
        for zz in range(ZS):
            for yy in range(self.ny):
                self.own[zz, yy] = (self.own[zz, yy].astype(F32) + self.from_core[zz, yy].astype(F32)).astype(LOW)
        for step in range(1, self.ny):
            self.to_y(step).start()

    def two(self):
        for step in range(1, self.ny):
            self.to_y(step).wait_recv()
        for zz in range(ZS):
            total = self.own[zz, self.y].astype(F32)
            for step in range(1, self.ny):
                total += self.from_y[step - 1, zz].astype(F32)
            self.sum_two[zz] = total.astype(LOW)
        for step in range(1, ZS):
            self.to_z(step).start()

    def three(self, out, alone=False):
        for step in range(1, ZS):
            self.to_z(step).wait_recv()
        total = self.sum_two[self.z].astype(F32)
        for step in range(1, ZS):
            total += self.from_z[step - 1].astype(F32)
        if alone:
            out[...] = total
        else:
            out[:, self.cols] = total

    def finish(self):
        self.to_core().wait_send()
        for step in range(1, self.ny):
            self.to_y(step).wait_send()
        for step in range(1, ZS):
            self.to_z(step).wait_send()


SCATTER_BUFS, SCATTER_SEMS = 5, 7


def scatter_scratch(ny, rl, cols):
    sem = pltpu.SemaphoreType.DMA
    other = max(ny - 1, 1)
    return [pltpu.VMEM((ZS, ny, rl, cols), LOW), pltpu.VMEM((ZS, ny, rl, cols), LOW), pltpu.VMEM((other, ZS, rl, cols), LOW),
            pltpu.VMEM((ZS, rl, cols), LOW), pltpu.VMEM((ZS - 1, rl, cols), LOW),
            sem((1,)), sem((1,)), sem((1,)), sem((other,)), sem((other,)), sem((ZS - 1,)), sem((ZS - 1,))]


def make_scatters(ny, plan, scratch):
    n = SCATTER_BUFS + SCATTER_SEMS
    result = []
    for i, (parts, cols) in enumerate(plan):
        mine = scratch[i * n:(i + 1) * n]
        result.append(Scatter(ny, parts, cols, mine[:SCATTER_BUFS], mine[SCATTER_BUFS:]))
    return result

def middle_kernel(dims, tokens, context_all, cotangent, full_qkv, full_out, full_up, full_down,
                  resid_grad, base, mlp_low, grad_context, norm_two, parts_out, parts_up, parts_down, mine_down,
                  x_v, ctx_v, cot_v, norm_v, wo, wu, wd, n2, act, gu, resid, part, low, arrived, up_v, down_v, out_v, gctx_v,
                  base_v, mlp_v, in_sem, out_sem, slot_sem, x_send, x_recv, *scratch):
    ny, heads, rows, d_model, width, hidden, tile, size_f, first_cols = dims
    head = lax.axis_index("head")
    chunks = rows // tile
    (down,) = make_scatters(ny, [(down_v, pl.ds(0, first_cols))], scratch)
    own_cols = pl.ds(pl.multiple_of(head * width, width), width)

    def load(src, dst, i):
        return pltpu.make_async_copy(src, dst, in_sem.at[i])

    loads = [load(context_all, ctx_v, 0), load(full_out, wo, 1), load(tokens, x_v, 2), load(full_qkv.at[:, pl.ds(0, 128)], norm_v, 3),
             load(full_up, wu, 4), load(cotangent, cot_v, 5), load(full_down, wd, 6)]
    for item in loads:
        item.start()

    half = tile // 2

    def rows_of(i):
        if isinstance(i, int) and i == chunks:
            return pl.ds(0, half)
        if isinstance(i, int) and i == 0:
            return pl.ds(half, half)
        return pl.ds(pl.multiple_of(i * tile, tile), tile)

    def x_copy(i, step):
        at = rows_of(i)
        return remote(low.at[at], arrived.at[step - 1, at], x_send.at[i, step - 1], x_recv.at[i, step - 1],
                      {"head": (head + step) % heads})

    greet_all(ny, heads)
    for item in loads[:4]:
        item.wait()
    norms = norm_v[...].astype(F32).T
    gain, shift = norms[2:3], norms[3:4]

    def hat_of(value):
        centre = value - jnp.mean(value, axis=1, keepdims=True)
        spread = lax.rsqrt(jnp.mean(centre * centre, axis=1, keepdims=True) + 1e-05)
        return centre * spread, spread

    for item in loads[4:]:
        item.wait()
    norm_two[...] = jnp.zeros_like(norm_two)

    def forward_and_back(i):
        at = rows_of(i)
        value = x_v[at].astype(F32) + dot(ctx_v[at], wo[...], 1, 1)
        resid[at] = value
        hat = hat_of(value)[0]
        n2[at] = (hat * gain + shift).astype(LOW)
        for f in range(hidden // size_f):
            cols = slice(f * size_f, (f + 1) * size_f)
            u = dot(n2[at], wu[:, cols], 1, 0)
            ga = dot(cot_v[at], wd[:, cols], 1, 0)
            phi = 0.5 + 0.5 * lax.erf(u * (0.5 ** 0.5))
            act[at, cols] = (u * phi).astype(LOW)
            gu[at, cols] = (ga * (phi + u * (jnp.exp(u * u * -0.5) * 0.3989422804014327))).astype(LOW)
        total = dot(gu[at], wu[...], 1, 1)
        part[at] = total
        low[at] = total.astype(LOW)
        for step in range(1, heads):
            x_copy(i, step).start()
        hat, _ = hat_of(resid[at])
        norm_two[0:1] += jnp.sum(total * hat, axis=0, keepdims=True)
        norm_two[1:2] += jnp.sum(total, axis=0, keepdims=True)

    forward_and_back(chunks)
    forward_and_back(0)
    pl.loop(1, chunks)(forward_and_back)

    def weight_grad(src, other, dst):
        per_z = d_model // ZS
        pack = ZS // 2
        for f in range(hidden // size_f):
            cols = slice(f * size_f, (f + 1) * size_f)

            @pl.loop(0, pack)
            def _(j):
                at = pl.ds(pl.multiple_of(j * 2 * per_z, 2 * per_z), 2 * per_z)
                value = dot(src[:, at], other[:, cols], 0, 0).astype(LOW)
                dst[pl.ds(2 * j, 2), :, :, :, cols] = value.reshape(2, *dst.shape[1:4], size_f)

    weight_grad(cot_v, act, down_v)
    down.begin()
    weight_grad(n2, gu, up_v)
    down.one()
    stores = [pltpu.make_async_copy(up_v, parts_up, out_sem.at[0]), pltpu.make_async_copy(down_v, parts_down, out_sem.at[1])]
    for item in stores:
        item.start()

    def slot_copies(i):
        at = pl.ds(pl.multiple_of(i * tile, tile), tile)
        slot = i % 2
        return (pltpu.make_async_copy(base_v.at[slot], base.at[at], slot_sem.at[0, slot]),
                pltpu.make_async_copy(mlp_v.at[slot], mlp_low.at[at], slot_sem.at[1, slot]))

    def slot_loop(i):
        at = pl.ds(pl.multiple_of(i * tile, tile), tile)
        value = dot(act[at], wd[...], 1, 1)

        @pl.when(i >= 2)
        def _():
            for item in slot_copies(i - 2):
                item.wait()

        base_v[i % 2] = resid[at] + value
        mlp_v[i % 2] = value.astype(LOW)
        for item in slot_copies(i):
            item.start()

    pl.loop(0, chunks)(slot_loop)

    for i in range(max(0, chunks - 2), chunks):
        for item in slot_copies(i):
            item.wait()

    def chunk_stores(i):
        at = rows_of(i)
        return (pltpu.make_async_copy(part.at[at], resid_grad.at[at], out_sem.at[3 + 2 * i]),
                pltpu.make_async_copy(gctx_v.at[at], grad_context.at[at], out_sem.at[4 + 2 * i]))

    def receive(i):
        at = rows_of(i)
        total = part[at]
        for step in range(1, heads):
            x_copy(i, step).wait_recv()
            total += arrived[step - 1, at].astype(F32)
        hat, spread = hat_of(resid[at])
        scaled = total * gain
        inner = scaled - jnp.mean(scaled, axis=1, keepdims=True) - hat * jnp.mean(scaled * hat, axis=1, keepdims=True)
        total = cot_v[at].astype(F32) + inner * spread
        part[at] = total
        rounded = total.astype(LOW)
        n2[at] = rounded
        gctx_v[at] = dot(rounded, wo[:, own_cols], 1, 0).astype(LOW)
        for item in chunk_stores(i):
            item.start()

    receive(chunks)
    receive(0)
    if chunks > 2:
        pl.loop(1, chunks - 1)(receive)
    down.two()
    if chunks > 1:
        receive(chunks - 1)

    @pl.loop(0, 2)
    def _(j):
        at = pl.ds(pl.multiple_of(j * (d_model // 2), d_model // 2), d_model // 2)
        out_v[at] = dot(n2[:, at], ctx_v[:, own_cols], 0, 0).astype(LOW)

    store = pltpu.make_async_copy(out_v, parts_out, out_sem.at[2])
    store.start()
    for item in stores:
        item.wait()
    store.wait()
    down.three(mine_down)
    down.finish()
    for i in range(chunks + 1):
        for item in chunk_stores(i):
            item.wait()
        for step in range(1, heads):
            x_copy(i, step).wait_send()


def shares(hidden):
    n = hidden // 128
    first = 3 * n // 8
    second = n // 4
    return first * 128, second * 128, (n - first - second) * 128


def middle(tokens, context_all, cotangent, full_qkv, full_out, full_up, full_down, scenes, heads):
    ny = scenes // ZS
    rows, d_model = tokens.shape
    rl = d_model // (2 * scenes)
    hidden, width = full_up.shape[1], d_model // heads
    tile, size_f = min(256, rows), min(1024, hidden)
    chunks = rows // tile
    first_cols = shares(hidden)[0]
    others = max(heads - 1, 1)
    sem = pltpu.SemaphoreType.DMA
    shape, vmem = jax.ShapeDtypeStruct, pltpu.VMEM
    any_space, whole = pl.BlockSpec(memory_space=pl.ANY), pl.BlockSpec(memory_space=pltpu.VMEM)
    big, wide, blocks = (rows, d_model), (rows, hidden), (ZS, ny, 2, rl, hidden)
    scratch = [vmem(big, LOW), vmem(big, LOW), vmem(big, LOW), vmem((d_model, 128), LOW), vmem((d_model, d_model), LOW),
               vmem((d_model, hidden), LOW), vmem((d_model, hidden), LOW), vmem(big, LOW), vmem(wide, LOW), vmem(wide, LOW),
               vmem(big, F32), vmem(big, F32), vmem(big, LOW), vmem((others, *big), LOW), vmem(blocks, LOW),
               vmem(blocks, LOW), vmem((d_model, width), LOW), vmem((rows, width), LOW), vmem((2, tile, d_model), F32),
               vmem((2, tile, d_model), LOW), sem((7,)), sem((5 + 2 * chunks,)), sem((2, 2)), sem((chunks + 1, others)),
               sem((chunks + 1, others))]
    scratch += scatter_scratch(ny, rl, first_cols)
    return pl.pallas_call(
        partial(middle_kernel, (ny, heads, rows, d_model, width, hidden, tile, size_f, first_cols)),
        out_shape=[shape(big, F32), shape(big, F32), shape(big, LOW), shape((rows, width), LOW), shape((8, d_model), F32),
                   shape((d_model, width), LOW), shape(blocks, LOW), shape(blocks, LOW), shape((rl, first_cols), F32)],
        in_specs=[any_space] * 7,
        out_specs=[any_space] * 4 + [whole] + [any_space] * 3 + [whole],
        scratch_shapes=scratch,
        compiler_params=pltpu.CompilerParams(collective_id=3, has_side_effects=True, vmem_limit_bytes=63 * 2**20),
        cost_estimate=pl.CostEstimate(flops=14 * rows * d_model * hidden, bytes_accessed=50 * 2**20, transcendentals=0),
        name="middle_stage",
    )(tokens, context_all, cotangent, full_qkv, full_out, full_up, full_down)


def backward_kernel(dims, probs, queries, keys, values, grad, context, inverse, parts_out, parts_up, parts_down, mlp_low,
                    dq, gk, gv, mine_out, mine_up, mine_down, mlp_land,
                    dk_acc, dv_acc, kept, stage, landed, kv_send, kv_recv, m_send, m_recv, *scratch):
    ny, heads, rows, size, pairs, steps_q, halves, down_cols = dims
    pair, part = pl.program_id(0), pl.program_id(1)
    step = pair * steps_q + part
    total = pairs * steps_q
    block = grad.shape[0]
    z, y, core = place(ny)
    width = parts_out.shape[-1]
    cols_of = split_cols(parts_up.shape[-1], halves)
    plan = [(parts_out, pl.ds(0, width))] + [(parts_up, cols) for cols in cols_of] + [(parts_down, pl.ds(*down_cols))]
    scatters = make_scatters(ny, plan, scratch)
    targets = [mine_out] + [mine_up] * halves + [mine_down]

    def kv_copy(p, i):
        return remote(stage.at[p, i], landed.at[p, i], kv_send.at[p, i], kv_recv.at[p, i], {"seq": 1 - core})

    head = lax.axis_index("head")

    def mlp_copy(i, step):
        return remote(mlp_low.at[pl.ds(i * (rows // 4), rows // 4)], mlp_land.at[step - 1, pl.ds(i * (rows // 4), rows // 4)],
                      m_send.at[i, step - 1], m_recv.at[i, step - 1], {"head": (head + step) % heads})

    @pl.when(step == 0)
    def _():
        greet_all(ny, heads)
        for i in range(4):
            for j in range(1, heads):
                mlp_copy(i, j).start()
        for item in scatters:
            item.begin()

    slots = 2 * total
    plan_at = ((0.6, 3.2, 6.2), (1.2, 8.2, 13.2), (2.2, 13.2, 17), (3.2, 15.2, 17))
    events = sorted((plan_at[i][j], i, j + 1) for i in range(4) for j in range(3))

    def run(slot_in_step):
        for when, i, what in events:
            slot = min(int(when * min(1.0, slots / 16)), slots)
            if slot == slots or slot % 2 != slot_in_step:
                continue

            @pl.when(step == slot // 2)
            def _():
                if what == 1:
                    scatters[i].one()
                elif what == 2:
                    scatters[i].two()
                else:
                    scatters[i].three(targets[i], i == 3)

    @pl.when(part == 0)
    def _():
        dk_acc[...] = jnp.zeros_like(dk_acc)
        dv_acc[...] = jnp.zeros_like(dv_acc)

    upper = grad[...].astype(F32)
    inner = (upper * context[...].astype(F32)).T
    upper_t = upper.T
    row = lax.broadcasted_iota(jnp.int32, upper_t.shape, 0)
    keys_t = keys[...].T
    pieces = []
    for h in range(2):
        run(h)
        over = inverse[0, h:h + 1]
        shift = jnp.sum(inner[h * size:(h + 1) * size], axis=0, keepdims=True) * over
        scaled = jnp.where(row // size == h, upper_t * over, 0.0)
        dp = dot(values[...], scaled.astype(LOW), 1, 0) - shift
        low = probs[h]
        ds = (low.astype(F32) * dp).astype(LOW)
        dv_acc[...] += dot(low, scaled.T.astype(LOW), 1, 0)
        dk_acc[...] += dot(ds, only_head(queries[...], h, size), 1, 0)
        pieces.append(dot(keys_t, ds, 1, 0)[h * size:(h + 1) * size])
    dq[...] = (jnp.concatenate(pieces, axis=0) * size ** -0.5).T.astype(LOW)

    @pl.when(part == steps_q - 1)
    def _():
        for i, acc in enumerate((dk_acc, dv_acc)):
            stage[pair, i] = acc[rows:].astype(LOW)
            kv_copy(pair, i).start()
            kept[pair, i] = acc[:rows]

    @pl.when(step == total - 1)
    def _():
        for when, i, what in events:
            if min(int(when * min(1.0, slots / 16)), slots) == slots:
                if what == 1:
                    scatters[i].one()
                elif what == 2:
                    scatters[i].two()
                else:
                    scatters[i].three(targets[i], i == 3)
        for item in scatters:
            item.finish()
        for p in range(pairs):
            for i, dst in enumerate((gk, gv)):
                kv_copy(p, i).wait()
                dst[:, p * 2 * size:(p + 1) * 2 * size] = (kept[p, i] + landed[p, i].astype(F32)).astype(LOW)
        for i in range(4):
            for j in range(1, heads):
                mlp_copy(i, j).wait()


def backward(probs, q, k, v, grad, context, inverse, parts_out, parts_up, parts_down, mlp_low, scenes, heads, size):
    ny = scenes // ZS
    rows, width = q.shape
    pairs = width // (2 * size)
    block = min(512, rows)
    d_model, hidden = parts_out.shape[0], parts_up.shape[-1]
    rl = d_model // (2 * scenes)
    first, second, _ = shares(hidden)
    others = max(heads - 1, 1)
    halves = 2
    spec = pl.BlockSpec
    q_spec = spec((block, 2 * size), lambda p, i: (i, p))
    k_spec = spec((2 * rows, 2 * size), lambda p, i: (0, p))
    any_space = spec(memory_space=pl.ANY)
    whole = spec(memory_space=pltpu.VMEM)
    shape = jax.ShapeDtypeStruct
    sem = pltpu.SemaphoreType.DMA
    pair_buf = (pairs, 2, rows, 2 * size)
    scratch = [pltpu.VMEM((2 * rows, 2 * size), F32), pltpu.VMEM((2 * rows, 2 * size), F32), pltpu.VMEM(pair_buf, F32),
               pltpu.VMEM(pair_buf, LOW), pltpu.VMEM(pair_buf, LOW), sem((pairs, 2)), sem((pairs, 2)), sem((4, others)), sem((4, others))]
    scratch += scatter_scratch(ny, rl, width)
    for cols in [hidden // halves] * halves + [second]:
        scratch += scatter_scratch(ny, rl, cols)
    return pl.pallas_call(
        partial(backward_kernel, (ny, heads, rows, size, pairs, rows // block, halves, (first, second))),
        grid=(pairs, rows // block),
        out_shape=[shape((rows, width), LOW), shape((rows, width), LOW), shape((rows, width), LOW), shape((rl, width), F32),
                   shape((rl, hidden), F32), shape((rl, second), F32), shape((others, rows, d_model), LOW)],
        in_specs=[spec((2, 2 * rows, block), lambda p, i: (p, 0, i)), q_spec, k_spec, k_spec, q_spec, q_spec,
                  spec((1, 8, block), lambda p, i: (p, 0, i)), any_space, any_space, any_space, any_space],
        out_specs=[q_spec, whole, whole, whole, whole, whole, any_space],
        scratch_shapes=scratch,
        compiler_params=pltpu.CompilerParams(collective_id=1, has_side_effects=True, vmem_limit_bytes=60 * 2**20),
        cost_estimate=pl.CostEstimate(flops=16 * rows * rows * width, bytes_accessed=50 * 2**20, transcendentals=0),
        name="backward_attention",
    )(probs, q, k, v, grad, context, inverse, parts_out.reshape(ZS, ny, 2, rl, width), parts_up, parts_down,
      mlp_low)


def last_kernel(dims, gq, gk, gv, n1, tokens, resid, full_qkv, norm_two, parts_down, base, mlp_land, down_a, down_b,
                tokens_grad, output, mine_w, mine_norm, mine_down,
                gq_v, gk_v, gv_v, n1_v, x_v, res_v, w_v, in_sem,
                part_one, part_low, arrived, parts_qkv, norm_land, norm_own, out_v, x_send, x_recv, n_send, n_recv, out_sem,
                base_v, land_v, mine_qkv, base_sem, land_sem, res_sem, *scratch):
    ny, heads, rows, d_model, width, tile, split, down_cols = dims
    z, y, core = place(ny)
    head = lax.axis_index("head")
    wide = full_qkv.shape[1]
    rl = mine_qkv.shape[0]
    plan = [(parts_down, pl.ds(*down_cols)), (parts_qkv, pl.ds(0, split)), (parts_qkv, pl.ds(split, wide - split))]
    down, qkv_a, qkv_b = make_scatters(ny, plan, scratch)
    chunks = rows // tile
    loads = [pltpu.make_async_copy(src, dst, in_sem.at[i]) for i, (src, dst) in enumerate((
        (gq, gq_v), (full_qkv, w_v), (gk, gk_v), (gv, gv_v), (n1, n1_v), (tokens, x_v), (resid, res_v)))]
    for item in loads:
        item.start()
    base_load = pltpu.make_async_copy(base, base_v, base_sem.at[0])

    def land_load(i):
        return pltpu.make_async_copy(mlp_land.at[:, pl.ds(i * tile, tile)], land_v.at[i % 2], land_sem.at[i % 2])

    def result_copy(i):
        at = pl.ds(i * tile, tile)
        return pltpu.make_async_copy(base_v.at[at], output.at[at], res_sem.at[i])

    def finish_output(i):
        at = pl.ds(i * tile, tile)
        land_load(i).wait()
        total = base_v[at]
        for step in range(1, heads):
            total += land_v[i % 2, step - 1].astype(F32)
        base_v[at] = total
        result_copy(i).start()
        if i + 2 < chunks:
            land_load(i + 2).start()

    def x_copy(i, step):
        at = pl.ds(i * tile, tile)
        return remote(part_low.at[at], arrived.at[step - 1, at], x_send.at[i, step - 1], x_recv.at[i, step - 1],
                      {"head": (head + step) % heads})

    def n_copy(step):
        return remote(norm_own, norm_land.at[step - 1], n_send.at[step - 1], n_recv.at[step - 1], {"head": (head + step) % heads})

    def out_copy(i):
        at = pl.ds(i * tile, tile)
        return pltpu.make_async_copy(out_v.at[at], tokens_grad.at[at], out_sem.at[i])

    greet_all(ny, heads)
    down.begin()
    for item in loads[:4]:
        item.wait()
    for i in range(chunks):
        at = pl.ds(i * tile, tile)
        total = jnp.zeros((tile, d_model), F32)
        for c, g in enumerate((gq_v, gk_v, gv_v)):
            total += dot(g[at], w_v[:, 128 + c * width:128 + (c + 1) * width], 1, 1)
        part_one[at] = total
        part_low[at] = total.astype(LOW)
        for step in range(1, heads):
            x_copy(i, step).start()
        if i == 0:
            down.one()
    for item in loads[4:]:
        item.wait()
    per_z = d_model // ZS
    for zz in range(ZS):
        cols = n1_v[:, zz * per_z:(zz + 1) * per_z]
        for c, g in enumerate((gq_v, gk_v, gv_v)):
            value = dot(cols, g[...], 0, 0).astype(LOW)
            parts_qkv[zz, :, :, :, 128 + c * width:128 + (c + 1) * width] = value.reshape(ny, 2, rl, width)
    qkv_b.begin()
    base_load.start()
    for i in range(min(2, chunks)):
        land_load(i).start()
    gain = w_v[:, :128].astype(F32).T[0:1]

    def hat_of(at):
        x = x_v[at].astype(F32)
        centre = x - jnp.mean(x, axis=1, keepdims=True)
        spread = lax.rsqrt(jnp.mean(centre * centre, axis=1, keepdims=True) + 1e-05)
        return centre * spread, spread

    gain_sum = jnp.zeros((1, d_model), F32)
    shift_sum = jnp.zeros((1, d_model), F32)
    for i in range(chunks):
        at = pl.ds(i * tile, tile)
        hat, _ = hat_of(at)
        gain_sum += jnp.sum(part_one[at] * hat, axis=0, keepdims=True)
        shift_sum += jnp.sum(part_one[at], axis=0, keepdims=True)
        if i == chunks // 2:
            qkv_b.one()
    sums = jnp.concatenate([gain_sum, shift_sum, norm_two[0:2], jnp.zeros((124, d_model), F32)], axis=0).T.astype(LOW)
    parts_qkv[:, :, :, :, :128] = sums.reshape(ZS, ny, 2, rl, 128)
    qkv_a.begin()

    def receive(i):
        at = pl.ds(i * tile, tile)
        total = part_one[at]
        for step in range(1, heads):
            x_copy(i, step).wait_recv()
            total += arrived[step - 1, at].astype(F32)
        hat, spread = hat_of(at)
        scaled = total * gain
        inner = scaled - jnp.mean(scaled, axis=1, keepdims=True) - hat * jnp.mean(scaled * hat, axis=1, keepdims=True)
        out_v[at] = res_v[at] + inner * spread
        out_copy(i).start()

    mine_down[:, :down_a.shape[1]] = down_a[...]
    mine_down[:, down_a.shape[1]:down_cols[0]] = down_b[...]
    base_load.wait()
    stages = [lambda: qkv_a.one(), lambda: down.two(), lambda: qkv_b.two(), lambda: down.three(mine_down.at[:, pl.ds(*down_cols)], True), lambda: qkv_a.two(),
              lambda: qkv_b.three(mine_qkv), lambda: qkv_a.three(mine_qkv)]
    when = [0, 1, 3, 4, 5, 6, 7]
    for i in range(chunks):
        for at, stage in zip(when, stages):
            if at * chunks // 8 == i:
                stage()
        if i == chunks - 1:
            norm_own[...] = mine_qkv[:, :128]
            for step in range(1, heads):
                n_copy(step).start()
        finish_output(i)
        receive(i)
    total = mine_qkv[:, :128]
    for step in range(1, heads):
        n_copy(step).wait()
        total += norm_land[step - 1]
    mine_norm[...] = total.T[:8]
    for c in range(3):
        mine_w[c] = mine_qkv[:, 128 + c * width:128 + (c + 1) * width]
    for item in (down, qkv_a, qkv_b):
        item.finish()
    for i in range(chunks):
        out_copy(i).wait()
        result_copy(i).wait()
        for step in range(1, heads):
            x_copy(i, step).wait_send()


def last_stage(gq, gk, gv, n1, tokens, resid, full_qkv, norm_two, parts_down, base, mlp_land, down_a, down_b, scenes, heads):
    ny = scenes // ZS
    rows, d_model = tokens.shape
    width, hidden = gq.shape[1], parts_down.shape[-1]
    first, second, third = shares(hidden)
    rl = d_model // (2 * scenes)
    wide = full_qkv.shape[1]
    tile = min(128, rows)
    chunks = rows // tile
    split = (wide // 128 + 1) // 2 * 128
    others = max(heads - 1, 1)
    sem = pltpu.SemaphoreType.DMA
    shape, vmem = jax.ShapeDtypeStruct, pltpu.VMEM
    any_space, whole = pl.BlockSpec(memory_space=pl.ANY), pl.BlockSpec(memory_space=pltpu.VMEM)
    scratch = [vmem((rows, width), LOW), vmem((rows, width), LOW), vmem((rows, width), LOW), vmem((rows, d_model), LOW),
               vmem((rows, d_model), LOW), vmem((rows, d_model), F32), vmem((d_model, wide), LOW), sem((7,)),
               vmem((rows, d_model), F32), vmem((rows, d_model), LOW), vmem((others, rows, d_model), LOW),
               vmem((ZS, ny, 2, rl, wide), LOW), vmem((others, rl, 128), F32), vmem((rl, 128), F32),
               vmem((rows, d_model), F32), sem((chunks, others)), sem((chunks, others)), sem((others,)), sem((others,)),
               sem((chunks,)), vmem((rows, d_model), F32), vmem((2, others, tile, d_model), LOW), vmem((rl, wide), F32),
               sem((1,)), sem((2,)), sem((chunks,))]
    for cols in (third, split, wide - split):
        scratch += scatter_scratch(ny, rl, cols)
    return pl.pallas_call(
        partial(last_kernel, (ny, heads, rows, d_model, width, tile, split, (first + second, third))),
        out_shape=[shape((rows, d_model), F32), shape((rows, d_model), F32), shape((3, rl, width), F32), shape((8, rl), F32),
                   shape((rl, hidden), F32)],
        in_specs=[any_space] * 7 + [whole, any_space, any_space, any_space, whole, whole],
        out_specs=[any_space, any_space, whole, whole, whole],
        scratch_shapes=scratch,
        compiler_params=pltpu.CompilerParams(collective_id=2, has_side_effects=True, vmem_limit_bytes=63 * 2**20),
        cost_estimate=pl.CostEstimate(flops=12 * rows * d_model * width, bytes_accessed=30 * 2**20, transcendentals=0),
        name="last_stage",
    )(gq, gk, gv, n1, tokens, resid, full_qkv, norm_two, parts_down, base, mlp_land, down_a, down_b)


def on_device(n_scene, n_head, tokens, counts, w_qkv, w_out, w_up, w_down, gain_one, shift_one, gain_two, shift_two, cotangent):
    rows, d_model = tokens.shape
    width, hidden = w_qkv.shape[2], w_up.shape[1]
    size = 64
    core = lax.axis_index("seq")
    limits = jnp.stack([counts[0] - core * rows, counts[0] - (1 - core) * rows]).astype(jnp.int32)
    columns = jnp.pad(jnp.stack([gain_one, shift_one, gain_two, shift_two], axis=1), ((0, 0), (0, 124)))
    shard_qkv = jnp.concatenate([columns, w_qkv[0], w_qkv[1], w_qkv[2]], axis=1)
    n1, q, k, v, full_qkv, full_out, full_up, full_down, probs, context, context_all, inverse = forward(
        limits, shard_qkv, w_out.T, w_up, w_down.T, tokens, n_scene, n_head, size)
    grad_resid, base, mlp_low, grad_context, norm_two, grad_outproj, grad_up, grad_down, down_a = middle(
        tokens, context_all, cotangent, full_qkv, full_out, full_up, full_down, n_scene, n_head)
    gq, gk, gv, mine_out, mine_up, down_b, mlp_land = backward(
        probs, q, k, v, grad_context, context, inverse, grad_outproj, grad_up, grad_down, mlp_low, n_scene, n_head, size)
    tokens_grad, output, mine_qkv, norms, mine_down = last_stage(
        gq, gk, gv, n1, tokens, grad_resid, full_qkv, norm_two, grad_down, base, mlp_land, down_a, down_b, n_scene, n_head)
    return (output, tokens_grad, mine_qkv, mine_out.T, mine_up, mine_down.T, norms[0], norms[1], norms[2], norms[3])


def solution(mesh):
    rows, both = ("scene", "seq"), P(("scene", "seq"))
    weights = (P(None, rows, "head"), P("head", rows), P(rows, "head"), P("head", rows), both, both, both, both)
    return jax.shard_map(
        partial(on_device, mesh.shape["scene"], mesh.shape["head"]), mesh=mesh,
        in_specs=(P(rows, None), P("scene"), *weights, P(rows, None)),
        out_specs=(P(rows, None), P(rows, None), *weights),
        check_vma=False,
    )
```

```python
from functools import partial

import jax
import jax.numpy as jnp
from jax import lax
from jax.experimental import pallas as pl
from jax.experimental.pallas import tpu as pltpu
from jax.sharding import PartitionSpec as P

MESH = pl.DeviceIdType.MESH
ZS = 4


def place(ny):
    scene = lax.axis_index("scene")
    return scene // ny, scene % ny, lax.axis_index("seq")


def remote(src, dst, send_sem, recv_sem, device):
    return pltpu.make_async_remote_copy(
        src_ref=src, dst_ref=dst, send_sem=send_sem, recv_sem=recv_sem,
        device_id=device, device_id_type=MESH,
    )


F32 = jnp.float32
LOW = jnp.bfloat16


def dot(a, b, ca, cb):
    return lax.dot_general(a, b, (((ca,), (cb,)), ((), ())), preferred_element_type=F32)


def only_head(x, h, size):
    lane = lax.broadcasted_iota(jnp.int32, x.shape, 1)
    return jnp.where(lane // size == h, x, jnp.zeros_like(x))


class Gather:
    def __init__(self, ny, source, full, cols, sems):
        self.ny, self.source, self.full, self.cols = ny, source, full, cols
        self.rsend, self.rrecv, self.lsend, self.lrecv, self.ysend, self.yrecv, self.csend, self.crecv = sems
        self.z, self.y, self.core = place(ny)

    def at(self, zz, yy):
        return self.full.at[zz, yy, self.core, :, self.cols]

    def right(self, k):
        src = self.source() if k == 0 else self.at(self.z - k, self.y)
        dst = self.at(self.z - k, self.y)
        return remote(src, dst, self.rsend.at[k], self.rrecv.at[k], {"scene": (self.z + 1) * self.ny + self.y})

    def left(self, k):
        src = self.source() if k == 0 else self.at(self.z + k, self.y)
        dst = self.at(self.z + k, self.y)
        return remote(src, dst, self.lsend.at[k], self.lrecv.at[k], {"scene": (self.z - 1) * self.ny + self.y})

    def across(self, zz, step, own=False):
        src = self.source() if own else self.at(zz, self.y)
        peer = self.z * self.ny + (self.y + step) % self.ny
        return remote(src, self.at(zz, self.y), self.ysend.at[step - 1], self.yrecv.at[step - 1], {"scene": peer})

    def arrival(self, zz, step):
        yy = (self.y + self.ny - step) % self.ny
        return remote(self.at(zz, yy), self.at(zz, yy), self.ysend.at[step - 1], self.yrecv.at[step - 1],
                      {"scene": self.z * self.ny + yy})

    def twin(self, zz, step, own=False):
        src = self.source() if own else self.at(zz, (self.y + self.ny - step) % self.ny)
        dst = self.at(zz, (self.y + self.ny - step) % self.ny)
        return remote(src, dst, self.csend.at[0], self.crecv.at[0], {"seq": 1 - self.core})

    def column(self, step):
        yy = (self.y + self.ny - step) % self.ny
        all_z = self.full.at[:, yy, self.core, :, self.cols]
        return remote(all_z, all_z, self.ysend.at[step - 1], self.yrecv.at[step - 1], {"scene": self.z * self.ny + yy})

    def twins(self):
        mine, theirs = [self.full.at[:, :, c, :, self.cols] for c in (self.core, 1 - self.core)]
        return [remote(item, item, self.csend.at[0], self.crecv.at[0], {"seq": 1 - self.core}) for item in (mine, theirs)]

    def begin(self):
        @pl.when(self.z < ZS - 1)
        def _():
            self.right(0).start()

        @pl.when(self.z > 0)
        def _():
            self.left(0).start()

        for step in range(1, self.ny):
            self.across(self.z, step, True).start()
        self.twin(self.z, 0, True).start()

    def hop(self, k):
        @pl.when(self.z >= k)
        def _():
            self.right(k - 1).wait_recv()
            if k < ZS - 1:
                @pl.when(self.z < ZS - 1)
                def _():
                    self.right(k).start()
            for step in range(1, self.ny):
                self.across(self.z - k, step).start()
            self.twin(self.z - k, 0).start()

        @pl.when(self.z + k < ZS)
        def _():
            self.left(k - 1).wait_recv()
            if k < ZS - 1:
                @pl.when(self.z > 0)
                def _():
                    self.left(k).start()
            for step in range(1, self.ny):
                self.across(self.z + k, step).start()
            self.twin(self.z + k, 0).start()

    def spread(self):
        for step in range(1, self.ny):
            self.column(step).wait_recv()
            for zz in range(ZS):
                self.twin(zz, step).start()

    def finish(self):
        for k in range(ZS - 1):
            @pl.when((self.z < ZS - 1) & (self.z >= k))
            def _():
                self.right(k).wait_send()

            @pl.when((self.z > 0) & (self.z + k < ZS))
            def _():
                self.left(k).wait_send()
        for step in range(1, self.ny):
            self.column(step).wait_send()
        mine, theirs = self.twins()
        mine.wait_send()
        theirs.wait_recv()


class PairGather(Gather):
    def row(self, zz):
        return self.full.at[zz, :, self.core, :, self.cols]

    def right(self, k):
        return remote(self.row(self.z - k), self.row(self.z - k), self.rsend.at[k], self.rrecv.at[k],
                      {"scene": (self.z + 1) * self.ny + self.y})

    def left(self, k):
        return remote(self.row(self.z + k), self.row(self.z + k), self.lsend.at[k], self.lrecv.at[k],
                      {"scene": (self.z - 1) * self.ny + self.y})

    def twin(self, zz):
        return remote(self.row(zz), self.row(zz), self.csend.at[0], self.crecv.at[0], {"seq": 1 - self.core})

    def begin(self):
        for step in range(1, self.ny):
            self.across(self.z, step, True).start()

    def pair(self):
        for step in range(1, self.ny):
            self.arrival(self.z, step).wait_recv()

        @pl.when(self.z < ZS - 1)
        def _():
            self.right(0).start()

        @pl.when(self.z > 0)
        def _():
            self.left(0).start()

        self.twin(self.z).start()

    def hop(self, k):
        @pl.when(self.z >= k)
        def _():
            self.right(k - 1).wait_recv()
            if k < ZS - 1:
                @pl.when(self.z < ZS - 1)
                def _():
                    self.right(k).start()
            self.twin(self.z - k).start()

        @pl.when(self.z + k < ZS)
        def _():
            self.left(k - 1).wait_recv()
            if k < ZS - 1:
                @pl.when(self.z > 0)
                def _():
                    self.left(k).start()
            self.twin(self.z + k).start()

    def finish(self):
        for k in range(ZS - 1):
            @pl.when((self.z < ZS - 1) & (self.z >= k))
            def _():
                self.right(k).wait_send()

            @pl.when((self.z > 0) & (self.z + k < ZS))
            def _():
                self.left(k).wait_send()
        for step in range(1, self.ny):
            self.across(self.z, step).wait_send()
        mine, theirs = self.twins()
        mine.wait_send()
        theirs.wait_recv()


def gather_sems(ny):
    sem = pltpu.SemaphoreType.DMA
    return [sem((ZS - 1,)), sem((ZS - 1,)), sem((ZS - 1,)), sem((ZS - 1,)), sem((max(ny - 1, 1),)), sem((max(ny - 1, 1),)),
            sem((1,)), sem((1,))]


def greet_all(ny, heads):
    z, y, core = place(ny)
    head = lax.axis_index("head")
    barrier = pltpu.get_barrier_semaphore()

    def signal(device):
        pl.semaphore_signal(barrier, 1, device_id=device, device_id_type=MESH)

    for step in range(1, ZS):
        signal({"scene": (z + step) % ZS * ny + y})
    for step in range(1, ny):
        signal({"scene": z * ny + (y + step) % ny})
    for step in range(1, heads):
        signal({"head": (head + step) % heads})
    signal({"seq": 1 - core})
    pl.semaphore_wait(barrier, ZS + ny - 1 + heads - 1)


def split_cols(total, parts):
    size = total // parts
    return [pl.ds(i * size, size) for i in range(parts)]


def forward_kernel(dims, limits, shard_qkv, shard_out, shard_up, shard_down, tokens,
                   n1_out, q_out, k_out, v_out, full_qkv, full_out, full_up, full_down, probs, context, context_all, inverse,
                   w0, hat, n1, q_s, k_s, v_s, bias, ctx_s, scores, tops, local_sem, kv_send, kv_recv, xw_send, xw_recv, xt_send, xt_recv, xc_send, xc_recv, *sems):
    ny, heads, rows, width, size, block, pairs, steps_q, halves = dims
    pair, part = pl.program_id(0), pl.program_id(1)
    step = pair * steps_q + part
    z, y, core = place(ny)
    head = lax.axis_index("head")
    d_model = tokens.shape[1]
    per = 8
    own_cols = pl.ds(pl.multiple_of(head * width, width), width)

    def of(i):
        return sems[i * per:(i + 1) * per]

    group = 6 * size
    edges = [0] + [128 + (p + 1) * group for p in range(pairs)]
    firsts = []
    for p in range(pairs):
        cols = pl.ds(edges[p], edges[p + 1] - edges[p])
        firsts.append(Gather(ny, partial(lambda c: shard_qkv.at[:, c], cols), w0, cols, of(2 + 2 * halves + p)))
    outer = Gather(ny, lambda: shard_out, full_out, own_cols, of(1))
    thick = []
    for n, (shard, full) in enumerate(((shard_up, full_up), (shard_down, full_down))):
        for i, cols in enumerate(split_cols(full_up.shape[-1], halves)):
            kind = PairGather if n == 1 and i == halves - 1 else Gather
            thick.append(kind(ny, partial(lambda s, c: s.at[:, c], shard, cols), full, cols, of(2 + n * halves + i)))
    up_a, up_b, down_a, down_b = thick

    def local(src, dst, i):
        return pltpu.make_async_copy(src, dst, local_sem.at[i])

    def cols_of(step):
        return pl.ds(pl.multiple_of((head + heads - step) % heads * width, width), width)

    def out_copy(step):
        mine = full_out.at[:, :, core, :, own_cols]
        return remote(mine, mine, xw_send.at[step - 1], xw_recv.at[step - 1], {"head": (head + step) % heads})

    def out_twin(step):
        other = full_out.at[:, :, core, :, cols_of(step)]
        return remote(other, other, xt_send.at[step - 1], xt_recv.at[step - 1], {"seq": 1 - core})

    def kv_copy(p, i):
        src = (k_s, v_s)[i]
        cols = pl.ds(p * 2 * size, 2 * size)
        return remote(src.at[pl.ds(0, rows), cols], src.at[pl.ds(rows, rows), cols], kv_send.at[p, i], kv_recv.at[p, i],
                      {"seq": 1 - core})

    def project(p):
        tile = min(256, rows)

        @pl.loop(0, rows // tile)
        def _(i):
            at = pl.ds(pl.multiple_of(i * tile, tile), tile)
            w = w0[:, :, :, :, 128 + p * group:128 + (p + 1) * group].reshape(d_model, group)
            value = dot(n1[at], w, 1, 0).astype(LOW)
            cols = pl.ds(p * 2 * size, 2 * size)
            q_s[at, cols] = value[:, :2 * size] * LOW(size ** -0.5)
            k_s[at, cols] = value[:, 2 * size:4 * size]
            v_s[at, cols] = value[:, 4 * size:]

        for i in range(2):
            kv_copy(p, i).start()

    def ctx_copy(p, step):
        cols = pl.ds(pl.multiple_of(p * 2 * size, 2 * size), 2 * size)
        wide = pl.ds(pl.multiple_of(head * width + p * 2 * size, 2 * size), 2 * size)
        return remote(ctx_s.at[:, cols], context_all.at[:, wide], xc_send.at[p, step - 1], xc_recv.at[p, step - 1],
                      {"head": (head + step) % heads})

    own_blocks = [(shard_qkv, w0.at[z, y, core], 0), (shard_out, full_out.at[z, y, core, :, own_cols], 1),
                  (shard_up, full_up.at[z, y, core], 2), (shard_down, full_down.at[z, y, core], 3)]
    results = [(w0, full_qkv, 4), (n1, n1_out, 5), (q_s, q_out, 6), (k_s, k_out, 7), (v_s, v_out, 8)]
    ctx_local = (ctx_s, context_all.at[:, own_cols], 9)

    @pl.when(step == 0)
    def _():
        for item in own_blocks:
            local(*item).start()
        greet_all(ny, heads)
        for gather in firsts[:2]:
            gather.begin()
        tile = min(128, rows)

        @pl.loop(0, rows // tile)
        def _(i):
            at = pl.ds(pl.multiple_of(i * tile, tile), tile)
            x = tokens[at].astype(F32)
            centre = x - jnp.mean(x, axis=1, keepdims=True)
            spread = jnp.mean(centre * centre, axis=1, keepdims=True)
            hat[at] = centre * lax.rsqrt(spread + 1e-05)

        low_rows = lax.broadcasted_iota(jnp.int32, bias.shape, 0)
        lane = lax.broadcasted_iota(jnp.int32, bias.shape, 1)
        limit = jnp.where(low_rows < rows, limits[0], limits[1] + rows)
        bias[...] = jnp.where((low_rows >= limit) & (lane == 0), -1e30, 0.0).astype(LOW)
        after = [
            (0, lambda g: g.hop(1)), (2, lambda g: g.begin()), (0, lambda g: g.hop(2)), (1, lambda g: g.hop(1)), (0, lambda g: g.hop(3)),
            (3, lambda g: g.begin()), (1, lambda g: g.hop(2)), (0, lambda g: g.spread()), (1, lambda g: g.hop(3)),
            (2, lambda g: g.hop(1)), (1, lambda g: g.spread()), (2, lambda g: g.hop(2))]
        for p, act in after[:9]:
            if p < pairs:
                act(firsts[p])
        firsts[0].finish()
        for item in own_blocks:
            local(*item).wait()
        norms = w0[:, :, :, :, :128].reshape(d_model, 128).astype(F32).T
        gain, shift = norms[0:1], norms[1:2]
        tile = min(256, rows)

        @pl.loop(0, rows // tile)
        def _(i):
            at = pl.ds(pl.multiple_of(i * tile, tile), tile)
            n1[at] = (hat[at] * gain + shift).astype(LOW)

        local(*results[1]).start()
        project(0)
        for p, act in after[9:]:
            if p < pairs:
                act(firsts[p])

    total = pairs * steps_q
    per_slot = 2
    in_step = 4 * rows // min(256, rows) // per_slot
    slots = in_step * total

    def send_out():
        for i in range(1, heads):
            out_copy(i).start()

    def pass_out():
        for i in range(1, heads):
            out_copy(i).wait_recv()
            out_twin(i).start()

    def on_pair(p, what, *given):
        if p < pairs:
            getattr(firsts[p], what)(*given)

    events = [
        (0.1, lambda: on_pair(2, "hop", 3)), (0.3, lambda: on_pair(3, "hop", 1)), (0.4, outer.begin),
        (1, lambda: on_pair(3, "hop", 2)), (1.2, lambda: on_pair(2, "spread")), (1.4, up_a.begin),
        (2, lambda: on_pair(3, "hop", 3)), (2.6, lambda: outer.hop(1)), (3.2, lambda: outer.hop(2)), (3.2, up_b.begin),
        (3.8, lambda: on_pair(3, "spread")), (3.9, lambda: outer.hop(3)), (5.2, lambda: up_a.hop(1)), (6, outer.spread), (6.1, send_out),
        (6.5, lambda: up_a.hop(2)), (7, down_a.begin), (7.2, down_b.begin),
        (7.8, lambda: up_a.hop(3)), (9.2, lambda: up_b.hop(1)), (10.5, lambda: up_b.hop(2)), (10.6, pass_out), (10.8, down_b.pair),
        (11.8, lambda: up_b.hop(3)), (12, up_a.spread), (13.2, lambda: down_a.hop(1)), (14.5, lambda: down_a.hop(2)),
        (15.8, lambda: down_a.hop(3)), (16, up_b.spread), (16, lambda: down_b.hop(1)),
        (16, lambda: down_b.hop(2)), (16, down_a.spread), (16, lambda: down_b.hop(3))]

    def run(slot_in_step):
        for when, act in events:
            slot = min(int(when * slots / 16), slots - 1)
            if when < 16 and slot % in_step == slot_in_step:
                pl.when(step == slot // in_step)(act)

    for p in range(pairs):
        @pl.when(step == p * steps_q)
        def _():
            if p == 0:
                for i in range(2):
                    kv_copy(0, i).wait()
            if p + 1 < pairs:
                firsts[p + 1].finish()
                project(p + 1)
            else:
                for item in (results[0], *results[2:]):
                    local(*item).start()

        if p + 1 < pairs:
            @pl.when(step == (p + 1) * steps_q - 1)
            def _():
                for i in range(2):
                    kv_copy(p + 1, i).wait()

    width2, chunk = 2 * size, min(256, rows)
    n_chunks = 2 * rows // chunk
    ones = (lax.broadcasted_iota(jnp.int32, (block, bias.shape[1]), 1) == 0).astype(LOW)

    def asked(at, h):
        rows_at = pl.ds(pl.multiple_of(at % steps_q * block, block), block)
        cols_at = pl.ds(pl.multiple_of(at // steps_q * width2, width2), width2)
        return jnp.concatenate([only_head(q_s[rows_at, cols_at], h, size), ones], axis=1)

    def score(at, query, slot, c, top):
        cols_at = pl.ds(pl.multiple_of(at // steps_q * width2, width2), width2)
        keys_at = pl.ds(c * chunk, chunk)
        value = dot(jnp.concatenate([k_s[keys_at, cols_at], bias[keys_at]], axis=1), query, 1, 1)
        scores[slot, keys_at] = value
        return jnp.maximum(top, jnp.max(value.reshape(chunk // 8, 8, block), axis=0))

    def weigh(h, c, top, total_e):
        keys_at = pl.ds(c * chunk, chunk)
        expo = jnp.exp(scores[h, keys_at] - top)
        probs[h, keys_at] = expo.astype(LOW)
        return total_e + jnp.sum(expo.reshape(chunk // 8, 8, block), axis=0)

    lowest = jnp.full((8, block), -3e38, F32)

    @pl.when(step == 0)
    def _():
        top, query = lowest, asked(0, 0)
        for c in range(n_chunks):
            top = score(0, query, 0, c, top)
        tops[...] = top

    cols = pl.ds(pl.multiple_of(pair * width2, width2), width2)
    following = jnp.minimum(step + 1, total - 1)
    values_t = v_s[:, cols].T
    pieces = []
    for h in range(2):
        top = jnp.max(tops[...], axis=0, keepdims=True)
        total_e, next_top = jnp.zeros((8, block), F32), lowest
        ahead = (step, 1) if h == 0 else (following, 0)
        query = asked(*ahead)
        for c in range(n_chunks):
            if c % per_slot == 0:
                run(h * (n_chunks // per_slot) + c // per_slot)
            next_top = score(ahead[0], query, 1 - h, c, next_top)
            total_e = weigh(h, c, top, total_e)
        tops[...] = next_top
        over = 1.0 / jnp.sum(total_e, axis=0, keepdims=True)
        pieces.append(dot(values_t, probs[h], 1, 0)[h * size:(h + 1) * size] * over)
        inverse[0, h:h + 1] = over
    here = jnp.concatenate(pieces, axis=0).T.astype(LOW)
    context[...] = here
    ctx_s[pl.ds(pl.multiple_of(part * block, block), block), cols] = here

    @pl.when(part == steps_q - 1)
    def _():
        for i in range(1, heads):
            ctx_copy(pair, i).start()

    @pl.when(step == total - 1)
    def _():
        local(*ctx_local).start()
        for when, act in events:
            if when >= 16:
                act()
        for gather in (outer, *thick):
            gather.finish()
        for item in results:
            local(*item).wait()
        local(*ctx_local).wait()
        for i in range(1, heads):
            out_copy(i).wait_send()
            out_twin(i).wait()
            for p in range(pairs):
                ctx_copy(p, i).wait()


def forward(limits, shard_qkv, shard_out, shard_up, shard_down, tokens, scenes, heads, size):
    ny = scenes // ZS
    rows, d_model = tokens.shape
    rl, width = shard_out.shape
    hidden = shard_up.shape[1]
    pairs = width // (2 * size)
    block = min(512, rows)
    steps_q = rows // block
    halves = 2
    sem = pltpu.SemaphoreType.DMA
    any_space = pl.BlockSpec(memory_space=pl.ANY)
    shape = jax.ShapeDtypeStruct
    wide = shard_qkv.shape[1]
    outs = [shape((rows, d_model), LOW), shape((rows, width), LOW), shape((2 * rows, width), LOW), shape((2 * rows, width), LOW),
            shape((ZS, ny, 2, rl, wide), LOW), shape((ZS, ny, 2, rl, d_model), LOW), shape((ZS, ny, 2, rl, hidden), LOW),
            shape((ZS, ny, 2, rl, hidden), LOW), shape((2 * pairs, 2 * rows, rows), LOW), shape((rows, width), LOW),
            shape((rows, d_model), LOW), shape((pairs, 8, rows), F32)]
    out_specs = [any_space] * 8 + [
        pl.BlockSpec((2, 2 * rows, block), lambda p, i: (p, 0, i)), pl.BlockSpec((block, 2 * size), lambda p, i: (i, p)),
        any_space, pl.BlockSpec((1, 8, block), lambda p, i: (p, 0, i))]
    scratch = [pltpu.VMEM((ZS, ny, 2, rl, wide), LOW), pltpu.VMEM((rows, d_model), F32), pltpu.VMEM((rows, d_model), LOW),
               pltpu.VMEM((rows, width), LOW), pltpu.VMEM((2 * rows, width), LOW), pltpu.VMEM((2 * rows, width), LOW),
               pltpu.VMEM((2 * rows, 128), LOW), pltpu.VMEM((rows, width), LOW),
               pltpu.VMEM((2, 2 * rows, block), F32), pltpu.VMEM((8, block), F32), sem((10,)), sem((pairs, 2)), sem((pairs, 2)),
               sem((max(heads - 1, 1),)), sem((max(heads - 1, 1),)), sem((max(heads - 1, 1),)), sem((max(heads - 1, 1),)), sem((pairs, max(heads - 1, 1))), sem((pairs, max(heads - 1, 1)))]
    for _ in range(2 + 2 * halves + pairs):
        scratch += gather_sems(ny)
    dims = (ny, heads, rows, width, size, block, pairs, steps_q, halves)
    flops = 2 * rows * d_model * 3 * width + 8 * rows * rows * width
    results = pl.pallas_call(
        partial(forward_kernel, dims),
        grid=(pairs, steps_q),
        out_shape=outs,
        in_specs=[pl.BlockSpec(memory_space=pltpu.SMEM)] + [pl.BlockSpec(memory_space=pltpu.VMEM)] * 4 + [pl.BlockSpec(memory_space=pltpu.VMEM)],
        out_specs=out_specs,
        scratch_shapes=scratch,
        compiler_params=pltpu.CompilerParams(collective_id=0, has_side_effects=True, vmem_limit_bytes=60 * 2**20),
        cost_estimate=pl.CostEstimate(flops=flops, bytes_accessed=60 * 2**20, transcendentals=0),
        name="forward_attention",
    )(limits, shard_qkv, shard_out, shard_up, shard_down, tokens)
    n1, q, k, v, full_qkv, full_out, full_up, full_down, probs, context, context_all, inverse = results
    flat = lambda a: a.reshape(d_model, a.shape[-1])
    return n1, q, k, v, flat(full_qkv), flat(full_out), flat(full_up), flat(full_down), probs, context, context_all, inverse


class Scatter:
    def __init__(self, ny, parts, cols, bufs, sems):
        self.ny, self.parts, self.cols = ny, parts, cols
        self.own, self.from_core, self.from_y, self.sum_two, self.from_z = bufs
        self.load_sem, self.csend, self.crecv, self.ysend, self.yrecv, self.zsend, self.zrecv = sems
        self.z, self.y, self.core = place(ny)

    def load(self):
        return pltpu.make_async_copy(self.parts.at[:, :, self.core, :, self.cols], self.own, self.load_sem.at[0])

    def to_core(self):
        return remote(self.parts.at[:, :, 1 - self.core, :, self.cols], self.from_core, self.csend.at[0], self.crecv.at[0],
                      {"seq": 1 - self.core})

    def to_y(self, step):
        yy = (self.y + step) % self.ny
        return remote(self.own.at[:, yy], self.from_y.at[step - 1], self.ysend.at[step - 1], self.yrecv.at[step - 1],
                      {"scene": self.z * self.ny + yy})

    def to_z(self, step):
        zz = (self.z + step) % ZS
        return remote(self.sum_two.at[zz], self.from_z.at[step - 1], self.zsend.at[step - 1], self.zrecv.at[step - 1],
                      {"scene": zz * self.ny + self.y})

    def begin(self):
        self.load().start()
        self.to_core().start()

    def one(self):
        self.load().wait()
        self.to_core().wait_recv()
        for zz in range(ZS):
            for yy in range(self.ny):
                self.own[zz, yy] = (self.own[zz, yy].astype(F32) + self.from_core[zz, yy].astype(F32)).astype(LOW)
        for step in range(1, self.ny):
            self.to_y(step).start()

    def two(self):
        for step in range(1, self.ny):
            self.to_y(step).wait_recv()
        for zz in range(ZS):
            total = self.own[zz, self.y].astype(F32)
            for step in range(1, self.ny):
                total += self.from_y[step - 1, zz].astype(F32)
            self.sum_two[zz] = total.astype(LOW)
        for step in range(1, ZS):
            self.to_z(step).start()

    def three(self, out, alone=False):
        for step in range(1, ZS):
            self.to_z(step).wait_recv()
        total = self.sum_two[self.z].astype(F32)
        for step in range(1, ZS):
            total += self.from_z[step - 1].astype(F32)
        if alone:
            out[...] = total
        else:
            out[:, self.cols] = total

    def finish(self):
        self.to_core().wait_send()
        for step in range(1, self.ny):
            self.to_y(step).wait_send()
        for step in range(1, ZS):
            self.to_z(step).wait_send()


SCATTER_BUFS, SCATTER_SEMS = 5, 7


def scatter_scratch(ny, rl, cols):
    sem = pltpu.SemaphoreType.DMA
    other = max(ny - 1, 1)
    return [pltpu.VMEM((ZS, ny, rl, cols), LOW), pltpu.VMEM((ZS, ny, rl, cols), LOW), pltpu.VMEM((other, ZS, rl, cols), LOW),
            pltpu.VMEM((ZS, rl, cols), LOW), pltpu.VMEM((ZS - 1, rl, cols), LOW),
            sem((1,)), sem((1,)), sem((1,)), sem((other,)), sem((other,)), sem((ZS - 1,)), sem((ZS - 1,))]


def make_scatters(ny, plan, scratch):
    n = SCATTER_BUFS + SCATTER_SEMS
    result = []
    for i, (parts, cols) in enumerate(plan):
        mine = scratch[i * n:(i + 1) * n]
        result.append(Scatter(ny, parts, cols, mine[:SCATTER_BUFS], mine[SCATTER_BUFS:]))
    return result

def middle_kernel(dims, tokens, context_all, cotangent, full_qkv, full_out, full_up, full_down,
                  resid_grad, base, mlp_low, grad_context, norm_two, parts_out, parts_up, parts_down, mine_down,
                  x_v, ctx_v, cot_v, norm_v, wo, wu, wd, n2, act, gu, resid, part, low, arrived, up_v, down_v, out_v, gctx_v,
                  base_v, mlp_v, in_sem, out_sem, slot_sem, x_send, x_recv, *scratch):
    ny, heads, rows, d_model, width, hidden, tile, size_f, first_cols = dims
    head = lax.axis_index("head")
    chunks = rows // tile
    (down,) = make_scatters(ny, [(down_v, pl.ds(0, first_cols))], scratch)
    own_cols = pl.ds(pl.multiple_of(head * width, width), width)

    def load(src, dst, i):
        return pltpu.make_async_copy(src, dst, in_sem.at[i])

    loads = [load(context_all, ctx_v, 0), load(full_out, wo, 1), load(tokens, x_v, 2), load(full_qkv.at[:, pl.ds(0, 128)], norm_v, 3),
             load(full_up, wu, 4), load(cotangent, cot_v, 5), load(full_down, wd, 6)]
    for item in loads:
        item.start()

    half = tile // 2

    def rows_of(i):
        if isinstance(i, int) and i == chunks:
            return pl.ds(0, half)
        if isinstance(i, int) and i == 0:
            return pl.ds(half, half)
        return pl.ds(pl.multiple_of(i * tile, tile), tile)

    def x_copy(i, step):
        at = rows_of(i)
        return remote(low.at[at], arrived.at[step - 1, at], x_send.at[i, step - 1], x_recv.at[i, step - 1],
                      {"head": (head + step) % heads})

    greet_all(ny, heads)
    for item in loads[:4]:
        item.wait()
    norms = norm_v[...].astype(F32).T
    gain, shift = norms[2:3], norms[3:4]

    def hat_of(value):
        centre = value - jnp.mean(value, axis=1, keepdims=True)
        spread = lax.rsqrt(jnp.mean(centre * centre, axis=1, keepdims=True) + 1e-05)
        return centre * spread, spread

    for item in loads[4:]:
        item.wait()
    norm_two[...] = jnp.zeros_like(norm_two)

    def forward_and_back(i):
        at = rows_of(i)
        value = x_v[at].astype(F32) + dot(ctx_v[at], wo[...], 1, 1)
        resid[at] = value
        hat = hat_of(value)[0]
        n2[at] = (hat * gain + shift).astype(LOW)
        for f in range(hidden // size_f):
            cols = slice(f * size_f, (f + 1) * size_f)
            u = dot(n2[at], wu[:, cols], 1, 0)
            ga = dot(cot_v[at], wd[:, cols], 1, 0)
            phi = 0.5 + 0.5 * lax.erf(u * (0.5 ** 0.5))
            act[at, cols] = (u * phi).astype(LOW)
            gu[at, cols] = (ga * (phi + u * (jnp.exp(u * u * -0.5) * 0.3989422804014327))).astype(LOW)
        total = dot(gu[at], wu[...], 1, 1)
        part[at] = total
        low[at] = total.astype(LOW)
        for step in range(1, heads):
            x_copy(i, step).start()
        hat, _ = hat_of(resid[at])
        norm_two[0:1] += jnp.sum(total * hat, axis=0, keepdims=True)
        norm_two[1:2] += jnp.sum(total, axis=0, keepdims=True)

    forward_and_back(chunks)
    forward_and_back(0)
    pl.loop(1, chunks)(forward_and_back)

    def weight_grad(src, other, dst):
        per_z = d_model // ZS
        pack = ZS // 2
        for f in range(hidden // size_f):
            cols = slice(f * size_f, (f + 1) * size_f)

            @pl.loop(0, pack)
            def _(j):
                at = pl.ds(pl.multiple_of(j * 2 * per_z, 2 * per_z), 2 * per_z)
                value = dot(src[:, at], other[:, cols], 0, 0).astype(LOW)
                dst[pl.ds(2 * j, 2), :, :, :, cols] = value.reshape(2, *dst.shape[1:4], size_f)

    weight_grad(cot_v, act, down_v)
    down.begin()
    weight_grad(n2, gu, up_v)
    down.one()
    stores = [pltpu.make_async_copy(up_v, parts_up, out_sem.at[0]), pltpu.make_async_copy(down_v, parts_down, out_sem.at[1])]
    for item in stores:
        item.start()

    def slot_copies(i):
        at = pl.ds(pl.multiple_of(i * tile, tile), tile)
        slot = i % 2
        return (pltpu.make_async_copy(base_v.at[slot], base.at[at], slot_sem.at[0, slot]),
                pltpu.make_async_copy(mlp_v.at[slot], mlp_low.at[at], slot_sem.at[1, slot]))

    def slot_loop(i):
        at = pl.ds(pl.multiple_of(i * tile, tile), tile)
        value = dot(act[at], wd[...], 1, 1)

        @pl.when(i >= 2)
        def _():
            for item in slot_copies(i - 2):
                item.wait()

        base_v[i % 2] = resid[at] + value
        mlp_v[i % 2] = value.astype(LOW)
        for item in slot_copies(i):
            item.start()

    pl.loop(0, chunks)(slot_loop)

    for i in range(max(0, chunks - 2), chunks):
        for item in slot_copies(i):
            item.wait()

    def chunk_stores(i):
        at = rows_of(i)
        return (pltpu.make_async_copy(part.at[at], resid_grad.at[at], out_sem.at[3 + 2 * i]),
                pltpu.make_async_copy(gctx_v.at[at], grad_context.at[at], out_sem.at[4 + 2 * i]))

    def receive(i):
        at = rows_of(i)
        total = part[at]
        for step in range(1, heads):
            x_copy(i, step).wait_recv()
            total += arrived[step - 1, at].astype(F32)
        hat, spread = hat_of(resid[at])
        scaled = total * gain
        inner = scaled - jnp.mean(scaled, axis=1, keepdims=True) - hat * jnp.mean(scaled * hat, axis=1, keepdims=True)
        total = cot_v[at].astype(F32) + inner * spread
        part[at] = total
        rounded = total.astype(LOW)
        n2[at] = rounded
        gctx_v[at] = dot(rounded, wo[:, own_cols], 1, 0).astype(LOW)
        for item in chunk_stores(i):
            item.start()

    receive(chunks)
    receive(0)
    if chunks > 2:
        pl.loop(1, chunks - 1)(receive)
    down.two()
    if chunks > 1:
        receive(chunks - 1)

    @pl.loop(0, 2)
    def _(j):
        at = pl.ds(pl.multiple_of(j * (d_model // 2), d_model // 2), d_model // 2)
        out_v[at] = dot(n2[:, at], ctx_v[:, own_cols], 0, 0).astype(LOW)

    store = pltpu.make_async_copy(out_v, parts_out, out_sem.at[2])
    store.start()
    for item in stores:
        item.wait()
    store.wait()
    down.three(mine_down)
    down.finish()
    for i in range(chunks + 1):
        for item in chunk_stores(i):
            item.wait()
        for step in range(1, heads):
            x_copy(i, step).wait_send()


def shares(hidden):
    n = hidden // 128
    first = 3 * n // 8
    return first * 128, (n - first) * 128


def middle(tokens, context_all, cotangent, full_qkv, full_out, full_up, full_down, scenes, heads):
    ny = scenes // ZS
    rows, d_model = tokens.shape
    rl = d_model // (2 * scenes)
    hidden, width = full_up.shape[1], d_model // heads
    tile, size_f = min(256, rows), min(1024, hidden)
    chunks = rows // tile
    first_cols = shares(hidden)[0]
    others = max(heads - 1, 1)
    sem = pltpu.SemaphoreType.DMA
    shape, vmem = jax.ShapeDtypeStruct, pltpu.VMEM
    any_space, whole = pl.BlockSpec(memory_space=pl.ANY), pl.BlockSpec(memory_space=pltpu.VMEM)
    big, wide, blocks = (rows, d_model), (rows, hidden), (ZS, ny, 2, rl, hidden)
    scratch = [vmem(big, LOW), vmem(big, LOW), vmem(big, LOW), vmem((d_model, 128), LOW), vmem((d_model, d_model), LOW),
               vmem((d_model, hidden), LOW), vmem((d_model, hidden), LOW), vmem(big, LOW), vmem(wide, LOW), vmem(wide, LOW),
               vmem(big, F32), vmem(big, F32), vmem(big, LOW), vmem((others, *big), LOW), vmem(blocks, LOW),
               vmem(blocks, LOW), vmem((d_model, width), LOW), vmem((rows, width), LOW), vmem((2, tile, d_model), F32),
               vmem((2, tile, d_model), LOW), sem((7,)), sem((5 + 2 * chunks,)), sem((2, 2)), sem((chunks + 1, others)),
               sem((chunks + 1, others))]
    scratch += scatter_scratch(ny, rl, first_cols)
    return pl.pallas_call(
        partial(middle_kernel, (ny, heads, rows, d_model, width, hidden, tile, size_f, first_cols)),
        out_shape=[shape(big, F32), shape(big, F32), shape(big, LOW), shape((rows, width), LOW), shape((8, d_model), F32),
                   shape((d_model, width), LOW), shape(blocks, LOW), shape(blocks, LOW), shape((rl, first_cols), F32)],
        in_specs=[any_space] * 7,
        out_specs=[any_space] * 4 + [whole] + [any_space] * 3 + [whole],
        scratch_shapes=scratch,
        compiler_params=pltpu.CompilerParams(collective_id=3, has_side_effects=True, vmem_limit_bytes=63 * 2**20),
        cost_estimate=pl.CostEstimate(flops=14 * rows * d_model * hidden, bytes_accessed=50 * 2**20, transcendentals=0),
        name="middle_stage",
    )(tokens, context_all, cotangent, full_qkv, full_out, full_up, full_down)


def backward_kernel(dims, probs, queries, keys, values, grad, context, inverse, parts_out, parts_up, mlp_low,
                    grads, mine_out, mine_up, mlp_land,
                    dk_acc, dv_acc, kept, stage, landed, kv_send, kv_recv, m_send, m_recv, *scratch):
    ny, heads, rows, size, pairs, steps_q, halves = dims
    pair, part = pl.program_id(0), pl.program_id(1)
    step = pair * steps_q + part
    total = pairs * steps_q
    block = grad.shape[0]
    z, y, core = place(ny)
    width = parts_out.shape[-1]
    cols_of = split_cols(parts_up.shape[-1], halves)
    plan = [(parts_out, pl.ds(0, width))] + [(parts_up, cols) for cols in cols_of]
    scatters = make_scatters(ny, plan, scratch)
    targets = [mine_out] + [mine_up] * halves

    def kv_copy(p, i):
        return remote(stage.at[p, i], landed.at[p, i], kv_send.at[p, i], kv_recv.at[p, i], {"seq": 1 - core})

    head = lax.axis_index("head")

    def mlp_copy(i, step):
        return remote(mlp_low.at[pl.ds(i * (rows // 4), rows // 4)], mlp_land.at[step - 1, pl.ds(i * (rows // 4), rows // 4)],
                      m_send.at[i, step - 1], m_recv.at[i, step - 1], {"head": (head + step) % heads})

    @pl.when(step == 0)
    def _():
        greet_all(ny, heads)
        for i in range(4):
            for j in range(1, heads):
                mlp_copy(i, j).start()
        for item in scatters:
            item.begin()

    slots = 2 * total
    plan_at = ((0.6, 3.2, 6.2), (1.2, 8.2, 13.2), (2.2, 13.2, 17))
    events = sorted((plan_at[i][j], i, j + 1) for i in range(3) for j in range(3))

    def run(slot_in_step):
        for when, i, what in events:
            slot = min(int(when * min(1.0, slots / 16)), slots)
            if slot == slots or slot % 2 != slot_in_step:
                continue

            @pl.when(step == slot // 2)
            def _():
                if what == 1:
                    scatters[i].one()
                elif what == 2:
                    scatters[i].two()
                else:
                    scatters[i].three(targets[i])

    @pl.when(part == 0)
    def _():
        dk_acc[...] = jnp.zeros_like(dk_acc)
        dv_acc[...] = jnp.zeros_like(dv_acc)

    upper = grad[...].astype(F32)
    inner = (upper * context[...].astype(F32)).T
    upper_t = upper.T
    row = lax.broadcasted_iota(jnp.int32, upper_t.shape, 0)
    keys_t = keys[...].T
    pieces = []
    for h in range(2):
        run(h)
        over = inverse[0, h:h + 1]
        shift = jnp.sum(inner[h * size:(h + 1) * size], axis=0, keepdims=True) * over
        scaled = jnp.where(row // size == h, upper_t * over, 0.0)
        dp = dot(values[...], scaled.astype(LOW), 1, 0) - shift
        low = probs[h]
        ds = (low.astype(F32) * dp).astype(LOW)
        dv_acc[...] += dot(low, scaled.T.astype(LOW), 1, 0)
        dk_acc[...] += dot(ds, only_head(queries[...], h, size), 1, 0)
        pieces.append(dot(keys_t, ds, 1, 0)[h * size:(h + 1) * size])
    grads[pl.ds(pl.multiple_of(part * block, block), block), pl.ds(pl.multiple_of(pair * 6 * size, 2 * size), 2 * size)] = (
        (jnp.concatenate(pieces, axis=0) * size ** -0.5).T.astype(LOW))

    @pl.when(part == steps_q - 1)
    def _():
        for i, acc in enumerate((dk_acc, dv_acc)):
            stage[pair, i] = acc[rows:].astype(LOW)
            kv_copy(pair, i).start()
            kept[pair, i] = acc[:rows]

    @pl.when(step == total - 1)
    def _():
        for when, i, what in events:
            if min(int(when * min(1.0, slots / 16)), slots) == slots:
                if what == 1:
                    scatters[i].one()
                elif what == 2:
                    scatters[i].two()
                else:
                    scatters[i].three(targets[i])
        for item in scatters:
            item.finish()
        for p in range(pairs):
            for i in range(2):
                kv_copy(p, i).wait()
                grads[:, (3 * p + i + 1) * 2 * size:(3 * p + i + 2) * 2 * size] = (kept[p, i] + landed[p, i].astype(F32)).astype(LOW)
        for i in range(4):
            for j in range(1, heads):
                mlp_copy(i, j).wait()


def backward(probs, q, k, v, grad, context, inverse, parts_out, parts_up, mlp_low, scenes, heads, size):
    ny = scenes // ZS
    rows, width = q.shape
    pairs = width // (2 * size)
    block = min(512, rows)
    d_model, hidden = parts_out.shape[0], parts_up.shape[-1]
    rl = d_model // (2 * scenes)
    others = max(heads - 1, 1)
    halves = 2
    spec = pl.BlockSpec
    q_spec = spec((block, 2 * size), lambda p, i: (i, p))
    k_spec = spec((2 * rows, 2 * size), lambda p, i: (0, p))
    any_space = spec(memory_space=pl.ANY)
    whole = spec(memory_space=pltpu.VMEM)
    shape = jax.ShapeDtypeStruct
    sem = pltpu.SemaphoreType.DMA
    pair_buf = (pairs, 2, rows, 2 * size)
    scratch = [pltpu.VMEM((2 * rows, 2 * size), F32), pltpu.VMEM((2 * rows, 2 * size), F32), pltpu.VMEM(pair_buf, F32),
               pltpu.VMEM(pair_buf, LOW), pltpu.VMEM(pair_buf, LOW), sem((pairs, 2)), sem((pairs, 2)), sem((4, others)), sem((4, others))]
    scratch += scatter_scratch(ny, rl, width)
    for cols in [hidden // halves] * halves:
        scratch += scatter_scratch(ny, rl, cols)
    return pl.pallas_call(
        partial(backward_kernel, (ny, heads, rows, size, pairs, rows // block, halves)),
        grid=(pairs, rows // block),
        out_shape=[shape((rows, 3 * width), LOW), shape((rl, width), F32), shape((rl, hidden), F32), shape((others, rows, d_model), LOW)],
        in_specs=[spec((2, 2 * rows, block), lambda p, i: (p, 0, i)), q_spec, k_spec, k_spec, q_spec, q_spec,
                  spec((1, 8, block), lambda p, i: (p, 0, i)), any_space, any_space, any_space],
        out_specs=[whole, whole, whole, any_space],
        scratch_shapes=scratch,
        compiler_params=pltpu.CompilerParams(collective_id=1, has_side_effects=True, vmem_limit_bytes=60 * 2**20),
        cost_estimate=pl.CostEstimate(flops=16 * rows * rows * width, bytes_accessed=50 * 2**20, transcendentals=0),
        name="backward_attention",
    )(probs, q, k, v, grad, context, inverse, parts_out.reshape(ZS, ny, 2, rl, width), parts_up, mlp_low)


def last_kernel(dims, grads, n1, tokens, resid, full_qkv, norm_two, parts_down, base, mlp_land, down_a,
                tokens_grad, output, mine_w, mine_norm, mine_down,
                g_v, n1_v, x_v, res_v, w_v, in_sem,
                part_one, part_low, arrived, parts_qkv, norm_land, norm_own, out_v, x_send, x_recv, n_send, n_recv, out_sem,
                base_v, land_v, mine_qkv, base_sem, land_sem, res_sem, *scratch):
    ny, heads, rows, d_model, width, tile, split, down_cols = dims
    z, y, core = place(ny)
    head = lax.axis_index("head")
    wide = full_qkv.shape[1]
    rl = mine_qkv.shape[0]
    plan = [(parts_down, pl.ds(*down_cols)), (parts_qkv, pl.ds(0, split)), (parts_qkv, pl.ds(split, wide - split))]
    down, qkv_a, qkv_b = make_scatters(ny, plan, scratch)
    chunks = rows // tile
    loads = [pltpu.make_async_copy(src, dst, in_sem.at[i]) for i, (src, dst) in enumerate((
        (grads, g_v), (full_qkv, w_v), (n1, n1_v), (tokens, x_v), (resid, res_v)))]
    for item in loads:
        item.start()
    base_load = pltpu.make_async_copy(base, base_v, base_sem.at[0])

    def land_load(i):
        return pltpu.make_async_copy(mlp_land.at[:, pl.ds(i * tile, tile)], land_v.at[i % 2], land_sem.at[i % 2])

    def result_copy(i):
        at = pl.ds(i * tile, tile)
        return pltpu.make_async_copy(base_v.at[at], output.at[at], res_sem.at[i])

    def finish_output(i):
        at = pl.ds(i * tile, tile)
        land_load(i).wait()
        total = base_v[at]
        for step in range(1, heads):
            total += land_v[i % 2, step - 1].astype(F32)
        base_v[at] = total
        result_copy(i).start()
        if i + 2 < chunks:
            land_load(i + 2).start()

    def x_copy(i, step):
        at = pl.ds(i * tile, tile)
        return remote(part_low.at[at], arrived.at[step - 1, at], x_send.at[i, step - 1], x_recv.at[i, step - 1],
                      {"head": (head + step) % heads})

    def n_copy(step):
        return remote(norm_own, norm_land.at[step - 1], n_send.at[step - 1], n_recv.at[step - 1], {"head": (head + step) % heads})

    def out_copy(i):
        at = pl.ds(i * tile, tile)
        return pltpu.make_async_copy(out_v.at[at], tokens_grad.at[at], out_sem.at[i])

    greet_all(ny, heads)
    down.begin()
    for item in loads[:2]:
        item.wait()
    for i in range(chunks):
        at = pl.ds(i * tile, tile)
        total = dot(g_v[at], w_v[:, 128:], 1, 1)
        part_one[at] = total
        part_low[at] = total.astype(LOW)
        for step in range(1, heads):
            x_copy(i, step).start()
        if i == 0:
            down.one()
    for item in loads[2:]:
        item.wait()
    per_z = d_model // ZS
    for zz in range(0, ZS, 2):
        cols = n1_v[:, zz * per_z:(zz + 2) * per_z]
        value = dot(cols, g_v[...], 0, 0).astype(LOW)
        parts_qkv[zz:zz + 2, :, :, :, 128:] = value.reshape(2, ny, 2, rl, 3 * width)
    qkv_b.begin()
    base_load.start()
    for i in range(min(2, chunks)):
        land_load(i).start()
    gain = w_v[:, :128].astype(F32).T[0:1]

    def hat_of(at):
        x = x_v[at].astype(F32)
        centre = x - jnp.mean(x, axis=1, keepdims=True)
        spread = lax.rsqrt(jnp.mean(centre * centre, axis=1, keepdims=True) + 1e-05)
        return centre * spread, spread

    gain_sum = jnp.zeros((1, d_model), F32)
    shift_sum = jnp.zeros((1, d_model), F32)
    for i in range(chunks):
        at = pl.ds(i * tile, tile)
        hat, _ = hat_of(at)
        gain_sum += jnp.sum(part_one[at] * hat, axis=0, keepdims=True)
        shift_sum += jnp.sum(part_one[at], axis=0, keepdims=True)
        if i == chunks // 2:
            qkv_b.one()
    sums = jnp.concatenate([gain_sum, shift_sum, norm_two[0:2], jnp.zeros((124, d_model), F32)], axis=0).T.astype(LOW)
    parts_qkv[:, :, :, :, :128] = sums.reshape(ZS, ny, 2, rl, 128)
    qkv_a.begin()

    def receive(i):
        at = pl.ds(i * tile, tile)
        total = part_one[at]
        for step in range(1, heads):
            x_copy(i, step).wait_recv()
            total += arrived[step - 1, at].astype(F32)
        hat, spread = hat_of(at)
        scaled = total * gain
        inner = scaled - jnp.mean(scaled, axis=1, keepdims=True) - hat * jnp.mean(scaled * hat, axis=1, keepdims=True)
        out_v[at] = res_v[at] + inner * spread
        out_copy(i).start()

    mine_down[:, :down_a.shape[1]] = down_a[...]
    base_load.wait()
    stages = [lambda: qkv_a.one(), lambda: down.two(), lambda: qkv_b.two(), lambda: down.three(mine_down.at[:, pl.ds(*down_cols)], True), lambda: qkv_a.two(),
              lambda: qkv_b.three(mine_qkv), lambda: qkv_a.three(mine_qkv)]
    when = [0, 1, 3, 4, 5, 6, 7]
    for i in range(chunks):
        for at, stage in zip(when, stages):
            if at * chunks // 8 == i:
                stage()
        if i == chunks - 1:
            norm_own[...] = mine_qkv[:, :128]
            for step in range(1, heads):
                n_copy(step).start()
        finish_output(i)
        receive(i)
    total = mine_qkv[:, :128]
    for step in range(1, heads):
        n_copy(step).wait()
        total += norm_land[step - 1]
    mine_norm[...] = total.T[:8]
    for p in range(width // 128):
        for c in range(3):
            mine_w[c, :, p * 128:(p + 1) * 128] = mine_qkv[:, 128 * (3 * p + c + 1):128 * (3 * p + c + 2)]
    for item in (down, qkv_a, qkv_b):
        item.finish()
    for i in range(chunks):
        out_copy(i).wait()
        result_copy(i).wait()
        for step in range(1, heads):
            x_copy(i, step).wait_send()


def last_stage(grads, n1, tokens, resid, full_qkv, norm_two, parts_down, base, mlp_land, down_a, scenes, heads):
    ny = scenes // ZS
    rows, d_model = tokens.shape
    width, hidden = grads.shape[1] // 3, parts_down.shape[-1]
    first, third = shares(hidden)
    rl = d_model // (2 * scenes)
    wide = full_qkv.shape[1]
    tile = min(128, rows)
    chunks = rows // tile
    split = (wide // 128 + 1) // 2 * 128
    others = max(heads - 1, 1)
    sem = pltpu.SemaphoreType.DMA
    shape, vmem = jax.ShapeDtypeStruct, pltpu.VMEM
    any_space, whole = pl.BlockSpec(memory_space=pl.ANY), pl.BlockSpec(memory_space=pltpu.VMEM)
    scratch = [vmem((rows, 3 * width), LOW), vmem((rows, d_model), LOW),
               vmem((rows, d_model), LOW), vmem((rows, d_model), F32), vmem((d_model, wide), LOW), sem((7,)),
               vmem((rows, d_model), F32), vmem((rows, d_model), LOW), vmem((others, rows, d_model), LOW),
               vmem((ZS, ny, 2, rl, wide), LOW), vmem((others, rl, 128), F32), vmem((rl, 128), F32),
               vmem((rows, d_model), F32), sem((chunks, others)), sem((chunks, others)), sem((others,)), sem((others,)),
               sem((chunks,)), vmem((rows, d_model), F32), vmem((2, others, tile, d_model), LOW), vmem((rl, wide), F32),
               sem((1,)), sem((2,)), sem((chunks,))]
    for cols in (third, split, wide - split):
        scratch += scatter_scratch(ny, rl, cols)
    return pl.pallas_call(
        partial(last_kernel, (ny, heads, rows, d_model, width, tile, split, (first, third))),
        out_shape=[shape((rows, d_model), F32), shape((rows, d_model), F32), shape((3, rl, width), F32), shape((8, rl), F32),
                   shape((rl, hidden), F32)],
        in_specs=[any_space] * 5 + [whole, any_space, any_space, any_space, whole],
        out_specs=[any_space, any_space, whole, whole, whole],
        scratch_shapes=scratch,
        compiler_params=pltpu.CompilerParams(collective_id=2, has_side_effects=True, vmem_limit_bytes=63 * 2**20),
        cost_estimate=pl.CostEstimate(flops=12 * rows * d_model * width, bytes_accessed=30 * 2**20, transcendentals=0),
        name="last_stage",
    )(grads, n1, tokens, resid, full_qkv, norm_two, parts_down, base, mlp_land, down_a)


def on_device(n_scene, n_head, tokens, counts, w_qkv, w_out, w_up, w_down, gain_one, shift_one, gain_two, shift_two, cotangent):
    rows, d_model = tokens.shape
    width, hidden = w_qkv.shape[2], w_up.shape[1]
    size = 64
    core = lax.axis_index("seq")
    limits = jnp.stack([counts[0] - core * rows, counts[0] - (1 - core) * rows]).astype(jnp.int32)
    columns = jnp.pad(jnp.stack([gain_one, shift_one, gain_two, shift_two], axis=1), ((0, 0), (0, 124)))
    by_pair = w_qkv.reshape(3, -1, width // (2 * size), 2 * size).transpose(1, 2, 0, 3).reshape(-1, 3 * width)
    shard_qkv = jnp.concatenate([columns, by_pair], axis=1)
    n1, q, k, v, full_qkv, full_out, full_up, full_down, probs, context, context_all, inverse = forward(
        limits, shard_qkv, w_out.T, w_up, w_down.T, tokens, n_scene, n_head, size)
    grad_resid, base, mlp_low, grad_context, norm_two, grad_outproj, grad_up, grad_down, down_a = middle(
        tokens, context_all, cotangent, full_qkv, full_out, full_up, full_down, n_scene, n_head)
    grads, mine_out, mine_up, mlp_land = backward(
        probs, q, k, v, grad_context, context, inverse, grad_outproj, grad_up, mlp_low, n_scene, n_head, size)
    tokens_grad, output, mine_qkv, norms, mine_down = last_stage(
        grads, n1, tokens, grad_resid, full_qkv, norm_two, grad_down, base, mlp_land, down_a, n_scene, n_head)
    return (output, tokens_grad, mine_qkv, mine_out.T, mine_up, mine_down.T, norms[0], norms[1], norms[2], norms[3])


def solution(mesh):
    rows, both = ("scene", "seq"), P(("scene", "seq"))
    weights = (P(None, rows, "head"), P("head", rows), P(rows, "head"), P("head", rows), both, both, both, both)
    return jax.shard_map(
        partial(on_device, mesh.shape["scene"], mesh.shape["head"]), mesh=mesh,
        in_specs=(P(rows, None), P("scene"), *weights, P(rows, None)),
        out_specs=(P(rows, None), P(rows, None), *weights),
        check_vma=False,
    )
```

```python
from functools import partial

import jax
import jax.numpy as jnp
from jax import lax
from jax.experimental import pallas as pl
from jax.experimental.pallas import tpu as pltpu
from jax.sharding import PartitionSpec as P

MESH = pl.DeviceIdType.MESH
ZS = 4


def place(ny):
    scene = lax.axis_index("scene")
    return scene // ny, scene % ny, lax.axis_index("seq")


def remote(src, dst, send_sem, recv_sem, device):
    return pltpu.make_async_remote_copy(
        src_ref=src, dst_ref=dst, send_sem=send_sem, recv_sem=recv_sem,
        device_id=device, device_id_type=MESH,
    )


F32 = jnp.float32
LOW = jnp.bfloat16


def dot(a, b, ca, cb):
    return lax.dot_general(a, b, (((ca,), (cb,)), ((), ())), preferred_element_type=F32)


def only_head(x, h, size):
    lane = lax.broadcasted_iota(jnp.int32, x.shape, 1)
    return jnp.where(lane // size == h, x, jnp.zeros_like(x))


class Gather:
    def __init__(self, ny, source, full, cols, sems):
        self.ny, self.source, self.full, self.cols = ny, source, full, cols
        self.rsend, self.rrecv, self.lsend, self.lrecv, self.ysend, self.yrecv, self.csend, self.crecv = sems
        self.z, self.y, self.core = place(ny)

    def at(self, zz, yy):
        return self.full.at[zz, yy, self.core, :, self.cols]

    def right(self, k):
        src = self.source() if k == 0 else self.at(self.z - k, self.y)
        dst = self.at(self.z - k, self.y)
        return remote(src, dst, self.rsend.at[k], self.rrecv.at[k], {"scene": (self.z + 1) * self.ny + self.y})

    def left(self, k):
        src = self.source() if k == 0 else self.at(self.z + k, self.y)
        dst = self.at(self.z + k, self.y)
        return remote(src, dst, self.lsend.at[k], self.lrecv.at[k], {"scene": (self.z - 1) * self.ny + self.y})

    def across(self, zz, step, own=False):
        src = self.source() if own else self.at(zz, self.y)
        peer = self.z * self.ny + (self.y + step) % self.ny
        return remote(src, self.at(zz, self.y), self.ysend.at[step - 1], self.yrecv.at[step - 1], {"scene": peer})

    def arrival(self, zz, step):
        yy = (self.y + self.ny - step) % self.ny
        return remote(self.at(zz, yy), self.at(zz, yy), self.ysend.at[step - 1], self.yrecv.at[step - 1],
                      {"scene": self.z * self.ny + yy})

    def twin(self, zz, step, own=False):
        src = self.source() if own else self.at(zz, (self.y + self.ny - step) % self.ny)
        dst = self.at(zz, (self.y + self.ny - step) % self.ny)
        return remote(src, dst, self.csend.at[0], self.crecv.at[0], {"seq": 1 - self.core})

    def column(self, step):
        yy = (self.y + self.ny - step) % self.ny
        all_z = self.full.at[:, yy, self.core, :, self.cols]
        return remote(all_z, all_z, self.ysend.at[step - 1], self.yrecv.at[step - 1], {"scene": self.z * self.ny + yy})

    def twins(self):
        mine, theirs = [self.full.at[:, :, c, :, self.cols] for c in (self.core, 1 - self.core)]
        return [remote(item, item, self.csend.at[0], self.crecv.at[0], {"seq": 1 - self.core}) for item in (mine, theirs)]

    def begin(self):
        @pl.when(self.z < ZS - 1)
        def _():
            self.right(0).start()

        @pl.when(self.z > 0)
        def _():
            self.left(0).start()

        for step in range(1, self.ny):
            self.across(self.z, step, True).start()
        self.twin(self.z, 0, True).start()

    def hop(self, k):
        @pl.when(self.z >= k)
        def _():
            self.right(k - 1).wait_recv()
            if k < ZS - 1:
                @pl.when(self.z < ZS - 1)
                def _():
                    self.right(k).start()
            for step in range(1, self.ny):
                self.across(self.z - k, step).start()
            self.twin(self.z - k, 0).start()

        @pl.when(self.z + k < ZS)
        def _():
            self.left(k - 1).wait_recv()
            if k < ZS - 1:
                @pl.when(self.z > 0)
                def _():
                    self.left(k).start()
            for step in range(1, self.ny):
                self.across(self.z + k, step).start()
            self.twin(self.z + k, 0).start()

    def spread(self):
        for step in range(1, self.ny):
            self.column(step).wait_recv()
            for zz in range(ZS):
                self.twin(zz, step).start()

    def finish(self):
        for k in range(ZS - 1):
            @pl.when((self.z < ZS - 1) & (self.z >= k))
            def _():
                self.right(k).wait_send()

            @pl.when((self.z > 0) & (self.z + k < ZS))
            def _():
                self.left(k).wait_send()
        for step in range(1, self.ny):
            self.column(step).wait_send()
        mine, theirs = self.twins()
        mine.wait_send()
        theirs.wait_recv()


class PairGather(Gather):
    def row(self, zz):
        return self.full.at[zz, :, self.core, :, self.cols]

    def right(self, k):
        return remote(self.row(self.z - k), self.row(self.z - k), self.rsend.at[k], self.rrecv.at[k],
                      {"scene": (self.z + 1) * self.ny + self.y})

    def left(self, k):
        return remote(self.row(self.z + k), self.row(self.z + k), self.lsend.at[k], self.lrecv.at[k],
                      {"scene": (self.z - 1) * self.ny + self.y})

    def twin(self, zz):
        return remote(self.row(zz), self.row(zz), self.csend.at[0], self.crecv.at[0], {"seq": 1 - self.core})

    def begin(self):
        for step in range(1, self.ny):
            self.across(self.z, step, True).start()

    def pair(self):
        for step in range(1, self.ny):
            self.arrival(self.z, step).wait_recv()

        @pl.when(self.z < ZS - 1)
        def _():
            self.right(0).start()

        @pl.when(self.z > 0)
        def _():
            self.left(0).start()

        self.twin(self.z).start()

    def hop(self, k):
        @pl.when(self.z >= k)
        def _():
            self.right(k - 1).wait_recv()
            if k < ZS - 1:
                @pl.when(self.z < ZS - 1)
                def _():
                    self.right(k).start()
            self.twin(self.z - k).start()

        @pl.when(self.z + k < ZS)
        def _():
            self.left(k - 1).wait_recv()
            if k < ZS - 1:
                @pl.when(self.z > 0)
                def _():
                    self.left(k).start()
            self.twin(self.z + k).start()

    def finish(self):
        for k in range(ZS - 1):
            @pl.when((self.z < ZS - 1) & (self.z >= k))
            def _():
                self.right(k).wait_send()

            @pl.when((self.z > 0) & (self.z + k < ZS))
            def _():
                self.left(k).wait_send()
        for step in range(1, self.ny):
            self.across(self.z, step).wait_send()
        mine, theirs = self.twins()
        mine.wait_send()
        theirs.wait_recv()


def gather_sems(ny):
    sem = pltpu.SemaphoreType.DMA
    return [sem((ZS - 1,)), sem((ZS - 1,)), sem((ZS - 1,)), sem((ZS - 1,)), sem((max(ny - 1, 1),)), sem((max(ny - 1, 1),)),
            sem((1,)), sem((1,))]


def greet_all(ny, heads):
    z, y, core = place(ny)
    head = lax.axis_index("head")
    barrier = pltpu.get_barrier_semaphore()

    def signal(device):
        pl.semaphore_signal(barrier, 1, device_id=device, device_id_type=MESH)

    for step in range(1, ZS):
        signal({"scene": (z + step) % ZS * ny + y})
    for step in range(1, ny):
        signal({"scene": z * ny + (y + step) % ny})
    for step in range(1, heads):
        signal({"head": (head + step) % heads})
    signal({"seq": 1 - core})
    pl.semaphore_wait(barrier, ZS + ny - 1 + heads - 1)


def split_cols(total, parts):
    size = total // parts
    return [pl.ds(i * size, size) for i in range(parts)]


def forward_kernel(dims, limits, shard_qkv, shard_out, shard_up, shard_down, tokens,
                   n1_out, q_out, k_out, v_out, full_qkv, full_out, full_up, full_down, probs, context, context_all, inverse,
                   w0, hat, n1, q_s, k_s, v_s, bias, ctx_s, scores, tops, local_sem, kv_send, kv_recv, xw_send, xw_recv, xt_send, xt_recv, xc_send, xc_recv, *sems):
    ny, heads, rows, width, size, block, pairs, steps_q, halves = dims
    pair, part = pl.program_id(0), pl.program_id(1)
    step = pair * steps_q + part
    z, y, core = place(ny)
    head = lax.axis_index("head")
    d_model = tokens.shape[1]
    per = 8
    own_cols = pl.ds(pl.multiple_of(head * width, width), width)

    def of(i):
        return sems[i * per:(i + 1) * per]

    group = 6 * size
    edges = [0] + [128 + (p + 1) * group for p in range(pairs)]
    firsts = []
    for p in range(pairs):
        cols = pl.ds(edges[p], edges[p + 1] - edges[p])
        firsts.append(Gather(ny, partial(lambda c: shard_qkv.at[:, c], cols), w0, cols, of(2 + 2 * halves + p)))
    outer = Gather(ny, lambda: shard_out, full_out, own_cols, of(1))
    thick = []
    for n, (shard, full) in enumerate(((shard_up, full_up), (shard_down, full_down))):
        for i, cols in enumerate(split_cols(full_up.shape[-1], halves)):
            kind = PairGather if n == 1 and i == halves - 1 else Gather
            thick.append(kind(ny, partial(lambda s, c: s.at[:, c], shard, cols), full, cols, of(2 + n * halves + i)))
    up_a, up_b, down_a, down_b = thick

    def local(src, dst, i):
        return pltpu.make_async_copy(src, dst, local_sem.at[i])

    def cols_of(step):
        return pl.ds(pl.multiple_of((head + heads - step) % heads * width, width), width)

    def out_copy(step):
        mine = full_out.at[:, :, core, :, own_cols]
        return remote(mine, mine, xw_send.at[step - 1], xw_recv.at[step - 1], {"head": (head + step) % heads})

    def out_twin(step):
        other = full_out.at[:, :, core, :, cols_of(step)]
        return remote(other, other, xt_send.at[step - 1], xt_recv.at[step - 1], {"seq": 1 - core})

    def kv_copy(p, i):
        src = (k_s, v_s)[i]
        cols = pl.ds(p * 2 * size, 2 * size)
        return remote(src.at[pl.ds(0, rows), cols], src.at[pl.ds(rows, rows), cols], kv_send.at[p, i], kv_recv.at[p, i],
                      {"seq": 1 - core})

    def project(p):
        tile = min(256, rows)

        @pl.loop(0, rows // tile)
        def _(i):
            at = pl.ds(pl.multiple_of(i * tile, tile), tile)
            w = w0[:, :, :, :, 128 + p * group:128 + (p + 1) * group].reshape(d_model, group)
            value = dot(n1[at], w, 1, 0).astype(LOW)
            cols = pl.ds(p * 2 * size, 2 * size)
            q_s[at, cols] = value[:, :2 * size] * LOW(size ** -0.5)
            k_s[at, cols] = value[:, 2 * size:4 * size]
            v_s[at, cols] = value[:, 4 * size:]

        for i in range(2):
            kv_copy(p, i).start()

    def ctx_copy(p, step):
        cols = pl.ds(pl.multiple_of(p * 2 * size, 2 * size), 2 * size)
        wide = pl.ds(pl.multiple_of(head * width + p * 2 * size, 2 * size), 2 * size)
        return remote(ctx_s.at[:, cols], context_all.at[:, wide], xc_send.at[p, step - 1], xc_recv.at[p, step - 1],
                      {"head": (head + step) % heads})

    own_blocks = [(shard_qkv, w0.at[z, y, core], 0), (shard_out, full_out.at[z, y, core, :, own_cols], 1),
                  (shard_up, full_up.at[z, y, core], 2), (shard_down, full_down.at[z, y, core], 3)]
    results = [(w0, full_qkv, 4), (n1, n1_out, 5), (q_s, q_out, 6), (k_s, k_out, 7), (v_s, v_out, 8)]
    ctx_local = (ctx_s, context_all.at[:, own_cols], 9)

    @pl.when(step == 0)
    def _():
        for item in own_blocks:
            local(*item).start()
        greet_all(ny, heads)
        for gather in firsts[:2]:
            gather.begin()
        tile = min(128, rows)

        @pl.loop(0, rows // tile)
        def _(i):
            at = pl.ds(pl.multiple_of(i * tile, tile), tile)
            x = tokens[at].astype(F32)
            centre = x - jnp.mean(x, axis=1, keepdims=True)
            spread = jnp.mean(centre * centre, axis=1, keepdims=True)
            hat[at] = centre * lax.rsqrt(spread + 1e-05)

        low_rows = lax.broadcasted_iota(jnp.int32, bias.shape, 0)
        lane = lax.broadcasted_iota(jnp.int32, bias.shape, 1)
        limit = jnp.where(low_rows < rows, limits[0], limits[1] + rows)
        bias[...] = jnp.where((low_rows >= limit) & (lane == 0), -1e30, 0.0).astype(LOW)
        after = [
            (0, lambda g: g.hop(1)), (2, lambda g: g.begin()), (0, lambda g: g.hop(2)), (1, lambda g: g.hop(1)), (0, lambda g: g.hop(3)),
            (3, lambda g: g.begin()), (1, lambda g: g.hop(2)), (0, lambda g: g.spread()), (1, lambda g: g.hop(3)),
            (2, lambda g: g.hop(1)), (1, lambda g: g.spread()), (2, lambda g: g.hop(2))]
        for p, act in after[:9]:
            if p < pairs:
                act(firsts[p])
        firsts[0].finish()
        for item in own_blocks:
            local(*item).wait()
        norms = w0[:, :, :, :, :128].reshape(d_model, 128).astype(F32).T
        gain, shift = norms[0:1], norms[1:2]
        tile = min(256, rows)

        @pl.loop(0, rows // tile)
        def _(i):
            at = pl.ds(pl.multiple_of(i * tile, tile), tile)
            n1[at] = (hat[at] * gain + shift).astype(LOW)

        local(*results[1]).start()
        project(0)
        for p, act in after[9:]:
            if p < pairs:
                act(firsts[p])

    total = pairs * steps_q
    per_slot = 2
    in_step = 4 * rows // min(256, rows) // per_slot
    slots = in_step * total

    def send_out():
        for i in range(1, heads):
            out_copy(i).start()

    def pass_out():
        for i in range(1, heads):
            out_copy(i).wait_recv()
            out_twin(i).start()

    def on_pair(p, what, *given):
        if p < pairs:
            getattr(firsts[p], what)(*given)

    events = [
        (0.1, lambda: on_pair(2, "hop", 3)), (0.3, lambda: on_pair(3, "hop", 1)), (0.4, outer.begin),
        (1, lambda: on_pair(3, "hop", 2)), (1.2, lambda: on_pair(2, "spread")), (1.4, up_a.begin),
        (2, lambda: on_pair(3, "hop", 3)), (2.6, lambda: outer.hop(1)), (3.2, lambda: outer.hop(2)), (3.2, up_b.begin),
        (3.8, lambda: on_pair(3, "spread")), (3.9, lambda: outer.hop(3)), (5.2, lambda: up_a.hop(1)), (6, outer.spread), (6.1, send_out),
        (6.5, lambda: up_a.hop(2)), (7, down_a.begin), (7.2, down_b.begin),
        (7.8, lambda: up_a.hop(3)), (9.2, lambda: up_b.hop(1)), (10.5, lambda: up_b.hop(2)), (10.6, pass_out), (10.8, down_b.pair),
        (11.8, lambda: up_b.hop(3)), (12, up_a.spread), (13.2, lambda: down_a.hop(1)), (14.5, lambda: down_a.hop(2)),
        (15.8, lambda: down_a.hop(3)), (16, up_b.spread), (16, lambda: down_b.hop(1)),
        (16, lambda: down_b.hop(2)), (16, down_a.spread), (16, lambda: down_b.hop(3))]

    def run(slot_in_step):
        for when, act in events:
            slot = min(int(when * slots / 16), slots - 1)
            if when < 16 and slot % in_step == slot_in_step:
                pl.when(step == slot // in_step)(act)

    for p in range(pairs):
        @pl.when(step == p * steps_q)
        def _():
            if p == 0:
                for i in range(2):
                    kv_copy(0, i).wait()
            if p + 1 < pairs:
                firsts[p + 1].finish()
                project(p + 1)
            else:
                for item in (results[0], *results[2:]):
                    local(*item).start()

        if p + 1 < pairs:
            @pl.when(step == (p + 1) * steps_q - 1)
            def _():
                for i in range(2):
                    kv_copy(p + 1, i).wait()

    width2, chunk = 2 * size, min(256, rows)
    n_chunks = 2 * rows // chunk
    ones = (lax.broadcasted_iota(jnp.int32, (block, bias.shape[1]), 1) == 0).astype(LOW)

    def asked(at, h):
        rows_at = pl.ds(pl.multiple_of(at % steps_q * block, block), block)
        cols_at = pl.ds(pl.multiple_of(at // steps_q * width2, width2), width2)
        return jnp.concatenate([only_head(q_s[rows_at, cols_at], h, size), ones], axis=1)

    def score(at, query, slot, c, top):
        cols_at = pl.ds(pl.multiple_of(at // steps_q * width2, width2), width2)
        keys_at = pl.ds(c * chunk, chunk)
        value = dot(jnp.concatenate([k_s[keys_at, cols_at], bias[keys_at]], axis=1), query, 1, 1)
        scores[slot, keys_at] = value
        return jnp.maximum(top, jnp.max(value.reshape(chunk // 8, 8, block), axis=0))

    def weigh(h, c, top, total_e):
        keys_at = pl.ds(c * chunk, chunk)
        expo = jnp.exp(scores[h, keys_at] - top)
        probs[h, keys_at] = expo.astype(LOW)
        return total_e + jnp.sum(expo.reshape(chunk // 8, 8, block), axis=0)

    lowest = jnp.full((8, block), -3e38, F32)

    @pl.when(step == 0)
    def _():
        top, query = lowest, asked(0, 0)
        for c in range(n_chunks):
            top = score(0, query, 0, c, top)
        tops[...] = top

    cols = pl.ds(pl.multiple_of(pair * width2, width2), width2)
    following = jnp.minimum(step + 1, total - 1)
    values_t = v_s[:, cols].T
    pieces = []
    for h in range(2):
        top = jnp.max(tops[...], axis=0, keepdims=True)
        total_e, next_top = jnp.zeros((8, block), F32), lowest
        ahead = (step, 1) if h == 0 else (following, 0)
        query = asked(*ahead)
        for c in range(n_chunks):
            if c % per_slot == 0:
                run(h * (n_chunks // per_slot) + c // per_slot)
            next_top = score(ahead[0], query, 1 - h, c, next_top)
            total_e = weigh(h, c, top, total_e)
        tops[...] = next_top
        over = 1.0 / jnp.sum(total_e, axis=0, keepdims=True)
        pieces.append(dot(values_t, probs[h], 1, 0)[h * size:(h + 1) * size] * over)
        inverse[0, h:h + 1] = over
    here = jnp.concatenate(pieces, axis=0).T.astype(LOW)
    context[...] = here
    ctx_s[pl.ds(pl.multiple_of(part * block, block), block), cols] = here

    @pl.when(part == steps_q - 1)
    def _():
        for i in range(1, heads):
            ctx_copy(pair, i).start()

    @pl.when(step == total - 1)
    def _():
        local(*ctx_local).start()
        for when, act in events:
            if when >= 16:
                act()
        for gather in (outer, *thick):
            gather.finish()
        for item in results:
            local(*item).wait()
        local(*ctx_local).wait()
        for i in range(1, heads):
            out_copy(i).wait_send()
            out_twin(i).wait()
            for p in range(pairs):
                ctx_copy(p, i).wait()


def forward(limits, shard_qkv, shard_out, shard_up, shard_down, tokens, scenes, heads, size):
    ny = scenes // ZS
    rows, d_model = tokens.shape
    rl, width = shard_out.shape
    hidden = shard_up.shape[1]
    pairs = width // (2 * size)
    block = min(512, rows)
    steps_q = rows // block
    halves = 2
    sem = pltpu.SemaphoreType.DMA
    any_space = pl.BlockSpec(memory_space=pl.ANY)
    shape = jax.ShapeDtypeStruct
    wide = shard_qkv.shape[1]
    outs = [shape((rows, d_model), LOW), shape((rows, width), LOW), shape((2 * rows, width), LOW), shape((2 * rows, width), LOW),
            shape((ZS, ny, 2, rl, wide), LOW), shape((ZS, ny, 2, rl, d_model), LOW), shape((ZS, ny, 2, rl, hidden), LOW),
            shape((ZS, ny, 2, rl, hidden), LOW), shape((2 * pairs, 2 * rows, rows), LOW), shape((rows, width), LOW),
            shape((rows, d_model), LOW), shape((pairs, 8, rows), F32)]
    out_specs = [any_space] * 8 + [
        pl.BlockSpec((2, 2 * rows, block), lambda p, i: (p, 0, i)), pl.BlockSpec((block, 2 * size), lambda p, i: (i, p)),
        any_space, pl.BlockSpec((1, 8, block), lambda p, i: (p, 0, i))]
    scratch = [pltpu.VMEM((ZS, ny, 2, rl, wide), LOW), pltpu.VMEM((rows, d_model), F32), pltpu.VMEM((rows, d_model), LOW),
               pltpu.VMEM((rows, width), LOW), pltpu.VMEM((2 * rows, width), LOW), pltpu.VMEM((2 * rows, width), LOW),
               pltpu.VMEM((2 * rows, 128), LOW), pltpu.VMEM((rows, width), LOW),
               pltpu.VMEM((2, 2 * rows, block), F32), pltpu.VMEM((8, block), F32), sem((10,)), sem((pairs, 2)), sem((pairs, 2)),
               sem((max(heads - 1, 1),)), sem((max(heads - 1, 1),)), sem((max(heads - 1, 1),)), sem((max(heads - 1, 1),)), sem((pairs, max(heads - 1, 1))), sem((pairs, max(heads - 1, 1)))]
    for _ in range(2 + 2 * halves + pairs):
        scratch += gather_sems(ny)
    dims = (ny, heads, rows, width, size, block, pairs, steps_q, halves)
    flops = 2 * rows * d_model * 3 * width + 8 * rows * rows * width
    results = pl.pallas_call(
        partial(forward_kernel, dims),
        grid=(pairs, steps_q),
        out_shape=outs,
        in_specs=[pl.BlockSpec(memory_space=pltpu.SMEM)] + [pl.BlockSpec(memory_space=pltpu.VMEM)] * 4 + [pl.BlockSpec(memory_space=pltpu.VMEM)],
        out_specs=out_specs,
        scratch_shapes=scratch,
        compiler_params=pltpu.CompilerParams(collective_id=0, has_side_effects=True, vmem_limit_bytes=60 * 2**20),
        cost_estimate=pl.CostEstimate(flops=flops, bytes_accessed=60 * 2**20, transcendentals=0),
        name="forward_attention",
    )(limits, shard_qkv, shard_out, shard_up, shard_down, tokens)
    n1, q, k, v, full_qkv, full_out, full_up, full_down, probs, context, context_all, inverse = results
    flat = lambda a: a.reshape(d_model, a.shape[-1])
    return n1, q, k, v, flat(full_qkv), flat(full_out), flat(full_up), flat(full_down), probs, context, context_all, inverse


class Scatter:
    def __init__(self, ny, parts, cols, bufs, sems):
        self.ny, self.parts, self.cols = ny, parts, cols
        self.own, self.from_core, self.from_y, self.sum_two, self.from_z = bufs
        self.load_sem, self.csend, self.crecv, self.ysend, self.yrecv, self.zsend, self.zrecv = sems
        self.z, self.y, self.core = place(ny)

    def load(self):
        return pltpu.make_async_copy(self.parts.at[:, :, self.core, :, self.cols], self.own, self.load_sem.at[0])

    def to_core(self):
        return remote(self.parts.at[:, :, 1 - self.core, :, self.cols], self.from_core, self.csend.at[0], self.crecv.at[0],
                      {"seq": 1 - self.core})

    def to_y(self, step):
        yy = (self.y + step) % self.ny
        return remote(self.own.at[:, yy], self.from_y.at[step - 1], self.ysend.at[step - 1], self.yrecv.at[step - 1],
                      {"scene": self.z * self.ny + yy})

    def to_z(self, step):
        zz = (self.z + step) % ZS
        return remote(self.sum_two.at[zz], self.from_z.at[step - 1], self.zsend.at[step - 1], self.zrecv.at[step - 1],
                      {"scene": zz * self.ny + self.y})

    def begin(self):
        self.load().start()
        self.to_core().start()

    def one(self):
        self.load().wait()
        self.to_core().wait_recv()
        for zz in range(ZS):
            for yy in range(self.ny):
                self.own[zz, yy] = (self.own[zz, yy].astype(F32) + self.from_core[zz, yy].astype(F32)).astype(LOW)
        for step in range(1, self.ny):
            self.to_y(step).start()

    def two(self):
        for step in range(1, self.ny):
            self.to_y(step).wait_recv()
        for zz in range(ZS):
            total = self.own[zz, self.y].astype(F32)
            for step in range(1, self.ny):
                total += self.from_y[step - 1, zz].astype(F32)
            self.sum_two[zz] = total.astype(LOW)
        for step in range(1, ZS):
            self.to_z(step).start()

    def three(self, out, alone=False):
        for step in range(1, ZS):
            self.to_z(step).wait_recv()
        total = self.sum_two[self.z].astype(F32)
        for step in range(1, ZS):
            total += self.from_z[step - 1].astype(F32)
        if alone:
            out[...] = total
        else:
            out[:, self.cols] = total

    def finish(self):
        self.to_core().wait_send()
        for step in range(1, self.ny):
            self.to_y(step).wait_send()
        for step in range(1, ZS):
            self.to_z(step).wait_send()


SCATTER_BUFS, SCATTER_SEMS = 5, 7


def scatter_scratch(ny, rl, cols):
    sem = pltpu.SemaphoreType.DMA
    other = max(ny - 1, 1)
    return [pltpu.VMEM((ZS, ny, rl, cols), LOW), pltpu.VMEM((ZS, ny, rl, cols), LOW), pltpu.VMEM((other, ZS, rl, cols), LOW),
            pltpu.VMEM((ZS, rl, cols), LOW), pltpu.VMEM((ZS - 1, rl, cols), LOW),
            sem((1,)), sem((1,)), sem((1,)), sem((other,)), sem((other,)), sem((ZS - 1,)), sem((ZS - 1,))]


def make_scatters(ny, plan, scratch):
    n = SCATTER_BUFS + SCATTER_SEMS
    result = []
    for i, (parts, cols) in enumerate(plan):
        mine = scratch[i * n:(i + 1) * n]
        result.append(Scatter(ny, parts, cols, mine[:SCATTER_BUFS], mine[SCATTER_BUFS:]))
    return result

def middle_kernel(dims, tokens, context_all, cotangent, full_qkv, full_out, full_up, full_down,
                  resid_grad, base, mlp_low, grad_context, norm_two, parts_out, parts_up, parts_down, mine_down,
                  x_v, ctx_v, cot_v, norm_v, wo, wu, wd, n2, act, gu, resid, part, low, arrived, up_v, down_v, out_v, gctx_v,
                  base_v, mlp_v, in_sem, out_sem, slot_sem, x_send, x_recv, g_send, g_recv, *scratch):
    ny, heads, rows, d_model, width, hidden, tile, size_f, first_cols = dims
    head = lax.axis_index("head")
    chunks = rows // tile
    part_rows = rows // heads
    per_part = part_rows // tile
    (down,) = make_scatters(ny, [(down_v, pl.ds(0, first_cols))], scratch)
    own_rows = pl.ds(pl.multiple_of(head * part_rows, part_rows), part_rows)

    def load(src, dst, i):
        return pltpu.make_async_copy(src, dst, in_sem.at[i])

    loads = [load(context_all, ctx_v, 0), load(full_out, wo, 1), load(tokens, x_v, 2), load(full_qkv.at[:, pl.ds(0, 128)], norm_v, 3),
             load(full_up, wu, 4), load(cotangent, cot_v, 5), load(full_down, wd, 6)]
    for item in loads:
        item.start()
    half = tile // 2

    def place_of(i):
        whole_tile = not isinstance(i, int)
        number = 0 if not whole_tile and i == chunks else i
        step = number // per_part + 1
        within = number % per_part * tile
        size = tile if whole_tile or 0 < i < chunks else half
        within = within + (half if not whole_tile and i == 0 else 0)
        return step, within, size

    def rows_of(i):
        step, within, size = place_of(i)
        return pl.ds(pl.multiple_of((head + step) % heads * part_rows + within, half), size)

    def x_copy(i, step):
        _, within, size = place_of(i)
        return remote(low.at[rows_of(i)], arrived.at[step - 1, pl.ds(within, size)], x_send.at[i], x_recv.at[i],
                      {"head": (head + step) % heads})

    def g_copy(j, step):
        to = (head + step) % heads
        at = pl.ds(j * tile, tile)
        there = pl.ds(pl.multiple_of(head * part_rows + j * tile, tile), tile)
        return remote(gctx_v.at[at, pl.ds(pl.multiple_of(to * width, width), width)], grad_context.at[there],
                      g_send.at[j, step - 1], g_recv.at[j, step - 1], {"head": to})

    greet_all(ny, heads)
    for item in loads:
        item.wait()
    norms = norm_v[...].astype(F32).T
    gain, shift = norms[2:3], norms[3:4]

    def hat_of(value):
        centre = value - jnp.mean(value, axis=1, keepdims=True)
        spread = lax.rsqrt(jnp.mean(centre * centre, axis=1, keepdims=True) + 1e-05)
        return centre * spread, spread

    norm_two[...] = jnp.zeros_like(norm_two)

    def forward_and_back(i):
        at = rows_of(i)
        value = x_v[at].astype(F32) + dot(ctx_v[at], wo[...], 1, 1)
        resid[at] = value
        n2[at] = (hat_of(value)[0] * gain + shift).astype(LOW)
        for f in range(hidden // size_f):
            cols = slice(f * size_f, (f + 1) * size_f)
            u = dot(n2[at], wu[:, cols], 1, 0)
            ga = dot(cot_v[at], wd[:, cols], 1, 0)
            phi = 0.5 + 0.5 * lax.erf(u * (0.5 ** 0.5))
            act[at, cols] = (u * phi).astype(LOW)
            gu[at, cols] = (ga * (phi + u * (jnp.exp(u * u * -0.5) * 0.3989422804014327))).astype(LOW)
        total = dot(gu[at], wu[...], 1, 1)
        part[at] = total
        low[at] = total.astype(LOW)

    def sums(i):
        at = rows_of(i)
        total = part[at]
        hat, _ = hat_of(resid[at])
        norm_two[0:1] += jnp.sum(total * hat, axis=0, keepdims=True)
        norm_two[1:2] += jnp.sum(total, axis=0, keepdims=True)

    if heads > 1:
        forward_and_back(chunks)
        x_copy(chunks, 1).start()
        forward_and_back(0)
        x_copy(0, 1).start()
        for step in range(1, heads):
            first = (step - 1) * per_part

            @pl.loop(max(first, 1), first + per_part)
            def _(i):
                forward_and_back(i)
                x_copy(i, step).start()

    else:
        forward_and_back(chunks)
        forward_and_back(0)

    @pl.loop(max(chunks - per_part, 1), chunks)
    def _(i):
        forward_and_back(i)

    def weight_grad(src, other, dst, count):
        per_z = d_model // ZS
        for f in range(count // size_f):
            cols = slice(f * size_f, (f + 1) * size_f)

            @pl.loop(0, ZS // 2)
            def _(j):
                at = pl.ds(pl.multiple_of(j * 2 * per_z, 2 * per_z), 2 * per_z)
                value = dot(src[:, at], other[:, cols], 0, 0).astype(LOW)
                dst[pl.ds(2 * j, 2), :, :, :, cols] = value.reshape(2, *dst.shape[1:4], size_f)

    weight_grad(cot_v, act, down_v, hidden)
    down.begin()

    def own_store(j):
        at = pl.ds(j * tile, tile)
        there = pl.ds(pl.multiple_of(head * part_rows + j * tile, tile), tile)
        return (pltpu.make_async_copy(part.at[there], resid_grad.at[at], out_sem.at[3 + 2 * j]),
                pltpu.make_async_copy(gctx_v.at[at, pl.ds(pl.multiple_of(head * width, width), width)], grad_context.at[there],
                                      out_sem.at[4 + 2 * j]))

    for j in range(per_part):
        at = pl.ds(pl.multiple_of(head * part_rows + j * tile, tile), tile)
        total = part[at]
        for step in range(1, heads):
            i = (step - 1) * per_part + j
            x_copy(i, step).wait_recv()
            if i == 0:
                x_copy(chunks, step).wait_recv()
            total += arrived[step - 1, j * tile:(j + 1) * tile].astype(F32)
        hat, spread = hat_of(resid[at])
        own_part = part[at]
        norm_two[0:1] += jnp.sum(own_part * hat, axis=0, keepdims=True)
        norm_two[1:2] += jnp.sum(own_part, axis=0, keepdims=True)
        scaled = total * gain
        inner = scaled - jnp.mean(scaled, axis=1, keepdims=True) - hat * jnp.mean(scaled * hat, axis=1, keepdims=True)
        total = cot_v[at].astype(F32) + inner * spread
        part[at] = total
        rounded = total.astype(LOW)
        low[at] = rounded
        gctx_v[j * tile:(j + 1) * tile] = dot(rounded, wo[...], 1, 0).astype(LOW)
        for step in range(1, heads):
            g_copy(j, step).start()
        for item in own_store(j):
            item.start()
    down.one()
    weight_grad(n2, gu, up_v, hidden)
    stores = [pltpu.make_async_copy(up_v, parts_up, out_sem.at[0]), pltpu.make_async_copy(down_v, parts_down, out_sem.at[1]),
              pltpu.make_async_copy(out_v, parts_out, out_sem.at[2])]
    for item in stores[:2]:
        item.start()
    down.two()
    weight_grad(low.at[own_rows], ctx_v.at[own_rows], out_v, d_model)
    stores[2].start()

    def slot_copies(i):
        at = pl.ds(pl.multiple_of(i * tile, tile), tile)
        slot = i % 2
        return (pltpu.make_async_copy(base_v.at[slot], base.at[at], slot_sem.at[0, slot]),
                pltpu.make_async_copy(mlp_v.at[slot], mlp_low.at[at], slot_sem.at[1, slot]))

    def slot_loop(i):
        at = pl.ds(pl.multiple_of(i * tile, tile), tile)
        value = dot(act[at], wd[...], 1, 1)

        @pl.when(i >= 2)
        def _():
            for item in slot_copies(i - 2):
                item.wait()

        base_v[i % 2] = resid[at] + value
        mlp_v[i % 2] = value.astype(LOW)
        for item in slot_copies(i):
            item.start()

    pl.loop(0, chunks)(slot_loop)
    if heads > 1:
        sums(chunks)
        sums(0)
        pl.loop(1, chunks - per_part)(sums)
    for i in range(max(0, chunks - 2), chunks):
        for item in slot_copies(i):
            item.wait()
    down.three(mine_down)
    down.finish()
    for item in stores:
        item.wait()
    for j in range(per_part):
        for item in own_store(j):
            item.wait()
        for step in range(1, heads):
            g_copy(j, step).wait()
    for step in range(1, heads):
        for j in range(per_part):
            x_copy((step - 1) * per_part + j, step).wait_send()
    if heads > 1:
        x_copy(chunks, 1).wait_send()


def shares(hidden):
    n = hidden // 128
    first = max(n // 8, 1)
    return first * 128, (n - first) * 128


def middle(tokens, context_all, cotangent, full_qkv, full_out, full_up, full_down, scenes, heads):
    ny = scenes // ZS
    rows, d_model = tokens.shape
    rl = d_model // (2 * scenes)
    hidden, width = full_up.shape[1], d_model // heads
    tile, size_f = min(256, rows // heads), min(1024, hidden)
    part_rows = rows // heads
    per_part = part_rows // tile
    chunks = rows // tile
    first_cols = shares(hidden)[0]
    others = max(heads - 1, 1)
    sem = pltpu.SemaphoreType.DMA
    shape, vmem = jax.ShapeDtypeStruct, pltpu.VMEM
    any_space, whole = pl.BlockSpec(memory_space=pl.ANY), pl.BlockSpec(memory_space=pltpu.VMEM)
    big, wide, blocks = (rows, d_model), (rows, hidden), (ZS, ny, 2, rl, hidden)
    scratch = [vmem(big, LOW), vmem(big, LOW), vmem(big, LOW), vmem((d_model, 128), LOW), vmem((d_model, d_model), LOW),
               vmem((d_model, hidden), LOW), vmem((d_model, hidden), LOW), vmem(big, LOW), vmem(wide, LOW), vmem(wide, LOW),
               vmem(big, F32), vmem(big, F32), vmem(big, LOW), vmem((others, part_rows, d_model), LOW), vmem(blocks, LOW),
               vmem(blocks, LOW), vmem((ZS, ny, 2, rl, d_model), LOW), vmem((part_rows, d_model), LOW), vmem((2, tile, d_model), F32),
               vmem((2, tile, d_model), LOW), sem((7,)), sem((3 + 2 * per_part,)), sem((2, 2)), sem((chunks + 1,)),
               sem((chunks + 1,)), sem((per_part, others)), sem((per_part, others))]
    scratch += scatter_scratch(ny, rl, first_cols)
    return pl.pallas_call(
        partial(middle_kernel, (ny, heads, rows, d_model, width, hidden, tile, size_f, first_cols)),
        out_shape=[shape((part_rows, d_model), F32), shape(big, F32), shape(big, LOW), shape((rows, width), LOW), shape((8, d_model), F32),
                   shape((ZS, ny, 2, rl, d_model), LOW), shape(blocks, LOW), shape(blocks, LOW), shape((rl, first_cols), F32)],
        in_specs=[any_space] * 7,
        out_specs=[any_space] * 4 + [whole] + [any_space] * 3 + [whole],
        scratch_shapes=scratch,
        compiler_params=pltpu.CompilerParams(collective_id=3, has_side_effects=True, vmem_limit_bytes=63 * 2**20),
        cost_estimate=pl.CostEstimate(flops=14 * rows * d_model * hidden, bytes_accessed=50 * 2**20, transcendentals=0),
        name="middle_stage",
    )(tokens, context_all, cotangent, full_qkv, full_out, full_up, full_down)


def backward_kernel(dims, probs, queries, keys, values, grad, context, inverse, parts_out, parts_up, mlp_low,
                    grads, mine_out, mine_up, mlp_land,
                    dk_acc, dv_acc, kept, stage, landed, kv_send, kv_recv, m_send, m_recv, *scratch):
    ny, heads, rows, size, pairs, steps_q, halves = dims
    pair, part = pl.program_id(0), pl.program_id(1)
    step = pair * steps_q + part
    total = pairs * steps_q
    block = grad.shape[0]
    z, y, core = place(ny)
    width = parts_out.shape[-1]
    cols_of = split_cols(parts_up.shape[-1], halves)
    plan = [(parts_out, pl.ds(0, width))] + [(parts_up, cols) for cols in cols_of]
    scatters = make_scatters(ny, plan, scratch)
    targets = [mine_out] + [mine_up] * halves

    def kv_copy(p, i):
        return remote(stage.at[p, i], landed.at[p, i], kv_send.at[p, i], kv_recv.at[p, i], {"seq": 1 - core})

    head = lax.axis_index("head")

    def mlp_copy(i, step):
        return remote(mlp_low.at[pl.ds(i * (rows // 4), rows // 4)], mlp_land.at[step - 1, pl.ds(i * (rows // 4), rows // 4)],
                      m_send.at[i, step - 1], m_recv.at[i, step - 1], {"head": (head + step) % heads})

    @pl.when(step == 0)
    def _():
        greet_all(ny, heads)
        for i in range(4):
            for j in range(1, heads):
                mlp_copy(i, j).start()
        for item in scatters:
            item.begin()

    slots = 2 * total
    plan_at = ((0.6, 5.6, 10.4), (1.4, 10.2, 15.2), (2.4, 15.2, 17))
    events = sorted((plan_at[i][j], i, j + 1) for i in range(3) for j in range(3))

    def run(slot_in_step):
        for when, i, what in events:
            slot = min(int(when * min(1.0, slots / 16)), slots)
            if slot == slots or slot % 2 != slot_in_step:
                continue

            @pl.when(step == slot // 2)
            def _():
                if what == 1:
                    scatters[i].one()
                elif what == 2:
                    scatters[i].two()
                else:
                    scatters[i].three(targets[i])

    @pl.when(part == 0)
    def _():
        dk_acc[...] = jnp.zeros_like(dk_acc)
        dv_acc[...] = jnp.zeros_like(dv_acc)

    upper = grad[...].astype(F32)
    inner = (upper * context[...].astype(F32)).T
    upper_t = upper.T
    row = lax.broadcasted_iota(jnp.int32, upper_t.shape, 0)
    keys_t = keys[...].T
    pieces = []
    for h in range(2):
        run(h)
        over = inverse[0, h:h + 1]
        shift = jnp.sum(inner[h * size:(h + 1) * size], axis=0, keepdims=True) * over
        scaled = jnp.where(row // size == h, upper_t * over, 0.0)
        dp = dot(values[...], scaled.astype(LOW), 1, 0) - shift
        low = probs[h]
        ds = (low.astype(F32) * dp).astype(LOW)
        dv_acc[...] += dot(low, scaled.T.astype(LOW), 1, 0)
        dk_acc[...] += dot(ds, only_head(queries[...], h, size), 1, 0)
        pieces.append(dot(keys_t, ds, 1, 0)[h * size:(h + 1) * size])
    grads[pl.ds(pl.multiple_of(part * block, block), block), pl.ds(pl.multiple_of(pair * 6 * size, 2 * size), 2 * size)] = (
        (jnp.concatenate(pieces, axis=0) * size ** -0.5).T.astype(LOW))

    @pl.when(part == steps_q - 1)
    def _():
        for i, acc in enumerate((dk_acc, dv_acc)):
            stage[pair, i] = acc[rows:].astype(LOW)
            kv_copy(pair, i).start()
            kept[pair, i] = acc[:rows]

    @pl.when(step == total - 1)
    def _():
        for when, i, what in events:
            if min(int(when * min(1.0, slots / 16)), slots) == slots:
                if what == 1:
                    scatters[i].one()
                elif what == 2:
                    scatters[i].two()
                else:
                    scatters[i].three(targets[i])
        for item in scatters:
            item.finish()
        for p in range(pairs):
            for i in range(2):
                kv_copy(p, i).wait()
                grads[:, (3 * p + i + 1) * 2 * size:(3 * p + i + 2) * 2 * size] = (kept[p, i] + landed[p, i].astype(F32)).astype(LOW)
        for i in range(4):
            for j in range(1, heads):
                mlp_copy(i, j).wait()


def backward(probs, q, k, v, grad, context, inverse, parts_out, parts_up, mlp_low, scenes, heads, size):
    ny = scenes // ZS
    rows, width = q.shape
    pairs = width // (2 * size)
    block = min(512, rows)
    d_model, hidden = parts_out.shape[-1], parts_up.shape[-1]
    rl = d_model // (2 * scenes)
    others = max(heads - 1, 1)
    halves = 2
    spec = pl.BlockSpec
    q_spec = spec((block, 2 * size), lambda p, i: (i, p))
    k_spec = spec((2 * rows, 2 * size), lambda p, i: (0, p))
    any_space = spec(memory_space=pl.ANY)
    whole = spec(memory_space=pltpu.VMEM)
    shape = jax.ShapeDtypeStruct
    sem = pltpu.SemaphoreType.DMA
    pair_buf = (pairs, 2, rows, 2 * size)
    scratch = [pltpu.VMEM((2 * rows, 2 * size), F32), pltpu.VMEM((2 * rows, 2 * size), F32), pltpu.VMEM(pair_buf, F32),
               pltpu.VMEM(pair_buf, LOW), pltpu.VMEM(pair_buf, LOW), sem((pairs, 2)), sem((pairs, 2)), sem((4, others)), sem((4, others))]
    scratch += scatter_scratch(ny, rl, d_model)
    for cols in [hidden // halves] * halves:
        scratch += scatter_scratch(ny, rl, cols)
    return pl.pallas_call(
        partial(backward_kernel, (ny, heads, rows, size, pairs, rows // block, halves)),
        grid=(pairs, rows // block),
        out_shape=[shape((rows, 3 * width), LOW), shape((rl, d_model), F32), shape((rl, hidden), F32), shape((others, rows, d_model), LOW)],
        in_specs=[spec((2, 2 * rows, block), lambda p, i: (p, 0, i)), q_spec, k_spec, k_spec, q_spec, q_spec,
                  spec((1, 8, block), lambda p, i: (p, 0, i)), any_space, any_space, any_space],
        out_specs=[whole, whole, whole, any_space],
        scratch_shapes=scratch,
        compiler_params=pltpu.CompilerParams(collective_id=1, has_side_effects=True, vmem_limit_bytes=60 * 2**20),
        cost_estimate=pl.CostEstimate(flops=16 * rows * rows * width, bytes_accessed=50 * 2**20, transcendentals=0),
        name="backward_attention",
    )(probs, q, k, v, grad, context, inverse, parts_out, parts_up, mlp_low)


def last_kernel(dims, grads, n1, tokens, resid, full_qkv, norm_two, parts_down, base, mlp_land, down_a, out_all,
                tokens_grad, output, mine_w, mine_norm, mine_out, mine_down,
                g_v, n1_v, x_v, res_v, w_v, in_sem,
                part_one, part_low, arrived, parts_qkv, tiny_land, tiny_own, out_v, done_low, done_land, x_send, x_recv, t_send, t_recv,
                n_send, n_recv, o_send, o_recv, out_sem, base_v, land_v, mine_qkv, base_sem, land_sem, res_sem, out_land, *scratch):
    ny, heads, rows, d_model, width, tile, split, down_cols, down_split = dims
    z, y, core = place(ny)
    head = lax.axis_index("head")
    wide = full_qkv.shape[1]
    rl = mine_qkv.shape[0]
    plan = [(parts_down, pl.ds(down_cols[0], down_split)), (parts_down, pl.ds(down_cols[0] + down_split, down_cols[1] - down_split)),
            (parts_qkv, pl.ds(0, split)), (parts_qkv, pl.ds(split, wide - split))]
    down_x, down_y, qkv_a, qkv_b = make_scatters(ny, plan, scratch)
    chunks = rows // tile
    part_rows = rows // heads
    per_part = part_rows // tile
    loads = [pltpu.make_async_copy(src, dst, in_sem.at[i]) for i, (src, dst) in enumerate((
        (grads, g_v), (full_qkv, w_v), (n1, n1_v), (tokens, x_v), (resid, res_v)))]
    for item in loads:
        item.start()
    base_load = pltpu.make_async_copy(base, base_v, base_sem.at[0])

    def land_load(i):
        return pltpu.make_async_copy(mlp_land.at[:, pl.ds(i * tile, tile)], land_v.at[i % 2], land_sem.at[i % 2])

    def result_copy(i):
        at = pl.ds(i * tile, tile)
        return pltpu.make_async_copy(base_v.at[at], output.at[at], res_sem.at[i])

    def finish_output(i):
        at = pl.ds(i * tile, tile)
        land_load(i).wait()
        total = base_v[at]
        for step in range(1, heads):
            total += land_v[i % 2, step - 1].astype(F32)
        base_v[at] = total
        result_copy(i).start()
        if i + 2 < chunks:
            land_load(i + 2).start()

    def rows_at(step, j):
        return pl.ds(pl.multiple_of((head + heads + step) % heads * part_rows + j * tile, tile), tile)

    def x_copy(step, j):
        return remote(part_low.at[rows_at(step, j)], arrived.at[step - 1, pl.ds(j * tile, tile)], x_send.at[step - 1, j],
                      x_recv.at[step - 1, j], {"head": (head + step) % heads})

    def t_copy(step, j):
        at = pl.ds(j * tile, tile)
        return remote(done_low.at[at], done_land.at[step - 1, at], t_send.at[step - 1, j], t_recv.at[step - 1, j],
                      {"head": (head + step) % heads})

    def n_copy(step):
        return remote(tiny_own, tiny_land.at[step - 1], n_send.at[step - 1], n_recv.at[step - 1], {"head": (head + step) % heads})

    def o_copy(step):
        to = (head + step) % heads
        return remote(out_all.at[:, pl.ds(pl.multiple_of(to * width, width), width)], out_land.at[step - 1], o_send.at[step - 1],
                      o_recv.at[step - 1], {"head": to})

    def out_copy(step, j):
        at = rows_at(step, j)
        return pltpu.make_async_copy(out_v.at[at], tokens_grad.at[at], out_sem.at[step, j])

    greet_all(ny, heads)
    down_x.begin()
    down_y.begin()
    for item in loads[:2]:
        item.wait()

    def partial_sum(step, j):
        at = rows_at(step, j)
        total = dot(g_v[at], w_v[:, 128:], 1, 1)
        part_one[at] = total
        part_low[at] = total.astype(LOW)

    for step in range(1, heads):
        for j in range(per_part):
            partial_sum(step, j)
            x_copy(step, j).start()
    for step in range(1, heads):
        o_copy(step).start()
    down_x.one()
    for j in range(per_part):
        partial_sum(0, j)
    down_y.one()
    for item in loads[2:]:
        item.wait()
    per_z = d_model // ZS
    for zz in range(0, ZS, 2):
        cols = n1_v[:, zz * per_z:(zz + 2) * per_z]
        value = dot(cols, g_v[...], 0, 0).astype(LOW)
        parts_qkv[zz:zz + 2, :, :, :, 128:] = value.reshape(2, ny, 2, rl, 3 * width)
    qkv_b.begin()
    base_load.start()
    for i in range(min(2, chunks)):
        land_load(i).start()
    gain = w_v[:, :128].astype(F32).T[0:1]

    def hat_of(at):
        x = x_v[at].astype(F32)
        centre = x - jnp.mean(x, axis=1, keepdims=True)
        spread = lax.rsqrt(jnp.mean(centre * centre, axis=1, keepdims=True) + 1e-05)
        return centre * spread, spread

    gain_sum = jnp.zeros((1, d_model), F32)
    shift_sum = jnp.zeros((1, d_model), F32)
    for i in range(chunks):
        at = pl.ds(i * tile, tile)
        hat, _ = hat_of(at)
        gain_sum += jnp.sum(part_one[at] * hat, axis=0, keepdims=True)
        shift_sum += jnp.sum(part_one[at], axis=0, keepdims=True)
        if i == chunks // 2:
            qkv_b.one()
    sums = jnp.concatenate([gain_sum, shift_sum, norm_two[0:2], jnp.zeros((124, d_model), F32)], axis=0).T.astype(LOW)
    parts_qkv[:, :, :, :, :128] = sums.reshape(ZS, ny, 2, rl, 128)
    qkv_a.begin()

    def receive(j):
        at = rows_at(0, j)
        here = pl.ds(j * tile, tile)
        total = part_one[at]
        for step in range(1, heads):
            x_copy(step, j).wait_recv()
            total += arrived[step - 1, here].astype(F32)
        hat, spread = hat_of(at)
        scaled = total * gain
        inner = scaled - jnp.mean(scaled, axis=1, keepdims=True) - hat * jnp.mean(scaled * hat, axis=1, keepdims=True)
        total = res_v[here] + inner * spread
        out_v[at] = total
        out_copy(0, j).start()
        done_low[here] = total.astype(LOW)
        for step in range(1, heads):
            t_copy(step, j).start()

    def land(step, j):
        at = rows_at(-step, j)
        t_copy(step, j).wait_recv()
        out_v[at] = done_land[step - 1, j * tile:(j + 1) * tile].astype(F32)
        out_copy(heads - step, j).start()

    receive(0)
    qkv_a.one()
    for j in range(1, per_part):
        receive(j)
    mine_down[:, :down_a.shape[1]] = down_a[...]
    first = pl.ds(pl.multiple_of(head * width, width), width)
    total = out_all[:, first]
    for step in range(1, heads):
        o_copy(step).wait()
        total += out_land[step - 1]
    mine_out[...] = total
    down_x.two()
    base_load.wait()
    for i in range(chunks // 2):
        finish_output(i)
    down_y.two()
    for i in range(chunks // 2, chunks):
        finish_output(i)
    down_x.three(mine_down.at[:, pl.ds(down_cols[0], down_split)], True)
    qkv_b.two()
    down_y.three(mine_down.at[:, pl.ds(down_cols[0] + down_split, down_cols[1] - down_split)], True)
    waits = [(step, j) for j in range(per_part) for step in range(1, heads)]
    for item in waits[:len(waits) // 2]:
        land(*item)
    qkv_a.two()
    for item in waits[len(waits) // 2:-1]:
        land(*item)
    qkv_b.three(mine_qkv)
    qkv_a.three(mine_qkv)
    tiny_own[...] = mine_qkv[:, :128]
    for step in range(1, heads):
        n_copy(step).start()
    for item in waits[-1:]:
        land(*item)
    total = mine_qkv[:, :128]
    for step in range(1, heads):
        n_copy(step).wait()
        total += tiny_land[step - 1]
    mine_norm[...] = total.T[:8]
    for p in range(width // 128):
        for c in range(3):
            mine_w[c, :, p * 128:(p + 1) * 128] = mine_qkv[:, 128 * (3 * p + c + 1):128 * (3 * p + c + 2)]
    for item in (down_x, down_y, qkv_a, qkv_b):
        item.finish()
    for j in range(per_part):
        out_copy(0, j).wait()
        for step in range(1, heads):
            out_copy(step, j).wait()
            x_copy(step, j).wait_send()
            t_copy(step, j).wait_send()
    for i in range(chunks):
        result_copy(i).wait()


def last_stage(grads, n1, tokens, resid, full_qkv, norm_two, parts_down, base, mlp_land, down_a, out_all, scenes, heads):
    ny = scenes // ZS
    rows, d_model = tokens.shape
    width, hidden = grads.shape[1] // 3, parts_down.shape[-1]
    first, third = shares(hidden)
    rl = d_model // (2 * scenes)
    wide = full_qkv.shape[1]
    part_rows = rows // heads
    tile = min(128, part_rows)
    chunks, per_part = rows // tile, part_rows // tile
    split = (wide // 128 + 1) // 2 * 128
    down_split = (third // 128 + 1) // 2 * 128
    others = max(heads - 1, 1)
    sem = pltpu.SemaphoreType.DMA
    shape, vmem = jax.ShapeDtypeStruct, pltpu.VMEM
    any_space, whole = pl.BlockSpec(memory_space=pl.ANY), pl.BlockSpec(memory_space=pltpu.VMEM)
    big, own = (rows, d_model), (part_rows, d_model)
    scratch = [vmem((rows, 3 * width), LOW), vmem(big, LOW), vmem(big, LOW), vmem(own, F32), vmem((d_model, wide), LOW), sem((5,)),
               vmem(big, F32), vmem(big, LOW), vmem((others, *own), LOW), vmem((ZS, ny, 2, rl, wide), LOW), vmem((others, rl, 128), F32),
               vmem((rl, 128), F32), vmem(big, F32), vmem(own, LOW), vmem((others, *own), LOW), sem((others, per_part)),
               sem((others, per_part)), sem((others, per_part)), sem((others, per_part)), sem((others,)), sem((others,)),
               sem((others,)), sem((others,)), sem((heads, per_part)), vmem(big, F32), vmem((2, others, tile, d_model), LOW),
               vmem((rl, wide), F32), sem((1,)), sem((2,)), sem((chunks,)), vmem((others, rl, width), F32)]
    for cols in (down_split, third - down_split, split, wide - split):
        scratch += scatter_scratch(ny, rl, cols)
    return pl.pallas_call(
        partial(last_kernel, (ny, heads, rows, d_model, width, tile, split, (first, third), down_split)),
        out_shape=[shape(big, F32), shape(big, F32), shape((3, rl, width), F32), shape((8, rl), F32), shape((rl, width), F32),
                   shape((rl, hidden), F32)],
        in_specs=[any_space] * 5 + [whole, any_space, any_space, any_space, whole, whole],
        out_specs=[any_space, any_space, whole, whole, whole, whole],
        scratch_shapes=scratch,
        compiler_params=pltpu.CompilerParams(collective_id=2, has_side_effects=True, vmem_limit_bytes=63 * 2**20),
        cost_estimate=pl.CostEstimate(flops=12 * rows * d_model * width, bytes_accessed=30 * 2**20, transcendentals=0),
        name="last_stage",
    )(grads, n1, tokens, resid, full_qkv, norm_two, parts_down, base, mlp_land, down_a, out_all)


def on_device(n_scene, n_head, tokens, counts, w_qkv, w_out, w_up, w_down, gain_one, shift_one, gain_two, shift_two, cotangent):
    rows, d_model = tokens.shape
    width, hidden = w_qkv.shape[2], w_up.shape[1]
    size = 64
    core = lax.axis_index("seq")
    limits = jnp.stack([counts[0] - core * rows, counts[0] - (1 - core) * rows]).astype(jnp.int32)
    columns = jnp.pad(jnp.stack([gain_one, shift_one, gain_two, shift_two], axis=1), ((0, 0), (0, 124)))
    by_pair = w_qkv.reshape(3, -1, width // (2 * size), 2 * size).transpose(1, 2, 0, 3).reshape(-1, 3 * width)
    shard_qkv = jnp.concatenate([columns, by_pair], axis=1)
    n1, q, k, v, full_qkv, full_out, full_up, full_down, probs, context, context_all, inverse = forward(
        limits, shard_qkv, w_out.T, w_up, w_down.T, tokens, n_scene, n_head, size)
    grad_resid, base, mlp_low, grad_context, norm_two, grad_outproj, grad_up, grad_down, down_a = middle(
        tokens, context_all, cotangent, full_qkv, full_out, full_up, full_down, n_scene, n_head)
    grads, out_all, mine_up, mlp_land = backward(
        probs, q, k, v, grad_context, context, inverse, grad_outproj, grad_up, mlp_low, n_scene, n_head, size)
    tokens_grad, output, mine_qkv, norms, mine_out, mine_down = last_stage(
        grads, n1, tokens, grad_resid, full_qkv, norm_two, grad_down, base, mlp_land, down_a, out_all, n_scene, n_head)
    return (output, tokens_grad, mine_qkv, mine_out.T, mine_up, mine_down.T, norms[0], norms[1], norms[2], norms[3])


def solution(mesh):
    rows, both = ("scene", "seq"), P(("scene", "seq"))
    weights = (P(None, rows, "head"), P("head", rows), P(rows, "head"), P("head", rows), both, both, both, both)
    return jax.shard_map(
        partial(on_device, mesh.shape["scene"], mesh.shape["head"]), mesh=mesh,
        in_specs=(P(rows, None), P("scene"), *weights, P(rows, None)),
        out_specs=(P(rows, None), P(rows, None), *weights),
        check_vma=False,
    )
```

```python
from functools import partial

import jax
import jax.numpy as jnp
from jax import lax
from jax.experimental import pallas as pl
from jax.experimental.pallas import tpu as pltpu
from jax.sharding import PartitionSpec as P

MESH = pl.DeviceIdType.MESH
ZS = 4


def place(ny):
    scene = lax.axis_index("scene")
    return scene // ny, scene % ny, lax.axis_index("seq")


def remote(src, dst, send_sem, recv_sem, device):
    return pltpu.make_async_remote_copy(
        src_ref=src, dst_ref=dst, send_sem=send_sem, recv_sem=recv_sem,
        device_id=device, device_id_type=MESH,
    )


F32 = jnp.float32
LOW = jnp.bfloat16


def dot(a, b, ca, cb):
    return lax.dot_general(a, b, (((ca,), (cb,)), ((), ())), preferred_element_type=F32)


def only_head(x, h, size):
    lane = lax.broadcasted_iota(jnp.int32, x.shape, 1)
    return jnp.where(lane // size == h, x, jnp.zeros_like(x))


class Gather:
    def __init__(self, ny, source, full, cols, sems):
        self.ny, self.source, self.full, self.cols = ny, source, full, cols
        self.rsend, self.rrecv, self.lsend, self.lrecv, self.ysend, self.yrecv, self.csend, self.crecv = sems
        self.z, self.y, self.core = place(ny)

    def at(self, zz, yy):
        return self.full.at[zz, yy, self.core, :, self.cols]

    def right(self, k):
        src = self.source() if k == 0 else self.at(self.z - k, self.y)
        dst = self.at(self.z - k, self.y)
        return remote(src, dst, self.rsend.at[k], self.rrecv.at[k], {"scene": (self.z + 1) * self.ny + self.y})

    def left(self, k):
        src = self.source() if k == 0 else self.at(self.z + k, self.y)
        dst = self.at(self.z + k, self.y)
        return remote(src, dst, self.lsend.at[k], self.lrecv.at[k], {"scene": (self.z - 1) * self.ny + self.y})

    def across(self, zz, step, own=False):
        src = self.source() if own else self.at(zz, self.y)
        peer = self.z * self.ny + (self.y + step) % self.ny
        return remote(src, self.at(zz, self.y), self.ysend.at[step - 1], self.yrecv.at[step - 1], {"scene": peer})

    def arrival(self, zz, step):
        yy = (self.y + self.ny - step) % self.ny
        return remote(self.at(zz, yy), self.at(zz, yy), self.ysend.at[step - 1], self.yrecv.at[step - 1],
                      {"scene": self.z * self.ny + yy})

    def twin(self, zz, step, own=False):
        src = self.source() if own else self.at(zz, (self.y + self.ny - step) % self.ny)
        dst = self.at(zz, (self.y + self.ny - step) % self.ny)
        return remote(src, dst, self.csend.at[0], self.crecv.at[0], {"seq": 1 - self.core})

    def column(self, step):
        yy = (self.y + self.ny - step) % self.ny
        all_z = self.full.at[:, yy, self.core, :, self.cols]
        return remote(all_z, all_z, self.ysend.at[step - 1], self.yrecv.at[step - 1], {"scene": self.z * self.ny + yy})

    def twins(self):
        mine, theirs = [self.full.at[:, :, c, :, self.cols] for c in (self.core, 1 - self.core)]
        return [remote(item, item, self.csend.at[0], self.crecv.at[0], {"seq": 1 - self.core}) for item in (mine, theirs)]

    def begin(self):
        @pl.when(self.z < ZS - 1)
        def _():
            self.right(0).start()

        @pl.when(self.z > 0)
        def _():
            self.left(0).start()

        for step in range(1, self.ny):
            self.across(self.z, step, True).start()
        self.twin(self.z, 0, True).start()

    def hop(self, k):
        @pl.when(self.z >= k)
        def _():
            self.right(k - 1).wait_recv()
            if k < ZS - 1:
                @pl.when(self.z < ZS - 1)
                def _():
                    self.right(k).start()
            for step in range(1, self.ny):
                self.across(self.z - k, step).start()
            self.twin(self.z - k, 0).start()

        @pl.when(self.z + k < ZS)
        def _():
            self.left(k - 1).wait_recv()
            if k < ZS - 1:
                @pl.when(self.z > 0)
                def _():
                    self.left(k).start()
            for step in range(1, self.ny):
                self.across(self.z + k, step).start()
            self.twin(self.z + k, 0).start()

    def spread(self):
        for step in range(1, self.ny):
            self.column(step).wait_recv()
            for zz in range(ZS):
                self.twin(zz, step).start()

    def finish(self):
        for k in range(ZS - 1):
            @pl.when((self.z < ZS - 1) & (self.z >= k))
            def _():
                self.right(k).wait_send()

            @pl.when((self.z > 0) & (self.z + k < ZS))
            def _():
                self.left(k).wait_send()
        for step in range(1, self.ny):
            self.column(step).wait_send()
        mine, theirs = self.twins()
        mine.wait_send()
        theirs.wait_recv()


class PairGather(Gather):
    def row(self, zz):
        return self.full.at[zz, :, self.core, :, self.cols]

    def right(self, k):
        return remote(self.row(self.z - k), self.row(self.z - k), self.rsend.at[k], self.rrecv.at[k],
                      {"scene": (self.z + 1) * self.ny + self.y})

    def left(self, k):
        return remote(self.row(self.z + k), self.row(self.z + k), self.lsend.at[k], self.lrecv.at[k],
                      {"scene": (self.z - 1) * self.ny + self.y})

    def twin(self, zz):
        return remote(self.row(zz), self.row(zz), self.csend.at[0], self.crecv.at[0], {"seq": 1 - self.core})

    def begin(self):
        for step in range(1, self.ny):
            self.across(self.z, step, True).start()

    def pair(self):
        for step in range(1, self.ny):
            self.arrival(self.z, step).wait_recv()

        @pl.when(self.z < ZS - 1)
        def _():
            self.right(0).start()

        @pl.when(self.z > 0)
        def _():
            self.left(0).start()

        self.twin(self.z).start()

    def hop(self, k):
        @pl.when(self.z >= k)
        def _():
            self.right(k - 1).wait_recv()
            if k < ZS - 1:
                @pl.when(self.z < ZS - 1)
                def _():
                    self.right(k).start()
            self.twin(self.z - k).start()

        @pl.when(self.z + k < ZS)
        def _():
            self.left(k - 1).wait_recv()
            if k < ZS - 1:
                @pl.when(self.z > 0)
                def _():
                    self.left(k).start()
            self.twin(self.z + k).start()

    def finish(self):
        for k in range(ZS - 1):
            @pl.when((self.z < ZS - 1) & (self.z >= k))
            def _():
                self.right(k).wait_send()

            @pl.when((self.z > 0) & (self.z + k < ZS))
            def _():
                self.left(k).wait_send()
        for step in range(1, self.ny):
            self.across(self.z, step).wait_send()
        mine, theirs = self.twins()
        mine.wait_send()
        theirs.wait_recv()


def gather_sems(ny):
    sem = pltpu.SemaphoreType.DMA
    return [sem((ZS - 1,)), sem((ZS - 1,)), sem((ZS - 1,)), sem((ZS - 1,)), sem((max(ny - 1, 1),)), sem((max(ny - 1, 1),)),
            sem((1,)), sem((1,))]


def greet_all(ny, heads):
    z, y, core = place(ny)
    head = lax.axis_index("head")
    barrier = pltpu.get_barrier_semaphore()

    def signal(device):
        pl.semaphore_signal(barrier, 1, device_id=device, device_id_type=MESH)

    for step in range(1, ZS):
        signal({"scene": (z + step) % ZS * ny + y})
    for step in range(1, ny):
        signal({"scene": z * ny + (y + step) % ny})
    for step in range(1, heads):
        signal({"head": (head + step) % heads})
    signal({"seq": 1 - core})
    pl.semaphore_wait(barrier, ZS + ny - 1 + heads - 1)


def split_cols(total, parts):
    size = total // parts
    return [pl.ds(i * size, size) for i in range(parts)]


def forward_kernel(dims, limits, shard_qkv, shard_out, shard_up, shard_down, tokens,
                   n1_out, q_out, k_out, v_out, full_qkv, full_out, full_up, full_down, probs, context, context_all, inverse,
                   w0, hat, n1, q_s, k_s, v_s, bias, ctx_s, scores, tops, local_sem, kv_send, kv_recv, xw_send, xw_recv, xt_send, xt_recv, xc_send, xc_recv, *sems):
    ny, heads, rows, width, size, block, pairs, steps_q, halves = dims
    pair, part = pl.program_id(0), pl.program_id(1)
    step = pair * steps_q + part
    z, y, core = place(ny)
    head = lax.axis_index("head")
    d_model = tokens.shape[1]
    per = 8
    own_cols = pl.ds(pl.multiple_of(head * width, width), width)

    def of(i):
        return sems[i * per:(i + 1) * per]

    group = 6 * size
    edges = [0] + [128 + (p + 1) * group for p in range(pairs)]
    firsts = []
    for p in range(pairs):
        cols = pl.ds(edges[p], edges[p + 1] - edges[p])
        firsts.append(Gather(ny, partial(lambda c: shard_qkv.at[:, c], cols), w0, cols, of(2 + 2 * halves + p)))
    outer = Gather(ny, lambda: shard_out, full_out, own_cols, of(1))
    thick = []
    for n, (shard, full) in enumerate(((shard_up, full_up), (shard_down, full_down))):
        for i, cols in enumerate(split_cols(full_up.shape[-1], halves)):
            kind = PairGather if n == 1 and i == halves - 1 else Gather
            thick.append(kind(ny, partial(lambda s, c: s.at[:, c], shard, cols), full, cols, of(2 + n * halves + i)))
    up_a, up_b, down_a, down_b = thick

    def local(src, dst, i):
        return pltpu.make_async_copy(src, dst, local_sem.at[i])

    def cols_of(step):
        return pl.ds(pl.multiple_of((head + heads - step) % heads * width, width), width)

    def out_copy(step):
        mine = full_out.at[:, :, core, :, own_cols]
        return remote(mine, mine, xw_send.at[step - 1], xw_recv.at[step - 1], {"head": (head + step) % heads})

    def out_twin(step):
        other = full_out.at[:, :, core, :, cols_of(step)]
        return remote(other, other, xt_send.at[step - 1], xt_recv.at[step - 1], {"seq": 1 - core})

    def kv_copy(p, i):
        src = (k_s, v_s)[i]
        cols = pl.ds(p * 2 * size, 2 * size)
        return remote(src.at[pl.ds(0, rows), cols], src.at[pl.ds(rows, rows), cols], kv_send.at[p, i], kv_recv.at[p, i],
                      {"seq": 1 - core})

    def project(p):
        tile = min(256, rows)

        @pl.loop(0, rows // tile)
        def _(i):
            at = pl.ds(pl.multiple_of(i * tile, tile), tile)
            w = w0[:, :, :, :, 128 + p * group:128 + (p + 1) * group].reshape(d_model, group)
            value = dot(n1[at], w, 1, 0).astype(LOW)
            cols = pl.ds(p * 2 * size, 2 * size)
            q_s[at, cols] = value[:, :2 * size] * LOW(size ** -0.5)
            k_s[at, cols] = value[:, 2 * size:4 * size]
            v_s[at, cols] = value[:, 4 * size:]

        for i in range(2):
            kv_copy(p, i).start()

    def ctx_copy(p, step):
        cols = pl.ds(pl.multiple_of(p * 2 * size, 2 * size), 2 * size)
        wide = pl.ds(pl.multiple_of(head * width + p * 2 * size, 2 * size), 2 * size)
        return remote(ctx_s.at[:, cols], context_all.at[:, wide], xc_send.at[p, step - 1], xc_recv.at[p, step - 1],
                      {"head": (head + step) % heads})

    own_blocks = [(shard_qkv, w0.at[z, y, core], 0), (shard_out, full_out.at[z, y, core, :, own_cols], 1),
                  (shard_up, full_up.at[z, y, core], 2), (shard_down, full_down.at[z, y, core], 3)]
    results = [(w0, full_qkv, 4), (n1, n1_out, 5), (q_s, q_out, 6), (k_s, k_out, 7), (v_s, v_out, 8)]
    ctx_local = (ctx_s, context_all.at[:, own_cols], 9)

    @pl.when(step == 0)
    def _():
        for item in own_blocks:
            local(*item).start()
        greet_all(ny, heads)
        for gather in firsts[:2]:
            gather.begin()
        tile = min(128, rows)

        @pl.loop(0, rows // tile)
        def _(i):
            at = pl.ds(pl.multiple_of(i * tile, tile), tile)
            x = tokens[at].astype(F32)
            centre = x - jnp.mean(x, axis=1, keepdims=True)
            spread = jnp.mean(centre * centre, axis=1, keepdims=True)
            hat[at] = centre * lax.rsqrt(spread + 1e-05)

        low_rows = lax.broadcasted_iota(jnp.int32, bias.shape, 0)
        lane = lax.broadcasted_iota(jnp.int32, bias.shape, 1)
        limit = jnp.where(low_rows < rows, limits[0], limits[1] + rows)
        bias[...] = jnp.where((low_rows >= limit) & (lane == 0), -1e30, 0.0).astype(LOW)
        after = [
            (0, lambda g: g.hop(1)), (2, lambda g: g.begin()), (0, lambda g: g.hop(2)), (1, lambda g: g.hop(1)), (0, lambda g: g.hop(3)),
            (3, lambda g: g.begin()), (1, lambda g: g.hop(2)), (0, lambda g: g.spread()), (1, lambda g: g.hop(3)),
            (2, lambda g: g.hop(1)), (1, lambda g: g.spread()), (2, lambda g: g.hop(2))]
        for p, act in after[:9]:
            if p < pairs:
                act(firsts[p])
        firsts[0].finish()
        for item in own_blocks:
            local(*item).wait()
        norms = w0[:, :, :, :, :128].reshape(d_model, 128).astype(F32).T
        gain, shift = norms[0:1], norms[1:2]
        tile = min(256, rows)

        @pl.loop(0, rows // tile)
        def _(i):
            at = pl.ds(pl.multiple_of(i * tile, tile), tile)
            n1[at] = (hat[at] * gain + shift).astype(LOW)

        local(*results[1]).start()
        project(0)
        for p, act in after[9:]:
            if p < pairs:
                act(firsts[p])

    total = pairs * steps_q
    per_slot = 2
    in_step = 4 * rows // min(256, rows) // per_slot
    slots = in_step * total

    def send_out():
        for i in range(1, heads):
            out_copy(i).start()

    def pass_out():
        for i in range(1, heads):
            out_copy(i).wait_recv()
            out_twin(i).start()

    def on_pair(p, what, *given):
        if p < pairs:
            getattr(firsts[p], what)(*given)

    events = [
        (0.1, lambda: on_pair(2, "hop", 3)), (0.3, lambda: on_pair(3, "hop", 1)), (0.4, outer.begin),
        (1, lambda: on_pair(3, "hop", 2)), (1.2, lambda: on_pair(2, "spread")), (1.4, up_a.begin),
        (2, lambda: on_pair(3, "hop", 3)), (2.6, lambda: outer.hop(1)), (3.2, lambda: outer.hop(2)), (3.2, up_b.begin),
        (3.8, lambda: on_pair(3, "spread")), (3.9, lambda: outer.hop(3)), (5.2, lambda: up_a.hop(1)), (6, outer.spread), (6.1, send_out),
        (6.5, lambda: up_a.hop(2)), (7, down_a.begin), (7.2, down_b.begin),
        (7.8, lambda: up_a.hop(3)), (9.2, lambda: up_b.hop(1)), (10.5, lambda: up_b.hop(2)), (10.6, pass_out), (10.8, down_b.pair),
        (11.8, lambda: up_b.hop(3)), (12, up_a.spread), (13.2, lambda: down_a.hop(1)), (14.5, lambda: down_a.hop(2)),
        (15.8, lambda: down_a.hop(3)), (16, up_b.spread), (16, lambda: down_b.hop(1)),
        (16, lambda: down_b.hop(2)), (16, down_a.spread), (16, lambda: down_b.hop(3))]

    def run(slot_in_step):
        for when, act in events:
            slot = min(int(when * slots / 16), slots - 1)
            if when < 16 and slot % in_step == slot_in_step:
                pl.when(step == slot // in_step)(act)

    for p in range(pairs):
        @pl.when(step == p * steps_q)
        def _():
            if p == 0:
                for i in range(2):
                    kv_copy(0, i).wait()
            if p + 1 < pairs:
                firsts[p + 1].finish()
                project(p + 1)
            else:
                for item in (results[0], *results[2:]):
                    local(*item).start()

        if p + 1 < pairs:
            @pl.when(step == (p + 1) * steps_q - 1)
            def _():
                for i in range(2):
                    kv_copy(p + 1, i).wait()

    width2, chunk = 2 * size, min(256, rows)
    n_chunks = 2 * rows // chunk
    ones = (lax.broadcasted_iota(jnp.int32, (block, bias.shape[1]), 1) == 0).astype(LOW)

    def asked(at, h):
        rows_at = pl.ds(pl.multiple_of(at % steps_q * block, block), block)
        cols_at = pl.ds(pl.multiple_of(at // steps_q * width2, width2), width2)
        return jnp.concatenate([only_head(q_s[rows_at, cols_at], h, size), ones], axis=1)

    def score(at, query, slot, c, top):
        cols_at = pl.ds(pl.multiple_of(at // steps_q * width2, width2), width2)
        keys_at = pl.ds(c * chunk, chunk)
        value = dot(jnp.concatenate([k_s[keys_at, cols_at], bias[keys_at]], axis=1), query, 1, 1)
        scores[slot, keys_at] = value
        return jnp.maximum(top, jnp.max(value.reshape(chunk // 8, 8, block), axis=0))

    def weigh(h, c, top, total_e):
        keys_at = pl.ds(c * chunk, chunk)
        expo = jnp.exp(scores[h, keys_at] - top)
        probs[h, keys_at] = expo.astype(LOW)
        return total_e + jnp.sum(expo.reshape(chunk // 8, 8, block), axis=0)

    lowest = jnp.full((8, block), -3e38, F32)

    @pl.when(step == 0)
    def _():
        top, query = lowest, asked(0, 0)
        for c in range(n_chunks):
            top = score(0, query, 0, c, top)
        tops[...] = top

    cols = pl.ds(pl.multiple_of(pair * width2, width2), width2)
    following = jnp.minimum(step + 1, total - 1)
    values_t = v_s[:, cols].T
    pieces = []
    for h in range(2):
        top = jnp.max(tops[...], axis=0, keepdims=True)
        total_e, next_top = jnp.zeros((8, block), F32), lowest
        ahead = (step, 1) if h == 0 else (following, 0)
        query = asked(*ahead)
        for c in range(n_chunks):
            if c % per_slot == 0:
                run(h * (n_chunks // per_slot) + c // per_slot)
            next_top = score(ahead[0], query, 1 - h, c, next_top)
            total_e = weigh(h, c, top, total_e)
        tops[...] = next_top
        over = 1.0 / jnp.sum(total_e, axis=0, keepdims=True)
        pieces.append(dot(values_t, probs[h], 1, 0)[h * size:(h + 1) * size] * over)
        inverse[0, h:h + 1] = over
    here = jnp.concatenate(pieces, axis=0).T.astype(LOW)
    context[...] = here
    ctx_s[pl.ds(pl.multiple_of(part * block, block), block), cols] = here

    @pl.when(part == steps_q - 1)
    def _():
        for i in range(1, heads):
            ctx_copy(pair, i).start()

    @pl.when(step == total - 1)
    def _():
        local(*ctx_local).start()
        for when, act in events:
            if when >= 16:
                act()
        for gather in (outer, *thick):
            gather.finish()
        for item in results:
            local(*item).wait()
        local(*ctx_local).wait()
        for i in range(1, heads):
            out_copy(i).wait_send()
            out_twin(i).wait()
            for p in range(pairs):
                ctx_copy(p, i).wait()


def forward(limits, shard_qkv, shard_out, shard_up, shard_down, tokens, scenes, heads, size):
    ny = scenes // ZS
    rows, d_model = tokens.shape
    rl, width = shard_out.shape
    hidden = shard_up.shape[1]
    pairs = width // (2 * size)
    block = min(512, rows)
    steps_q = rows // block
    halves = 2
    sem = pltpu.SemaphoreType.DMA
    any_space = pl.BlockSpec(memory_space=pl.ANY)
    shape = jax.ShapeDtypeStruct
    wide = shard_qkv.shape[1]
    outs = [shape((rows, d_model), LOW), shape((rows, width), LOW), shape((2 * rows, width), LOW), shape((2 * rows, width), LOW),
            shape((ZS, ny, 2, rl, wide), LOW), shape((ZS, ny, 2, rl, d_model), LOW), shape((ZS, ny, 2, rl, hidden), LOW),
            shape((ZS, ny, 2, rl, hidden), LOW), shape((2 * pairs, 2 * rows, rows), LOW), shape((rows, width), LOW),
            shape((rows, d_model), LOW), shape((pairs, 8, rows), F32)]
    out_specs = [any_space] * 8 + [
        pl.BlockSpec((2, 2 * rows, block), lambda p, i: (p, 0, i)), pl.BlockSpec((block, 2 * size), lambda p, i: (i, p)),
        any_space, pl.BlockSpec((1, 8, block), lambda p, i: (p, 0, i))]
    scratch = [pltpu.VMEM((ZS, ny, 2, rl, wide), LOW), pltpu.VMEM((rows, d_model), F32), pltpu.VMEM((rows, d_model), LOW),
               pltpu.VMEM((rows, width), LOW), pltpu.VMEM((2 * rows, width), LOW), pltpu.VMEM((2 * rows, width), LOW),
               pltpu.VMEM((2 * rows, 128), LOW), pltpu.VMEM((rows, width), LOW),
               pltpu.VMEM((2, 2 * rows, block), F32), pltpu.VMEM((8, block), F32), sem((10,)), sem((pairs, 2)), sem((pairs, 2)),
               sem((max(heads - 1, 1),)), sem((max(heads - 1, 1),)), sem((max(heads - 1, 1),)), sem((max(heads - 1, 1),)), sem((pairs, max(heads - 1, 1))), sem((pairs, max(heads - 1, 1)))]
    for _ in range(2 + 2 * halves + pairs):
        scratch += gather_sems(ny)
    dims = (ny, heads, rows, width, size, block, pairs, steps_q, halves)
    flops = 2 * rows * d_model * 3 * width + 8 * rows * rows * width
    results = pl.pallas_call(
        partial(forward_kernel, dims),
        grid=(pairs, steps_q),
        out_shape=outs,
        in_specs=[pl.BlockSpec(memory_space=pltpu.SMEM)] + [pl.BlockSpec(memory_space=pltpu.VMEM)] * 4 + [pl.BlockSpec(memory_space=pltpu.VMEM)],
        out_specs=out_specs,
        scratch_shapes=scratch,
        compiler_params=pltpu.CompilerParams(collective_id=0, has_side_effects=True, vmem_limit_bytes=60 * 2**20),
        cost_estimate=pl.CostEstimate(flops=flops, bytes_accessed=60 * 2**20, transcendentals=0),
        name="forward_attention",
    )(limits, shard_qkv, shard_out, shard_up, shard_down, tokens)
    n1, q, k, v, full_qkv, full_out, full_up, full_down, probs, context, context_all, inverse = results
    flat = lambda a: a.reshape(d_model, a.shape[-1])
    return n1, q, k, v, flat(full_qkv), flat(full_out), flat(full_up), flat(full_down), probs, context, context_all, inverse


class Scatter:
    def __init__(self, ny, parts, cols, bufs, sems):
        self.ny, self.parts, self.cols = ny, parts, cols
        self.own, self.from_core, self.from_y, self.sum_two, self.from_z = bufs
        self.load_sem, self.csend, self.crecv, self.ysend, self.yrecv, self.zsend, self.zrecv = sems
        self.z, self.y, self.core = place(ny)

    def load(self):
        return pltpu.make_async_copy(self.parts.at[:, :, self.core, :, self.cols], self.own, self.load_sem.at[0])

    def to_core(self):
        return remote(self.parts.at[:, :, 1 - self.core, :, self.cols], self.from_core, self.csend.at[0], self.crecv.at[0],
                      {"seq": 1 - self.core})

    def to_y(self, step):
        yy = (self.y + step) % self.ny
        return remote(self.own.at[:, yy], self.from_y.at[step - 1], self.ysend.at[step - 1], self.yrecv.at[step - 1],
                      {"scene": self.z * self.ny + yy})

    def to_z(self, step):
        zz = (self.z + step) % ZS
        return remote(self.sum_two.at[zz], self.from_z.at[step - 1], self.zsend.at[step - 1], self.zrecv.at[step - 1],
                      {"scene": zz * self.ny + self.y})

    def begin(self):
        self.load().start()
        self.to_core().start()

    def one(self):
        self.load().wait()
        self.to_core().wait_recv()
        for zz in range(ZS):
            for yy in range(self.ny):
                self.own[zz, yy] = (self.own[zz, yy].astype(F32) + self.from_core[zz, yy].astype(F32)).astype(LOW)
        for step in range(1, self.ny):
            self.to_y(step).start()

    def two(self):
        for step in range(1, self.ny):
            self.to_y(step).wait_recv()
        for zz in range(ZS):
            total = self.own[zz, self.y].astype(F32)
            for step in range(1, self.ny):
                total += self.from_y[step - 1, zz].astype(F32)
            self.sum_two[zz] = total.astype(LOW)
        for step in range(1, ZS):
            self.to_z(step).start()

    def three(self, out, alone=False):
        for step in range(1, ZS):
            self.to_z(step).wait_recv()
        total = self.sum_two[self.z].astype(F32)
        for step in range(1, ZS):
            total += self.from_z[step - 1].astype(F32)
        if alone:
            out[...] = total
        else:
            out[:, self.cols] = total

    def finish(self):
        self.to_core().wait_send()
        for step in range(1, self.ny):
            self.to_y(step).wait_send()
        for step in range(1, ZS):
            self.to_z(step).wait_send()


SCATTER_BUFS, SCATTER_SEMS = 5, 7


def scatter_scratch(ny, rl, cols):
    sem = pltpu.SemaphoreType.DMA
    other = max(ny - 1, 1)
    return [pltpu.VMEM((ZS, ny, rl, cols), LOW), pltpu.VMEM((ZS, ny, rl, cols), LOW), pltpu.VMEM((other, ZS, rl, cols), LOW),
            pltpu.VMEM((ZS, rl, cols), LOW), pltpu.VMEM((ZS - 1, rl, cols), LOW),
            sem((1,)), sem((1,)), sem((1,)), sem((other,)), sem((other,)), sem((ZS - 1,)), sem((ZS - 1,))]


def make_scatters(ny, plan, scratch):
    n = SCATTER_BUFS + SCATTER_SEMS
    result = []
    for i, (parts, cols) in enumerate(plan):
        mine = scratch[i * n:(i + 1) * n]
        result.append(Scatter(ny, parts, cols, mine[:SCATTER_BUFS], mine[SCATTER_BUFS:]))
    return result

def middle_kernel(dims, tokens, context_all, cotangent, full_qkv, full_out, full_up, full_down,
                  resid_grad, base, mlp_low, grad_context, norm_two, parts_out, parts_up, parts_down, mine_down,
                  x_v, ctx_v, cot_v, norm_v, wo, wu, wd, n2, act, gu, resid, part, low, arrived, up_v, down_v, out_v, gctx_v,
                  base_v, mlp_v, in_sem, out_sem, slot_sem, x_send, x_recv, g_send, g_recv, *scratch):
    ny, heads, rows, d_model, width, hidden, tile, size_f, first_cols = dims
    head = lax.axis_index("head")
    chunks = rows // tile
    part_rows = rows // heads
    per_part = part_rows // tile
    (down,) = make_scatters(ny, [(down_v, pl.ds(0, first_cols))], scratch)
    own_rows = pl.ds(pl.multiple_of(head * part_rows, part_rows), part_rows)

    def load(src, dst, i):
        return pltpu.make_async_copy(src, dst, in_sem.at[i])

    loads = [load(context_all, ctx_v, 0), load(full_out, wo, 1), load(tokens, x_v, 2), load(full_qkv.at[:, pl.ds(0, 128)], norm_v, 3),
             load(full_up, wu, 4), load(cotangent, cot_v, 5), load(full_down, wd, 6)]
    for item in loads:
        item.start()
    half = tile // 2

    def place_of(i):
        whole_tile = not isinstance(i, int)
        number = 0 if not whole_tile and i == chunks else i
        step = number // per_part + 1
        within = number % per_part * tile
        size = tile if whole_tile or 0 < i < chunks else half
        within = within + (half if not whole_tile and i == 0 else 0)
        return step, within, size

    def rows_of(i):
        step, within, size = place_of(i)
        return pl.ds(pl.multiple_of((head + step) % heads * part_rows + within, half), size)

    def x_copy(i, step):
        _, within, size = place_of(i)
        return remote(low.at[rows_of(i)], arrived.at[step - 1, pl.ds(within, size)], x_send.at[i], x_recv.at[i],
                      {"head": (head + step) % heads})

    def g_copy(j, step):
        to = (head + step) % heads
        at = pl.ds(j * tile, tile)
        there = pl.ds(pl.multiple_of(head * part_rows + j * tile, tile), tile)
        return remote(gctx_v.at[at, pl.ds(pl.multiple_of(to * width, width), width)], grad_context.at[there],
                      g_send.at[j, step - 1], g_recv.at[j, step - 1], {"head": to})

    greet_all(ny, heads)
    for item in loads:
        item.wait()
    norms = norm_v[...].astype(F32).T
    gain, shift = norms[2:3], norms[3:4]

    def hat_of(value):
        centre = value - jnp.mean(value, axis=1, keepdims=True)
        spread = lax.rsqrt(jnp.mean(centre * centre, axis=1, keepdims=True) + 1e-05)
        return centre * spread, spread

    norm_two[...] = jnp.zeros_like(norm_two)

    def forward_and_back(i):
        at = rows_of(i)
        value = x_v[at].astype(F32) + dot(ctx_v[at], wo[...], 1, 1)
        resid[at] = value
        n2[at] = (hat_of(value)[0] * gain + shift).astype(LOW)
        for f in range(hidden // size_f):
            cols = slice(f * size_f, (f + 1) * size_f)
            u = dot(n2[at], wu[:, cols], 1, 0)
            ga = dot(cot_v[at], wd[:, cols], 1, 0)
            phi = 0.5 + 0.5 * lax.erf(u * (0.5 ** 0.5))
            act[at, cols] = (u * phi).astype(LOW)
            gu[at, cols] = (ga * (phi + u * (jnp.exp(u * u * -0.5) * 0.3989422804014327))).astype(LOW)
        total = dot(gu[at], wu[...], 1, 1)
        part[at] = total
        low[at] = total.astype(LOW)

    def sums(i):
        at = rows_of(i)
        total = part[at]
        hat, _ = hat_of(resid[at])
        norm_two[0:1] += jnp.sum(total * hat, axis=0, keepdims=True)
        norm_two[1:2] += jnp.sum(total, axis=0, keepdims=True)

    if heads > 1:
        forward_and_back(chunks)
        x_copy(chunks, 1).start()
        forward_and_back(0)
        x_copy(0, 1).start()
        for step in range(1, heads):
            first = (step - 1) * per_part

            @pl.loop(max(first, 1), first + per_part)
            def _(i):
                forward_and_back(i)
                x_copy(i, step).start()

    else:
        forward_and_back(chunks)
        forward_and_back(0)

    @pl.loop(max(chunks - per_part, 1), chunks)
    def _(i):
        forward_and_back(i)

    def weight_grad(src, other, dst, count):
        per_z = d_model // ZS
        for f in range(count // size_f):
            cols = slice(f * size_f, (f + 1) * size_f)

            @pl.loop(0, ZS // 2)
            def _(j):
                at = pl.ds(pl.multiple_of(j * 2 * per_z, 2 * per_z), 2 * per_z)
                value = dot(src[:, at], other[:, cols], 0, 0).astype(LOW)
                dst[pl.ds(2 * j, 2), :, :, :, cols] = value.reshape(2, *dst.shape[1:4], size_f)

    weight_grad(cot_v, act, down_v, hidden)
    down.begin()

    def own_store(j):
        at = pl.ds(j * tile, tile)
        there = pl.ds(pl.multiple_of(head * part_rows + j * tile, tile), tile)
        return (pltpu.make_async_copy(part.at[there], resid_grad.at[at], out_sem.at[3 + 2 * j]),
                pltpu.make_async_copy(gctx_v.at[at, pl.ds(pl.multiple_of(head * width, width), width)], grad_context.at[there],
                                      out_sem.at[4 + 2 * j]))

    for j in range(per_part):
        at = pl.ds(pl.multiple_of(head * part_rows + j * tile, tile), tile)
        total = part[at]
        for step in range(1, heads):
            i = (step - 1) * per_part + j
            x_copy(i, step).wait_recv()
            if i == 0:
                x_copy(chunks, step).wait_recv()
            total += arrived[step - 1, j * tile:(j + 1) * tile].astype(F32)
        hat, spread = hat_of(resid[at])
        own_part = part[at]
        norm_two[0:1] += jnp.sum(own_part * hat, axis=0, keepdims=True)
        norm_two[1:2] += jnp.sum(own_part, axis=0, keepdims=True)
        scaled = total * gain
        inner = scaled - jnp.mean(scaled, axis=1, keepdims=True) - hat * jnp.mean(scaled * hat, axis=1, keepdims=True)
        total = cot_v[at].astype(F32) + inner * spread
        part[at] = total
        rounded = total.astype(LOW)
        low[at] = rounded
        gctx_v[j * tile:(j + 1) * tile] = dot(rounded, wo[...], 1, 0).astype(LOW)
        for step in range(1, heads):
            g_copy(j, step).start()
        for item in own_store(j):
            item.start()
    down.one()
    weight_grad(n2, gu, up_v, hidden)
    stores = [pltpu.make_async_copy(up_v, parts_up, out_sem.at[0]), pltpu.make_async_copy(down_v, parts_down, out_sem.at[1]),
              pltpu.make_async_copy(out_v, parts_out, out_sem.at[2])]
    for item in stores[:2]:
        item.start()
    down.two()
    weight_grad(low.at[own_rows], ctx_v.at[own_rows], out_v, d_model)
    stores[2].start()

    def slot_copies(i):
        at = pl.ds(pl.multiple_of(i * tile, tile), tile)
        slot = i % 2
        return (pltpu.make_async_copy(base_v.at[slot], base.at[at], slot_sem.at[0, slot]),
                pltpu.make_async_copy(mlp_v.at[slot], mlp_low.at[at], slot_sem.at[1, slot]))

    def slot_loop(i):
        at = pl.ds(pl.multiple_of(i * tile, tile), tile)
        value = dot(act[at], wd[...], 1, 1)

        @pl.when(i >= 2)
        def _():
            for item in slot_copies(i - 2):
                item.wait()

        base_v[i % 2] = resid[at] + value
        mlp_v[i % 2] = value.astype(LOW)
        for item in slot_copies(i):
            item.start()

    pl.loop(0, chunks)(slot_loop)
    if heads > 1:
        sums(chunks)
        sums(0)
        pl.loop(1, chunks - per_part)(sums)
    for i in range(max(0, chunks - 2), chunks):
        for item in slot_copies(i):
            item.wait()
    down.three(mine_down)
    down.finish()
    for item in stores:
        item.wait()
    for j in range(per_part):
        for item in own_store(j):
            item.wait()
        for step in range(1, heads):
            g_copy(j, step).wait()
    for step in range(1, heads):
        for j in range(per_part):
            x_copy((step - 1) * per_part + j, step).wait_send()
    if heads > 1:
        x_copy(chunks, 1).wait_send()


def shares(hidden):
    n = hidden // 128
    first = max(n // 8, 1)
    return first * 128, (n - first) * 128


def middle(tokens, context_all, cotangent, full_qkv, full_out, full_up, full_down, scenes, heads):
    ny = scenes // ZS
    rows, d_model = tokens.shape
    rl = d_model // (2 * scenes)
    hidden, width = full_up.shape[1], d_model // heads
    tile, size_f = min(256, rows // heads), min(1024, hidden)
    part_rows = rows // heads
    per_part = part_rows // tile
    chunks = rows // tile
    first_cols = shares(hidden)[0]
    others = max(heads - 1, 1)
    sem = pltpu.SemaphoreType.DMA
    shape, vmem = jax.ShapeDtypeStruct, pltpu.VMEM
    any_space, whole = pl.BlockSpec(memory_space=pl.ANY), pl.BlockSpec(memory_space=pltpu.VMEM)
    big, wide, blocks = (rows, d_model), (rows, hidden), (ZS, ny, 2, rl, hidden)
    scratch = [vmem(big, LOW), vmem(big, LOW), vmem(big, LOW), vmem((d_model, 128), LOW), vmem((d_model, d_model), LOW),
               vmem((d_model, hidden), LOW), vmem((d_model, hidden), LOW), vmem(big, LOW), vmem(wide, LOW), vmem(wide, LOW),
               vmem(big, F32), vmem(big, F32), vmem(big, LOW), vmem((others, part_rows, d_model), LOW), vmem(blocks, LOW),
               vmem(blocks, LOW), vmem((ZS, ny, 2, rl, d_model), LOW), vmem((part_rows, d_model), LOW), vmem((2, tile, d_model), F32),
               vmem((2, tile, d_model), LOW), sem((7,)), sem((3 + 2 * per_part,)), sem((2, 2)), sem((chunks + 1,)),
               sem((chunks + 1,)), sem((per_part, others)), sem((per_part, others))]
    scratch += scatter_scratch(ny, rl, first_cols)
    return pl.pallas_call(
        partial(middle_kernel, (ny, heads, rows, d_model, width, hidden, tile, size_f, first_cols)),
        out_shape=[shape((part_rows, d_model), F32), shape(big, F32), shape(big, LOW), shape((rows, width), LOW), shape((8, d_model), F32),
                   shape((ZS, ny, 2, rl, d_model), LOW), shape(blocks, LOW), shape(blocks, LOW), shape((rl, first_cols), F32)],
        in_specs=[any_space] * 7,
        out_specs=[any_space] * 4 + [whole] + [any_space] * 3 + [whole],
        scratch_shapes=scratch,
        compiler_params=pltpu.CompilerParams(collective_id=3, has_side_effects=True, vmem_limit_bytes=63 * 2**20),
        cost_estimate=pl.CostEstimate(flops=14 * rows * d_model * hidden, bytes_accessed=50 * 2**20, transcendentals=0),
        name="middle_stage",
    )(tokens, context_all, cotangent, full_qkv, full_out, full_up, full_down)


def backward_kernel(dims, probs, queries, keys, values, grad, context, inverse, parts_out, parts_up, mlp_low,
                    grads, mine_out, mine_up, mlp_land,
                    dk_acc, dv_acc, kept, stage, landed, kv_send, kv_recv, m_send, m_recv, *scratch):
    ny, heads, rows, size, pairs, steps_q, halves = dims
    pair, part = pl.program_id(0), pl.program_id(1)
    step = pair * steps_q + part
    total = pairs * steps_q
    block = grad.shape[0]
    z, y, core = place(ny)
    width = parts_out.shape[-1]
    ends = split_cols(width, 2)
    plan = [(parts_out, ends[0])] + [(parts_up, cols) for cols in split_cols(parts_up.shape[-1], halves)] + [(parts_out, ends[1])]
    scatters = make_scatters(ny, plan, scratch)
    targets = [mine_out] + [mine_up] * halves + [mine_out]

    def kv_copy(p, i):
        return remote(stage.at[p, i], landed.at[p, i], kv_send.at[p, i], kv_recv.at[p, i], {"seq": 1 - core})

    head = lax.axis_index("head")

    def mlp_copy(i, step):
        return remote(mlp_low.at[pl.ds(i * (rows // 4), rows // 4)], mlp_land.at[step - 1, pl.ds(i * (rows // 4), rows // 4)],
                      m_send.at[i, step - 1], m_recv.at[i, step - 1], {"head": (head + step) % heads})

    @pl.when(step == 0)
    def _():
        greet_all(ny, heads)
        for i in range(4):
            for j in range(1, heads):
                mlp_copy(i, j).start()
        for item in scatters:
            item.begin()

    slots = 2 * total
    plan_at = [(0.4 + 0.5 * i, 3.4 + 2.3 * i, 5.9 + 2.3 * i) for i in range(len(scatters))]
    events = sorted((plan_at[i][j], i, j + 1) for i in range(len(scatters)) for j in range(3))

    def run(slot_in_step):
        for when, i, what in events:
            slot = min(int(when * min(1.0, slots / 16)), slots)
            if slot == slots or slot % 2 != slot_in_step:
                continue

            @pl.when(step == slot // 2)
            def _():
                if what == 1:
                    scatters[i].one()
                elif what == 2:
                    scatters[i].two()
                else:
                    scatters[i].three(targets[i])

    @pl.when(part == 0)
    def _():
        dk_acc[...] = jnp.zeros_like(dk_acc)
        dv_acc[...] = jnp.zeros_like(dv_acc)

    upper = grad[...].astype(F32)
    inner = (upper * context[...].astype(F32)).T
    upper_t = upper.T
    row = lax.broadcasted_iota(jnp.int32, upper_t.shape, 0)
    keys_t = keys[...].T
    pieces = []
    for h in range(2):
        run(h)
        over = inverse[0, h:h + 1]
        shift = jnp.sum(inner[h * size:(h + 1) * size], axis=0, keepdims=True) * over
        scaled = jnp.where(row // size == h, upper_t * over, 0.0)
        dp = dot(values[...], scaled.astype(LOW), 1, 0) - shift
        low = probs[h]
        ds = (low.astype(F32) * dp).astype(LOW)
        dv_acc[...] += dot(low, scaled.T.astype(LOW), 1, 0)
        dk_acc[...] += dot(ds, only_head(queries[...], h, size), 1, 0)
        pieces.append(dot(keys_t, ds, 1, 0)[h * size:(h + 1) * size])
    grads[pl.ds(pl.multiple_of(part * block, block), block), pl.ds(pl.multiple_of(pair * 6 * size, 2 * size), 2 * size)] = (
        (jnp.concatenate(pieces, axis=0) * size ** -0.5).T.astype(LOW))

    @pl.when(part == steps_q - 1)
    def _():
        for i, acc in enumerate((dk_acc, dv_acc)):
            stage[pair, i] = acc[rows:].astype(LOW)
            kv_copy(pair, i).start()
            kept[pair, i] = acc[:rows]

    @pl.when(step == total - 1)
    def _():
        for when, i, what in events:
            if min(int(when * min(1.0, slots / 16)), slots) == slots:
                if what == 1:
                    scatters[i].one()
                elif what == 2:
                    scatters[i].two()
                else:
                    scatters[i].three(targets[i])
        for item in scatters:
            item.finish()
        for p in range(pairs):
            for i in range(2):
                kv_copy(p, i).wait()
                grads[:, (3 * p + i + 1) * 2 * size:(3 * p + i + 2) * 2 * size] = (kept[p, i] + landed[p, i].astype(F32)).astype(LOW)
        for i in range(4):
            for j in range(1, heads):
                mlp_copy(i, j).wait()


def backward(probs, q, k, v, grad, context, inverse, parts_out, parts_up, mlp_low, scenes, heads, size):
    ny = scenes // ZS
    rows, width = q.shape
    pairs = width // (2 * size)
    block = min(512, rows)
    d_model, hidden = parts_out.shape[-1], parts_up.shape[-1]
    rl = d_model // (2 * scenes)
    others = max(heads - 1, 1)
    halves = 4
    spec = pl.BlockSpec
    q_spec = spec((block, 2 * size), lambda p, i: (i, p))
    k_spec = spec((2 * rows, 2 * size), lambda p, i: (0, p))
    any_space = spec(memory_space=pl.ANY)
    whole = spec(memory_space=pltpu.VMEM)
    shape = jax.ShapeDtypeStruct
    sem = pltpu.SemaphoreType.DMA
    pair_buf = (pairs, 2, rows, 2 * size)
    scratch = [pltpu.VMEM((2 * rows, 2 * size), F32), pltpu.VMEM((2 * rows, 2 * size), F32), pltpu.VMEM(pair_buf, F32),
               pltpu.VMEM(pair_buf, LOW), pltpu.VMEM(pair_buf, LOW), sem((pairs, 2)), sem((pairs, 2)), sem((4, others)), sem((4, others))]
    for cols in [d_model // 2] + [hidden // halves] * halves + [d_model // 2]:
        scratch += scatter_scratch(ny, rl, cols)
    return pl.pallas_call(
        partial(backward_kernel, (ny, heads, rows, size, pairs, rows // block, halves)),
        grid=(pairs, rows // block),
        out_shape=[shape((rows, 3 * width), LOW), shape((rl, d_model), F32), shape((rl, hidden), F32), shape((others, rows, d_model), LOW)],
        in_specs=[spec((2, 2 * rows, block), lambda p, i: (p, 0, i)), q_spec, k_spec, k_spec, q_spec, q_spec,
                  spec((1, 8, block), lambda p, i: (p, 0, i)), any_space, any_space, any_space],
        out_specs=[whole, whole, whole, any_space],
        scratch_shapes=scratch,
        compiler_params=pltpu.CompilerParams(collective_id=1, has_side_effects=True, vmem_limit_bytes=60 * 2**20),
        cost_estimate=pl.CostEstimate(flops=16 * rows * rows * width, bytes_accessed=50 * 2**20, transcendentals=0),
        name="backward_attention",
    )(probs, q, k, v, grad, context, inverse, parts_out, parts_up, mlp_low)


def last_kernel(dims, grads, n1, tokens, resid, full_qkv, norm_two, parts_down, down_a, out_all,
                own_grad, done_land, mine_w, mine_norm, mine_out, mine_down,
                g_v, n1_v, x_v, res_v, w_v, in_sem,
                part_one, part_low, arrived, parts_qkv, tiny_land, tiny_own, out_v, done_low, x_send, x_recv, t_send, t_recv,
                n_send, n_recv, o_send, o_recv, out_sem, mine_qkv, out_land, *scratch):
    ny, heads, rows, d_model, width, tile, split, down_cols, down_split = dims
    z, y, core = place(ny)
    head = lax.axis_index("head")
    wide = full_qkv.shape[1]
    rl = mine_qkv.shape[0]
    plan = [(parts_down, pl.ds(down_cols[0], down_split)), (parts_down, pl.ds(down_cols[0] + down_split, down_cols[1] - down_split)),
            (parts_qkv, pl.ds(0, split)), (parts_qkv, pl.ds(split, wide - split))]
    down_x, down_y, qkv_a, qkv_b = make_scatters(ny, plan, scratch)
    chunks = rows // tile
    part_rows = rows // heads
    per_part = part_rows // tile
    loads = [pltpu.make_async_copy(src, dst, in_sem.at[i]) for i, (src, dst) in enumerate((
        (grads, g_v), (full_qkv, w_v), (n1, n1_v), (tokens, x_v), (resid, res_v)))]
    for item in loads:
        item.start()
    def rows_at(step, j):
        return pl.ds(pl.multiple_of((head + heads + step) % heads * part_rows + j * tile, tile), tile)

    def x_copy(step, j):
        return remote(part_low.at[rows_at(step, j)], arrived.at[step - 1, pl.ds(j * tile, tile)], x_send.at[step - 1, j],
                      x_recv.at[step - 1, j], {"head": (head + step) % heads})

    def t_copy(step, j):
        at = pl.ds(j * tile, tile)
        return remote(done_low.at[at], done_land.at[step - 1, at], t_send.at[step - 1, j], t_recv.at[step - 1, j],
                      {"head": (head + step) % heads})

    def n_copy(step):
        return remote(tiny_own, tiny_land.at[step - 1], n_send.at[step - 1], n_recv.at[step - 1], {"head": (head + step) % heads})

    def o_copy(step):
        to = (head + step) % heads
        return remote(out_all.at[:, pl.ds(pl.multiple_of(to * width, width), width)], out_land.at[step - 1], o_send.at[step - 1],
                      o_recv.at[step - 1], {"head": to})

    def out_copy(j):
        at = pl.ds(j * tile, tile)
        return pltpu.make_async_copy(out_v.at[at], own_grad.at[at], out_sem.at[j])

    greet_all(ny, heads)
    down_x.begin()
    down_y.begin()
    for item in loads[:2]:
        item.wait()

    def partial_sum(step, j):
        at = rows_at(step, j)
        total = dot(g_v[at], w_v[:, 128:], 1, 1)
        part_one[at] = total
        part_low[at] = total.astype(LOW)

    for step in range(1, heads):
        for j in range(per_part):
            partial_sum(step, j)
            x_copy(step, j).start()
    for step in range(1, heads):
        o_copy(step).start()
    down_x.one()
    for j in range(per_part):
        partial_sum(0, j)
    for item in loads[2:]:
        item.wait()
    per_z = d_model // ZS
    for zz in range(0, ZS, 2):
        cols = n1_v[:, zz * per_z:(zz + 2) * per_z]
        value = dot(cols, g_v[...], 0, 0).astype(LOW)
        parts_qkv[zz:zz + 2, :, :, :, 128:] = value.reshape(2, ny, 2, rl, 3 * width)
    qkv_b.begin()
    gain = w_v[:, :128].astype(F32).T[0:1]

    def hat_of(at):
        x = x_v[at].astype(F32)
        centre = x - jnp.mean(x, axis=1, keepdims=True)
        spread = lax.rsqrt(jnp.mean(centre * centre, axis=1, keepdims=True) + 1e-05)
        return centre * spread, spread

    gain_sum = jnp.zeros((1, d_model), F32)
    shift_sum = jnp.zeros((1, d_model), F32)
    for i in range(chunks):
        at = pl.ds(i * tile, tile)
        hat, _ = hat_of(at)
        gain_sum += jnp.sum(part_one[at] * hat, axis=0, keepdims=True)
        shift_sum += jnp.sum(part_one[at], axis=0, keepdims=True)
        if i == chunks // 2:
            qkv_b.one()
    sums = jnp.concatenate([gain_sum, shift_sum, norm_two[0:2], jnp.zeros((124, d_model), F32)], axis=0).T.astype(LOW)
    parts_qkv[:, :, :, :, :128] = sums.reshape(ZS, ny, 2, rl, 128)
    qkv_a.begin()

    def receive(j):
        at = rows_at(0, j)
        here = pl.ds(j * tile, tile)
        total = part_one[at]
        for step in range(1, heads):
            x_copy(step, j).wait_recv()
            total += arrived[step - 1, here].astype(F32)
        hat, spread = hat_of(at)
        scaled = total * gain
        inner = scaled - jnp.mean(scaled, axis=1, keepdims=True) - hat * jnp.mean(scaled * hat, axis=1, keepdims=True)
        total = res_v[here] + inner * spread
        out_v[here] = total
        out_copy(j).start()
        done_low[here] = total.astype(LOW)
        for step in range(1, heads):
            t_copy(step, j).start()

    first = pl.ds(pl.multiple_of(head * width, width), width)

    def share(items, i, n):
        return items[len(items) * i // n:len(items) * (i + 1) // n]

    def receive_some(i):
        for j in share(range(per_part), i, 4):
            receive(j)

    def send_norms():
        tiny_own[...] = mine_qkv[:, :128]
        for step in range(1, heads):
            n_copy(step).start()

    down_x.two()
    receive_some(0)
    qkv_a.one()
    down_y.one()
    receive_some(1)
    mine_down[:, :down_a.shape[1]] = down_a[...]
    total = out_all[:, first]
    for step in range(1, heads):
        o_copy(step).wait()
        total += out_land[step - 1]
    mine_out[...] = total
    receive_some(2)
    qkv_b.two()
    down_x.three(mine_down.at[:, pl.ds(down_cols[0], down_split)], True)
    receive_some(3)
    qkv_a.two()
    qkv_b.three(mine_qkv)
    qkv_a.three(mine_qkv)
    send_norms()
    down_y.two()
    down_y.three(mine_down.at[:, pl.ds(down_cols[0] + down_split, down_cols[1] - down_split)], True)
    total = mine_qkv[:, :128]
    for step in range(1, heads):
        n_copy(step).wait()
        total += tiny_land[step - 1]
    mine_norm[...] = total.T[:8]
    for p in range(width // 128):
        for c in range(3):
            mine_w[c, :, p * 128:(p + 1) * 128] = mine_qkv[:, 128 * (3 * p + c + 1):128 * (3 * p + c + 2)]
    for item in (down_x, down_y, qkv_a, qkv_b):
        item.finish()
    for j in range(per_part):
        out_copy(j).wait()
        for step in range(1, heads):
            x_copy(step, j).wait_send()
            t_copy(step, j).wait()


def last_stage(grads, n1, tokens, resid, full_qkv, norm_two, parts_down, down_a, out_all, scenes, heads):
    ny = scenes // ZS
    rows, d_model = tokens.shape
    width, hidden = grads.shape[1] // 3, parts_down.shape[-1]
    first, third = shares(hidden)
    rl = d_model // (2 * scenes)
    wide = full_qkv.shape[1]
    part_rows = rows // heads
    tile = min(128, part_rows)
    chunks, per_part = rows // tile, part_rows // tile
    split = (wide // 128 + 1) // 2 * 128
    down_split = (third // 128 + 1) // 2 * 128
    others = max(heads - 1, 1)
    sem = pltpu.SemaphoreType.DMA
    shape, vmem = jax.ShapeDtypeStruct, pltpu.VMEM
    any_space, whole = pl.BlockSpec(memory_space=pl.ANY), pl.BlockSpec(memory_space=pltpu.VMEM)
    big, own = (rows, d_model), (part_rows, d_model)
    scratch = [vmem((rows, 3 * width), LOW), vmem(big, LOW), vmem(big, LOW), vmem(own, F32), vmem((d_model, wide), LOW), sem((5,)),
               vmem(big, F32), vmem(big, LOW), vmem((others, *own), LOW), vmem((ZS, ny, 2, rl, wide), LOW), vmem((others, rl, 128), F32),
               vmem((rl, 128), F32), vmem(own, F32), vmem(own, LOW), sem((others, per_part)),
               sem((others, per_part)), sem((others, per_part)), sem((others, per_part)), sem((others,)), sem((others,)),
               sem((others,)), sem((others,)), sem((per_part,)), vmem((rl, wide), F32), vmem((others, rl, width), F32)]
    for cols in (down_split, third - down_split, split, wide - split):
        scratch += scatter_scratch(ny, rl, cols)
    return pl.pallas_call(
        partial(last_kernel, (ny, heads, rows, d_model, width, tile, split, (first, third), down_split)),
        out_shape=[shape(own, F32), shape((others, *own), LOW), shape((3, rl, width), F32), shape((8, rl), F32), shape((rl, width), F32),
                   shape((rl, hidden), F32)],
        in_specs=[any_space] * 5 + [whole, any_space, whole, whole],
        out_specs=[any_space, any_space, whole, whole, whole, whole],
        scratch_shapes=scratch,
        compiler_params=pltpu.CompilerParams(collective_id=2, has_side_effects=True, vmem_limit_bytes=63 * 2**20),
        cost_estimate=pl.CostEstimate(flops=12 * rows * d_model * width, bytes_accessed=30 * 2**20, transcendentals=0),
        name="last_stage",
    )(grads, n1, tokens, resid, full_qkv, norm_two, parts_down, down_a, out_all)


def finish_kernel(heads, per_part, head_ref, base, mlp_land, own, land, w, out, up, down, norm,
                  output, tokens_grad, w_o, out_o, up_o, down_o, norm_o):
    part = pl.program_id(0) // per_part
    total = base[...]
    for step in range(1, heads):
        total += mlp_land[step - 1].astype(F32)
    output[...] = total

    @pl.when(part == head_ref[0])
    def _():
        tokens_grad[...] = own[...]

    @pl.when(part != head_ref[0])
    def _():
        tokens_grad[...] = land[0].astype(F32)

    for src, dst in ((w, w_o), (out, out_o), (up, up_o), (down, down_o), (norm, norm_o)):
        dst[...] = src[...]


def finish(head, base, mlp_land, own, land, w, out, up, down, norm, heads):
    rows, d_model = base.shape
    part_rows = rows // heads
    tile = min(128, part_rows)
    per_part = part_rows // tile
    rl = up.shape[0]
    last = rl // 8 - 1
    spec, shape = pl.BlockSpec, jax.ShapeDtypeStruct

    def small(a):
        if a.ndim == 3:
            return spec((3, 8, a.shape[2]), lambda i, h: (0, jnp.minimum(i, last), 0))
        return spec((8, a.shape[1]), lambda i, h: (jnp.minimum(i, last), 0))

    row = spec((tile, d_model), lambda i, h: (i, 0))
    norm_spec = spec(norm.shape, lambda i, h: (0, 0))
    smalls = [small(a) for a in (w, out, up, down)] + [norm_spec]

    def land_at(i, h):
        step = (h[0] + heads - i // per_part) % heads
        return jnp.maximum(step - 1, 0), i % per_part, 0

    return pl.pallas_call(
        partial(finish_kernel, heads, per_part),
        grid_spec=pltpu.PrefetchScalarGridSpec(
            num_scalar_prefetch=1, grid=(rows // tile,),
            in_specs=[row, spec((max(heads - 1, 1), tile, d_model), lambda i, h: (0, i, 0)),
                      spec((tile, d_model), lambda i, h: (i % per_part, 0)), spec((1, tile, d_model), land_at)] + smalls,
            out_specs=[row, row] + smalls),
        out_shape=[shape((rows, d_model), F32), shape((rows, d_model), F32)] + [shape(a.shape, F32) for a in (w, out, up, down, norm)],
        compiler_params=pltpu.CompilerParams(vmem_limit_bytes=63 * 2**20),
        name="finish",
    )(head, base, mlp_land, own, land, w, out, up, down, norm)


def on_device(n_scene, n_head, tokens, counts, w_qkv, w_out, w_up, w_down, gain_one, shift_one, gain_two, shift_two, cotangent):
    rows, d_model = tokens.shape
    width, hidden = w_qkv.shape[2], w_up.shape[1]
    size = 64
    core = lax.axis_index("seq")
    limits = jnp.stack([counts[0] - core * rows, counts[0] - (1 - core) * rows]).astype(jnp.int32)
    columns = jnp.pad(jnp.stack([gain_one, shift_one, gain_two, shift_two], axis=1), ((0, 0), (0, 124)))
    by_pair = w_qkv.reshape(3, -1, width // (2 * size), 2 * size).transpose(1, 2, 0, 3).reshape(-1, 3 * width)
    shard_qkv = jnp.concatenate([columns, by_pair], axis=1)
    n1, q, k, v, full_qkv, full_out, full_up, full_down, probs, context, context_all, inverse = forward(
        limits, shard_qkv, w_out.T, w_up, w_down.T, tokens, n_scene, n_head, size)
    grad_resid, base, mlp_low, grad_context, norm_two, grad_outproj, grad_up, grad_down, down_a = middle(
        tokens, context_all, cotangent, full_qkv, full_out, full_up, full_down, n_scene, n_head)
    grads, out_all, mine_up, mlp_land = backward(
        probs, q, k, v, grad_context, context, inverse, grad_outproj, grad_up, mlp_low, n_scene, n_head, size)
    own, land, mine_qkv, norms, mine_out, mine_down = last_stage(
        grads, n1, tokens, grad_resid, full_qkv, norm_two, grad_down, down_a, out_all, n_scene, n_head)
    head = lax.axis_index("head").reshape(1).astype(jnp.int32)
    output, tokens_grad, mine_qkv, mine_out, mine_up, mine_down, norms = finish(
        head, base, mlp_land, own, land, mine_qkv, mine_out, mine_up, mine_down, norms, n_head)
    return (output, tokens_grad, mine_qkv, mine_out.T, mine_up, mine_down.T, norms[0], norms[1], norms[2], norms[3])


def solution(mesh):
    rows, both = ("scene", "seq"), P(("scene", "seq"))
    weights = (P(None, rows, "head"), P("head", rows), P(rows, "head"), P("head", rows), both, both, both, both)
    return jax.shard_map(
        partial(on_device, mesh.shape["scene"], mesh.shape["head"]), mesh=mesh,
        in_specs=(P(rows, None), P("scene"), *weights, P(rows, None)),
        out_specs=(P(rows, None), P(rows, None), *weights),
        check_vma=False,
    )
```

```python
from functools import partial

import jax
import jax.numpy as jnp
from jax import lax
from jax.experimental import pallas as pl
from jax.experimental.pallas import tpu as pltpu
from jax.sharding import PartitionSpec as P

MESH = pl.DeviceIdType.MESH
ZS = 4


def place(ny):
    scene = lax.axis_index("scene")
    return scene // ny, scene % ny, lax.axis_index("seq")


def remote(src, dst, send_sem, recv_sem, device):
    return pltpu.make_async_remote_copy(
        src_ref=src, dst_ref=dst, send_sem=send_sem, recv_sem=recv_sem,
        device_id=device, device_id_type=MESH,
    )


F32 = jnp.float32
LOW = jnp.bfloat16


def dot(a, b, ca, cb):
    return lax.dot_general(a, b, (((ca,), (cb,)), ((), ())), preferred_element_type=F32)


def only_head(x, h, size):
    lane = lax.broadcasted_iota(jnp.int32, x.shape, 1)
    return jnp.where(lane // size == h, x, jnp.zeros_like(x))


class Gather:
    def __init__(self, ny, source, full, cols, sems):
        self.ny, self.source, self.full, self.cols = ny, source, full, cols
        self.rsend, self.rrecv, self.lsend, self.lrecv, self.ysend, self.yrecv, self.csend, self.crecv = sems
        self.z, self.y, self.core = place(ny)

    def at(self, zz, yy):
        return self.full.at[zz, yy, self.core, :, self.cols]

    def right(self, k):
        src = self.source() if k == 0 else self.at(self.z - k, self.y)
        dst = self.at(self.z - k, self.y)
        return remote(src, dst, self.rsend.at[k], self.rrecv.at[k], {"scene": (self.z + 1) * self.ny + self.y})

    def left(self, k):
        src = self.source() if k == 0 else self.at(self.z + k, self.y)
        dst = self.at(self.z + k, self.y)
        return remote(src, dst, self.lsend.at[k], self.lrecv.at[k], {"scene": (self.z - 1) * self.ny + self.y})

    def across(self, zz, step, own=False):
        src = self.source() if own else self.at(zz, self.y)
        peer = self.z * self.ny + (self.y + step) % self.ny
        return remote(src, self.at(zz, self.y), self.ysend.at[step - 1], self.yrecv.at[step - 1], {"scene": peer})

    def arrival(self, zz, step):
        yy = (self.y + self.ny - step) % self.ny
        return remote(self.at(zz, yy), self.at(zz, yy), self.ysend.at[step - 1], self.yrecv.at[step - 1],
                      {"scene": self.z * self.ny + yy})

    def twin(self, zz, step, own=False):
        src = self.source() if own else self.at(zz, (self.y + self.ny - step) % self.ny)
        dst = self.at(zz, (self.y + self.ny - step) % self.ny)
        return remote(src, dst, self.csend.at[0], self.crecv.at[0], {"seq": 1 - self.core})

    def column(self, step):
        yy = (self.y + self.ny - step) % self.ny
        all_z = self.full.at[:, yy, self.core, :, self.cols]
        return remote(all_z, all_z, self.ysend.at[step - 1], self.yrecv.at[step - 1], {"scene": self.z * self.ny + yy})

    def twins(self):
        mine, theirs = [self.full.at[:, :, c, :, self.cols] for c in (self.core, 1 - self.core)]
        return [remote(item, item, self.csend.at[0], self.crecv.at[0], {"seq": 1 - self.core}) for item in (mine, theirs)]

    def begin(self):
        @pl.when(self.z < ZS - 1)
        def _():
            self.right(0).start()

        @pl.when(self.z > 0)
        def _():
            self.left(0).start()

        for step in range(1, self.ny):
            self.across(self.z, step, True).start()
        self.twin(self.z, 0, True).start()

    def hop(self, k):
        @pl.when(self.z >= k)
        def _():
            self.right(k - 1).wait_recv()
            if k < ZS - 1:
                @pl.when(self.z < ZS - 1)
                def _():
                    self.right(k).start()
            for step in range(1, self.ny):
                self.across(self.z - k, step).start()
            self.twin(self.z - k, 0).start()

        @pl.when(self.z + k < ZS)
        def _():
            self.left(k - 1).wait_recv()
            if k < ZS - 1:
                @pl.when(self.z > 0)
                def _():
                    self.left(k).start()
            for step in range(1, self.ny):
                self.across(self.z + k, step).start()
            self.twin(self.z + k, 0).start()

    def spread(self):
        for step in range(1, self.ny):
            self.column(step).wait_recv()
            for zz in range(ZS):
                self.twin(zz, step).start()

    def finish(self):
        for k in range(ZS - 1):
            @pl.when((self.z < ZS - 1) & (self.z >= k))
            def _():
                self.right(k).wait_send()

            @pl.when((self.z > 0) & (self.z + k < ZS))
            def _():
                self.left(k).wait_send()
        for step in range(1, self.ny):
            self.column(step).wait_send()
        mine, theirs = self.twins()
        mine.wait_send()
        theirs.wait_recv()


class PairGather(Gather):
    def row(self, zz):
        return self.full.at[zz, :, self.core, :, self.cols]

    def right(self, k):
        return remote(self.row(self.z - k), self.row(self.z - k), self.rsend.at[k], self.rrecv.at[k],
                      {"scene": (self.z + 1) * self.ny + self.y})

    def left(self, k):
        return remote(self.row(self.z + k), self.row(self.z + k), self.lsend.at[k], self.lrecv.at[k],
                      {"scene": (self.z - 1) * self.ny + self.y})

    def twin(self, zz):
        return remote(self.row(zz), self.row(zz), self.csend.at[0], self.crecv.at[0], {"seq": 1 - self.core})

    def begin(self):
        for step in range(1, self.ny):
            self.across(self.z, step, True).start()

    def pair(self):
        for step in range(1, self.ny):
            self.arrival(self.z, step).wait_recv()

        @pl.when(self.z < ZS - 1)
        def _():
            self.right(0).start()

        @pl.when(self.z > 0)
        def _():
            self.left(0).start()

        self.twin(self.z).start()

    def hop(self, k):
        @pl.when(self.z >= k)
        def _():
            self.right(k - 1).wait_recv()
            if k < ZS - 1:
                @pl.when(self.z < ZS - 1)
                def _():
                    self.right(k).start()
            self.twin(self.z - k).start()

        @pl.when(self.z + k < ZS)
        def _():
            self.left(k - 1).wait_recv()
            if k < ZS - 1:
                @pl.when(self.z > 0)
                def _():
                    self.left(k).start()
            self.twin(self.z + k).start()

    def finish(self):
        for k in range(ZS - 1):
            @pl.when((self.z < ZS - 1) & (self.z >= k))
            def _():
                self.right(k).wait_send()

            @pl.when((self.z > 0) & (self.z + k < ZS))
            def _():
                self.left(k).wait_send()
        for step in range(1, self.ny):
            self.across(self.z, step).wait_send()
        mine, theirs = self.twins()
        mine.wait_send()
        theirs.wait_recv()


def gather_sems(ny):
    sem = pltpu.SemaphoreType.DMA
    return [sem((ZS - 1,)), sem((ZS - 1,)), sem((ZS - 1,)), sem((ZS - 1,)), sem((max(ny - 1, 1),)), sem((max(ny - 1, 1),)),
            sem((1,)), sem((1,))]


def greet_all(ny, heads):
    z, y, core = place(ny)
    head = lax.axis_index("head")
    barrier = pltpu.get_barrier_semaphore()

    def signal(device):
        pl.semaphore_signal(barrier, 1, device_id=device, device_id_type=MESH)

    for step in range(1, ZS):
        signal({"scene": (z + step) % ZS * ny + y})
    for step in range(1, ny):
        signal({"scene": z * ny + (y + step) % ny})
    for step in range(1, heads):
        signal({"head": (head + step) % heads})
    signal({"seq": 1 - core})
    pl.semaphore_wait(barrier, ZS + ny - 1 + heads - 1)


def split_cols(total, parts):
    size = total // parts
    return [pl.ds(i * size, size) for i in range(parts)]


def forward_kernel(dims, counts, gain_one, shift_one, gain_two, shift_two, w_qkv, shard_out, shard_up, shard_down, tokens,
                   n1_out, q_out, k_out, v_out, full_qkv, full_out, full_up, full_down, probs, context, context_all, inverse,
                   w0, hat, n1, q_s, k_s, v_s, bias, ctx_s, scores, tops, local_sem, kv_send, kv_recv, xw_send, xw_recv, xt_send, xt_recv, xc_send, xc_recv, *sems):
    ny, heads, rows, width, size, block, pairs, steps_q, halves = dims
    pair, part = pl.program_id(0), pl.program_id(1)
    step = pair * steps_q + part
    z, y, core = place(ny)
    head = lax.axis_index("head")
    d_model = tokens.shape[1]
    per = 8
    own_cols = pl.ds(pl.multiple_of(head * width, width), width)

    def of(i):
        return sems[i * per:(i + 1) * per]

    group = 6 * size
    edges = [0] + [128 + (p + 1) * group for p in range(pairs)]
    firsts = []
    for p in range(pairs):
        cols = pl.ds(edges[p], edges[p + 1] - edges[p])
        firsts.append(Gather(ny, partial(lambda c: w0.at[z, y, core, :, c], cols), w0, cols, of(2 + 2 * halves + p)))
    outer = Gather(ny, lambda: shard_out, full_out, own_cols, of(1))
    thick = []
    for n, (shard, full) in enumerate(((shard_up, full_up), (shard_down, full_down))):
        for i, cols in enumerate(split_cols(full_up.shape[-1], halves)):
            kind = PairGather if n == 1 and i == halves - 1 else Gather
            thick.append(kind(ny, partial(lambda s, c: s.at[:, c], shard, cols), full, cols, of(2 + n * halves + i)))
    up_a, up_b, down_a, down_b = thick

    def local(src, dst, i):
        return pltpu.make_async_copy(src, dst, local_sem.at[i])

    def cols_of(step):
        return pl.ds(pl.multiple_of((head + heads - step) % heads * width, width), width)

    def out_copy(step):
        mine = full_out.at[:, :, core, :, own_cols]
        return remote(mine, mine, xw_send.at[step - 1], xw_recv.at[step - 1], {"head": (head + step) % heads})

    def out_twin(step):
        other = full_out.at[:, :, core, :, cols_of(step)]
        return remote(other, other, xt_send.at[step - 1], xt_recv.at[step - 1], {"seq": 1 - core})

    def kv_copy(p, i):
        src = (k_s, v_s)[i]
        cols = pl.ds(p * 2 * size, 2 * size)
        return remote(src.at[pl.ds(0, rows), cols], src.at[pl.ds(rows, rows), cols], kv_send.at[p, i], kv_recv.at[p, i],
                      {"seq": 1 - core})

    def project(p):
        tile = min(256, rows)

        @pl.loop(0, rows // tile)
        def _(i):
            at = pl.ds(pl.multiple_of(i * tile, tile), tile)
            w = w0[:, :, :, :, 128 + p * group:128 + (p + 1) * group].reshape(d_model, group)
            value = dot(n1[at], w, 1, 0).astype(LOW)
            cols = pl.ds(p * 2 * size, 2 * size)
            q_s[at, cols] = value[:, :2 * size] * LOW(size ** -0.5)
            k_s[at, cols] = value[:, 2 * size:4 * size]
            v_s[at, cols] = value[:, 4 * size:]

        for i in range(2):
            kv_copy(p, i).start()

    def ctx_copy(p, step):
        cols = pl.ds(pl.multiple_of(p * 2 * size, 2 * size), 2 * size)
        wide = pl.ds(pl.multiple_of(head * width + p * 2 * size, 2 * size), 2 * size)
        return remote(ctx_s.at[:, cols], context_all.at[:, wide], xc_send.at[p, step - 1], xc_recv.at[p, step - 1],
                      {"head": (head + step) % heads})

    own_blocks = [(shard_out, full_out.at[z, y, core, :, own_cols], 1),
                  (shard_up, full_up.at[z, y, core], 2), (shard_down, full_down.at[z, y, core], 3)]
    results = [(w0, full_qkv, 4), (n1, n1_out, 5), (q_s, q_out, 6), (k_s, k_out, 7), (v_s, v_out, 8)]
    ctx_local = (ctx_s, context_all.at[:, own_cols], 9)

    @pl.when(step == 0)
    def _():
        for item in own_blocks:
            local(*item).start()
        greet_all(ny, heads)
        columns = jnp.concatenate([a[...].astype(F32) for a in (gain_one, shift_one, gain_two, shift_two)]
                                  + [jnp.zeros((124, gain_one.shape[1]), F32)], axis=0)
        w0[z, y, core, :, :128] = columns.T.astype(LOW)
        for p in range(pairs):
            for c in range(3):
                w0[z, y, core, :, 128 * (3 * p + c + 1):128 * (3 * p + c + 2)] = w_qkv[c, :, 128 * p:128 * (p + 1)]
            if p < 2:
                firsts[p].begin()
        tile = min(128, rows)

        @pl.loop(0, rows // tile)
        def _(i):
            at = pl.ds(pl.multiple_of(i * tile, tile), tile)
            x = tokens[at].astype(F32)
            centre = x - jnp.mean(x, axis=1, keepdims=True)
            spread = jnp.mean(centre * centre, axis=1, keepdims=True)
            hat[at] = centre * lax.rsqrt(spread + 1e-05)

        low_rows = lax.broadcasted_iota(jnp.int32, bias.shape, 0)
        lane = lax.broadcasted_iota(jnp.int32, bias.shape, 1)
        limit = jnp.where(low_rows < rows, counts[0] - core * rows, counts[0] - (1 - core) * rows + rows)
        bias[...] = jnp.where((low_rows >= limit) & (lane == 0), -1e30, 0.0).astype(LOW)
        after = [
            (0, lambda g: g.hop(1)), (2, lambda g: g.begin()), (0, lambda g: g.hop(2)), (1, lambda g: g.hop(1)), (0, lambda g: g.hop(3)),
            (3, lambda g: g.begin()), (1, lambda g: g.hop(2)), (0, lambda g: g.spread()), (1, lambda g: g.hop(3)),
            (2, lambda g: g.hop(1)), (1, lambda g: g.spread()), (2, lambda g: g.hop(2))]
        for p, act in after[:9]:
            if p < pairs:
                act(firsts[p])
        firsts[0].finish()
        for item in own_blocks:
            local(*item).wait()
        norms = w0[:, :, :, :, :128].reshape(d_model, 128).astype(F32).T
        gain, shift = norms[0:1], norms[1:2]
        tile = min(256, rows)

        @pl.loop(0, rows // tile)
        def _(i):
            at = pl.ds(pl.multiple_of(i * tile, tile), tile)
            n1[at] = (hat[at] * gain + shift).astype(LOW)

        local(*results[1]).start()
        project(0)
        for p, act in after[9:]:
            if p < pairs:
                act(firsts[p])

    total = pairs * steps_q
    per_slot = 2
    in_step = 4 * rows // min(256, rows) // per_slot
    slots = in_step * total

    def send_out():
        for i in range(1, heads):
            out_copy(i).start()

    def pass_out():
        for i in range(1, heads):
            out_copy(i).wait_recv()
            out_twin(i).start()

    def on_pair(p, what, *given):
        if p < pairs:
            getattr(firsts[p], what)(*given)

    events = [
        (0.1, lambda: on_pair(2, "hop", 3)), (0.3, lambda: on_pair(3, "hop", 1)), (0.4, outer.begin),
        (1, lambda: on_pair(3, "hop", 2)), (1.2, lambda: on_pair(2, "spread")), (1.4, up_a.begin),
        (2, lambda: on_pair(3, "hop", 3)), (2.6, lambda: outer.hop(1)), (3.2, lambda: outer.hop(2)), (3.2, up_b.begin),
        (3.8, lambda: on_pair(3, "spread")), (3.9, lambda: outer.hop(3)), (5.2, lambda: up_a.hop(1)), (6, outer.spread), (6.1, send_out),
        (6.5, lambda: up_a.hop(2)), (7, down_a.begin), (7.2, down_b.begin),
        (7.8, lambda: up_a.hop(3)), (9.2, lambda: up_b.hop(1)), (10.5, lambda: up_b.hop(2)), (10.6, pass_out), (10.8, down_b.pair),
        (11.8, lambda: up_b.hop(3)), (12, up_a.spread), (13.2, lambda: down_a.hop(1)), (14.5, lambda: down_a.hop(2)),
        (15.8, lambda: down_a.hop(3)), (16, up_b.spread), (16, lambda: down_b.hop(1)),
        (16, lambda: down_b.hop(2)), (16, down_a.spread), (16, lambda: down_b.hop(3))]

    def run(slot_in_step):
        for when, act in events:
            slot = min(int(when * slots / 16), slots - 1)
            if when < 16 and slot % in_step == slot_in_step:
                pl.when(step == slot // in_step)(act)

    for p in range(pairs):
        @pl.when(step == p * steps_q)
        def _():
            if p == 0:
                for i in range(2):
                    kv_copy(0, i).wait()
            if p + 1 < pairs:
                firsts[p + 1].finish()
                project(p + 1)
            else:
                for item in (results[0], *results[2:]):
                    local(*item).start()

        if p + 1 < pairs:
            @pl.when(step == (p + 1) * steps_q - 1)
            def _():
                for i in range(2):
                    kv_copy(p + 1, i).wait()

    width2, chunk = 2 * size, min(256, rows)
    n_chunks = 2 * rows // chunk
    ones = (lax.broadcasted_iota(jnp.int32, (block, bias.shape[1]), 1) == 0).astype(LOW)

    def asked(at, h):
        rows_at = pl.ds(pl.multiple_of(at % steps_q * block, block), block)
        cols_at = pl.ds(pl.multiple_of(at // steps_q * width2, width2), width2)
        return jnp.concatenate([only_head(q_s[rows_at, cols_at], h, size), ones], axis=1)

    def score(at, query, slot, c, top):
        cols_at = pl.ds(pl.multiple_of(at // steps_q * width2, width2), width2)
        keys_at = pl.ds(c * chunk, chunk)
        value = dot(jnp.concatenate([k_s[keys_at, cols_at], bias[keys_at]], axis=1), query, 1, 1)
        scores[slot, keys_at] = value
        return jnp.maximum(top, jnp.max(value.reshape(chunk // 8, 8, block), axis=0))

    def weigh(h, c, top, total_e):
        keys_at = pl.ds(c * chunk, chunk)
        expo = jnp.exp(scores[h, keys_at] - top)
        probs[h, keys_at] = expo.astype(LOW)
        return total_e + jnp.sum(expo.reshape(chunk // 8, 8, block), axis=0)

    lowest = jnp.full((8, block), -3e38, F32)

    @pl.when(step == 0)
    def _():
        top, query = lowest, asked(0, 0)
        for c in range(n_chunks):
            top = score(0, query, 0, c, top)
        tops[...] = top

    cols = pl.ds(pl.multiple_of(pair * width2, width2), width2)
    following = jnp.minimum(step + 1, total - 1)
    values_t = v_s[:, cols].T
    pieces = []
    for h in range(2):
        top = jnp.max(tops[...], axis=0, keepdims=True)
        total_e, next_top = jnp.zeros((8, block), F32), lowest
        ahead = (step, 1) if h == 0 else (following, 0)
        query = asked(*ahead)
        for c in range(n_chunks):
            if c % per_slot == 0:
                run(h * (n_chunks // per_slot) + c // per_slot)
            next_top = score(ahead[0], query, 1 - h, c, next_top)
            total_e = weigh(h, c, top, total_e)
        tops[...] = next_top
        over = 1.0 / jnp.sum(total_e, axis=0, keepdims=True)
        pieces.append(dot(values_t, probs[h], 1, 0)[h * size:(h + 1) * size] * over)
        inverse[0, h:h + 1] = over
    here = jnp.concatenate(pieces, axis=0).T.astype(LOW)
    context[...] = here
    ctx_s[pl.ds(pl.multiple_of(part * block, block), block), cols] = here

    @pl.when(part == steps_q - 1)
    def _():
        for i in range(1, heads):
            ctx_copy(pair, i).start()

    @pl.when(step == total - 1)
    def _():
        local(*ctx_local).start()
        for when, act in events:
            if when >= 16:
                act()
        for gather in (outer, *thick):
            gather.finish()
        for item in results:
            local(*item).wait()
        local(*ctx_local).wait()
        for i in range(1, heads):
            out_copy(i).wait_send()
            out_twin(i).wait()
            for p in range(pairs):
                ctx_copy(p, i).wait()


def forward(counts, norms, w_qkv, shard_out, shard_up, shard_down, tokens, scenes, heads, size):
    ny = scenes // ZS
    rows, d_model = tokens.shape
    rl, width = shard_out.shape
    hidden = shard_up.shape[1]
    pairs = width // (2 * size)
    block = min(512, rows)
    steps_q = rows // block
    halves = 2
    sem = pltpu.SemaphoreType.DMA
    any_space = pl.BlockSpec(memory_space=pl.ANY)
    shape = jax.ShapeDtypeStruct
    wide = 128 + 3 * width
    outs = [shape((rows, d_model), LOW), shape((rows, width), LOW), shape((2 * rows, width), LOW), shape((2 * rows, width), LOW),
            shape((ZS, ny, 2, rl, wide), LOW), shape((ZS, ny, 2, rl, d_model), LOW), shape((ZS, ny, 2, rl, hidden), LOW),
            shape((ZS, ny, 2, rl, hidden), LOW), shape((2 * pairs, 2 * rows, rows), LOW), shape((rows, width), LOW),
            shape((rows, d_model), LOW), shape((pairs, 8, rows), F32)]
    out_specs = [any_space] * 8 + [
        pl.BlockSpec((2, 2 * rows, block), lambda p, i: (p, 0, i)), pl.BlockSpec((block, 2 * size), lambda p, i: (i, p)),
        any_space, pl.BlockSpec((1, 8, block), lambda p, i: (p, 0, i))]
    scratch = [pltpu.VMEM((ZS, ny, 2, rl, wide), LOW), pltpu.VMEM((rows, d_model), F32), pltpu.VMEM((rows, d_model), LOW),
               pltpu.VMEM((rows, width), LOW), pltpu.VMEM((2 * rows, width), LOW), pltpu.VMEM((2 * rows, width), LOW),
               pltpu.VMEM((2 * rows, 128), LOW), pltpu.VMEM((rows, width), LOW),
               pltpu.VMEM((2, 2 * rows, block), F32), pltpu.VMEM((8, block), F32), sem((10,)), sem((pairs, 2)), sem((pairs, 2)),
               sem((max(heads - 1, 1),)), sem((max(heads - 1, 1),)), sem((max(heads - 1, 1),)), sem((max(heads - 1, 1),)), sem((pairs, max(heads - 1, 1))), sem((pairs, max(heads - 1, 1)))]
    for _ in range(2 + 2 * halves + pairs):
        scratch += gather_sems(ny)
    dims = (ny, heads, rows, width, size, block, pairs, steps_q, halves)
    flops = 2 * rows * d_model * 3 * width + 8 * rows * rows * width
    results = pl.pallas_call(
        partial(forward_kernel, dims),
        grid=(pairs, steps_q),
        out_shape=outs,
        in_specs=[pl.BlockSpec(memory_space=pltpu.SMEM)] + [pl.BlockSpec(memory_space=pltpu.VMEM)] * 8 + [pl.BlockSpec(memory_space=pltpu.VMEM)],
        out_specs=out_specs,
        scratch_shapes=scratch,
        compiler_params=pltpu.CompilerParams(collective_id=0, has_side_effects=True, vmem_limit_bytes=60 * 2**20),
        cost_estimate=pl.CostEstimate(flops=flops, bytes_accessed=60 * 2**20, transcendentals=0),
        name="forward_attention",
    )(counts, *[a.reshape(1, rl) for a in norms], w_qkv, shard_out, shard_up, shard_down, tokens)
    n1, q, k, v, full_qkv, full_out, full_up, full_down, probs, context, context_all, inverse = results
    flat = lambda a: a.reshape(d_model, a.shape[-1])
    return n1, q, k, v, flat(full_qkv), flat(full_out), flat(full_up), flat(full_down), probs, context, context_all, inverse


class Scatter:
    def __init__(self, ny, parts, cols, bufs, sems):
        self.ny, self.parts, self.cols = ny, parts, cols
        self.own, self.from_core, self.from_y, self.sum_two, self.from_z = bufs
        self.load_sem, self.csend, self.crecv, self.ysend, self.yrecv, self.zsend, self.zrecv = sems
        self.z, self.y, self.core = place(ny)

    def load(self):
        return pltpu.make_async_copy(self.parts.at[:, :, self.core, :, self.cols], self.own, self.load_sem.at[0])

    def to_core(self):
        return remote(self.parts.at[:, :, 1 - self.core, :, self.cols], self.from_core, self.csend.at[0], self.crecv.at[0],
                      {"seq": 1 - self.core})

    def to_y(self, step):
        yy = (self.y + step) % self.ny
        return remote(self.own.at[:, yy], self.from_y.at[step - 1], self.ysend.at[step - 1], self.yrecv.at[step - 1],
                      {"scene": self.z * self.ny + yy})

    def to_z(self, step):
        zz = (self.z + step) % ZS
        return remote(self.sum_two.at[zz], self.from_z.at[step - 1], self.zsend.at[step - 1], self.zrecv.at[step - 1],
                      {"scene": zz * self.ny + self.y})

    def begin(self):
        self.load().start()
        self.to_core().start()

    def one(self):
        self.load().wait()
        self.to_core().wait_recv()
        for zz in range(ZS):
            for yy in range(self.ny):
                self.own[zz, yy] = (self.own[zz, yy].astype(F32) + self.from_core[zz, yy].astype(F32)).astype(LOW)
        for step in range(1, self.ny):
            self.to_y(step).start()

    def two(self):
        for step in range(1, self.ny):
            self.to_y(step).wait_recv()
        for zz in range(ZS):
            total = self.own[zz, self.y].astype(F32)
            for step in range(1, self.ny):
                total += self.from_y[step - 1, zz].astype(F32)
            self.sum_two[zz] = total.astype(LOW)
        for step in range(1, ZS):
            self.to_z(step).start()

    def three(self, out, alone=False):
        for step in range(1, ZS):
            self.to_z(step).wait_recv()
        total = self.sum_two[self.z].astype(F32)
        for step in range(1, ZS):
            total += self.from_z[step - 1].astype(F32)
        if alone:
            out[...] = total
        else:
            out[:, self.cols] = total

    def finish(self):
        self.to_core().wait_send()
        for step in range(1, self.ny):
            self.to_y(step).wait_send()
        for step in range(1, ZS):
            self.to_z(step).wait_send()


SCATTER_BUFS, SCATTER_SEMS = 5, 7


def scatter_scratch(ny, rl, cols):
    sem = pltpu.SemaphoreType.DMA
    other = max(ny - 1, 1)
    return [pltpu.VMEM((ZS, ny, rl, cols), LOW), pltpu.VMEM((ZS, ny, rl, cols), LOW), pltpu.VMEM((other, ZS, rl, cols), LOW),
            pltpu.VMEM((ZS, rl, cols), LOW), pltpu.VMEM((ZS - 1, rl, cols), LOW),
            sem((1,)), sem((1,)), sem((1,)), sem((other,)), sem((other,)), sem((ZS - 1,)), sem((ZS - 1,))]


def make_scatters(ny, plan, scratch):
    n = SCATTER_BUFS + SCATTER_SEMS
    result = []
    for i, (parts, cols) in enumerate(plan):
        mine = scratch[i * n:(i + 1) * n]
        result.append(Scatter(ny, parts, cols, mine[:SCATTER_BUFS], mine[SCATTER_BUFS:]))
    return result

def middle_kernel(dims, tokens, context_all, cotangent, full_qkv, full_out, full_up, full_down,
                  resid_grad, base, mlp_low, grad_context, norm_two, parts_out, parts_up, parts_down, mine_down,
                  x_v, ctx_v, cot_v, norm_v, wo, wu, wd, n2, act, gu, resid, part, low, arrived, up_v, down_v, out_v, gctx_v,
                  base_v, mlp_v, in_sem, out_sem, slot_sem, x_send, x_recv, g_send, g_recv, *scratch):
    ny, heads, rows, d_model, width, hidden, tile, size_f, first_cols = dims
    head = lax.axis_index("head")
    chunks = rows // tile
    part_rows = rows // heads
    per_part = part_rows // tile
    (down,) = make_scatters(ny, [(down_v, pl.ds(0, first_cols))], scratch)
    own_rows = pl.ds(pl.multiple_of(head * part_rows, part_rows), part_rows)

    def load(src, dst, i):
        return pltpu.make_async_copy(src, dst, in_sem.at[i])

    loads = [load(context_all, ctx_v, 0), load(full_out, wo, 1), load(tokens, x_v, 2), load(full_qkv.at[:, pl.ds(0, 128)], norm_v, 3),
             load(full_up, wu, 4), load(cotangent, cot_v, 5), load(full_down, wd, 6)]
    for item in loads:
        item.start()
    half = tile // 2

    def place_of(i):
        whole_tile = not isinstance(i, int)
        number = 0 if not whole_tile and i == chunks else i
        step = number // per_part + 1
        within = number % per_part * tile
        size = tile if whole_tile or 0 < i < chunks else half
        within = within + (half if not whole_tile and i == 0 else 0)
        return step, within, size

    def rows_of(i):
        step, within, size = place_of(i)
        return pl.ds(pl.multiple_of((head + step) % heads * part_rows + within, half), size)

    def x_copy(i, step):
        _, within, size = place_of(i)
        return remote(low.at[rows_of(i)], arrived.at[step - 1, pl.ds(within, size)], x_send.at[i], x_recv.at[i],
                      {"head": (head + step) % heads})

    def g_copy(j, step):
        to = (head + step) % heads
        at = pl.ds(j * tile, tile)
        there = pl.ds(pl.multiple_of(head * part_rows + j * tile, tile), tile)
        return remote(gctx_v.at[at, pl.ds(pl.multiple_of(to * width, width), width)], grad_context.at[there],
                      g_send.at[j, step - 1], g_recv.at[j, step - 1], {"head": to})

    greet_all(ny, heads)
    for item in loads:
        item.wait()
    norms = norm_v[...].astype(F32).T
    gain, shift = norms[2:3], norms[3:4]

    def hat_of(value):
        centre = value - jnp.mean(value, axis=1, keepdims=True)
        spread = lax.rsqrt(jnp.mean(centre * centre, axis=1, keepdims=True) + 1e-05)
        return centre * spread, spread

    norm_two[...] = jnp.zeros_like(norm_two)

    def forward_and_back(i):
        at = rows_of(i)
        value = x_v[at].astype(F32) + dot(ctx_v[at], wo[...], 1, 1)
        resid[at] = value
        n2[at] = (hat_of(value)[0] * gain + shift).astype(LOW)
        for f in range(hidden // size_f):
            cols = slice(f * size_f, (f + 1) * size_f)
            u = dot(n2[at], wu[:, cols], 1, 0)
            ga = dot(cot_v[at], wd[:, cols], 1, 0)
            phi = 0.5 + 0.5 * lax.erf(u * (0.5 ** 0.5))
            act[at, cols] = (u * phi).astype(LOW)
            gu[at, cols] = (ga * (phi + u * (jnp.exp(u * u * -0.5) * 0.3989422804014327))).astype(LOW)
        total = dot(gu[at], wu[...], 1, 1)
        part[at] = total
        low[at] = total.astype(LOW)

    def sums(i):
        at = rows_of(i)
        total = part[at]
        hat, _ = hat_of(resid[at])
        norm_two[0:1] += jnp.sum(total * hat, axis=0, keepdims=True)
        norm_two[1:2] += jnp.sum(total, axis=0, keepdims=True)

    if heads > 1:
        forward_and_back(chunks)
        x_copy(chunks, 1).start()
        forward_and_back(0)
        x_copy(0, 1).start()
        for step in range(1, heads):
            first = (step - 1) * per_part

            @pl.loop(max(first, 1), first + per_part)
            def _(i):
                forward_and_back(i)
                x_copy(i, step).start()

    else:
        forward_and_back(chunks)
        forward_and_back(0)

    @pl.loop(max(chunks - per_part, 1), chunks)
    def _(i):
        forward_and_back(i)

    def weight_grad(src, other, dst, count):
        per_z = d_model // ZS
        for f in range(count // size_f):
            cols = slice(f * size_f, (f + 1) * size_f)

            @pl.loop(0, ZS // 2)
            def _(j):
                at = pl.ds(pl.multiple_of(j * 2 * per_z, 2 * per_z), 2 * per_z)
                value = dot(src[:, at], other[:, cols], 0, 0).astype(LOW)
                dst[pl.ds(2 * j, 2), :, :, :, cols] = value.reshape(2, *dst.shape[1:4], size_f)

    weight_grad(cot_v, act, down_v, hidden)
    down.begin()

    def own_store(j):
        at = pl.ds(j * tile, tile)
        there = pl.ds(pl.multiple_of(head * part_rows + j * tile, tile), tile)
        return (pltpu.make_async_copy(part.at[there], resid_grad.at[at], out_sem.at[3 + 2 * j]),
                pltpu.make_async_copy(gctx_v.at[at, pl.ds(pl.multiple_of(head * width, width), width)], grad_context.at[there],
                                      out_sem.at[4 + 2 * j]))

    for j in range(per_part):
        at = pl.ds(pl.multiple_of(head * part_rows + j * tile, tile), tile)
        total = part[at]
        for step in range(1, heads):
            i = (step - 1) * per_part + j
            x_copy(i, step).wait_recv()
            if i == 0:
                x_copy(chunks, step).wait_recv()
            total += arrived[step - 1, j * tile:(j + 1) * tile].astype(F32)
        hat, spread = hat_of(resid[at])
        own_part = part[at]
        norm_two[0:1] += jnp.sum(own_part * hat, axis=0, keepdims=True)
        norm_two[1:2] += jnp.sum(own_part, axis=0, keepdims=True)
        scaled = total * gain
        inner = scaled - jnp.mean(scaled, axis=1, keepdims=True) - hat * jnp.mean(scaled * hat, axis=1, keepdims=True)
        total = cot_v[at].astype(F32) + inner * spread
        part[at] = total
        rounded = total.astype(LOW)
        low[at] = rounded
        gctx_v[j * tile:(j + 1) * tile] = dot(rounded, wo[...], 1, 0).astype(LOW)
        for step in range(1, heads):
            g_copy(j, step).start()
        for item in own_store(j):
            item.start()
    down.one()
    weight_grad(n2, gu, up_v, hidden)
    stores = [pltpu.make_async_copy(up_v, parts_up, out_sem.at[0]), pltpu.make_async_copy(down_v, parts_down, out_sem.at[1]),
              pltpu.make_async_copy(out_v, parts_out, out_sem.at[2])]
    for item in stores[:2]:
        item.start()
    down.two()
    weight_grad(low.at[own_rows], ctx_v.at[own_rows], out_v, d_model)
    stores[2].start()

    def slot_copies(i):
        at = pl.ds(pl.multiple_of(i * tile, tile), tile)
        slot = i % 2
        return (pltpu.make_async_copy(base_v.at[slot], base.at[at], slot_sem.at[0, slot]),
                pltpu.make_async_copy(mlp_v.at[slot], mlp_low.at[at], slot_sem.at[1, slot]))

    def slot_loop(i):
        at = pl.ds(pl.multiple_of(i * tile, tile), tile)
        value = dot(act[at], wd[...], 1, 1)

        @pl.when(i >= 2)
        def _():
            for item in slot_copies(i - 2):
                item.wait()

        base_v[i % 2] = resid[at] + value
        mlp_v[i % 2] = value.astype(LOW)
        for item in slot_copies(i):
            item.start()

    pl.loop(0, chunks)(slot_loop)
    if heads > 1:
        sums(chunks)
        sums(0)
        pl.loop(1, chunks - per_part)(sums)
    for i in range(max(0, chunks - 2), chunks):
        for item in slot_copies(i):
            item.wait()
    down.three(mine_down)
    down.finish()
    for item in stores:
        item.wait()
    for j in range(per_part):
        for item in own_store(j):
            item.wait()
        for step in range(1, heads):
            g_copy(j, step).wait()
    for step in range(1, heads):
        for j in range(per_part):
            x_copy((step - 1) * per_part + j, step).wait_send()
    if heads > 1:
        x_copy(chunks, 1).wait_send()


def shares(hidden):
    n = hidden // 128
    first = max(n // 8, 1)
    return first * 128, (n - first) * 128


def middle(tokens, context_all, cotangent, full_qkv, full_out, full_up, full_down, scenes, heads):
    ny = scenes // ZS
    rows, d_model = tokens.shape
    rl = d_model // (2 * scenes)
    hidden, width = full_up.shape[1], d_model // heads
    tile, size_f = min(256, rows // heads), min(1024, hidden)
    part_rows = rows // heads
    per_part = part_rows // tile
    chunks = rows // tile
    first_cols = shares(hidden)[0]
    others = max(heads - 1, 1)
    sem = pltpu.SemaphoreType.DMA
    shape, vmem = jax.ShapeDtypeStruct, pltpu.VMEM
    any_space, whole = pl.BlockSpec(memory_space=pl.ANY), pl.BlockSpec(memory_space=pltpu.VMEM)
    big, wide, blocks = (rows, d_model), (rows, hidden), (ZS, ny, 2, rl, hidden)
    scratch = [vmem(big, LOW), vmem(big, LOW), vmem(big, LOW), vmem((d_model, 128), LOW), vmem((d_model, d_model), LOW),
               vmem((d_model, hidden), LOW), vmem((d_model, hidden), LOW), vmem(big, LOW), vmem(wide, LOW), vmem(wide, LOW),
               vmem(big, F32), vmem(big, F32), vmem(big, LOW), vmem((others, part_rows, d_model), LOW), vmem(blocks, LOW),
               vmem(blocks, LOW), vmem((ZS, ny, 2, rl, d_model), LOW), vmem((part_rows, d_model), LOW), vmem((2, tile, d_model), F32),
               vmem((2, tile, d_model), LOW), sem((7,)), sem((3 + 2 * per_part,)), sem((2, 2)), sem((chunks + 1,)),
               sem((chunks + 1,)), sem((per_part, others)), sem((per_part, others))]
    scratch += scatter_scratch(ny, rl, first_cols)
    return pl.pallas_call(
        partial(middle_kernel, (ny, heads, rows, d_model, width, hidden, tile, size_f, first_cols)),
        out_shape=[shape((part_rows, d_model), F32), shape(big, F32), shape(big, LOW), shape((rows, width), LOW), shape((8, d_model), F32),
                   shape((ZS, ny, 2, rl, d_model), LOW), shape(blocks, LOW), shape(blocks, LOW), shape((rl, first_cols), F32)],
        in_specs=[any_space] * 7,
        out_specs=[any_space] * 4 + [whole] + [any_space] * 3 + [whole],
        scratch_shapes=scratch,
        compiler_params=pltpu.CompilerParams(collective_id=3, has_side_effects=True, vmem_limit_bytes=63 * 2**20),
        cost_estimate=pl.CostEstimate(flops=14 * rows * d_model * hidden, bytes_accessed=50 * 2**20, transcendentals=0),
        name="middle_stage",
    )(tokens, context_all, cotangent, full_qkv, full_out, full_up, full_down)


def backward_kernel(dims, probs, queries, keys, values, grad, context, inverse, parts_out, parts_up, mlp_low,
                    grads, mine_out, mine_up, mlp_land,
                    dk_acc, dv_acc, kept, stage, landed, kv_send, kv_recv, m_send, m_recv, *scratch):
    ny, heads, rows, size, pairs, steps_q, halves = dims
    pair, part = pl.program_id(0), pl.program_id(1)
    step = pair * steps_q + part
    total = pairs * steps_q
    block = grad.shape[0]
    z, y, core = place(ny)
    width = parts_out.shape[-1]
    ends = split_cols(width, 2)
    plan = [(parts_out, ends[0])] + [(parts_up, cols) for cols in split_cols(parts_up.shape[-1], halves)] + [(parts_out, ends[1])]
    scatters = make_scatters(ny, plan, scratch)
    targets = [mine_out] + [mine_up] * halves + [mine_out]

    def kv_copy(p, i):
        return remote(stage.at[p, i], landed.at[p, i], kv_send.at[p, i], kv_recv.at[p, i], {"seq": 1 - core})

    head = lax.axis_index("head")

    def mlp_copy(i, step):
        return remote(mlp_low.at[pl.ds(i * (rows // 4), rows // 4)], mlp_land.at[step - 1, pl.ds(i * (rows // 4), rows // 4)],
                      m_send.at[i, step - 1], m_recv.at[i, step - 1], {"head": (head + step) % heads})

    @pl.when(step == 0)
    def _():
        greet_all(ny, heads)
        for i in range(4):
            for j in range(1, heads):
                mlp_copy(i, j).start()
        for item in scatters:
            item.begin()

    slots = 2 * total
    plan_at = [(0.4 + 0.5 * i, 3.4 + 2.3 * i, 5.9 + 2.3 * i) for i in range(len(scatters))]
    events = sorted((plan_at[i][j], i, j + 1) for i in range(len(scatters)) for j in range(3))

    def run(slot_in_step):
        for when, i, what in events:
            slot = min(int(when * min(1.0, slots / 16)), slots)
            if slot == slots or slot % 2 != slot_in_step:
                continue

            @pl.when(step == slot // 2)
            def _():
                if what == 1:
                    scatters[i].one()
                elif what == 2:
                    scatters[i].two()
                else:
                    scatters[i].three(targets[i])

    @pl.when(part == 0)
    def _():
        dk_acc[...] = jnp.zeros_like(dk_acc)
        dv_acc[...] = jnp.zeros_like(dv_acc)

    upper = grad[...].astype(F32)
    inner = (upper * context[...].astype(F32)).T
    upper_t = upper.T
    row = lax.broadcasted_iota(jnp.int32, upper_t.shape, 0)
    keys_t = keys[...].T
    pieces = []
    for h in range(2):
        run(h)
        over = inverse[0, h:h + 1]
        shift = jnp.sum(inner[h * size:(h + 1) * size], axis=0, keepdims=True) * over
        scaled = jnp.where(row // size == h, upper_t * over, 0.0)
        dp = dot(values[...], scaled.astype(LOW), 1, 0) - shift
        low = probs[h]
        ds = (low.astype(F32) * dp).astype(LOW)
        dv_acc[...] += dot(low, scaled.T.astype(LOW), 1, 0)
        dk_acc[...] += dot(ds, only_head(queries[...], h, size), 1, 0)
        pieces.append(dot(keys_t, ds, 1, 0)[h * size:(h + 1) * size])
    grads[pl.ds(pl.multiple_of(part * block, block), block), pl.ds(pl.multiple_of(pair * 6 * size, 2 * size), 2 * size)] = (
        (jnp.concatenate(pieces, axis=0) * size ** -0.5).T.astype(LOW))

    @pl.when(part == steps_q - 1)
    def _():
        for i, acc in enumerate((dk_acc, dv_acc)):
            stage[pair, i] = acc[rows:].astype(LOW)
            kv_copy(pair, i).start()
            kept[pair, i] = acc[:rows]

    @pl.when(step == total - 1)
    def _():
        for when, i, what in events:
            if min(int(when * min(1.0, slots / 16)), slots) == slots:
                if what == 1:
                    scatters[i].one()
                elif what == 2:
                    scatters[i].two()
                else:
                    scatters[i].three(targets[i])
        for item in scatters:
            item.finish()
        for p in range(pairs):
            for i in range(2):
                kv_copy(p, i).wait()
                grads[:, (3 * p + i + 1) * 2 * size:(3 * p + i + 2) * 2 * size] = (kept[p, i] + landed[p, i].astype(F32)).astype(LOW)
        for i in range(4):
            for j in range(1, heads):
                mlp_copy(i, j).wait()


def backward(probs, q, k, v, grad, context, inverse, parts_out, parts_up, mlp_low, scenes, heads, size):
    ny = scenes // ZS
    rows, width = q.shape
    pairs = width // (2 * size)
    block = min(512, rows)
    d_model, hidden = parts_out.shape[-1], parts_up.shape[-1]
    rl = d_model // (2 * scenes)
    others = max(heads - 1, 1)
    halves = 4
    spec = pl.BlockSpec
    q_spec = spec((block, 2 * size), lambda p, i: (i, p))
    k_spec = spec((2 * rows, 2 * size), lambda p, i: (0, p))
    any_space = spec(memory_space=pl.ANY)
    whole = spec(memory_space=pltpu.VMEM)
    shape = jax.ShapeDtypeStruct
    sem = pltpu.SemaphoreType.DMA
    pair_buf = (pairs, 2, rows, 2 * size)
    scratch = [pltpu.VMEM((2 * rows, 2 * size), F32), pltpu.VMEM((2 * rows, 2 * size), F32), pltpu.VMEM(pair_buf, F32),
               pltpu.VMEM(pair_buf, LOW), pltpu.VMEM(pair_buf, LOW), sem((pairs, 2)), sem((pairs, 2)), sem((4, others)), sem((4, others))]
    for cols in [d_model // 2] + [hidden // halves] * halves + [d_model // 2]:
        scratch += scatter_scratch(ny, rl, cols)
    return pl.pallas_call(
        partial(backward_kernel, (ny, heads, rows, size, pairs, rows // block, halves)),
        grid=(pairs, rows // block),
        out_shape=[shape((rows, 3 * width), LOW), shape((rl, d_model), F32), shape((rl, hidden), F32), shape((others, rows, d_model), LOW)],
        in_specs=[spec((2, 2 * rows, block), lambda p, i: (p, 0, i)), q_spec, k_spec, k_spec, q_spec, q_spec,
                  spec((1, 8, block), lambda p, i: (p, 0, i)), any_space, any_space, any_space],
        out_specs=[whole, whole, whole, any_space],
        scratch_shapes=scratch,
        compiler_params=pltpu.CompilerParams(collective_id=1, has_side_effects=True, vmem_limit_bytes=60 * 2**20),
        cost_estimate=pl.CostEstimate(flops=16 * rows * rows * width, bytes_accessed=50 * 2**20, transcendentals=0),
        name="backward_attention",
    )(probs, q, k, v, grad, context, inverse, parts_out, parts_up, mlp_low)


def thirds(start, count):
    n = count // 128
    edges = [start + n * i // 3 * 128 for i in range(4)]
    return [(a, b - a) for a, b in zip(edges, edges[1:])]


def last_kernel(dims, grads, n1, tokens, resid, full_qkv, norm_two, parts_down, down_a, out_all,
                own_grad, done_land, mine_w, mine_norm, mine_out, mine_down,
                g_v, n1_v, x_v, res_v, w_v, in_sem,
                part_one, part_low, arrived, parts_qkv, tiny_land, tiny_own, out_v, done_low, x_send, x_recv, t_send, t_recv,
                n_send, n_recv, o_send, o_recv, out_sem, mine_qkv, out_land, *scratch):
    ny, heads, rows, d_model, width, tile, down_at, qkv_at = dims
    z, y, core = place(ny)
    head = lax.axis_index("head")
    wide = full_qkv.shape[1]
    rl = mine_qkv.shape[0]
    plan = [(parts_down, pl.ds(*item)) for item in down_at] + [(parts_qkv, pl.ds(*item)) for item in qkv_at]
    scatters = make_scatters(ny, plan, scratch)
    downs, qkvs = scatters[:len(down_at)], scatters[len(down_at):]
    down_x, down_y, down_z = downs

    def down_done(i):
        downs[i].three(mine_down.at[:, pl.ds(*down_at[i])], True)

    chunks = rows // tile
    part_rows = rows // heads
    per_part = part_rows // tile
    loads = [pltpu.make_async_copy(src, dst, in_sem.at[i]) for i, (src, dst) in enumerate((
        (grads, g_v), (full_qkv, w_v), (n1, n1_v), (tokens, x_v), (resid, res_v)))]
    for item in loads:
        item.start()
    def rows_at(step, j):
        return pl.ds(pl.multiple_of((head + heads + step) % heads * part_rows + j * tile, tile), tile)

    def x_copy(step, j):
        return remote(part_low.at[rows_at(step, j)], arrived.at[step - 1, pl.ds(j * tile, tile)], x_send.at[step - 1, j],
                      x_recv.at[step - 1, j], {"head": (head + step) % heads})

    def t_copy(step, j):
        at = pl.ds(j * tile, tile)
        return remote(done_low.at[at], done_land.at[step - 1, at], t_send.at[step - 1, j], t_recv.at[step - 1, j],
                      {"head": (head + step) % heads})

    def n_copy(step):
        return remote(tiny_own, tiny_land.at[step - 1], n_send.at[step - 1], n_recv.at[step - 1], {"head": (head + step) % heads})

    def o_copy(step):
        to = (head + step) % heads
        return remote(out_all.at[:, pl.ds(pl.multiple_of(to * width, width), width)], out_land.at[step - 1], o_send.at[step - 1],
                      o_recv.at[step - 1], {"head": to})

    def out_copy(j):
        at = pl.ds(j * tile, tile)
        return pltpu.make_async_copy(out_v.at[at], own_grad.at[at], out_sem.at[j])

    greet_all(ny, heads)
    for item in downs:
        item.begin()
    for item in loads[:2]:
        item.wait()

    def partial_sum(step, j):
        at = rows_at(step, j)
        total = dot(g_v[at], w_v[:, 128:], 1, 1)
        part_one[at] = total
        part_low[at] = total.astype(LOW)

    for step in range(1, heads):
        for j in range(per_part):
            partial_sum(step, j)
            x_copy(step, j).start()
    for step in range(1, heads):
        o_copy(step).start()
    down_x.one()
    down_y.one()
    for j in range(per_part):
        partial_sum(0, j)
    for item in loads[2:]:
        item.wait()
    per_z = d_model // ZS
    for zz in range(0, ZS, 2):
        cols = n1_v[:, zz * per_z:(zz + 2) * per_z]
        value = dot(cols, g_v[...], 0, 0).astype(LOW)
        parts_qkv[zz:zz + 2, :, :, :, 128:] = value.reshape(2, ny, 2, rl, 3 * width)
    for item in qkvs[1:]:
        item.begin()
    gain = w_v[:, :128].astype(F32).T[0:1]

    def hat_of(at):
        x = x_v[at].astype(F32)
        centre = x - jnp.mean(x, axis=1, keepdims=True)
        spread = lax.rsqrt(jnp.mean(centre * centre, axis=1, keepdims=True) + 1e-05)
        return centre * spread, spread

    gain_sum = jnp.zeros((1, d_model), F32)
    shift_sum = jnp.zeros((1, d_model), F32)
    for i in range(chunks):
        at = pl.ds(i * tile, tile)
        hat, _ = hat_of(at)
        gain_sum += jnp.sum(part_one[at] * hat, axis=0, keepdims=True)
        shift_sum += jnp.sum(part_one[at], axis=0, keepdims=True)
        if i == chunks // 4:
            qkvs[1].one()
            down_x.two()
        if i == chunks // 2:
            qkvs[2].one()
    sums = jnp.concatenate([gain_sum, shift_sum, norm_two[0:2], jnp.zeros((124, d_model), F32)], axis=0).T.astype(LOW)
    parts_qkv[:, :, :, :, :128] = sums.reshape(ZS, ny, 2, rl, 128)
    qkvs[0].begin()

    def receive(j):
        at = rows_at(0, j)
        here = pl.ds(j * tile, tile)
        total = part_one[at]
        for step in range(1, heads):
            x_copy(step, j).wait_recv()
            total += arrived[step - 1, here].astype(F32)
        hat, spread = hat_of(at)
        scaled = total * gain
        inner = scaled - jnp.mean(scaled, axis=1, keepdims=True) - hat * jnp.mean(scaled * hat, axis=1, keepdims=True)
        total = res_v[here] + inner * spread
        out_v[here] = total
        out_copy(j).start()
        done_low[here] = total.astype(LOW)
        for step in range(1, heads):
            t_copy(step, j).start()

    first = pl.ds(pl.multiple_of(head * width, width), width)

    def share(items, i, n):
        return items[len(items) * i // n:len(items) * (i + 1) // n]

    def receive_some(i):
        for j in share(range(per_part), i, 4):
            receive(j)

    def send_norms():
        tiny_own[...] = mine_qkv[:, :128]
        for step in range(1, heads):
            n_copy(step).start()

    receive_some(0)
    qkvs[0].one()
    down_z.one()
    down_y.two()
    receive_some(1)
    mine_down[:, :down_a.shape[1]] = down_a[...]
    down_done(0)
    receive_some(2)
    qkvs[1].two()
    down_done(1)
    receive_some(3)
    qkvs[2].two()
    qkvs[1].three(mine_qkv)
    total = out_all[:, first]
    for step in range(1, heads):
        o_copy(step).wait()
        total += out_land[step - 1]
    mine_out[...] = total
    qkvs[0].two()
    qkvs[2].three(mine_qkv)
    down_z.two()
    qkvs[0].three(mine_qkv)
    send_norms()
    down_done(2)
    total = mine_qkv[:, :128]
    for step in range(1, heads):
        n_copy(step).wait()
        total += tiny_land[step - 1]
    mine_norm[...] = total.T[:8]
    for p in range(width // 128):
        for c in range(3):
            mine_w[c, :, p * 128:(p + 1) * 128] = mine_qkv[:, 128 * (3 * p + c + 1):128 * (3 * p + c + 2)]
    for item in scatters:
        item.finish()
    for j in range(per_part):
        out_copy(j).wait()
        for step in range(1, heads):
            x_copy(step, j).wait_send()
            t_copy(step, j).wait()


def last_stage(grads, n1, tokens, resid, full_qkv, norm_two, parts_down, down_a, out_all, scenes, heads):
    ny = scenes // ZS
    rows, d_model = tokens.shape
    width, hidden = grads.shape[1] // 3, parts_down.shape[-1]
    first, third = shares(hidden)
    rl = d_model // (2 * scenes)
    wide = full_qkv.shape[1]
    part_rows = rows // heads
    tile = min(128, part_rows)
    chunks, per_part = rows // tile, part_rows // tile
    down_at, qkv_at = thirds(first, third), thirds(0, wide)
    others = max(heads - 1, 1)
    sem = pltpu.SemaphoreType.DMA
    shape, vmem = jax.ShapeDtypeStruct, pltpu.VMEM
    any_space, whole = pl.BlockSpec(memory_space=pl.ANY), pl.BlockSpec(memory_space=pltpu.VMEM)
    big, own = (rows, d_model), (part_rows, d_model)
    scratch = [vmem((rows, 3 * width), LOW), vmem(big, LOW), vmem(big, LOW), vmem(own, F32), vmem((d_model, wide), LOW), sem((5,)),
               vmem(big, F32), vmem(big, LOW), vmem((others, *own), LOW), vmem((ZS, ny, 2, rl, wide), LOW), vmem((others, rl, 128), F32),
               vmem((rl, 128), F32), vmem(own, F32), vmem(own, LOW), sem((others, per_part)),
               sem((others, per_part)), sem((others, per_part)), sem((others, per_part)), sem((others,)), sem((others,)),
               sem((others,)), sem((others,)), sem((per_part,)), vmem((rl, wide), F32), vmem((others, rl, width), F32)]
    for _, cols in down_at + qkv_at:
        scratch += scatter_scratch(ny, rl, cols)
    return pl.pallas_call(
        partial(last_kernel, (ny, heads, rows, d_model, width, tile, down_at, qkv_at)),
        out_shape=[shape(own, F32), shape((others, *own), LOW), shape((3, rl, width), F32), shape((8, rl), F32), shape((rl, width), F32),
                   shape((rl, hidden), F32)],
        in_specs=[any_space] * 5 + [whole, any_space, whole, whole],
        out_specs=[any_space, any_space, whole, whole, whole, whole],
        scratch_shapes=scratch,
        compiler_params=pltpu.CompilerParams(collective_id=2, has_side_effects=True, vmem_limit_bytes=63 * 2**20),
        cost_estimate=pl.CostEstimate(flops=12 * rows * d_model * width, bytes_accessed=30 * 2**20, transcendentals=0),
        name="last_stage",
    )(grads, n1, tokens, resid, full_qkv, norm_two, parts_down, down_a, out_all)


def finish_kernel(heads, per_part, head_ref, base, mlp_land, own, land, w, out, up, down, norm,
                  output, tokens_grad, w_o, out_o, up_o, down_o, *norm_o):
    part = pl.program_id(0) // per_part
    total = base[...]
    for step in range(1, heads):
        total += mlp_land[step - 1].astype(F32)
    output[...] = total

    @pl.when(part == head_ref[0])
    def _():
        tokens_grad[...] = own[...]

    @pl.when(part != head_ref[0])
    def _():
        tokens_grad[...] = land[0].astype(F32)

    @pl.when(pl.program_id(0) == 0)
    def _():
        for src, dst in ((w, w_o), (out, out_o), (up, up_o), (down, down_o)):
            dst[...] = src[...]
        for i, dst in enumerate(norm_o):
            dst[...] = norm[i:i + 1]


def finish(head, base, mlp_land, own, land, w, out, up, down, norm, heads):
    rows, d_model = base.shape
    part_rows = rows // heads
    tile = min(256, part_rows)
    per_part = part_rows // tile
    rl = up.shape[0]
    spec, shape = pl.BlockSpec, jax.ShapeDtypeStruct

    def small(a):
        return spec(a.shape, lambda i, h: (0,) * a.ndim)

    row = spec((tile, d_model), lambda i, h: (i, 0))
    smalls = [small(a) for a in (w, out, up, down, norm)]

    def own_at(i, h):
        first = h[0] * per_part
        return jnp.clip(i - first, 0, per_part - 1), 0

    def land_at(i, h):
        step = (h[0] + heads - i // per_part) % heads
        return jnp.maximum(step - 1, 0), i % per_part, 0

    return pl.pallas_call(
        partial(finish_kernel, heads, per_part),
        grid_spec=pltpu.PrefetchScalarGridSpec(
            num_scalar_prefetch=1, grid=(rows // tile,),
            in_specs=[row, spec((max(heads - 1, 1), tile, d_model), lambda i, h: (0, i, 0)),
                      spec((tile, d_model), own_at), spec((1, tile, d_model), land_at)] + smalls,
            out_specs=[row, row] + smalls[:4] + [spec((1, rl), lambda i, h: (0, 0))] * 4),
        out_shape=[shape((rows, d_model), F32), shape((rows, d_model), F32)] + [shape(a.shape, F32) for a in (w, out, up, down)]
        + [shape((1, rl), F32)] * 4,
        compiler_params=pltpu.CompilerParams(vmem_limit_bytes=63 * 2**20),
        name="finish",
    )(head, base, mlp_land, own, land, w, out, up, down, norm)


def on_device(n_scene, n_head, tokens, counts, w_qkv, w_out, w_up, w_down, gain_one, shift_one, gain_two, shift_two, cotangent):
    rows, d_model = tokens.shape
    width, hidden = w_qkv.shape[2], w_up.shape[1]
    size = 64
    n1, q, k, v, full_qkv, full_out, full_up, full_down, probs, context, context_all, inverse = forward(
        counts, (gain_one, shift_one, gain_two, shift_two), w_qkv, w_out.T, w_up, w_down.T, tokens, n_scene, n_head, size)
    grad_resid, base, mlp_low, grad_context, norm_two, grad_outproj, grad_up, grad_down, down_a = middle(
        tokens, context_all, cotangent, full_qkv, full_out, full_up, full_down, n_scene, n_head)
    grads, out_all, mine_up, mlp_land = backward(
        probs, q, k, v, grad_context, context, inverse, grad_outproj, grad_up, mlp_low, n_scene, n_head, size)
    own, land, mine_qkv, norms, mine_out, mine_down = last_stage(
        grads, n1, tokens, grad_resid, full_qkv, norm_two, grad_down, down_a, out_all, n_scene, n_head)
    head = lax.axis_index("head").reshape(1).astype(jnp.int32)
    output, tokens_grad, mine_qkv, mine_out, mine_up, mine_down, *norms = finish(
        head, base, mlp_land, own, land, mine_qkv, mine_out, mine_up, mine_down, norms, n_head)
    return (output, tokens_grad, mine_qkv, mine_out.T, mine_up, mine_down.T, *[a.reshape(-1) for a in norms])


def solution(mesh):
    rows, both = ("scene", "seq"), P(("scene", "seq"))
    weights = (P(None, rows, "head"), P("head", rows), P(rows, "head"), P("head", rows), both, both, both, both)
    return jax.shard_map(
        partial(on_device, mesh.shape["scene"], mesh.shape["head"]), mesh=mesh,
        in_specs=(P(rows, None), P("scene"), *weights, P(rows, None)),
        out_specs=(P(rows, None), P(rows, None), *weights),
        check_vma=False,
    )
```

```python
from functools import partial

import jax
import jax.numpy as jnp
from jax import lax
from jax.experimental import pallas as pl
from jax.experimental.pallas import tpu as pltpu
from jax.sharding import PartitionSpec as P

MESH = pl.DeviceIdType.MESH
ZS = 4


def place(ny):
    scene = lax.axis_index("scene")
    return scene // ny, scene % ny, lax.axis_index("seq")


def remote(src, dst, send_sem, recv_sem, device):
    return pltpu.make_async_remote_copy(
        src_ref=src, dst_ref=dst, send_sem=send_sem, recv_sem=recv_sem,
        device_id=device, device_id_type=MESH,
    )


F32 = jnp.float32
LOW = jnp.bfloat16


def dot(a, b, ca, cb):
    return lax.dot_general(a, b, (((ca,), (cb,)), ((), ())), preferred_element_type=F32)


def only_head(x, h, size):
    lane = lax.broadcasted_iota(jnp.int32, x.shape, 1)
    return jnp.where(lane // size == h, x, jnp.zeros_like(x))


class Gather:
    def __init__(self, ny, source, full, cols, sems):
        self.ny, self.source, self.full, self.cols = ny, source, full, cols
        self.rsend, self.rrecv, self.lsend, self.lrecv, self.ysend, self.yrecv, self.csend, self.crecv = sems
        self.z, self.y, self.core = place(ny)

    def at(self, zz, yy):
        return self.full.at[zz, yy, self.core, :, self.cols]

    def right(self, k):
        src = self.source() if k == 0 else self.at(self.z - k, self.y)
        dst = self.at(self.z - k, self.y)
        return remote(src, dst, self.rsend.at[k], self.rrecv.at[k], {"scene": (self.z + 1) * self.ny + self.y})

    def left(self, k):
        src = self.source() if k == 0 else self.at(self.z + k, self.y)
        dst = self.at(self.z + k, self.y)
        return remote(src, dst, self.lsend.at[k], self.lrecv.at[k], {"scene": (self.z - 1) * self.ny + self.y})

    def across(self, zz, step, own=False):
        src = self.source() if own else self.at(zz, self.y)
        peer = self.z * self.ny + (self.y + step) % self.ny
        return remote(src, self.at(zz, self.y), self.ysend.at[step - 1], self.yrecv.at[step - 1], {"scene": peer})

    def arrival(self, zz, step):
        yy = (self.y + self.ny - step) % self.ny
        return remote(self.at(zz, yy), self.at(zz, yy), self.ysend.at[step - 1], self.yrecv.at[step - 1],
                      {"scene": self.z * self.ny + yy})

    def twin(self, zz, step, own=False):
        src = self.source() if own else self.at(zz, (self.y + self.ny - step) % self.ny)
        dst = self.at(zz, (self.y + self.ny - step) % self.ny)
        return remote(src, dst, self.csend.at[0], self.crecv.at[0], {"seq": 1 - self.core})

    def column(self, step):
        yy = (self.y + self.ny - step) % self.ny
        all_z = self.full.at[:, yy, self.core, :, self.cols]
        return remote(all_z, all_z, self.ysend.at[step - 1], self.yrecv.at[step - 1], {"scene": self.z * self.ny + yy})

    def twins(self):
        mine, theirs = [self.full.at[:, :, c, :, self.cols] for c in (self.core, 1 - self.core)]
        return [remote(item, item, self.csend.at[0], self.crecv.at[0], {"seq": 1 - self.core}) for item in (mine, theirs)]

    def begin(self):
        @pl.when(self.z < ZS - 1)
        def _():
            self.right(0).start()

        @pl.when(self.z > 0)
        def _():
            self.left(0).start()

        for step in range(1, self.ny):
            self.across(self.z, step, True).start()
        self.twin(self.z, 0, True).start()

    def hop(self, k):
        @pl.when(self.z >= k)
        def _():
            self.right(k - 1).wait_recv()
            if k < ZS - 1:
                @pl.when(self.z < ZS - 1)
                def _():
                    self.right(k).start()
            for step in range(1, self.ny):
                self.across(self.z - k, step).start()
            self.twin(self.z - k, 0).start()

        @pl.when(self.z + k < ZS)
        def _():
            self.left(k - 1).wait_recv()
            if k < ZS - 1:
                @pl.when(self.z > 0)
                def _():
                    self.left(k).start()
            for step in range(1, self.ny):
                self.across(self.z + k, step).start()
            self.twin(self.z + k, 0).start()

    def spread(self):
        for step in range(1, self.ny):
            self.column(step).wait_recv()
            for zz in range(ZS):
                self.twin(zz, step).start()

    def finish(self):
        for k in range(ZS - 1):
            @pl.when((self.z < ZS - 1) & (self.z >= k))
            def _():
                self.right(k).wait_send()

            @pl.when((self.z > 0) & (self.z + k < ZS))
            def _():
                self.left(k).wait_send()
        for step in range(1, self.ny):
            self.column(step).wait_send()
        mine, theirs = self.twins()
        mine.wait_send()
        theirs.wait_recv()


class PairGather(Gather):
    def row(self, zz):
        return self.full.at[zz, :, self.core, :, self.cols]

    def right(self, k):
        return remote(self.row(self.z - k), self.row(self.z - k), self.rsend.at[k], self.rrecv.at[k],
                      {"scene": (self.z + 1) * self.ny + self.y})

    def left(self, k):
        return remote(self.row(self.z + k), self.row(self.z + k), self.lsend.at[k], self.lrecv.at[k],
                      {"scene": (self.z - 1) * self.ny + self.y})

    def twin(self, zz):
        return remote(self.row(zz), self.row(zz), self.csend.at[0], self.crecv.at[0], {"seq": 1 - self.core})

    def begin(self):
        for step in range(1, self.ny):
            self.across(self.z, step, True).start()

    def pair(self):
        for step in range(1, self.ny):
            self.arrival(self.z, step).wait_recv()

        @pl.when(self.z < ZS - 1)
        def _():
            self.right(0).start()

        @pl.when(self.z > 0)
        def _():
            self.left(0).start()

        self.twin(self.z).start()

    def hop(self, k):
        @pl.when(self.z >= k)
        def _():
            self.right(k - 1).wait_recv()
            if k < ZS - 1:
                @pl.when(self.z < ZS - 1)
                def _():
                    self.right(k).start()
            self.twin(self.z - k).start()

        @pl.when(self.z + k < ZS)
        def _():
            self.left(k - 1).wait_recv()
            if k < ZS - 1:
                @pl.when(self.z > 0)
                def _():
                    self.left(k).start()
            self.twin(self.z + k).start()

    def finish(self):
        for k in range(ZS - 1):
            @pl.when((self.z < ZS - 1) & (self.z >= k))
            def _():
                self.right(k).wait_send()

            @pl.when((self.z > 0) & (self.z + k < ZS))
            def _():
                self.left(k).wait_send()
        for step in range(1, self.ny):
            self.across(self.z, step).wait_send()
        mine, theirs = self.twins()
        mine.wait_send()
        theirs.wait_recv()


def gather_sems(ny):
    sem = pltpu.SemaphoreType.DMA
    return [sem((ZS - 1,)), sem((ZS - 1,)), sem((ZS - 1,)), sem((ZS - 1,)), sem((max(ny - 1, 1),)), sem((max(ny - 1, 1),)),
            sem((1,)), sem((1,))]


def greet_all(ny, heads):
    z, y, core = place(ny)
    head = lax.axis_index("head")
    barrier = pltpu.get_barrier_semaphore()

    def signal(device):
        pl.semaphore_signal(barrier, 1, device_id=device, device_id_type=MESH)

    for step in range(1, ZS):
        signal({"scene": (z + step) % ZS * ny + y})
    for step in range(1, ny):
        signal({"scene": z * ny + (y + step) % ny})
    for step in range(1, heads):
        signal({"head": (head + step) % heads})
    signal({"seq": 1 - core})
    pl.semaphore_wait(barrier, ZS + ny - 1 + heads - 1)


def split_cols(total, parts):
    size = total // parts
    return [pl.ds(i * size, size) for i in range(parts)]


def forward_kernel(dims, counts, gain_one, shift_one, gain_two, shift_two, w_qkv, shard_out, shard_up, shard_down, tokens,
                   n1_out, q_out, k_out, v_out, full_qkv, full_out, full_up, full_down, probs, context, context_all, inverse,
                   w0, hat, n1, q_s, k_s, v_s, bias, ctx_s, scores, tops, probs_v, probs_sem, local_sem, kv_send, kv_recv, xw_send, xw_recv, xt_send, xt_recv, xc_send, xc_recv, *sems):
    ny, heads, rows, width, size, block, pairs, steps_q, halves = dims
    pair, part = pl.program_id(0), pl.program_id(1)
    step = pair * steps_q + part
    z, y, core = place(ny)
    head = lax.axis_index("head")
    d_model = tokens.shape[1]
    per = 8
    own_cols = pl.ds(pl.multiple_of(head * width, width), width)

    def of(i):
        return sems[i * per:(i + 1) * per]

    group = 6 * size
    edges = [0] + [128 + (p + 1) * group for p in range(pairs)]
    firsts = []
    for p in range(pairs):
        cols = pl.ds(edges[p], edges[p + 1] - edges[p])
        firsts.append(Gather(ny, partial(lambda c: w0.at[z, y, core, :, c], cols), w0, cols, of(2 + 2 * halves + p)))
    outer = Gather(ny, lambda: shard_out, full_out, own_cols, of(1))
    thick = []
    for n, (shard, full) in enumerate(((shard_up, full_up), (shard_down, full_down))):
        for i, cols in enumerate(split_cols(full_up.shape[-1], halves)):
            kind = PairGather if n == 1 and i == halves - 1 else Gather
            thick.append(kind(ny, partial(lambda s, c: s.at[:, c], shard, cols), full, cols, of(2 + n * halves + i)))
    up_a, up_b, down_a, down_b = thick

    def local(src, dst, i):
        return pltpu.make_async_copy(src, dst, local_sem.at[i])

    def cols_of(step):
        return pl.ds(pl.multiple_of((head + heads - step) % heads * width, width), width)

    def out_copy(step):
        mine = full_out.at[:, :, core, :, own_cols]
        return remote(mine, mine, xw_send.at[step - 1], xw_recv.at[step - 1], {"head": (head + step) % heads})

    def out_twin(step):
        other = full_out.at[:, :, core, :, cols_of(step)]
        return remote(other, other, xt_send.at[step - 1], xt_recv.at[step - 1], {"seq": 1 - core})

    def kv_copy(p, i):
        src = (k_s, v_s)[i]
        cols = pl.ds(p * 2 * size, 2 * size)
        return remote(src.at[pl.ds(0, rows), cols], src.at[pl.ds(rows, rows), cols], kv_send.at[p, i], kv_recv.at[p, i],
                      {"seq": 1 - core})

    def project(p):
        tile = min(256, rows)

        @pl.loop(0, rows // tile)
        def _(i):
            at = pl.ds(pl.multiple_of(i * tile, tile), tile)
            w = w0[:, :, :, :, 128 + p * group:128 + (p + 1) * group].reshape(d_model, group)
            value = dot(n1[at], w, 1, 0).astype(LOW)
            cols = pl.ds(p * 2 * size, 2 * size)
            q_s[at, cols] = value[:, :2 * size] * LOW(size ** -0.5)
            k_s[at, cols] = value[:, 2 * size:4 * size]
            v_s[at, cols] = value[:, 4 * size:]

        for i in range(2):
            kv_copy(p, i).start()

    def ctx_copy(p, step):
        cols = pl.ds(pl.multiple_of(p * 2 * size, 2 * size), 2 * size)
        wide = pl.ds(pl.multiple_of(head * width + p * 2 * size, 2 * size), 2 * size)
        return remote(ctx_s.at[:, cols], context_all.at[:, wide], xc_send.at[p, step - 1], xc_recv.at[p, step - 1],
                      {"head": (head + step) % heads})

    own_blocks = [(shard_out, full_out.at[z, y, core, :, own_cols], 1),
                  (shard_up, full_up.at[z, y, core], 2), (shard_down, full_down.at[z, y, core], 3)]
    results = [(w0, full_qkv, 4), (n1, n1_out, 5), (q_s, q_out, 6), (k_s, k_out, 7), (v_s, v_out, 8)]
    ctx_local = (ctx_s, context_all.at[:, own_cols], 9)

    @pl.when(step == 0)
    def _():
        for item in own_blocks:
            local(*item).start()
        greet_all(ny, heads)
        columns = jnp.concatenate([a[...].astype(F32) for a in (gain_one, shift_one, gain_two, shift_two)]
                                  + [jnp.zeros((124, gain_one.shape[1]), F32)], axis=0)
        w0[z, y, core, :, :128] = columns.T.astype(LOW)
        for p in range(pairs):
            for c in range(3):
                w0[z, y, core, :, 128 * (3 * p + c + 1):128 * (3 * p + c + 2)] = w_qkv[c, :, 128 * p:128 * (p + 1)]
            if p < 2:
                firsts[p].begin()
        tile = min(128, rows)

        @pl.loop(0, rows // tile)
        def _(i):
            at = pl.ds(pl.multiple_of(i * tile, tile), tile)
            x = tokens[at].astype(F32)
            centre = x - jnp.mean(x, axis=1, keepdims=True)
            spread = jnp.mean(centre * centre, axis=1, keepdims=True)
            hat[at] = centre * lax.rsqrt(spread + 1e-05)

        low_rows = lax.broadcasted_iota(jnp.int32, bias.shape, 0)
        lane = lax.broadcasted_iota(jnp.int32, bias.shape, 1)
        limit = jnp.where(low_rows < rows, counts[0] - core * rows, counts[0] - (1 - core) * rows + rows)
        bias[...] = jnp.where((low_rows >= limit) & (lane == 0), -1e30, 0.0).astype(LOW)
        after = [
            (0, lambda g: g.hop(1)), (2, lambda g: g.begin()), (0, lambda g: g.hop(2)), (1, lambda g: g.hop(1)), (0, lambda g: g.hop(3)),
            (3, lambda g: g.begin()), (1, lambda g: g.hop(2)), (0, lambda g: g.spread()), (1, lambda g: g.hop(3)),
            (2, lambda g: g.hop(1)), (1, lambda g: g.spread()), (2, lambda g: g.hop(2))]
        for p, act in after[:9]:
            if p < pairs:
                act(firsts[p])
        firsts[0].finish()
        for item in own_blocks:
            local(*item).wait()
        norms = w0[:, :, :, :, :128].reshape(d_model, 128).astype(F32).T
        gain, shift = norms[0:1], norms[1:2]
        tile = min(256, rows)

        @pl.loop(0, rows // tile)
        def _(i):
            at = pl.ds(pl.multiple_of(i * tile, tile), tile)
            n1[at] = (hat[at] * gain + shift).astype(LOW)

        local(*results[1]).start()
        project(0)
        for p, act in after[9:]:
            if p < pairs:
                act(firsts[p])

    total = pairs * steps_q
    per_slot = 2
    in_step = 4 * rows // min(256, rows) // per_slot
    slots = in_step * total

    def send_out():
        for i in range(1, heads):
            out_copy(i).start()

    def pass_out():
        for i in range(1, heads):
            out_copy(i).wait_recv()
            out_twin(i).start()

    def on_pair(p, what, *given):
        if p < pairs:
            getattr(firsts[p], what)(*given)

    events = [
        (0.1, lambda: on_pair(2, "hop", 3)), (0.3, lambda: on_pair(3, "hop", 1)), (0.4, outer.begin),
        (1, lambda: on_pair(3, "hop", 2)), (1.2, lambda: on_pair(2, "spread")), (1.4, up_a.begin),
        (2, lambda: on_pair(3, "hop", 3)), (2.6, lambda: outer.hop(1)), (3.2, lambda: outer.hop(2)), (3.2, up_b.begin),
        (3.8, lambda: on_pair(3, "spread")), (3.9, lambda: outer.hop(3)), (5.2, lambda: up_a.hop(1)), (6, outer.spread), (6.1, send_out),
        (6.5, lambda: up_a.hop(2)), (7, down_a.begin), (7.2, down_b.begin),
        (7.8, lambda: up_a.hop(3)), (9.2, lambda: up_b.hop(1)), (10.5, lambda: up_b.hop(2)), (10.6, pass_out), (10.8, down_b.pair),
        (11.8, lambda: up_b.hop(3)), (12, up_a.spread), (13.2, lambda: down_a.hop(1)), (14.5, lambda: down_a.hop(2)),
        (15.8, lambda: down_a.hop(3)), (16, up_b.spread), (16, lambda: down_b.hop(1)),
        (16, lambda: down_b.hop(2)), (16, down_a.spread), (16, lambda: down_b.hop(3))]

    def run(slot_in_step):
        for when, act in events:
            slot = min(int(when * slots / 16), slots - 1)
            if when < 16 and slot % in_step == slot_in_step:
                pl.when(step == slot // in_step)(act)

    for p in range(pairs):
        @pl.when(step == p * steps_q)
        def _():
            if p == 0:
                for i in range(2):
                    kv_copy(0, i).wait()
            if p + 1 < pairs:
                firsts[p + 1].finish()
                project(p + 1)
            else:
                for item in (results[0], *results[2:]):
                    local(*item).start()

        if p + 1 < pairs:
            @pl.when(step == (p + 1) * steps_q - 1)
            def _():
                for i in range(2):
                    kv_copy(p + 1, i).wait()

    width2, chunk = 2 * size, min(256, rows)
    n_chunks = 2 * rows // chunk
    ones = (lax.broadcasted_iota(jnp.int32, (block, bias.shape[1]), 1) == 0).astype(LOW)

    def asked(at, h):
        rows_at = pl.ds(pl.multiple_of(at % steps_q * block, block), block)
        cols_at = pl.ds(pl.multiple_of(at // steps_q * width2, width2), width2)
        return jnp.concatenate([only_head(q_s[rows_at, cols_at], h, size), ones], axis=1)

    def score(at, query, slot, c, top):
        cols_at = pl.ds(pl.multiple_of(at // steps_q * width2, width2), width2)
        keys_at = pl.ds(c * chunk, chunk)
        value = dot(jnp.concatenate([k_s[keys_at, cols_at], bias[keys_at]], axis=1), query, 1, 1)
        scores[slot, keys_at] = value
        return jnp.maximum(top, jnp.max(value.reshape(chunk // 8, 8, block), axis=0))

    def weigh(h, c, top, total_e):
        keys_at = pl.ds(c * chunk, chunk)
        expo = jnp.exp(scores[h, keys_at] - top)
        probs_v[slot_now, h, keys_at] = expo.astype(LOW)
        return total_e + jnp.sum(expo.reshape(chunk // 8, 8, block), axis=0)

    slot_now = step % 2

    def probs_copy(at):
        there = pl.ds(pl.multiple_of(at % steps_q * block, block), block)
        return pltpu.make_async_copy(probs_v.at[at % 2], probs.at[pl.ds(at // steps_q * 2, 2), :, there], probs_sem.at[at % 2])

    @pl.when(step >= 2)
    def _():
        probs_copy(step - 2).wait()

    lowest = jnp.full((8, block), -3e38, F32)

    @pl.when(step == 0)
    def _():
        top, query = lowest, asked(0, 0)
        for c in range(n_chunks):
            top = score(0, query, 0, c, top)
        tops[...] = top

    cols = pl.ds(pl.multiple_of(pair * width2, width2), width2)
    following = jnp.minimum(step + 1, total - 1)
    values_t = v_s[:, cols].T
    pieces = []
    for h in range(2):
        top = jnp.max(tops[...], axis=0, keepdims=True)
        total_e, next_top = jnp.zeros((8, block), F32), lowest
        ahead = (step, 1) if h == 0 else (following, 0)
        query = asked(*ahead)
        for c in range(n_chunks):
            if c % per_slot == 0:
                run(h * (n_chunks // per_slot) + c // per_slot)
            next_top = score(ahead[0], query, 1 - h, c, next_top)
            total_e = weigh(h, c, top, total_e)
        tops[...] = next_top
        over = 1.0 / jnp.sum(total_e, axis=0, keepdims=True)
        pieces.append(dot(values_t, probs_v[slot_now, h], 1, 0)[h * size:(h + 1) * size] * over)
        inverse[0, h:h + 1] = over
    here = jnp.concatenate(pieces, axis=0).T.astype(LOW)
    probs_copy(step).start()
    context[...] = here
    ctx_s[pl.ds(pl.multiple_of(part * block, block), block), cols] = here

    @pl.when(part == steps_q - 1)
    def _():
        for i in range(1, heads):
            ctx_copy(pair, i).start()

    @pl.when(step == total - 1)
    def _():
        local(*ctx_local).start()
        for when, act in events:
            if when >= 16:
                act()
        for gather in (outer, *thick):
            gather.finish()
        for item in results:
            local(*item).wait()
        local(*ctx_local).wait()
        for at in range(max(total - 2, 0), total):
            probs_copy(at).wait()
        for i in range(1, heads):
            out_copy(i).wait_send()
            out_twin(i).wait()
            for p in range(pairs):
                ctx_copy(p, i).wait()


def forward(counts, norms, w_qkv, shard_out, shard_up, shard_down, tokens, scenes, heads, size):
    ny = scenes // ZS
    rows, d_model = tokens.shape
    rl, width = shard_out.shape
    hidden = shard_up.shape[1]
    pairs = width // (2 * size)
    block = min(512, rows)
    steps_q = rows // block
    halves = 2
    sem = pltpu.SemaphoreType.DMA
    any_space = pl.BlockSpec(memory_space=pl.ANY)
    shape = jax.ShapeDtypeStruct
    wide = 128 + 3 * width
    outs = [shape((rows, d_model), LOW), shape((rows, width), LOW), shape((2 * rows, width), LOW), shape((2 * rows, width), LOW),
            shape((ZS, ny, 2, rl, wide), LOW), shape((ZS, ny, 2, rl, d_model), LOW), shape((ZS, ny, 2, rl, hidden), LOW),
            shape((ZS, ny, 2, rl, hidden), LOW), shape((2 * pairs, 2 * rows, rows), LOW), shape((rows, width), LOW),
            shape((rows, d_model), LOW), shape((pairs, 8, rows), F32)]
    out_specs = [any_space] * 8 + [
        any_space, pl.BlockSpec((block, 2 * size), lambda p, i: (i, p)),
        any_space, pl.BlockSpec((1, 8, block), lambda p, i: (p, 0, i))]
    scratch = [pltpu.VMEM((ZS, ny, 2, rl, wide), LOW), pltpu.VMEM((rows, d_model), F32), pltpu.VMEM((rows, d_model), LOW),
               pltpu.VMEM((rows, width), LOW), pltpu.VMEM((2 * rows, width), LOW), pltpu.VMEM((2 * rows, width), LOW),
               pltpu.VMEM((2 * rows, 128), LOW), pltpu.VMEM((rows, width), LOW),
               pltpu.VMEM((2, 2 * rows, block), F32), pltpu.VMEM((8, block), F32),
               pltpu.VMEM((2, 2, 2 * rows, block), LOW), sem((2,)), sem((10,)), sem((pairs, 2)), sem((pairs, 2)),
               sem((max(heads - 1, 1),)), sem((max(heads - 1, 1),)), sem((max(heads - 1, 1),)), sem((max(heads - 1, 1),)), sem((pairs, max(heads - 1, 1))), sem((pairs, max(heads - 1, 1)))]
    for _ in range(2 + 2 * halves + pairs):
        scratch += gather_sems(ny)
    dims = (ny, heads, rows, width, size, block, pairs, steps_q, halves)
    flops = 2 * rows * d_model * 3 * width + 8 * rows * rows * width
    results = pl.pallas_call(
        partial(forward_kernel, dims),
        grid=(pairs, steps_q),
        out_shape=outs,
        in_specs=[pl.BlockSpec(memory_space=pltpu.SMEM)] + [pl.BlockSpec(memory_space=pltpu.VMEM)] * 8 + [pl.BlockSpec(memory_space=pltpu.VMEM)],
        out_specs=out_specs,
        scratch_shapes=scratch,
        compiler_params=pltpu.CompilerParams(collective_id=0, has_side_effects=True, vmem_limit_bytes=60 * 2**20),
        cost_estimate=pl.CostEstimate(flops=flops, bytes_accessed=60 * 2**20, transcendentals=0),
        name="forward_attention",
    )(counts, *[a.reshape(1, rl) for a in norms], w_qkv, shard_out, shard_up, shard_down, tokens)
    n1, q, k, v, full_qkv, full_out, full_up, full_down, probs, context, context_all, inverse = results
    flat = lambda a: a.reshape(d_model, a.shape[-1])
    return n1, q, k, v, flat(full_qkv), flat(full_out), flat(full_up), flat(full_down), probs, context, context_all, inverse


class Scatter:
    def __init__(self, ny, parts, cols, bufs, sems):
        self.ny, self.parts, self.cols = ny, parts, cols
        self.own, self.from_core, self.from_y, self.sum_two, self.from_z = bufs
        self.load_sem, self.csend, self.crecv, self.ysend, self.yrecv, self.zsend, self.zrecv = sems
        self.z, self.y, self.core = place(ny)

    def load(self):
        return pltpu.make_async_copy(self.parts.at[:, :, self.core, :, self.cols], self.own, self.load_sem.at[0])

    def to_core(self):
        return remote(self.parts.at[:, :, 1 - self.core, :, self.cols], self.from_core, self.csend.at[0], self.crecv.at[0],
                      {"seq": 1 - self.core})

    def to_y(self, step):
        yy = (self.y + step) % self.ny
        return remote(self.own.at[:, yy], self.from_y.at[step - 1], self.ysend.at[step - 1], self.yrecv.at[step - 1],
                      {"scene": self.z * self.ny + yy})

    def to_z(self, step):
        zz = (self.z + step) % ZS
        return remote(self.sum_two.at[zz], self.from_z.at[step - 1], self.zsend.at[step - 1], self.zrecv.at[step - 1],
                      {"scene": zz * self.ny + self.y})

    def begin(self):
        self.load().start()
        self.to_core().start()

    def one(self):
        self.load().wait()
        self.to_core().wait_recv()
        for zz in range(ZS):
            for yy in range(self.ny):
                self.own[zz, yy] = (self.own[zz, yy].astype(F32) + self.from_core[zz, yy].astype(F32)).astype(LOW)
        for step in range(1, self.ny):
            self.to_y(step).start()

    def two(self):
        for step in range(1, self.ny):
            self.to_y(step).wait_recv()
        for zz in range(ZS):
            total = self.own[zz, self.y].astype(F32)
            for step in range(1, self.ny):
                total += self.from_y[step - 1, zz].astype(F32)
            self.sum_two[zz] = total.astype(LOW)
        for step in range(1, ZS):
            self.to_z(step).start()

    def three(self, out, alone=False):
        for step in range(1, ZS):
            self.to_z(step).wait_recv()
        total = self.sum_two[self.z].astype(F32)
        for step in range(1, ZS):
            total += self.from_z[step - 1].astype(F32)
        if alone:
            out[...] = total
        else:
            out[:, self.cols] = total

    def finish(self):
        self.to_core().wait_send()
        for step in range(1, self.ny):
            self.to_y(step).wait_send()
        for step in range(1, ZS):
            self.to_z(step).wait_send()


SCATTER_BUFS, SCATTER_SEMS = 5, 7


def scatter_scratch(ny, rl, cols):
    sem = pltpu.SemaphoreType.DMA
    other = max(ny - 1, 1)
    return [pltpu.VMEM((ZS, ny, rl, cols), LOW), pltpu.VMEM((ZS, ny, rl, cols), LOW), pltpu.VMEM((other, ZS, rl, cols), LOW),
            pltpu.VMEM((ZS, rl, cols), LOW), pltpu.VMEM((ZS - 1, rl, cols), LOW),
            sem((1,)), sem((1,)), sem((1,)), sem((other,)), sem((other,)), sem((ZS - 1,)), sem((ZS - 1,))]


def make_scatters(ny, plan, scratch):
    n = SCATTER_BUFS + SCATTER_SEMS
    result = []
    for i, (parts, cols) in enumerate(plan):
        mine = scratch[i * n:(i + 1) * n]
        result.append(Scatter(ny, parts, cols, mine[:SCATTER_BUFS], mine[SCATTER_BUFS:]))
    return result

def middle_kernel(dims, tokens, context_all, cotangent, full_qkv, full_out, full_up, full_down,
                  resid_grad, base, mlp_low, grad_context, norm_two, parts_out, parts_up, parts_down, mine_down,
                  x_v, ctx_v, cot_v, norm_v, wo, wu, wd, n2, act, gu, resid, part, low, arrived, up_v, down_v, out_v, gctx_v,
                  base_v, mlp_v, in_sem, out_sem, slot_sem, x_send, x_recv, g_send, g_recv, *scratch):
    ny, heads, rows, d_model, width, hidden, tile, size_f, first_cols = dims
    head = lax.axis_index("head")
    chunks = rows // tile
    part_rows = rows // heads
    per_part = part_rows // tile
    (down,) = make_scatters(ny, [(down_v, pl.ds(0, first_cols))], scratch)
    own_rows = pl.ds(pl.multiple_of(head * part_rows, part_rows), part_rows)

    def load(src, dst, i):
        return pltpu.make_async_copy(src, dst, in_sem.at[i])

    loads = [load(context_all, ctx_v, 0), load(full_out, wo, 1), load(tokens, x_v, 2), load(full_qkv.at[:, pl.ds(0, 128)], norm_v, 3),
             load(full_up, wu, 4), load(cotangent, cot_v, 5), load(full_down, wd, 6)]
    for item in loads:
        item.start()
    half = tile // 2

    def place_of(i):
        whole_tile = not isinstance(i, int)
        number = 0 if not whole_tile and i == chunks else i
        step = number // per_part + 1
        within = number % per_part * tile
        size = tile if whole_tile or 0 < i < chunks else half
        within = within + (half if not whole_tile and i == 0 else 0)
        return step, within, size

    def rows_of(i):
        step, within, size = place_of(i)
        return pl.ds(pl.multiple_of((head + step) % heads * part_rows + within, half), size)

    def x_copy(i, step):
        _, within, size = place_of(i)
        return remote(low.at[rows_of(i)], arrived.at[step - 1, pl.ds(within, size)], x_send.at[i], x_recv.at[i],
                      {"head": (head + step) % heads})

    def g_copy(j, step):
        to = (head + step) % heads
        at = pl.ds(j * tile, tile)
        there = pl.ds(pl.multiple_of(head * part_rows + j * tile, tile), tile)
        return remote(gctx_v.at[at, pl.ds(pl.multiple_of(to * width, width), width)], grad_context.at[there],
                      g_send.at[j, step - 1], g_recv.at[j, step - 1], {"head": to})

    greet_all(ny, heads)
    for item in loads[:4]:
        item.wait()
    norms = norm_v[...].astype(F32).T
    gain, shift = norms[2:3], norms[3:4]

    def hat_of(value):
        centre = value - jnp.mean(value, axis=1, keepdims=True)
        spread = lax.rsqrt(jnp.mean(centre * centre, axis=1, keepdims=True) + 1e-05)
        return centre * spread, spread

    norm_two[...] = jnp.zeros_like(norm_two)

    def forward_and_back(i, early=False):
        at = rows_of(i)
        value = x_v[at].astype(F32) + dot(ctx_v[at], wo[...], 1, 1)
        resid[at] = value
        n2[at] = (hat_of(value)[0] * gain + shift).astype(LOW)
        if early:
            loads[4].wait()
        for f in range(hidden // size_f):
            cols = slice(f * size_f, (f + 1) * size_f)
            u = dot(n2[at], wu[:, cols], 1, 0)
            if early and f == 0:
                loads[5].wait()
                loads[6].wait()
            ga = dot(cot_v[at], wd[:, cols], 1, 0)
            phi = 0.5 + 0.5 * lax.erf(u * (0.5 ** 0.5))
            act[at, cols] = (u * phi).astype(LOW)
            gu[at, cols] = (ga * (phi + u * (jnp.exp(u * u * -0.5) * 0.3989422804014327))).astype(LOW)
        total = dot(gu[at], wu[...], 1, 1)
        part[at] = total
        low[at] = total.astype(LOW)

    def sums(i):
        at = rows_of(i)
        total = part[at]
        hat, _ = hat_of(resid[at])
        norm_two[0:1] += jnp.sum(total * hat, axis=0, keepdims=True)
        norm_two[1:2] += jnp.sum(total, axis=0, keepdims=True)

    if heads > 1:
        forward_and_back(chunks, True)
        x_copy(chunks, 1).start()
        forward_and_back(0)
        x_copy(0, 1).start()
        for step in range(1, heads):
            first = (step - 1) * per_part

            @pl.loop(max(first, 1), first + per_part)
            def _(i):
                forward_and_back(i)
                x_copy(i, step).start()

    else:
        forward_and_back(chunks, True)
        forward_and_back(0)

    @pl.loop(max(chunks - per_part, 1), chunks)
    def _(i):
        forward_and_back(i)

    def weight_grad(src, other, dst, count):
        per_z = d_model // ZS
        for f in range(count // size_f):
            cols = slice(f * size_f, (f + 1) * size_f)

            @pl.loop(0, ZS // 2)
            def _(j):
                at = pl.ds(pl.multiple_of(j * 2 * per_z, 2 * per_z), 2 * per_z)
                value = dot(src[:, at], other[:, cols], 0, 0).astype(LOW)
                dst[pl.ds(2 * j, 2), :, :, :, cols] = value.reshape(2, *dst.shape[1:4], size_f)

    weight_grad(cot_v, act, down_v, hidden)
    down.begin()

    def own_store(j):
        at = pl.ds(j * tile, tile)
        there = pl.ds(pl.multiple_of(head * part_rows + j * tile, tile), tile)
        return (pltpu.make_async_copy(part.at[there], resid_grad.at[at], out_sem.at[3 + 2 * j]),
                pltpu.make_async_copy(gctx_v.at[at, pl.ds(pl.multiple_of(head * width, width), width)], grad_context.at[there],
                                      out_sem.at[4 + 2 * j]))

    for j in range(per_part):
        at = pl.ds(pl.multiple_of(head * part_rows + j * tile, tile), tile)
        total = part[at]
        for step in range(1, heads):
            i = (step - 1) * per_part + j
            x_copy(i, step).wait_recv()
            if i == 0:
                x_copy(chunks, step).wait_recv()
            total += arrived[step - 1, j * tile:(j + 1) * tile].astype(F32)
        hat, spread = hat_of(resid[at])
        own_part = part[at]
        norm_two[0:1] += jnp.sum(own_part * hat, axis=0, keepdims=True)
        norm_two[1:2] += jnp.sum(own_part, axis=0, keepdims=True)
        scaled = total * gain
        inner = scaled - jnp.mean(scaled, axis=1, keepdims=True) - hat * jnp.mean(scaled * hat, axis=1, keepdims=True)
        total = cot_v[at].astype(F32) + inner * spread
        part[at] = total
        rounded = total.astype(LOW)
        low[at] = rounded
        gctx_v[j * tile:(j + 1) * tile] = dot(rounded, wo[...], 1, 0).astype(LOW)
        for step in range(1, heads):
            g_copy(j, step).start()
        for item in own_store(j):
            item.start()
    down.one()
    weight_grad(n2, gu, up_v, hidden)
    stores = [pltpu.make_async_copy(up_v, parts_up, out_sem.at[0]), pltpu.make_async_copy(down_v, parts_down, out_sem.at[1]),
              pltpu.make_async_copy(out_v, parts_out, out_sem.at[2])]
    for item in stores[:2]:
        item.start()
    down.two()
    weight_grad(low.at[own_rows], ctx_v.at[own_rows], out_v, d_model)
    stores[2].start()

    def slot_copies(i):
        at = pl.ds(pl.multiple_of(i * tile, tile), tile)
        slot = i % 2
        return (pltpu.make_async_copy(base_v.at[slot], base.at[at], slot_sem.at[0, slot]),
                pltpu.make_async_copy(mlp_v.at[slot], mlp_low.at[at], slot_sem.at[1, slot]))

    def slot_loop(i):
        at = pl.ds(pl.multiple_of(i * tile, tile), tile)
        value = dot(act[at], wd[...], 1, 1)

        @pl.when(i >= 2)
        def _():
            for item in slot_copies(i - 2):
                item.wait()

        base_v[i % 2] = (resid[at] + value).astype(LOW)
        mlp_v[i % 2] = value.astype(LOW)
        for item in slot_copies(i):
            item.start()

    pl.loop(0, chunks)(slot_loop)
    if heads > 1:
        sums(chunks)
        sums(0)
        pl.loop(1, chunks - per_part)(sums)
    for i in range(max(0, chunks - 2), chunks):
        for item in slot_copies(i):
            item.wait()
    down.three(mine_down)
    down.finish()
    for item in stores:
        item.wait()
    for j in range(per_part):
        for item in own_store(j):
            item.wait()
        for step in range(1, heads):
            g_copy(j, step).wait()
    for step in range(1, heads):
        for j in range(per_part):
            x_copy((step - 1) * per_part + j, step).wait_send()
    if heads > 1:
        x_copy(chunks, 1).wait_send()


def shares(hidden):
    n = hidden // 128
    first = max(n // 8, 1)
    return first * 128, (n - first) * 128


def middle(tokens, context_all, cotangent, full_qkv, full_out, full_up, full_down, scenes, heads):
    ny = scenes // ZS
    rows, d_model = tokens.shape
    rl = d_model // (2 * scenes)
    hidden, width = full_up.shape[1], d_model // heads
    tile, size_f = min(256, rows // heads), min(1024, hidden)
    part_rows = rows // heads
    per_part = part_rows // tile
    chunks = rows // tile
    first_cols = shares(hidden)[0]
    others = max(heads - 1, 1)
    sem = pltpu.SemaphoreType.DMA
    shape, vmem = jax.ShapeDtypeStruct, pltpu.VMEM
    any_space, whole = pl.BlockSpec(memory_space=pl.ANY), pl.BlockSpec(memory_space=pltpu.VMEM)
    big, wide, blocks = (rows, d_model), (rows, hidden), (ZS, ny, 2, rl, hidden)
    scratch = [vmem(big, LOW), vmem(big, LOW), vmem(big, LOW), vmem((d_model, 128), LOW), vmem((d_model, d_model), LOW),
               vmem((d_model, hidden), LOW), vmem((d_model, hidden), LOW), vmem(big, LOW), vmem(wide, LOW), vmem(wide, LOW),
               vmem(big, F32), vmem(big, F32), vmem(big, LOW), vmem((others, part_rows, d_model), LOW), vmem(blocks, LOW),
               vmem(blocks, LOW), vmem((ZS, ny, 2, rl, d_model), LOW), vmem((part_rows, d_model), LOW), vmem((2, tile, d_model), LOW),
               vmem((2, tile, d_model), LOW), sem((7,)), sem((3 + 2 * per_part,)), sem((2, 2)), sem((chunks + 1,)),
               sem((chunks + 1,)), sem((per_part, others)), sem((per_part, others))]
    scratch += scatter_scratch(ny, rl, first_cols)
    return pl.pallas_call(
        partial(middle_kernel, (ny, heads, rows, d_model, width, hidden, tile, size_f, first_cols)),
        out_shape=[shape((part_rows, d_model), F32), shape(big, LOW), shape(big, LOW), shape((rows, width), LOW), shape((8, d_model), F32),
                   shape((ZS, ny, 2, rl, d_model), LOW), shape(blocks, LOW), shape(blocks, LOW), shape((rl, first_cols), F32)],
        in_specs=[any_space] * 7,
        out_specs=[any_space] * 4 + [whole] + [any_space] * 3 + [whole],
        scratch_shapes=scratch,
        compiler_params=pltpu.CompilerParams(collective_id=3, has_side_effects=True, vmem_limit_bytes=63 * 2**20),
        cost_estimate=pl.CostEstimate(flops=14 * rows * d_model * hidden, bytes_accessed=50 * 2**20, transcendentals=0),
        name="middle_stage",
    )(tokens, context_all, cotangent, full_qkv, full_out, full_up, full_down)


def backward_kernel(dims, probs, queries, keys, values, grad, context, inverse, parts_out, parts_up, mlp_low,
                    grads_out, mine_out, mine_up, mlp_land,
                    grads, grads_sem,
                    dk_acc, dv_acc, kept, stage, landed, kv_send, kv_recv, m_send, m_recv, *scratch):
    ny, heads, rows, size, pairs, steps_q, halves = dims
    pair, part = pl.program_id(0), pl.program_id(1)
    step = pair * steps_q + part
    total = pairs * steps_q
    block = grad.shape[0]
    z, y, core = place(ny)
    width = parts_out.shape[-1]
    ends = split_cols(width, 2)
    plan = [(parts_out, ends[0])] + [(parts_up, cols) for cols in split_cols(parts_up.shape[-1], halves)] + [(parts_out, ends[1])]
    scatters = make_scatters(ny, plan, scratch)
    targets = [mine_out] + [mine_up] * halves + [mine_out]

    def kv_copy(p, i):
        return remote(stage.at[p, i], landed.at[p, i], kv_send.at[p, i], kv_recv.at[p, i], {"seq": 1 - core})

    head = lax.axis_index("head")

    def mlp_copy(i, step):
        return remote(mlp_low.at[pl.ds(i * (rows // 4), rows // 4)], mlp_land.at[step - 1, pl.ds(i * (rows // 4), rows // 4)],
                      m_send.at[i, step - 1], m_recv.at[i, step - 1], {"head": (head + step) % heads})

    @pl.when(step == 0)
    def _():
        greet_all(ny, heads)
        for i in range(4):
            for j in range(1, heads):
                mlp_copy(i, j).start()
        for item in scatters:
            item.begin()

    slots = 2 * total
    plan_at = [(0.4 + 0.5 * i, 3.4 + 2.3 * i, 5.9 + 2.3 * i) for i in range(len(scatters))]
    events = sorted((plan_at[i][j], i, j + 1) for i in range(len(scatters)) for j in range(3))

    def run(slot_in_step):
        for when, i, what in events:
            slot = min(int(when * min(1.0, slots / 16)), slots)
            if slot == slots or slot % 2 != slot_in_step:
                continue

            @pl.when(step == slot // 2)
            def _():
                if what == 1:
                    scatters[i].one()
                elif what == 2:
                    scatters[i].two()
                else:
                    scatters[i].three(targets[i])

    @pl.when(part == 0)
    def _():
        dk_acc[...] = jnp.zeros_like(dk_acc)
        dv_acc[...] = jnp.zeros_like(dv_acc)

    upper = grad[...].astype(F32)
    inner = (upper * context[...].astype(F32)).T
    upper_t = upper.T
    row = lax.broadcasted_iota(jnp.int32, upper_t.shape, 0)
    keys_t = keys[...].T
    pieces = []
    for h in range(2):
        run(h)
        over = inverse[0, h:h + 1]
        shift = jnp.sum(inner[h * size:(h + 1) * size], axis=0, keepdims=True) * over
        scaled = jnp.where(row // size == h, upper_t * over, 0.0)
        dp = dot(values[...], scaled.astype(LOW), 1, 0) - shift
        low = probs[h]
        ds = (low.astype(F32) * dp).astype(LOW)
        dv_acc[...] += dot(low, scaled.T.astype(LOW), 1, 0)
        dk_acc[...] += dot(ds, only_head(queries[...], h, size), 1, 0)
        pieces.append(dot(keys_t, ds, 1, 0)[h * size:(h + 1) * size])
    grads[pl.ds(pl.multiple_of(part * block, block), block), pl.ds(pl.multiple_of(pair * 6 * size, 2 * size), 2 * size)] = (
        (jnp.concatenate(pieces, axis=0) * size ** -0.5).T.astype(LOW))

    @pl.when(part == steps_q - 1)
    def _():
        for i, acc in enumerate((dk_acc, dv_acc)):
            stage[pair, i] = acc[rows:].astype(LOW)
            kv_copy(pair, i).start()
            kept[pair, i] = acc[:rows]

    @pl.when(step == total - 1)
    def _():
        for when, i, what in events:
            if min(int(when * min(1.0, slots / 16)), slots) == slots:
                if what == 1:
                    scatters[i].one()
                elif what == 2:
                    scatters[i].two()
                else:
                    scatters[i].three(targets[i])
        for item in scatters:
            item.finish()
        for p in range(pairs):
            for i in range(2):
                kv_copy(p, i).wait()
                grads[:, (3 * p + i + 1) * 2 * size:(3 * p + i + 2) * 2 * size] = (kept[p, i] + landed[p, i].astype(F32)).astype(LOW)
        store = pltpu.make_async_copy(grads, grads_out, grads_sem)
        store.start()
        for i in range(4):
            for j in range(1, heads):
                mlp_copy(i, j).wait()
        store.wait()


def backward(probs, q, k, v, grad, context, inverse, parts_out, parts_up, mlp_low, scenes, heads, size):
    ny = scenes // ZS
    rows, width = q.shape
    pairs = width // (2 * size)
    block = min(512, rows)
    d_model, hidden = parts_out.shape[-1], parts_up.shape[-1]
    rl = d_model // (2 * scenes)
    others = max(heads - 1, 1)
    halves = 4
    spec = pl.BlockSpec
    q_spec = spec((block, 2 * size), lambda p, i: (i, p))
    k_spec = spec((2 * rows, 2 * size), lambda p, i: (0, p))
    any_space = spec(memory_space=pl.ANY)
    whole = spec(memory_space=pltpu.VMEM)
    shape = jax.ShapeDtypeStruct
    sem = pltpu.SemaphoreType.DMA
    pair_buf = (pairs, 2, rows, 2 * size)
    scratch = [pltpu.VMEM((rows, 3 * width), LOW), sem, pltpu.VMEM((2 * rows, 2 * size), F32), pltpu.VMEM((2 * rows, 2 * size), F32), pltpu.VMEM(pair_buf, F32),
               pltpu.VMEM(pair_buf, LOW), pltpu.VMEM(pair_buf, LOW), sem((pairs, 2)), sem((pairs, 2)), sem((4, others)), sem((4, others))]
    for cols in [d_model // 2] + [hidden // halves] * halves + [d_model // 2]:
        scratch += scatter_scratch(ny, rl, cols)
    return pl.pallas_call(
        partial(backward_kernel, (ny, heads, rows, size, pairs, rows // block, halves)),
        grid=(pairs, rows // block),
        out_shape=[shape((rows, 3 * width), LOW), shape((rl, d_model), F32), shape((rl, hidden), F32), shape((others, rows, d_model), LOW)],
        in_specs=[spec((2, 2 * rows, block), lambda p, i: (p, 0, i)), q_spec, k_spec, k_spec, q_spec, q_spec,
                  spec((1, 8, block), lambda p, i: (p, 0, i)), any_space, any_space, any_space],
        out_specs=[any_space, whole, whole, any_space],
        scratch_shapes=scratch,
        compiler_params=pltpu.CompilerParams(collective_id=1, has_side_effects=True, vmem_limit_bytes=60 * 2**20),
        cost_estimate=pl.CostEstimate(flops=16 * rows * rows * width, bytes_accessed=50 * 2**20, transcendentals=0),
        name="backward_attention",
    )(probs, q, k, v, grad, context, inverse, parts_out, parts_up, mlp_low)


def thirds(start, count):
    n = count // 128
    edges = [start + n * i // 3 * 128 for i in range(4)]
    return [(a, b - a) for a, b in zip(edges, edges[1:])]


def last_kernel(dims, grads, n1, tokens, resid, full_qkv, norm_two, parts_down, down_a, out_all,
                own_grad, done_land, mine_w, mine_norm, mine_out, mine_down,
                g_v, n1_v, x_v, res_v, w_v, in_sem,
                part_one, part_low, arrived, parts_qkv, tiny_land, tiny_own, done_low, x_send, x_recv, t_send, t_recv,
                n_send, n_recv, o_send, o_recv, out_sem, mine_qkv, out_land, *scratch):
    ny, heads, rows, d_model, width, tile, down_at, qkv_at = dims
    z, y, core = place(ny)
    head = lax.axis_index("head")
    wide = full_qkv.shape[1]
    rl = mine_qkv.shape[0]
    plan = [(parts_down, pl.ds(*item)) for item in down_at] + [(parts_qkv, pl.ds(*item)) for item in qkv_at]
    scatters = make_scatters(ny, plan, scratch)
    downs, qkvs = scatters[:len(down_at)], scatters[len(down_at):]
    down_x, down_y, down_z = downs

    def down_done(i):
        downs[i].three(mine_down.at[:, pl.ds(*down_at[i])], True)

    chunks = rows // tile
    part_rows = rows // heads
    per_part = part_rows // tile
    loads = [pltpu.make_async_copy(src, dst, in_sem.at[i]) for i, (src, dst) in enumerate((
        (grads, g_v), (full_qkv, w_v), (n1, n1_v), (tokens, x_v), (resid, res_v)))]
    for item in loads:
        item.start()
    def rows_at(step, j):
        return pl.ds(pl.multiple_of((head + heads + step) % heads * part_rows + j * tile, tile), tile)

    def x_copy(step, j):
        return remote(part_low.at[rows_at(step, j)], arrived.at[step - 1, pl.ds(j * tile, tile)], x_send.at[step - 1, j],
                      x_recv.at[step - 1, j], {"head": (head + step) % heads})

    def t_copy(step, j):
        at = pl.ds(j * tile, tile)
        return remote(done_low.at[at], done_land.at[step - 1, at], t_send.at[step - 1, j], t_recv.at[step - 1, j],
                      {"head": (head + step) % heads})

    def n_copy(step):
        return remote(tiny_own, tiny_land.at[step - 1], n_send.at[step - 1], n_recv.at[step - 1], {"head": (head + step) % heads})

    def o_copy(step):
        to = (head + step) % heads
        return remote(out_all.at[:, pl.ds(pl.multiple_of(to * width, width), width)], out_land.at[step - 1], o_send.at[step - 1],
                      o_recv.at[step - 1], {"head": to})

    def out_copy(j):
        at = pl.ds(j * tile, tile)
        return pltpu.make_async_copy(done_low.at[at], own_grad.at[at], out_sem.at[j])

    greet_all(ny, heads)
    for item in downs:
        item.begin()
    for item in loads[:2]:
        item.wait()

    def partial_sum(step, j):
        at = rows_at(step, j)
        total = dot(g_v[at], w_v[:, 128:], 1, 1)
        part_one[at] = total
        part_low[at] = total.astype(LOW)

    for step in range(1, heads):
        for j in range(per_part):
            partial_sum(step, j)
            x_copy(step, j).start()
    for step in range(1, heads):
        o_copy(step).start()
    down_x.one()
    down_y.one()
    for j in range(per_part):
        partial_sum(0, j)
    for item in loads[2:]:
        item.wait()
    per_z = d_model // ZS
    for zz in range(0, ZS, 2):
        cols = n1_v[:, zz * per_z:(zz + 2) * per_z]
        value = dot(cols, g_v[...], 0, 0).astype(LOW)
        parts_qkv[zz:zz + 2, :, :, :, 128:] = value.reshape(2, ny, 2, rl, 3 * width)
    for item in qkvs[1:]:
        item.begin()
    gain = w_v[:, :128].astype(F32).T[0:1]

    def hat_of(at):
        x = x_v[at].astype(F32)
        centre = x - jnp.mean(x, axis=1, keepdims=True)
        spread = lax.rsqrt(jnp.mean(centre * centre, axis=1, keepdims=True) + 1e-05)
        return centre * spread, spread

    gain_sum = jnp.zeros((1, d_model), F32)
    shift_sum = jnp.zeros((1, d_model), F32)
    for i in range(chunks):
        at = pl.ds(i * tile, tile)
        hat, _ = hat_of(at)
        gain_sum += jnp.sum(part_one[at] * hat, axis=0, keepdims=True)
        shift_sum += jnp.sum(part_one[at], axis=0, keepdims=True)
        if i == chunks // 4:
            qkvs[1].one()
            down_x.two()
        if i == chunks // 2:
            qkvs[2].one()
    sums = jnp.concatenate([gain_sum, shift_sum, norm_two[0:2], jnp.zeros((124, d_model), F32)], axis=0).T.astype(LOW)
    parts_qkv[:, :, :, :, :128] = sums.reshape(ZS, ny, 2, rl, 128)
    qkvs[0].begin()

    def receive(j):
        at = rows_at(0, j)
        here = pl.ds(j * tile, tile)
        total = part_one[at]
        for step in range(1, heads):
            x_copy(step, j).wait_recv()
            total += arrived[step - 1, here].astype(F32)
        hat, spread = hat_of(at)
        scaled = total * gain
        inner = scaled - jnp.mean(scaled, axis=1, keepdims=True) - hat * jnp.mean(scaled * hat, axis=1, keepdims=True)
        total = res_v[here] + inner * spread
        done_low[here] = total.astype(LOW)
        out_copy(j).start()
        for step in range(1, heads):
            t_copy(step, j).start()

    first = pl.ds(pl.multiple_of(head * width, width), width)

    def share(items, i, n):
        return items[len(items) * i // n:len(items) * (i + 1) // n]

    def receive_some(i):
        for j in share(range(per_part), i, 4):
            receive(j)

    def send_norms():
        tiny_own[...] = mine_qkv[:, :128]
        for step in range(1, heads):
            n_copy(step).start()

    receive_some(0)
    qkvs[0].one()
    down_z.one()
    down_y.two()
    receive_some(1)
    mine_down[:, :down_a.shape[1]] = down_a[...]
    down_done(0)
    receive_some(2)
    qkvs[1].two()
    down_done(1)
    receive_some(3)
    qkvs[2].two()
    qkvs[1].three(mine_qkv)
    total = out_all[:, first]
    for step in range(1, heads):
        o_copy(step).wait()
        total += out_land[step - 1]
    mine_out[...] = total
    qkvs[0].two()
    qkvs[2].three(mine_qkv)
    down_z.two()
    qkvs[0].three(mine_qkv)
    send_norms()
    down_done(2)
    total = mine_qkv[:, :128]
    for step in range(1, heads):
        n_copy(step).wait()
        total += tiny_land[step - 1]
    mine_norm[...] = total.T[:8]
    for p in range(width // 128):
        for c in range(3):
            mine_w[c, :, p * 128:(p + 1) * 128] = mine_qkv[:, 128 * (3 * p + c + 1):128 * (3 * p + c + 2)]
    for item in scatters:
        item.finish()
    for j in range(per_part):
        out_copy(j).wait()
        for step in range(1, heads):
            x_copy(step, j).wait_send()
            t_copy(step, j).wait()


def last_stage(grads, n1, tokens, resid, full_qkv, norm_two, parts_down, down_a, out_all, scenes, heads):
    ny = scenes // ZS
    rows, d_model = tokens.shape
    width, hidden = grads.shape[1] // 3, parts_down.shape[-1]
    first, third = shares(hidden)
    rl = d_model // (2 * scenes)
    wide = full_qkv.shape[1]
    part_rows = rows // heads
    tile = min(128, part_rows)
    chunks, per_part = rows // tile, part_rows // tile
    down_at, qkv_at = thirds(first, third), thirds(0, wide)
    others = max(heads - 1, 1)
    sem = pltpu.SemaphoreType.DMA
    shape, vmem = jax.ShapeDtypeStruct, pltpu.VMEM
    any_space, whole = pl.BlockSpec(memory_space=pl.ANY), pl.BlockSpec(memory_space=pltpu.VMEM)
    big, own = (rows, d_model), (part_rows, d_model)
    scratch = [vmem((rows, 3 * width), LOW), vmem(big, LOW), vmem(big, LOW), vmem(own, F32), vmem((d_model, wide), LOW), sem((5,)),
               vmem(big, F32), vmem(big, LOW), vmem((others, *own), LOW), vmem((ZS, ny, 2, rl, wide), LOW), vmem((others, rl, 128), F32),
               vmem((rl, 128), F32), vmem(own, LOW), sem((others, per_part)),
               sem((others, per_part)), sem((others, per_part)), sem((others, per_part)), sem((others,)), sem((others,)),
               sem((others,)), sem((others,)), sem((per_part,)), vmem((rl, wide), F32), vmem((others, rl, width), F32)]
    for _, cols in down_at + qkv_at:
        scratch += scatter_scratch(ny, rl, cols)
    return pl.pallas_call(
        partial(last_kernel, (ny, heads, rows, d_model, width, tile, down_at, qkv_at)),
        out_shape=[shape(own, LOW), shape((others, *own), LOW), shape((3, rl, width), F32), shape((8, rl), F32), shape((rl, width), F32),
                   shape((rl, hidden), F32)],
        in_specs=[any_space] * 5 + [whole, any_space, whole, whole],
        out_specs=[any_space, any_space, whole, whole, whole, whole],
        scratch_shapes=scratch,
        compiler_params=pltpu.CompilerParams(collective_id=2, has_side_effects=True, vmem_limit_bytes=63 * 2**20),
        cost_estimate=pl.CostEstimate(flops=12 * rows * d_model * width, bytes_accessed=30 * 2**20, transcendentals=0),
        name="last_stage",
    )(grads, n1, tokens, resid, full_qkv, norm_two, parts_down, down_a, out_all)


def finish_kernel(heads, tile, base, mlp_land, own, land, w, out, up, down, norm,
                  output, tokens_grad, w_o, out_o, up_o, down_o, n_a, n_b, n_c, n_d,
                  sum_v, base_v, own_v, mlp_v, grad_v, land_v, w_v, out_v, up_v, down_v, base_sem, mlp_sem, own_sem, land_sem, small_sem,
                  out_sem, back_sem, far_sem, last_sem):
    rows = base.shape[0]
    part_rows = rows // heads
    chunks, per_part = rows // tile, part_rows // tile
    head = lax.axis_index("head")
    copy = pltpu.make_async_copy

    def rows_at(step, j):
        return pl.ds(pl.multiple_of((head + heads - step) % heads * part_rows + j * tile, tile), tile)

    def loads(i):
        at = pl.ds(i * tile, tile)
        return copy(base.at[at], base_v.at[at], base_sem.at[i]), copy(mlp_land.at[:, at], mlp_v.at[:, at], mlp_sem.at[i])

    def own_load(j):
        at = pl.ds(j * tile, tile)
        return copy(own.at[at], own_v.at[at], own_sem.at[j])

    land_load = copy(land, land_v, land_sem.at[0])
    smalls = ((w, w_v, w_o), (out, out_v, out_o), (up, up_v, up_o), (down, down_v, down_o))
    small_loads = [copy(src, mid, small_sem.at[i]) for i, (src, mid, _) in enumerate(smalls)]
    small_stores = [copy(mid, dst, last_sem.at[i]) for i, (_, mid, dst) in enumerate(smalls)]

    def out_store(i):
        at = pl.ds(i * tile, tile)
        return copy(sum_v.at[at], output.at[at], out_sem.at[i])

    def own_store(j):
        return copy(grad_v.at[rows_at(0, j)], tokens_grad.at[rows_at(0, j)], back_sem.at[j])

    def far_store(step, j):
        return copy(grad_v.at[rows_at(step, j)], tokens_grad.at[rows_at(step, j)], far_sem.at[step - 1, j])

    for j in range(per_part):
        own_load(j).start()
    if heads > 1:
        land_load.start()
    for i in range(chunks):
        for item in loads(i):
            item.start()
    for item in small_loads:
        item.start()
    for i, dst in enumerate((n_a, n_b, n_c, n_d)):
        dst[...] = norm[i:i + 1]
    for j in range(per_part):
        own_load(j).wait()
        grad_v[rows_at(0, j)] = own_v[j * tile:(j + 1) * tile].astype(F32)
        own_store(j).start()
    if heads > 1:
        land_load.wait()
        for step in range(1, heads):
            for j in range(per_part):
                grad_v[rows_at(step, j)] = land_v[step - 1, j * tile:(j + 1) * tile].astype(F32)
                far_store(step, j).start()
    for i in range(chunks):
        at = pl.ds(i * tile, tile)
        for item in loads(i):
            item.wait()
        total = base_v[at].astype(F32)
        for step in range(1, heads):
            total += mlp_v[step - 1, at].astype(F32)
        sum_v[at] = total
        out_store(i).start()
    for first, second in zip(small_loads, small_stores):
        first.wait()
        second.start()
    for j in range(per_part):
        own_store(j).wait()
        for step in range(1, heads):
            far_store(step, j).wait()
    for i in range(chunks):
        out_store(i).wait()
    for item in small_stores:
        item.wait()


def finish(base, mlp_land, own, land, w, out, up, down, norm, heads):
    rows, d_model = base.shape
    part_rows = rows // heads
    tile = min(128, part_rows)
    chunks, per_part = rows // tile, part_rows // tile
    rl, others = up.shape[0], max(heads - 1, 1)
    spec, shape, vmem, sem = pl.BlockSpec, jax.ShapeDtypeStruct, pltpu.VMEM, pltpu.SemaphoreType.DMA
    any_space, whole = spec(memory_space=pl.ANY), spec(memory_space=pltpu.VMEM)
    return pl.pallas_call(
        partial(finish_kernel, heads, tile),
        in_specs=[any_space] * 8 + [whole],
        out_specs=[any_space] * 6 + [whole] * 4,
        out_shape=[shape((rows, d_model), F32), shape((rows, d_model), F32)] + [shape(a.shape, F32) for a in (w, out, up, down)]
        + [shape((1, rl), F32)] * 4,
        scratch_shapes=[vmem(base.shape, F32), vmem(base.shape, LOW), vmem(own.shape, LOW), vmem(mlp_land.shape, LOW), vmem(base.shape, F32), vmem(land.shape, LOW)]
        + [vmem(a.shape, F32) for a in (w, out, up, down)]
        + [sem((chunks,)), sem((chunks,)), sem((per_part,)), sem((1,)), sem((4,)), sem((chunks,)), sem((per_part,)),
           sem((others, per_part)), sem((4,))],
        compiler_params=pltpu.CompilerParams(vmem_limit_bytes=63 * 2**20),
        name="finish",
    )(base, mlp_land, own, land, w, out, up, down, norm)


def on_device(n_scene, n_head, tokens, counts, w_qkv, w_out, w_up, w_down, gain_one, shift_one, gain_two, shift_two, cotangent):
    rows, d_model = tokens.shape
    width, hidden = w_qkv.shape[2], w_up.shape[1]
    size = 64
    n1, q, k, v, full_qkv, full_out, full_up, full_down, probs, context, context_all, inverse = forward(
        counts, (gain_one, shift_one, gain_two, shift_two), w_qkv, w_out.T, w_up, w_down.T, tokens, n_scene, n_head, size)
    grad_resid, base, mlp_low, grad_context, norm_two, grad_outproj, grad_up, grad_down, down_a = middle(
        tokens, context_all, cotangent, full_qkv, full_out, full_up, full_down, n_scene, n_head)
    grads, out_all, mine_up, mlp_land = backward(
        probs, q, k, v, grad_context, context, inverse, grad_outproj, grad_up, mlp_low, n_scene, n_head, size)
    own, land, mine_qkv, norms, mine_out, mine_down = last_stage(
        grads, n1, tokens, grad_resid, full_qkv, norm_two, grad_down, down_a, out_all, n_scene, n_head)
    output, tokens_grad, mine_qkv, mine_out, mine_up, mine_down, *norms = finish(
        base, mlp_land, own, land, mine_qkv, mine_out, mine_up, mine_down, norms, n_head)
    return (output, tokens_grad, mine_qkv, mine_out.T, mine_up, mine_down.T, *[a.reshape(-1) for a in norms])


def solution(mesh):
    rows, both = ("scene", "seq"), P(("scene", "seq"))
    weights = (P(None, rows, "head"), P("head", rows), P(rows, "head"), P("head", rows), both, both, both, both)
    return jax.shard_map(
        partial(on_device, mesh.shape["scene"], mesh.shape["head"]), mesh=mesh,
        in_specs=(P(rows, None), P("scene"), *weights, P(rows, None)),
        out_specs=(P(rows, None), P(rows, None), *weights),
        check_vma=False,
    )
```

```python
from functools import partial

import jax
import jax.numpy as jnp
from jax import lax
from jax.experimental import pallas as pl
from jax.experimental.pallas import tpu as pltpu
from jax.sharding import PartitionSpec as P

MESH = pl.DeviceIdType.MESH
ZS = 4


def place(ny):
    scene = lax.axis_index("scene")
    return scene // ny, scene % ny, lax.axis_index("seq")


def remote(src, dst, send_sem, recv_sem, device):
    return pltpu.make_async_remote_copy(
        src_ref=src, dst_ref=dst, send_sem=send_sem, recv_sem=recv_sem,
        device_id=device, device_id_type=MESH,
    )


F32 = jnp.float32
LOW = jnp.bfloat16


def dot(a, b, ca, cb):
    return lax.dot_general(a, b, (((ca,), (cb,)), ((), ())), preferred_element_type=F32)


def only_head(x, h, size):
    lane = lax.broadcasted_iota(jnp.int32, x.shape, 1)
    return jnp.where(lane // size == h, x, jnp.zeros_like(x))


class Gather:
    def __init__(self, ny, source, full, cols, sems):
        self.ny, self.source, self.full, self.cols = ny, source, full, cols
        self.rsend, self.rrecv, self.lsend, self.lrecv, self.ysend, self.yrecv, self.csend, self.crecv = sems
        self.z, self.y, self.core = place(ny)

    def at(self, zz, yy):
        return self.full.at[zz, yy, self.core, :, self.cols]

    def right(self, k):
        src = self.source() if k == 0 else self.at(self.z - k, self.y)
        dst = self.at(self.z - k, self.y)
        return remote(src, dst, self.rsend.at[k], self.rrecv.at[k], {"scene": (self.z + 1) * self.ny + self.y})

    def left(self, k):
        src = self.source() if k == 0 else self.at(self.z + k, self.y)
        dst = self.at(self.z + k, self.y)
        return remote(src, dst, self.lsend.at[k], self.lrecv.at[k], {"scene": (self.z - 1) * self.ny + self.y})

    def across(self, zz, step, own=False):
        src = self.source() if own else self.at(zz, self.y)
        peer = self.z * self.ny + (self.y + step) % self.ny
        return remote(src, self.at(zz, self.y), self.ysend.at[step - 1], self.yrecv.at[step - 1], {"scene": peer})

    def arrival(self, zz, step):
        yy = (self.y + self.ny - step) % self.ny
        return remote(self.at(zz, yy), self.at(zz, yy), self.ysend.at[step - 1], self.yrecv.at[step - 1],
                      {"scene": self.z * self.ny + yy})

    def twin(self, zz, step, own=False):
        src = self.source() if own else self.at(zz, (self.y + self.ny - step) % self.ny)
        dst = self.at(zz, (self.y + self.ny - step) % self.ny)
        return remote(src, dst, self.csend.at[0], self.crecv.at[0], {"seq": 1 - self.core})

    def column(self, step):
        yy = (self.y + self.ny - step) % self.ny
        all_z = self.full.at[:, yy, self.core, :, self.cols]
        return remote(all_z, all_z, self.ysend.at[step - 1], self.yrecv.at[step - 1], {"scene": self.z * self.ny + yy})

    def twins(self):
        mine, theirs = [self.full.at[:, :, c, :, self.cols] for c in (self.core, 1 - self.core)]
        return [remote(item, item, self.csend.at[0], self.crecv.at[0], {"seq": 1 - self.core}) for item in (mine, theirs)]

    def begin(self):
        @pl.when(self.z < ZS - 1)
        def _():
            self.right(0).start()

        @pl.when(self.z > 0)
        def _():
            self.left(0).start()

        for step in range(1, self.ny):
            self.across(self.z, step, True).start()
        self.twin(self.z, 0, True).start()

    def hop(self, k):
        @pl.when(self.z >= k)
        def _():
            self.right(k - 1).wait_recv()
            if k < ZS - 1:
                @pl.when(self.z < ZS - 1)
                def _():
                    self.right(k).start()
            for step in range(1, self.ny):
                self.across(self.z - k, step).start()
            self.twin(self.z - k, 0).start()

        @pl.when(self.z + k < ZS)
        def _():
            self.left(k - 1).wait_recv()
            if k < ZS - 1:
                @pl.when(self.z > 0)
                def _():
                    self.left(k).start()
            for step in range(1, self.ny):
                self.across(self.z + k, step).start()
            self.twin(self.z + k, 0).start()

    def spread(self):
        for step in range(1, self.ny):
            self.column(step).wait_recv()
            for zz in range(ZS):
                self.twin(zz, step).start()

    def finish(self):
        for k in range(ZS - 1):
            @pl.when((self.z < ZS - 1) & (self.z >= k))
            def _():
                self.right(k).wait_send()

            @pl.when((self.z > 0) & (self.z + k < ZS))
            def _():
                self.left(k).wait_send()
        for step in range(1, self.ny):
            self.column(step).wait_send()
        mine, theirs = self.twins()
        mine.wait_send()
        theirs.wait_recv()


class PairGather(Gather):
    def row(self, zz):
        return self.full.at[zz, :, self.core, :, self.cols]

    def right(self, k):
        return remote(self.row(self.z - k), self.row(self.z - k), self.rsend.at[k], self.rrecv.at[k],
                      {"scene": (self.z + 1) * self.ny + self.y})

    def left(self, k):
        return remote(self.row(self.z + k), self.row(self.z + k), self.lsend.at[k], self.lrecv.at[k],
                      {"scene": (self.z - 1) * self.ny + self.y})

    def twin(self, zz):
        return remote(self.row(zz), self.row(zz), self.csend.at[0], self.crecv.at[0], {"seq": 1 - self.core})

    def begin(self):
        for step in range(1, self.ny):
            self.across(self.z, step, True).start()

    def pair(self):
        for step in range(1, self.ny):
            self.arrival(self.z, step).wait_recv()

        @pl.when(self.z < ZS - 1)
        def _():
            self.right(0).start()

        @pl.when(self.z > 0)
        def _():
            self.left(0).start()

        self.twin(self.z).start()

    def hop(self, k):
        @pl.when(self.z >= k)
        def _():
            self.right(k - 1).wait_recv()
            if k < ZS - 1:
                @pl.when(self.z < ZS - 1)
                def _():
                    self.right(k).start()
            self.twin(self.z - k).start()

        @pl.when(self.z + k < ZS)
        def _():
            self.left(k - 1).wait_recv()
            if k < ZS - 1:
                @pl.when(self.z > 0)
                def _():
                    self.left(k).start()
            self.twin(self.z + k).start()

    def finish(self):
        for k in range(ZS - 1):
            @pl.when((self.z < ZS - 1) & (self.z >= k))
            def _():
                self.right(k).wait_send()

            @pl.when((self.z > 0) & (self.z + k < ZS))
            def _():
                self.left(k).wait_send()
        for step in range(1, self.ny):
            self.across(self.z, step).wait_send()
        mine, theirs = self.twins()
        mine.wait_send()
        theirs.wait_recv()


def gather_sems(ny):
    sem = pltpu.SemaphoreType.DMA
    return [sem((ZS - 1,)), sem((ZS - 1,)), sem((ZS - 1,)), sem((ZS - 1,)), sem((max(ny - 1, 1),)), sem((max(ny - 1, 1),)),
            sem((1,)), sem((1,))]


def greet_all(ny, heads):
    z, y, core = place(ny)
    head = lax.axis_index("head")
    barrier = pltpu.get_barrier_semaphore()

    def signal(device):
        pl.semaphore_signal(barrier, 1, device_id=device, device_id_type=MESH)

    for step in range(1, ZS):
        signal({"scene": (z + step) % ZS * ny + y})
    for step in range(1, ny):
        signal({"scene": z * ny + (y + step) % ny})
    for step in range(1, heads):
        signal({"head": (head + step) % heads})
    signal({"seq": 1 - core})
    pl.semaphore_wait(barrier, ZS + ny - 1 + heads - 1)


def split_cols(total, parts):
    size = total // parts
    return [pl.ds(i * size, size) for i in range(parts)]


def forward_kernel(dims, counts, gain_one, shift_one, gain_two, shift_two, w_qkv, shard_out, shard_up, shard_down, tokens,
                   n1_out, q_out, k_out, v_out, full_qkv, full_out, full_up, full_down, probs, context, context_all, inverse,
                   w0, hat, n1, q_s, k_s, v_s, bias, ctx_s, scores, tops, probs_v, probs_sem, local_sem, kv_send, kv_recv, xw_send, xw_recv, xt_send, xt_recv, xc_send, xc_recv, *sems):
    ny, heads, rows, width, size, block, pairs, steps_q, halves = dims
    pair, part = pl.program_id(0), pl.program_id(1)
    step = pair * steps_q + part
    z, y, core = place(ny)
    head = lax.axis_index("head")
    d_model = tokens.shape[1]
    per = 8
    own_cols = pl.ds(pl.multiple_of(head * width, width), width)

    def of(i):
        return sems[i * per:(i + 1) * per]

    group = 6 * size
    edges = [0] + [128 + (p + 1) * group for p in range(pairs)]
    firsts = []
    for p in range(pairs):
        cols = pl.ds(edges[p], edges[p + 1] - edges[p])
        firsts.append(Gather(ny, partial(lambda c: w0.at[z, y, core, :, c], cols), w0, cols, of(2 + 2 * halves + p)))
    outer = Gather(ny, lambda: shard_out, full_out, own_cols, of(1))
    thick = []
    for n, (shard, full) in enumerate(((shard_up, full_up), (shard_down, full_down))):
        for i, cols in enumerate(split_cols(full_up.shape[-1], halves)):
            kind = PairGather if n == 1 and i == halves - 1 else Gather
            thick.append(kind(ny, partial(lambda s, c: s.at[:, c], shard, cols), full, cols, of(2 + n * halves + i)))
    up_a, up_b, down_a, down_b = thick

    def local(src, dst, i):
        return pltpu.make_async_copy(src, dst, local_sem.at[i])

    def cols_of(step):
        return pl.ds(pl.multiple_of((head + heads - step) % heads * width, width), width)

    def out_copy(step):
        mine = full_out.at[:, :, core, :, own_cols]
        return remote(mine, mine, xw_send.at[step - 1], xw_recv.at[step - 1], {"head": (head + step) % heads})

    def out_twin(step):
        other = full_out.at[:, :, core, :, cols_of(step)]
        return remote(other, other, xt_send.at[step - 1], xt_recv.at[step - 1], {"seq": 1 - core})

    def kv_copy(p, i):
        src = (k_s, v_s)[i]
        cols = pl.ds(p * 2 * size, 2 * size)
        return remote(src.at[pl.ds(0, rows), cols], src.at[pl.ds(rows, rows), cols], kv_send.at[p, i], kv_recv.at[p, i],
                      {"seq": 1 - core})

    def project(p):
        tile = min(256, rows)

        @pl.loop(0, rows // tile)
        def _(i):
            at = pl.ds(pl.multiple_of(i * tile, tile), tile)
            w = w0[:, :, :, :, 128 + p * group:128 + (p + 1) * group].reshape(d_model, group)
            value = dot(n1[at], w, 1, 0).astype(LOW)
            cols = pl.ds(p * 2 * size, 2 * size)
            q_s[at, cols] = value[:, :2 * size] * LOW(size ** -0.5)
            k_s[at, cols] = value[:, 2 * size:4 * size]
            v_s[at, cols] = value[:, 4 * size:]

        for i in range(2):
            kv_copy(p, i).start()

    def ctx_copy(p, step):
        cols = pl.ds(pl.multiple_of(p * 2 * size, 2 * size), 2 * size)
        wide = pl.ds(pl.multiple_of(head * width + p * 2 * size, 2 * size), 2 * size)
        return remote(ctx_s.at[:, cols], context_all.at[:, wide], xc_send.at[p, step - 1], xc_recv.at[p, step - 1],
                      {"head": (head + step) % heads})

    own_blocks = [(shard_out, full_out.at[z, y, core, :, own_cols], 1),
                  (shard_up, full_up.at[z, y, core], 2), (shard_down, full_down.at[z, y, core], 3)]
    results = [(w0, full_qkv, 4), (n1, n1_out, 5), (q_s, q_out, 6), (k_s, k_out, 7), (v_s, v_out, 8)]
    ctx_local = (ctx_s, context_all.at[:, own_cols], 9)

    @pl.when(step == 0)
    def _():
        for item in own_blocks:
            local(*item).start()
        greet_all(ny, heads)
        columns = jnp.concatenate([a[...].astype(F32) for a in (gain_one, shift_one, gain_two, shift_two)]
                                  + [jnp.zeros((124, gain_one.shape[1]), F32)], axis=0)
        w0[z, y, core, :, :128] = columns.T.astype(LOW)
        for p in range(pairs):
            for c in range(3):
                w0[z, y, core, :, 128 * (3 * p + c + 1):128 * (3 * p + c + 2)] = w_qkv[c, :, 128 * p:128 * (p + 1)]
            if p < 2:
                firsts[p].begin()
        tile = min(128, rows)

        @pl.loop(0, rows // tile)
        def _(i):
            at = pl.ds(pl.multiple_of(i * tile, tile), tile)
            x = tokens[at].astype(F32)
            centre = x - jnp.mean(x, axis=1, keepdims=True)
            spread = jnp.mean(centre * centre, axis=1, keepdims=True)
            hat[at] = centre * lax.rsqrt(spread + 1e-05)

        low_rows = lax.broadcasted_iota(jnp.int32, bias.shape, 0)
        lane = lax.broadcasted_iota(jnp.int32, bias.shape, 1)
        limit = jnp.where(low_rows < rows, counts[0] - core * rows, counts[0] - (1 - core) * rows + rows)
        bias[...] = jnp.where((low_rows >= limit) & (lane == 0), -1e30, 0.0).astype(LOW)
        after = [
            (0, lambda g: g.hop(1)), (2, lambda g: g.begin()), (0, lambda g: g.hop(2)), (1, lambda g: g.hop(1)), (0, lambda g: g.hop(3)),
            (3, lambda g: g.begin()), (1, lambda g: g.hop(2)), (0, lambda g: g.spread()), (1, lambda g: g.hop(3)),
            (2, lambda g: g.hop(1)), (1, lambda g: g.spread()), (2, lambda g: g.hop(2))]
        for p, act in after[:9]:
            if p < pairs:
                act(firsts[p])
        firsts[0].finish()
        for item in own_blocks:
            local(*item).wait()
        norms = w0[:, :, :, :, :128].reshape(d_model, 128).astype(F32).T
        gain, shift = norms[0:1], norms[1:2]
        tile = min(256, rows)

        @pl.loop(0, rows // tile)
        def _(i):
            at = pl.ds(pl.multiple_of(i * tile, tile), tile)
            n1[at] = (hat[at] * gain + shift).astype(LOW)

        local(*results[1]).start()
        project(0)
        for p, act in after[9:]:
            if p < pairs:
                act(firsts[p])

    total = pairs * steps_q
    per_slot = 2
    in_step = 4 * rows // min(256, rows) // per_slot
    slots = in_step * total

    def send_out():
        for i in range(1, heads):
            out_copy(i).start()

    def pass_out():
        for i in range(1, heads):
            out_copy(i).wait_recv()
            out_twin(i).start()

    def on_pair(p, what, *given):
        if p < pairs:
            getattr(firsts[p], what)(*given)

    events = [
        (0.1, lambda: on_pair(2, "hop", 3)), (0.3, lambda: on_pair(3, "hop", 1)), (0.4, outer.begin),
        (1, lambda: on_pair(3, "hop", 2)), (1.2, lambda: on_pair(2, "spread")), (1.4, up_a.begin),
        (2, lambda: on_pair(3, "hop", 3)), (2.6, lambda: outer.hop(1)), (3.2, lambda: outer.hop(2)), (3.2, up_b.begin),
        (3.8, lambda: on_pair(3, "spread")), (3.9, lambda: outer.hop(3)), (5.2, lambda: up_a.hop(1)), (6, outer.spread), (6.1, send_out),
        (6.5, lambda: up_a.hop(2)), (7, down_a.begin), (7.2, down_b.begin),
        (7.8, lambda: up_a.hop(3)), (9.2, lambda: up_b.hop(1)), (10.5, lambda: up_b.hop(2)), (10.6, pass_out), (10.8, down_b.pair),
        (11.8, lambda: up_b.hop(3)), (12, up_a.spread), (13.2, lambda: down_a.hop(1)), (14.5, lambda: down_a.hop(2)),
        (15.8, lambda: down_a.hop(3)), (16, up_b.spread), (16, lambda: down_b.hop(1)),
        (16, lambda: down_b.hop(2)), (16, down_a.spread), (16, lambda: down_b.hop(3))]

    def run(slot_in_step):
        for when, act in events:
            slot = min(int(when * slots / 16), slots - 1)
            if when < 16 and slot % in_step == slot_in_step:
                pl.when(step == slot // in_step)(act)

    for p in range(pairs):
        @pl.when(step == p * steps_q)
        def _():
            if p == 0:
                for i in range(2):
                    kv_copy(0, i).wait()
            if p + 1 < pairs:
                firsts[p + 1].finish()
                project(p + 1)
            else:
                for item in (results[0], *results[2:]):
                    local(*item).start()

        if p + 1 < pairs:
            @pl.when(step == (p + 1) * steps_q - 1)
            def _():
                for i in range(2):
                    kv_copy(p + 1, i).wait()

    width2, chunk = 2 * size, min(256, rows)
    n_chunks = 2 * rows // chunk
    ones = (lax.broadcasted_iota(jnp.int32, (block, bias.shape[1]), 1) == 0).astype(LOW)

    def asked(at, h):
        rows_at = pl.ds(pl.multiple_of(at % steps_q * block, block), block)
        cols_at = pl.ds(pl.multiple_of(at // steps_q * width2, width2), width2)
        return jnp.concatenate([only_head(q_s[rows_at, cols_at], h, size), ones], axis=1)

    def score(at, query, slot, c, top):
        cols_at = pl.ds(pl.multiple_of(at // steps_q * width2, width2), width2)
        keys_at = pl.ds(c * chunk, chunk)
        value = dot(jnp.concatenate([k_s[keys_at, cols_at], bias[keys_at]], axis=1), query, 1, 1)
        scores[slot, keys_at] = value
        return jnp.maximum(top, jnp.max(value.reshape(chunk // 8, 8, block), axis=0))

    def weigh(h, c, top, total_e):
        keys_at = pl.ds(c * chunk, chunk)
        expo = jnp.exp(scores[h, keys_at] - top)
        probs_v[slot_now, h, keys_at] = expo.astype(LOW)
        return total_e + jnp.sum(expo.reshape(chunk // 8, 8, block), axis=0)

    slot_now = step % 2

    def probs_copy(at):
        there = pl.ds(pl.multiple_of(at % steps_q * block, block), block)
        return pltpu.make_async_copy(probs_v.at[at % 2], probs.at[pl.ds(at // steps_q * 2, 2), :, there], probs_sem.at[at % 2])

    @pl.when(step >= 2)
    def _():
        probs_copy(step - 2).wait()

    lowest = jnp.full((8, block), -3e38, F32)

    @pl.when(step == 0)
    def _():
        top, query = lowest, asked(0, 0)
        for c in range(n_chunks):
            top = score(0, query, 0, c, top)
        tops[...] = top

    cols = pl.ds(pl.multiple_of(pair * width2, width2), width2)
    following = jnp.minimum(step + 1, total - 1)
    values_t = v_s[:, cols].T
    pieces = []
    for h in range(2):
        top = jnp.max(tops[...], axis=0, keepdims=True)
        total_e, next_top = jnp.zeros((8, block), F32), lowest
        ahead = (step, 1) if h == 0 else (following, 0)
        query = asked(*ahead)
        for c in range(n_chunks):
            if c % per_slot == 0:
                run(h * (n_chunks // per_slot) + c // per_slot)
            next_top = score(ahead[0], query, 1 - h, c, next_top)
            total_e = weigh(h, c, top, total_e)
        tops[...] = next_top
        over = 1.0 / jnp.sum(total_e, axis=0, keepdims=True)
        pieces.append(dot(values_t, probs_v[slot_now, h], 1, 0)[h * size:(h + 1) * size] * over)
        inverse[0, h:h + 1] = over
    here = jnp.concatenate(pieces, axis=0).T.astype(LOW)
    probs_copy(step).start()
    context[...] = here
    ctx_s[pl.ds(pl.multiple_of(part * block, block), block), cols] = here

    @pl.when(part == steps_q - 1)
    def _():
        for i in range(1, heads):
            ctx_copy(pair, i).start()

    @pl.when(step == total - 1)
    def _():
        local(*ctx_local).start()
        for when, act in events:
            if when >= 16:
                act()
        for gather in (outer, *thick):
            gather.finish()
        for item in results:
            local(*item).wait()
        local(*ctx_local).wait()
        for at in range(max(total - 2, 0), total):
            probs_copy(at).wait()
        for i in range(1, heads):
            out_copy(i).wait_send()
            out_twin(i).wait()
            for p in range(pairs):
                ctx_copy(p, i).wait()


def forward(counts, norms, w_qkv, shard_out, shard_up, shard_down, tokens, scenes, heads, size):
    ny = scenes // ZS
    rows, d_model = tokens.shape
    rl, width = shard_out.shape
    hidden = shard_up.shape[1]
    pairs = width // (2 * size)
    block = min(512, rows)
    steps_q = rows // block
    halves = 2
    sem = pltpu.SemaphoreType.DMA
    any_space = pl.BlockSpec(memory_space=pl.ANY)
    shape = jax.ShapeDtypeStruct
    wide = 128 + 3 * width
    outs = [shape((rows, d_model), LOW), shape((rows, width), LOW), shape((2 * rows, width), LOW), shape((2 * rows, width), LOW),
            shape((ZS, ny, 2, rl, wide), LOW), shape((ZS, ny, 2, rl, d_model), LOW), shape((ZS, ny, 2, rl, hidden), LOW),
            shape((ZS, ny, 2, rl, hidden), LOW), shape((2 * pairs, 2 * rows, rows), LOW), shape((rows, width), LOW),
            shape((rows, d_model), LOW), shape((pairs, 8, rows), F32)]
    out_specs = [any_space] * 8 + [
        any_space, pl.BlockSpec((block, 2 * size), lambda p, i: (i, p)),
        any_space, pl.BlockSpec((1, 8, block), lambda p, i: (p, 0, i))]
    scratch = [pltpu.VMEM((ZS, ny, 2, rl, wide), LOW), pltpu.VMEM((rows, d_model), F32), pltpu.VMEM((rows, d_model), LOW),
               pltpu.VMEM((rows, width), LOW), pltpu.VMEM((2 * rows, width), LOW), pltpu.VMEM((2 * rows, width), LOW),
               pltpu.VMEM((2 * rows, 128), LOW), pltpu.VMEM((rows, width), LOW),
               pltpu.VMEM((2, 2 * rows, block), F32), pltpu.VMEM((8, block), F32),
               pltpu.VMEM((2, 2, 2 * rows, block), LOW), sem((2,)), sem((10,)), sem((pairs, 2)), sem((pairs, 2)),
               sem((max(heads - 1, 1),)), sem((max(heads - 1, 1),)), sem((max(heads - 1, 1),)), sem((max(heads - 1, 1),)), sem((pairs, max(heads - 1, 1))), sem((pairs, max(heads - 1, 1)))]
    for _ in range(2 + 2 * halves + pairs):
        scratch += gather_sems(ny)
    dims = (ny, heads, rows, width, size, block, pairs, steps_q, halves)
    flops = 2 * rows * d_model * 3 * width + 8 * rows * rows * width
    results = pl.pallas_call(
        partial(forward_kernel, dims),
        grid=(pairs, steps_q),
        out_shape=outs,
        in_specs=[pl.BlockSpec(memory_space=pltpu.SMEM)] + [pl.BlockSpec(memory_space=pltpu.VMEM)] * 8 + [pl.BlockSpec(memory_space=pltpu.VMEM)],
        out_specs=out_specs,
        scratch_shapes=scratch,
        compiler_params=pltpu.CompilerParams(collective_id=0, has_side_effects=True, vmem_limit_bytes=60 * 2**20),
        cost_estimate=pl.CostEstimate(flops=flops, bytes_accessed=60 * 2**20, transcendentals=0),
        name="forward_attention",
    )(counts, *[a.reshape(1, rl) for a in norms], w_qkv, shard_out, shard_up, shard_down, tokens)
    n1, q, k, v, full_qkv, full_out, full_up, full_down, probs, context, context_all, inverse = results
    flat = lambda a: a.reshape(d_model, a.shape[-1])
    return n1, q, k, v, flat(full_qkv), flat(full_out), flat(full_up), flat(full_down), probs, context, context_all, inverse


class Scatter:
    def __init__(self, ny, parts, cols, bufs, sems):
        self.ny, self.parts, self.cols = ny, parts, cols
        self.own, self.from_core, self.from_y, self.sum_two, self.from_z = bufs
        self.load_sem, self.csend, self.crecv, self.ysend, self.yrecv, self.zsend, self.zrecv = sems
        self.z, self.y, self.core = place(ny)

    def load(self):
        return pltpu.make_async_copy(self.parts.at[:, :, self.core, :, self.cols], self.own, self.load_sem.at[0])

    def to_core(self):
        return remote(self.parts.at[:, :, 1 - self.core, :, self.cols], self.from_core, self.csend.at[0], self.crecv.at[0],
                      {"seq": 1 - self.core})

    def to_y(self, step):
        yy = (self.y + step) % self.ny
        return remote(self.own.at[:, yy], self.from_y.at[step - 1], self.ysend.at[step - 1], self.yrecv.at[step - 1],
                      {"scene": self.z * self.ny + yy})

    def to_z(self, step):
        zz = (self.z + step) % ZS
        return remote(self.sum_two.at[zz], self.from_z.at[step - 1], self.zsend.at[step - 1], self.zrecv.at[step - 1],
                      {"scene": zz * self.ny + self.y})

    def begin(self):
        self.load().start()
        self.to_core().start()

    def one(self):
        self.load().wait()
        self.to_core().wait_recv()
        for zz in range(ZS):
            for yy in range(self.ny):
                self.own[zz, yy] = (self.own[zz, yy].astype(F32) + self.from_core[zz, yy].astype(F32)).astype(LOW)
        for step in range(1, self.ny):
            self.to_y(step).start()

    def two(self):
        for step in range(1, self.ny):
            self.to_y(step).wait_recv()
        for zz in range(ZS):
            total = self.own[zz, self.y].astype(F32)
            for step in range(1, self.ny):
                total += self.from_y[step - 1, zz].astype(F32)
            self.sum_two[zz] = total.astype(LOW)
        for step in range(1, ZS):
            self.to_z(step).start()

    def three(self, out, alone=False):
        for step in range(1, ZS):
            self.to_z(step).wait_recv()
        total = self.sum_two[self.z].astype(F32)
        for step in range(1, ZS):
            total += self.from_z[step - 1].astype(F32)
        if alone:
            out[...] = total
        else:
            out[:, self.cols] = total

    def finish(self):
        self.to_core().wait_send()
        for step in range(1, self.ny):
            self.to_y(step).wait_send()
        for step in range(1, ZS):
            self.to_z(step).wait_send()


SCATTER_BUFS, SCATTER_SEMS = 5, 7


def scatter_scratch(ny, rl, cols):
    sem = pltpu.SemaphoreType.DMA
    other = max(ny - 1, 1)
    return [pltpu.VMEM((ZS, ny, rl, cols), LOW), pltpu.VMEM((ZS, ny, rl, cols), LOW), pltpu.VMEM((other, ZS, rl, cols), LOW),
            pltpu.VMEM((ZS, rl, cols), LOW), pltpu.VMEM((ZS - 1, rl, cols), LOW),
            sem((1,)), sem((1,)), sem((1,)), sem((other,)), sem((other,)), sem((ZS - 1,)), sem((ZS - 1,))]


def make_scatters(ny, plan, scratch):
    n = SCATTER_BUFS + SCATTER_SEMS
    result = []
    for i, (parts, cols) in enumerate(plan):
        mine = scratch[i * n:(i + 1) * n]
        result.append(Scatter(ny, parts, cols, mine[:SCATTER_BUFS], mine[SCATTER_BUFS:]))
    return result

def middle_kernel(dims, tokens, context_all, cotangent, full_qkv, full_out, full_up, full_down,
                  resid_grad, base, mlp_low, grad_context, norm_two, parts_out, parts_up, parts_down, mine_down,
                  x_v, ctx_v, cot_v, norm_v, wo, wu, wd, n2, act, gu, resid, part, low, arrived, up_v, down_v, out_v, gctx_v,
                  base_v, mlp_v, in_sem, out_sem, slot_sem, x_send, x_recv, g_send, g_recv, *scratch):
    ny, heads, rows, d_model, width, hidden, tile, size_f, first_cols = dims
    head = lax.axis_index("head")
    chunks = rows // tile
    part_rows = rows // heads
    per_part = part_rows // tile
    (down,) = make_scatters(ny, [(down_v, pl.ds(0, first_cols))], scratch)
    own_rows = pl.ds(pl.multiple_of(head * part_rows, part_rows), part_rows)

    def load(src, dst, i):
        return pltpu.make_async_copy(src, dst, in_sem.at[i])

    loads = [load(context_all, ctx_v, 0), load(full_out, wo, 1), load(tokens, x_v, 2), load(full_qkv.at[:, pl.ds(0, 128)], norm_v, 3),
             load(full_up, wu, 4), load(cotangent, cot_v, 5), load(full_down, wd, 6)]
    for item in loads:
        item.start()
    half = tile // 2

    def place_of(i):
        whole_tile = not isinstance(i, int)
        number = 0 if not whole_tile and i == chunks else i
        step = number // per_part + 1
        within = number % per_part * tile
        size = tile if whole_tile or 0 < i < chunks else half
        within = within + (half if not whole_tile and i == 0 else 0)
        return step, within, size

    def rows_of(i):
        step, within, size = place_of(i)
        return pl.ds(pl.multiple_of((head + step) % heads * part_rows + within, half), size)

    def x_copy(i, step):
        _, within, size = place_of(i)
        return remote(low.at[rows_of(i)], arrived.at[step - 1, pl.ds(within, size)], x_send.at[i], x_recv.at[i],
                      {"head": (head + step) % heads})

    def g_copy(j, step):
        to = (head + step) % heads
        at = pl.ds(j * tile, tile)
        there = pl.ds(pl.multiple_of(head * part_rows + j * tile, tile), tile)
        return remote(gctx_v.at[at, pl.ds(pl.multiple_of(to * width, width), width)], grad_context.at[there],
                      g_send.at[j, step - 1], g_recv.at[j, step - 1], {"head": to})

    greet_all(ny, heads)
    for item in loads[:4]:
        item.wait()
    norms = norm_v[...].astype(F32).T
    gain, shift = norms[2:3], norms[3:4]

    def hat_of(value):
        centre = value - jnp.mean(value, axis=1, keepdims=True)
        spread = lax.rsqrt(jnp.mean(centre * centre, axis=1, keepdims=True) + 1e-05)
        return centre * spread, spread

    norm_two[...] = jnp.zeros_like(norm_two)

    def forward_and_back(i, early=False):
        at = rows_of(i)
        value = x_v[at].astype(F32) + dot(ctx_v[at], wo[...], 1, 1)
        resid[at] = value
        n2[at] = (hat_of(value)[0] * gain + shift).astype(LOW)
        if early:
            loads[4].wait()
        for f in range(hidden // size_f):
            cols = slice(f * size_f, (f + 1) * size_f)
            u = dot(n2[at], wu[:, cols], 1, 0)
            if early and f == 0:
                loads[5].wait()
                loads[6].wait()
            ga = dot(cot_v[at], wd[:, cols], 1, 0)
            phi = 0.5 + 0.5 * lax.erf(u * (0.5 ** 0.5))
            act[at, cols] = (u * phi).astype(LOW)
            gu[at, cols] = (ga * (phi + u * (jnp.exp(u * u * -0.5) * 0.3989422804014327))).astype(LOW)
        total = dot(gu[at], wu[...], 1, 1)
        part[at] = total
        low[at] = total.astype(LOW)

    def sums(i):
        at = rows_of(i)
        total = part[at]
        hat, _ = hat_of(resid[at])
        norm_two[0:1] += jnp.sum(total * hat, axis=0, keepdims=True)
        norm_two[1:2] += jnp.sum(total, axis=0, keepdims=True)

    if heads > 1:
        forward_and_back(chunks, True)
        x_copy(chunks, 1).start()
        forward_and_back(0)
        x_copy(0, 1).start()
        for step in range(1, heads):
            first = (step - 1) * per_part

            @pl.loop(max(first, 1), first + per_part)
            def _(i):
                forward_and_back(i)
                x_copy(i, step).start()

    else:
        forward_and_back(chunks, True)
        forward_and_back(0)

    @pl.loop(max(chunks - per_part, 1), chunks)
    def _(i):
        forward_and_back(i)

    def weight_grad(src, other, dst, count):
        per_z = d_model // ZS
        for f in range(count // size_f):
            cols = slice(f * size_f, (f + 1) * size_f)

            @pl.loop(0, ZS // 2)
            def _(j):
                at = pl.ds(pl.multiple_of(j * 2 * per_z, 2 * per_z), 2 * per_z)
                value = dot(src[:, at], other[:, cols], 0, 0).astype(LOW)
                dst[pl.ds(2 * j, 2), :, :, :, cols] = value.reshape(2, *dst.shape[1:4], size_f)

    weight_grad(cot_v, act, down_v, hidden)
    down.begin()

    def own_store(j):
        at = pl.ds(j * tile, tile)
        there = pl.ds(pl.multiple_of(head * part_rows + j * tile, tile), tile)
        return (pltpu.make_async_copy(part.at[there], resid_grad.at[at], out_sem.at[3 + 2 * j]),
                pltpu.make_async_copy(gctx_v.at[at, pl.ds(pl.multiple_of(head * width, width), width)], grad_context.at[there],
                                      out_sem.at[4 + 2 * j]))

    for j in range(per_part):
        at = pl.ds(pl.multiple_of(head * part_rows + j * tile, tile), tile)
        total = part[at]
        for step in range(1, heads):
            i = (step - 1) * per_part + j
            x_copy(i, step).wait_recv()
            if i == 0:
                x_copy(chunks, step).wait_recv()
            total += arrived[step - 1, j * tile:(j + 1) * tile].astype(F32)
        hat, spread = hat_of(resid[at])
        own_part = part[at]
        norm_two[0:1] += jnp.sum(own_part * hat, axis=0, keepdims=True)
        norm_two[1:2] += jnp.sum(own_part, axis=0, keepdims=True)
        scaled = total * gain
        inner = scaled - jnp.mean(scaled, axis=1, keepdims=True) - hat * jnp.mean(scaled * hat, axis=1, keepdims=True)
        total = cot_v[at].astype(F32) + inner * spread
        part[at] = total
        rounded = total.astype(LOW)
        low[at] = rounded
        gctx_v[j * tile:(j + 1) * tile] = dot(rounded, wo[...], 1, 0).astype(LOW)
        for step in range(1, heads):
            g_copy(j, step).start()
        for item in own_store(j):
            item.start()
    down.one()
    weight_grad(n2, gu, up_v, hidden)
    stores = [pltpu.make_async_copy(up_v, parts_up, out_sem.at[0]), pltpu.make_async_copy(down_v, parts_down, out_sem.at[1]),
              pltpu.make_async_copy(out_v, parts_out, out_sem.at[2])]
    for item in stores[:2]:
        item.start()
    down.two()
    weight_grad(low.at[own_rows], ctx_v.at[own_rows], out_v, d_model)
    stores[2].start()

    def slot_copies(i):
        at = pl.ds(pl.multiple_of(i * tile, tile), tile)
        slot = i % 2
        return (pltpu.make_async_copy(base_v.at[slot], base.at[at], slot_sem.at[0, slot]),
                pltpu.make_async_copy(mlp_v.at[slot], mlp_low.at[at], slot_sem.at[1, slot]))

    def slot_loop(i):
        at = pl.ds(pl.multiple_of(i * tile, tile), tile)
        value = dot(act[at], wd[...], 1, 1)

        @pl.when(i >= 2)
        def _():
            for item in slot_copies(i - 2):
                item.wait()

        base_v[i % 2] = (resid[at] + value).astype(LOW)
        mlp_v[i % 2] = value.astype(LOW)
        for item in slot_copies(i):
            item.start()

    pl.loop(0, chunks)(slot_loop)
    if heads > 1:
        sums(chunks)
        sums(0)
        pl.loop(1, chunks - per_part)(sums)
    for i in range(max(0, chunks - 2), chunks):
        for item in slot_copies(i):
            item.wait()
    down.three(mine_down)
    down.finish()
    for item in stores:
        item.wait()
    for j in range(per_part):
        for item in own_store(j):
            item.wait()
        for step in range(1, heads):
            g_copy(j, step).wait()
    for step in range(1, heads):
        for j in range(per_part):
            x_copy((step - 1) * per_part + j, step).wait_send()
    if heads > 1:
        x_copy(chunks, 1).wait_send()


def shares(hidden):
    n = hidden // 128
    first = max(n // 8, 1)
    return first * 128, (n - first) * 128


def middle(tokens, context_all, cotangent, full_qkv, full_out, full_up, full_down, scenes, heads):
    ny = scenes // ZS
    rows, d_model = tokens.shape
    rl = d_model // (2 * scenes)
    hidden, width = full_up.shape[1], d_model // heads
    tile, size_f = min(256, rows // heads), min(1024, hidden)
    part_rows = rows // heads
    per_part = part_rows // tile
    chunks = rows // tile
    first_cols = shares(hidden)[0]
    others = max(heads - 1, 1)
    sem = pltpu.SemaphoreType.DMA
    shape, vmem = jax.ShapeDtypeStruct, pltpu.VMEM
    any_space, whole = pl.BlockSpec(memory_space=pl.ANY), pl.BlockSpec(memory_space=pltpu.VMEM)
    big, wide, blocks = (rows, d_model), (rows, hidden), (ZS, ny, 2, rl, hidden)
    scratch = [vmem(big, LOW), vmem(big, LOW), vmem(big, LOW), vmem((d_model, 128), LOW), vmem((d_model, d_model), LOW),
               vmem((d_model, hidden), LOW), vmem((d_model, hidden), LOW), vmem(big, LOW), vmem(wide, LOW), vmem(wide, LOW),
               vmem(big, F32), vmem(big, F32), vmem(big, LOW), vmem((others, part_rows, d_model), LOW), vmem(blocks, LOW),
               vmem(blocks, LOW), vmem((ZS, ny, 2, rl, d_model), LOW), vmem((part_rows, d_model), LOW), vmem((2, tile, d_model), LOW),
               vmem((2, tile, d_model), LOW), sem((7,)), sem((3 + 2 * per_part,)), sem((2, 2)), sem((chunks + 1,)),
               sem((chunks + 1,)), sem((per_part, others)), sem((per_part, others))]
    scratch += scatter_scratch(ny, rl, first_cols)
    return pl.pallas_call(
        partial(middle_kernel, (ny, heads, rows, d_model, width, hidden, tile, size_f, first_cols)),
        out_shape=[shape((part_rows, d_model), F32), shape(big, LOW), shape(big, LOW), shape((rows, width), LOW), shape((8, d_model), F32),
                   shape((ZS, ny, 2, rl, d_model), LOW), shape(blocks, LOW), shape(blocks, LOW), shape((rl, first_cols), F32)],
        in_specs=[any_space] * 7,
        out_specs=[any_space] * 4 + [whole] + [any_space] * 3 + [whole],
        scratch_shapes=scratch,
        compiler_params=pltpu.CompilerParams(collective_id=3, has_side_effects=True, vmem_limit_bytes=63 * 2**20),
        cost_estimate=pl.CostEstimate(flops=14 * rows * d_model * hidden, bytes_accessed=50 * 2**20, transcendentals=0),
        name="middle_stage",
    )(tokens, context_all, cotangent, full_qkv, full_out, full_up, full_down)


def backward_kernel(dims, probs, queries, keys, values, grad, context, inverse, parts_out, parts_up, mlp_low,
                    grads_out, mine_out, mine_up, mlp_land,
                    grads, grads_sem,
                    dk_acc, dv_acc, kept, stage, landed, kv_send, kv_recv, m_send, m_recv, *scratch):
    ny, heads, rows, size, pairs, steps_q, halves = dims
    pair, part = pl.program_id(0), pl.program_id(1)
    step = pair * steps_q + part
    total = pairs * steps_q
    block = grad.shape[0]
    z, y, core = place(ny)
    width = parts_out.shape[-1]
    ends = split_cols(width, 2)
    plan = [(parts_out, ends[0])] + [(parts_up, cols) for cols in split_cols(parts_up.shape[-1], halves)] + [(parts_out, ends[1])]
    scatters = make_scatters(ny, plan, scratch)
    targets = [mine_out] + [mine_up] * halves + [mine_out]

    def kv_copy(p, i):
        return remote(stage.at[p, i], landed.at[p, i], kv_send.at[p, i], kv_recv.at[p, i], {"seq": 1 - core})

    head = lax.axis_index("head")

    def mlp_copy(i, step):
        return remote(mlp_low.at[pl.ds(i * (rows // 4), rows // 4)], mlp_land.at[step - 1, pl.ds(i * (rows // 4), rows // 4)],
                      m_send.at[i, step - 1], m_recv.at[i, step - 1], {"head": (head + step) % heads})

    @pl.when(step == 0)
    def _():
        greet_all(ny, heads)
        for i in range(4):
            for j in range(1, heads):
                mlp_copy(i, j).start()
        for item in scatters:
            item.begin()

    slots = 2 * total
    plan_at = [(0.3 + 0.3 * i, 3.5 + 2.3 * i, 7.0 + 2.3 * i) for i in range(len(scatters))]
    events = sorted((plan_at[i][j], i, j + 1) for i in range(len(scatters)) for j in range(3))

    def run(slot_in_step):
        for when, i, what in events:
            slot = min(int(when * min(1.0, slots / 16)), slots)
            if slot == slots or slot % 2 != slot_in_step:
                continue

            @pl.when(step == slot // 2)
            def _():
                if what == 1:
                    scatters[i].one()
                elif what == 2:
                    scatters[i].two()
                else:
                    scatters[i].three(targets[i])

    @pl.when(part == 0)
    def _():
        dk_acc[...] = jnp.zeros_like(dk_acc)
        dv_acc[...] = jnp.zeros_like(dv_acc)

    upper = grad[...].astype(F32)
    inner = (upper * context[...].astype(F32)).T
    upper_t = upper.T
    row = lax.broadcasted_iota(jnp.int32, upper_t.shape, 0)
    keys_t = keys[...].T
    pieces = []
    for h in range(2):
        run(h)
        over = inverse[0, h:h + 1]
        shift = jnp.sum(inner[h * size:(h + 1) * size], axis=0, keepdims=True) * over
        scaled = jnp.where(row // size == h, upper_t * over, 0.0)
        dp = dot(values[...], scaled.astype(LOW), 1, 0) - shift
        low = probs[h]
        ds = (low.astype(F32) * dp).astype(LOW)
        dv_acc[...] += dot(low, scaled.T.astype(LOW), 1, 0)
        dk_acc[...] += dot(ds, only_head(queries[...], h, size), 1, 0)
        pieces.append(dot(keys_t, ds, 1, 0)[h * size:(h + 1) * size])
    grads[pl.ds(pl.multiple_of(part * block, block), block), pl.ds(pl.multiple_of(pair * 6 * size, 2 * size), 2 * size)] = (
        (jnp.concatenate(pieces, axis=0) * size ** -0.5).T.astype(LOW))

    @pl.when(part == steps_q - 1)
    def _():
        for i, acc in enumerate((dk_acc, dv_acc)):
            stage[pair, i] = acc[rows:].astype(LOW)
            kv_copy(pair, i).start()
            kept[pair, i] = acc[:rows]

    @pl.when(step == total - 1)
    def _():
        for when, i, what in events:
            if min(int(when * min(1.0, slots / 16)), slots) == slots:
                if what == 1:
                    scatters[i].one()
                elif what == 2:
                    scatters[i].two()
                else:
                    scatters[i].three(targets[i])
        for item in scatters:
            item.finish()
        for p in range(pairs):
            for i in range(2):
                kv_copy(p, i).wait()
                grads[:, (3 * p + i + 1) * 2 * size:(3 * p + i + 2) * 2 * size] = (kept[p, i] + landed[p, i].astype(F32)).astype(LOW)
        store = pltpu.make_async_copy(grads, grads_out, grads_sem)
        store.start()
        for i in range(4):
            for j in range(1, heads):
                mlp_copy(i, j).wait()
        store.wait()


def backward(probs, q, k, v, grad, context, inverse, parts_out, parts_up, mlp_low, scenes, heads, size):
    ny = scenes // ZS
    rows, width = q.shape
    pairs = width // (2 * size)
    block = min(512, rows)
    d_model, hidden = parts_out.shape[-1], parts_up.shape[-1]
    rl = d_model // (2 * scenes)
    others = max(heads - 1, 1)
    halves = 4
    spec = pl.BlockSpec
    q_spec = spec((block, 2 * size), lambda p, i: (i, p))
    k_spec = spec((2 * rows, 2 * size), lambda p, i: (0, p))
    any_space = spec(memory_space=pl.ANY)
    whole = spec(memory_space=pltpu.VMEM)
    shape = jax.ShapeDtypeStruct
    sem = pltpu.SemaphoreType.DMA
    pair_buf = (pairs, 2, rows, 2 * size)
    scratch = [pltpu.VMEM((rows, 3 * width), LOW), sem, pltpu.VMEM((2 * rows, 2 * size), F32), pltpu.VMEM((2 * rows, 2 * size), F32), pltpu.VMEM(pair_buf, F32),
               pltpu.VMEM(pair_buf, LOW), pltpu.VMEM(pair_buf, LOW), sem((pairs, 2)), sem((pairs, 2)), sem((4, others)), sem((4, others))]
    for cols in [d_model // 2] + [hidden // halves] * halves + [d_model // 2]:
        scratch += scatter_scratch(ny, rl, cols)
    return pl.pallas_call(
        partial(backward_kernel, (ny, heads, rows, size, pairs, rows // block, halves)),
        grid=(pairs, rows // block),
        out_shape=[shape((rows, 3 * width), LOW), shape((rl, d_model), F32), shape((rl, hidden), F32), shape((others, rows, d_model), LOW)],
        in_specs=[spec((2, 2 * rows, block), lambda p, i: (p, 0, i)), q_spec, k_spec, k_spec, q_spec, q_spec,
                  spec((1, 8, block), lambda p, i: (p, 0, i)), any_space, any_space, any_space],
        out_specs=[any_space, whole, whole, any_space],
        scratch_shapes=scratch,
        compiler_params=pltpu.CompilerParams(collective_id=1, has_side_effects=True, vmem_limit_bytes=60 * 2**20),
        cost_estimate=pl.CostEstimate(flops=16 * rows * rows * width, bytes_accessed=50 * 2**20, transcendentals=0),
        name="backward_attention",
    )(probs, q, k, v, grad, context, inverse, parts_out, parts_up, mlp_low)


def thirds(start, count):
    n = count // 128
    edges = [start + n * i // 3 * 128 for i in range(4)]
    return [(a, b - a) for a, b in zip(edges, edges[1:])]


def last_kernel(dims, grads, n1, tokens, resid, full_qkv, norm_two, parts_down, down_a, out_all,
                own_grad, done_land, mine_w, mine_norm, mine_out, mine_down,
                g_v, n1_v, x_v, res_v, w_v, in_sem,
                part_one, part_low, arrived, parts_qkv, tiny_land, tiny_own, done_low, x_send, x_recv, t_send, t_recv,
                n_send, n_recv, o_send, o_recv, out_sem, mine_qkv, out_land, *scratch):
    ny, heads, rows, d_model, width, tile, down_at, qkv_at = dims
    z, y, core = place(ny)
    head = lax.axis_index("head")
    wide = full_qkv.shape[1]
    rl = mine_qkv.shape[0]
    plan = [(parts_down, pl.ds(*item)) for item in down_at] + [(parts_qkv, pl.ds(*item)) for item in qkv_at]
    scatters = make_scatters(ny, plan, scratch)
    downs, qkvs = scatters[:len(down_at)], scatters[len(down_at):]
    down_x, down_y, down_z = downs

    def down_done(i):
        downs[i].three(mine_down.at[:, pl.ds(*down_at[i])], True)

    chunks = rows // tile
    part_rows = rows // heads
    per_part = part_rows // tile
    loads = [pltpu.make_async_copy(src, dst, in_sem.at[i]) for i, (src, dst) in enumerate((
        (grads, g_v), (full_qkv, w_v), (n1, n1_v), (tokens, x_v), (resid, res_v)))]
    for item in loads:
        item.start()
    def rows_at(step, j):
        return pl.ds(pl.multiple_of((head + heads + step) % heads * part_rows + j * tile, tile), tile)

    def x_copy(step, j):
        return remote(part_low.at[rows_at(step, j)], arrived.at[step - 1, pl.ds(j * tile, tile)], x_send.at[step - 1, j],
                      x_recv.at[step - 1, j], {"head": (head + step) % heads})

    def t_copy(step, j):
        at = pl.ds(j * tile, tile)
        return remote(done_low.at[at], done_land.at[step - 1, at], t_send.at[step - 1, j], t_recv.at[step - 1, j],
                      {"head": (head + step) % heads})

    def n_copy(step):
        return remote(tiny_own, tiny_land.at[step - 1], n_send.at[step - 1], n_recv.at[step - 1], {"head": (head + step) % heads})

    def o_copy(step):
        to = (head + step) % heads
        return remote(out_all.at[:, pl.ds(pl.multiple_of(to * width, width), width)], out_land.at[step - 1], o_send.at[step - 1],
                      o_recv.at[step - 1], {"head": to})

    def out_copy(j):
        at = pl.ds(j * tile, tile)
        return pltpu.make_async_copy(done_low.at[at], own_grad.at[at], out_sem.at[j])

    greet_all(ny, heads)
    for item in downs:
        item.begin()
    for item in loads[:2]:
        item.wait()

    def partial_sum(step, j):
        at = rows_at(step, j)
        total = dot(g_v[at], w_v[:, 128:], 1, 1)
        part_one[at] = total
        part_low[at] = total.astype(LOW)

    for step in range(1, heads):
        for j in range(per_part):
            partial_sum(step, j)
            x_copy(step, j).start()
    for step in range(1, heads):
        o_copy(step).start()
    down_x.one()
    down_y.one()
    for j in range(per_part):
        partial_sum(0, j)
    for item in loads[2:]:
        item.wait()
    per_z = d_model // ZS
    for zz in range(0, ZS, 2):
        cols = n1_v[:, zz * per_z:(zz + 2) * per_z]
        value = dot(cols, g_v[...], 0, 0).astype(LOW)
        parts_qkv[zz:zz + 2, :, :, :, 128:] = value.reshape(2, ny, 2, rl, 3 * width)
    for item in qkvs[1:]:
        item.begin()
    gain = w_v[:, :128].astype(F32).T[0:1]

    def hat_of(at):
        x = x_v[at].astype(F32)
        centre = x - jnp.mean(x, axis=1, keepdims=True)
        spread = lax.rsqrt(jnp.mean(centre * centre, axis=1, keepdims=True) + 1e-05)
        return centre * spread, spread

    gain_sum = jnp.zeros((1, d_model), F32)
    shift_sum = jnp.zeros((1, d_model), F32)
    for i in range(chunks):
        at = pl.ds(i * tile, tile)
        hat, _ = hat_of(at)
        gain_sum += jnp.sum(part_one[at] * hat, axis=0, keepdims=True)
        shift_sum += jnp.sum(part_one[at], axis=0, keepdims=True)
        if i == chunks // 4:
            qkvs[1].one()
            down_x.two()
        if i == chunks // 2:
            qkvs[2].one()
    sums = jnp.concatenate([gain_sum, shift_sum, norm_two[0:2], jnp.zeros((124, d_model), F32)], axis=0).T.astype(LOW)
    parts_qkv[:, :, :, :, :128] = sums.reshape(ZS, ny, 2, rl, 128)
    qkvs[0].begin()

    def receive(j):
        at = rows_at(0, j)
        here = pl.ds(j * tile, tile)
        total = part_one[at]
        for step in range(1, heads):
            x_copy(step, j).wait_recv()
            total += arrived[step - 1, here].astype(F32)
        hat, spread = hat_of(at)
        scaled = total * gain
        inner = scaled - jnp.mean(scaled, axis=1, keepdims=True) - hat * jnp.mean(scaled * hat, axis=1, keepdims=True)
        total = res_v[here] + inner * spread
        done_low[here] = total.astype(LOW)
        out_copy(j).start()
        for step in range(1, heads):
            t_copy(step, j).start()

    first = pl.ds(pl.multiple_of(head * width, width), width)

    def share(items, i, n):
        return items[len(items) * i // n:len(items) * (i + 1) // n]

    def receive_some(i):
        for j in share(range(per_part), i, 4):
            receive(j)

    def send_norms():
        tiny_own[...] = mine_qkv[:, :128]
        for step in range(1, heads):
            n_copy(step).start()

    receive_some(0)
    qkvs[0].one()
    down_z.one()
    down_y.two()
    receive_some(1)
    mine_down[:, :down_a.shape[1]] = down_a[...]
    down_done(0)
    receive_some(2)
    qkvs[1].two()
    down_done(1)
    receive_some(3)
    qkvs[2].two()
    qkvs[1].three(mine_qkv)
    total = out_all[:, first]
    for step in range(1, heads):
        o_copy(step).wait()
        total += out_land[step - 1]
    mine_out[...] = total
    qkvs[0].two()
    qkvs[2].three(mine_qkv)
    down_z.two()
    qkvs[0].three(mine_qkv)
    send_norms()
    down_done(2)
    total = mine_qkv[:, :128]
    for step in range(1, heads):
        n_copy(step).wait()
        total += tiny_land[step - 1]
    mine_norm[...] = total.T[:8]
    for p in range(width // 128):
        for c in range(3):
            mine_w[c, :, p * 128:(p + 1) * 128] = mine_qkv[:, 128 * (3 * p + c + 1):128 * (3 * p + c + 2)]
    for item in scatters:
        item.finish()
    for j in range(per_part):
        out_copy(j).wait()
        for step in range(1, heads):
            x_copy(step, j).wait_send()
            t_copy(step, j).wait()


def last_stage(grads, n1, tokens, resid, full_qkv, norm_two, parts_down, down_a, out_all, scenes, heads):
    ny = scenes // ZS
    rows, d_model = tokens.shape
    width, hidden = grads.shape[1] // 3, parts_down.shape[-1]
    first, third = shares(hidden)
    rl = d_model // (2 * scenes)
    wide = full_qkv.shape[1]
    part_rows = rows // heads
    tile = min(128, part_rows)
    chunks, per_part = rows // tile, part_rows // tile
    down_at, qkv_at = thirds(first, third), thirds(0, wide)
    others = max(heads - 1, 1)
    sem = pltpu.SemaphoreType.DMA
    shape, vmem = jax.ShapeDtypeStruct, pltpu.VMEM
    any_space, whole = pl.BlockSpec(memory_space=pl.ANY), pl.BlockSpec(memory_space=pltpu.VMEM)
    big, own = (rows, d_model), (part_rows, d_model)
    scratch = [vmem((rows, 3 * width), LOW), vmem(big, LOW), vmem(big, LOW), vmem(own, F32), vmem((d_model, wide), LOW), sem((5,)),
               vmem(big, F32), vmem(big, LOW), vmem((others, *own), LOW), vmem((ZS, ny, 2, rl, wide), LOW), vmem((others, rl, 128), F32),
               vmem((rl, 128), F32), vmem(own, LOW), sem((others, per_part)),
               sem((others, per_part)), sem((others, per_part)), sem((others, per_part)), sem((others,)), sem((others,)),
               sem((others,)), sem((others,)), sem((per_part,)), vmem((rl, wide), F32), vmem((others, rl, width), F32)]
    for _, cols in down_at + qkv_at:
        scratch += scatter_scratch(ny, rl, cols)
    return pl.pallas_call(
        partial(last_kernel, (ny, heads, rows, d_model, width, tile, down_at, qkv_at)),
        out_shape=[shape(own, LOW), shape((others, *own), LOW), shape((3, rl, width), F32), shape((8, rl), F32), shape((rl, width), F32),
                   shape((rl, hidden), F32)],
        in_specs=[any_space] * 5 + [whole, any_space, whole, whole],
        out_specs=[any_space, any_space, whole, whole, whole, whole],
        scratch_shapes=scratch,
        compiler_params=pltpu.CompilerParams(collective_id=2, has_side_effects=True, vmem_limit_bytes=63 * 2**20),
        cost_estimate=pl.CostEstimate(flops=12 * rows * d_model * width, bytes_accessed=30 * 2**20, transcendentals=0),
        name="last_stage",
    )(grads, n1, tokens, resid, full_qkv, norm_two, parts_down, down_a, out_all)


def finish_kernel(heads, tile, base, mlp_land, own, land, w, out, up, down, norm,
                  output, tokens_grad, w_o, out_o, up_o, down_o, n_a, n_b, n_c, n_d,
                  sum_v, base_v, own_v, mlp_v, grad_v, land_v, w_v, out_v, up_v, down_v, base_sem, mlp_sem, own_sem, land_sem, small_sem,
                  out_sem, back_sem, far_sem, last_sem):
    rows = base.shape[0]
    part_rows = rows // heads
    chunks, per_part = rows // tile, part_rows // tile
    head = lax.axis_index("head")
    copy = pltpu.make_async_copy

    def rows_at(step, j):
        return pl.ds(pl.multiple_of((head + heads - step) % heads * part_rows + j * tile, tile), tile)

    def loads(i):
        at = pl.ds(i * tile, tile)
        return copy(base.at[at], base_v.at[at], base_sem.at[i]), copy(mlp_land.at[:, at], mlp_v.at[:, at], mlp_sem.at[i])

    def own_load(j):
        at = pl.ds(j * tile, tile)
        return copy(own.at[at], own_v.at[at], own_sem.at[j])

    land_load = copy(land, land_v, land_sem.at[0])
    smalls = ((w, w_v, w_o), (out, out_v, out_o), (up, up_v, up_o), (down, down_v, down_o))
    small_loads = [copy(src, mid, small_sem.at[i]) for i, (src, mid, _) in enumerate(smalls)]
    small_stores = [copy(mid, dst, last_sem.at[i]) for i, (_, mid, dst) in enumerate(smalls)]

    def out_store(i):
        at = pl.ds(i * tile, tile)
        return copy(sum_v.at[at], output.at[at], out_sem.at[i])

    def own_store(j):
        return copy(grad_v.at[rows_at(0, j)], tokens_grad.at[rows_at(0, j)], back_sem.at[j])

    def far_store(step, j):
        return copy(grad_v.at[rows_at(step, j)], tokens_grad.at[rows_at(step, j)], far_sem.at[step - 1, j])

    for j in range(per_part):
        own_load(j).start()
    if heads > 1:
        land_load.start()
    for i in range(chunks):
        for item in loads(i):
            item.start()
    for item in small_loads:
        item.start()
    for i, dst in enumerate((n_a, n_b, n_c, n_d)):
        dst[...] = norm[i:i + 1]
    for j in range(per_part):
        own_load(j).wait()
        grad_v[rows_at(0, j)] = own_v[j * tile:(j + 1) * tile].astype(F32)
        own_store(j).start()
    if heads > 1:
        land_load.wait()
        for step in range(1, heads):
            for j in range(per_part):
                grad_v[rows_at(step, j)] = land_v[step - 1, j * tile:(j + 1) * tile].astype(F32)
                far_store(step, j).start()
    for i in range(chunks):
        at = pl.ds(i * tile, tile)
        for item in loads(i):
            item.wait()
        total = base_v[at].astype(F32)
        for step in range(1, heads):
            total += mlp_v[step - 1, at].astype(F32)
        sum_v[at] = total
        out_store(i).start()
    for first, second in zip(small_loads, small_stores):
        first.wait()
        second.start()
    for j in range(per_part):
        own_store(j).wait()
        for step in range(1, heads):
            far_store(step, j).wait()
    for i in range(chunks):
        out_store(i).wait()
    for item in small_stores:
        item.wait()


def finish(base, mlp_land, own, land, w, out, up, down, norm, heads):
    rows, d_model = base.shape
    part_rows = rows // heads
    tile = min(128, part_rows)
    chunks, per_part = rows // tile, part_rows // tile
    rl, others = up.shape[0], max(heads - 1, 1)
    spec, shape, vmem, sem = pl.BlockSpec, jax.ShapeDtypeStruct, pltpu.VMEM, pltpu.SemaphoreType.DMA
    any_space, whole = spec(memory_space=pl.ANY), spec(memory_space=pltpu.VMEM)
    return pl.pallas_call(
        partial(finish_kernel, heads, tile),
        in_specs=[any_space] * 8 + [whole],
        out_specs=[any_space] * 6 + [whole] * 4,
        out_shape=[shape((rows, d_model), F32), shape((rows, d_model), F32)] + [shape(a.shape, F32) for a in (w, out, up, down)]
        + [shape((1, rl), F32)] * 4,
        scratch_shapes=[vmem(base.shape, F32), vmem(base.shape, LOW), vmem(own.shape, LOW), vmem(mlp_land.shape, LOW), vmem(base.shape, F32), vmem(land.shape, LOW)]
        + [vmem(a.shape, F32) for a in (w, out, up, down)]
        + [sem((chunks,)), sem((chunks,)), sem((per_part,)), sem((1,)), sem((4,)), sem((chunks,)), sem((per_part,)),
           sem((others, per_part)), sem((4,))],
        compiler_params=pltpu.CompilerParams(vmem_limit_bytes=63 * 2**20),
        name="finish",
    )(base, mlp_land, own, land, w, out, up, down, norm)


def on_device(n_scene, n_head, tokens, counts, w_qkv, w_out, w_up, w_down, gain_one, shift_one, gain_two, shift_two, cotangent):
    rows, d_model = tokens.shape
    width, hidden = w_qkv.shape[2], w_up.shape[1]
    size = 64
    n1, q, k, v, full_qkv, full_out, full_up, full_down, probs, context, context_all, inverse = forward(
        counts, (gain_one, shift_one, gain_two, shift_two), w_qkv, w_out.T, w_up, w_down.T, tokens, n_scene, n_head, size)
    grad_resid, base, mlp_low, grad_context, norm_two, grad_outproj, grad_up, grad_down, down_a = middle(
        tokens, context_all, cotangent, full_qkv, full_out, full_up, full_down, n_scene, n_head)
    grads, out_all, mine_up, mlp_land = backward(
        probs, q, k, v, grad_context, context, inverse, grad_outproj, grad_up, mlp_low, n_scene, n_head, size)
    own, land, mine_qkv, norms, mine_out, mine_down = last_stage(
        grads, n1, tokens, grad_resid, full_qkv, norm_two, grad_down, down_a, out_all, n_scene, n_head)
    output, tokens_grad, mine_qkv, mine_out, mine_up, mine_down, *norms = finish(
        base, mlp_land, own, land, mine_qkv, mine_out, mine_up, mine_down, norms, n_head)
    return (output, tokens_grad, mine_qkv, mine_out.T, mine_up, mine_down.T, *[a.reshape(-1) for a in norms])


def solution(mesh):
    rows, both = ("scene", "seq"), P(("scene", "seq"))
    weights = (P(None, rows, "head"), P("head", rows), P(rows, "head"), P("head", rows), both, both, both, both)
    return jax.shard_map(
        partial(on_device, mesh.shape["scene"], mesh.shape["head"]), mesh=mesh,
        in_specs=(P(rows, None), P("scene"), *weights, P(rows, None)),
        out_specs=(P(rows, None), P(rows, None), *weights),
        check_vma=False,
    )
```

```python
from functools import partial

import jax
import jax.numpy as jnp
from jax import lax
from jax.experimental import pallas as pl
from jax.experimental.pallas import tpu as pltpu
from jax.sharding import PartitionSpec as P

MESH = pl.DeviceIdType.MESH
ZS = 4


def place(ny):
    scene = lax.axis_index("scene")
    return scene // ny, scene % ny, lax.axis_index("seq")


def remote(src, dst, send_sem, recv_sem, device):
    return pltpu.make_async_remote_copy(
        src_ref=src, dst_ref=dst, send_sem=send_sem, recv_sem=recv_sem,
        device_id=device, device_id_type=MESH,
    )


F32 = jnp.float32
LOW = jnp.bfloat16


def dot(a, b, ca, cb):
    return lax.dot_general(a, b, (((ca,), (cb,)), ((), ())), preferred_element_type=F32)


def only_head(x, h, size):
    lane = lax.broadcasted_iota(jnp.int32, x.shape, 1)
    return jnp.where(lane // size == h, x, jnp.zeros_like(x))


class Gather:
    def __init__(self, ny, source, full, cols, sems):
        self.ny, self.source, self.full, self.cols = ny, source, full, cols
        self.rsend, self.rrecv, self.lsend, self.lrecv, self.ysend, self.yrecv, self.csend, self.crecv = sems
        self.z, self.y, self.core = place(ny)

    def at(self, zz, yy):
        return self.full.at[zz, yy, self.core, :, self.cols]

    def right(self, k):
        src = self.source() if k == 0 else self.at(self.z - k, self.y)
        dst = self.at(self.z - k, self.y)
        return remote(src, dst, self.rsend.at[k], self.rrecv.at[k], {"scene": (self.z + 1) * self.ny + self.y})

    def left(self, k):
        src = self.source() if k == 0 else self.at(self.z + k, self.y)
        dst = self.at(self.z + k, self.y)
        return remote(src, dst, self.lsend.at[k], self.lrecv.at[k], {"scene": (self.z - 1) * self.ny + self.y})

    def across(self, zz, step, own=False):
        src = self.source() if own else self.at(zz, self.y)
        peer = self.z * self.ny + (self.y + step) % self.ny
        return remote(src, self.at(zz, self.y), self.ysend.at[step - 1], self.yrecv.at[step - 1], {"scene": peer})

    def arrival(self, zz, step):
        yy = (self.y + self.ny - step) % self.ny
        return remote(self.at(zz, yy), self.at(zz, yy), self.ysend.at[step - 1], self.yrecv.at[step - 1],
                      {"scene": self.z * self.ny + yy})

    def twin(self, zz, step, own=False):
        src = self.source() if own else self.at(zz, (self.y + self.ny - step) % self.ny)
        dst = self.at(zz, (self.y + self.ny - step) % self.ny)
        return remote(src, dst, self.csend.at[0], self.crecv.at[0], {"seq": 1 - self.core})

    def column(self, step):
        yy = (self.y + self.ny - step) % self.ny
        all_z = self.full.at[:, yy, self.core, :, self.cols]
        return remote(all_z, all_z, self.ysend.at[step - 1], self.yrecv.at[step - 1], {"scene": self.z * self.ny + yy})

    def twins(self):
        mine, theirs = [self.full.at[:, :, c, :, self.cols] for c in (self.core, 1 - self.core)]
        return [remote(item, item, self.csend.at[0], self.crecv.at[0], {"seq": 1 - self.core}) for item in (mine, theirs)]

    def begin(self):
        @pl.when(self.z < ZS - 1)
        def _():
            self.right(0).start()

        @pl.when(self.z > 0)
        def _():
            self.left(0).start()

        for step in range(1, self.ny):
            self.across(self.z, step, True).start()
        self.twin(self.z, 0, True).start()

    def hop(self, k):
        @pl.when(self.z >= k)
        def _():
            self.right(k - 1).wait_recv()
            if k < ZS - 1:
                @pl.when(self.z < ZS - 1)
                def _():
                    self.right(k).start()
            for step in range(1, self.ny):
                self.across(self.z - k, step).start()
            self.twin(self.z - k, 0).start()

        @pl.when(self.z + k < ZS)
        def _():
            self.left(k - 1).wait_recv()
            if k < ZS - 1:
                @pl.when(self.z > 0)
                def _():
                    self.left(k).start()
            for step in range(1, self.ny):
                self.across(self.z + k, step).start()
            self.twin(self.z + k, 0).start()

    def spread(self):
        for step in range(1, self.ny):
            self.column(step).wait_recv()
            for zz in range(ZS):
                self.twin(zz, step).start()

    def finish(self):
        for k in range(ZS - 1):
            @pl.when((self.z < ZS - 1) & (self.z >= k))
            def _():
                self.right(k).wait_send()

            @pl.when((self.z > 0) & (self.z + k < ZS))
            def _():
                self.left(k).wait_send()
        for step in range(1, self.ny):
            self.column(step).wait_send()
        mine, theirs = self.twins()
        mine.wait_send()
        theirs.wait_recv()


class PairGather(Gather):
    def row(self, zz):
        return self.full.at[zz, :, self.core, :, self.cols]

    def right(self, k):
        return remote(self.row(self.z - k), self.row(self.z - k), self.rsend.at[k], self.rrecv.at[k],
                      {"scene": (self.z + 1) * self.ny + self.y})

    def left(self, k):
        return remote(self.row(self.z + k), self.row(self.z + k), self.lsend.at[k], self.lrecv.at[k],
                      {"scene": (self.z - 1) * self.ny + self.y})

    def twin(self, zz):
        return remote(self.row(zz), self.row(zz), self.csend.at[0], self.crecv.at[0], {"seq": 1 - self.core})

    def begin(self):
        for step in range(1, self.ny):
            self.across(self.z, step, True).start()

    def pair(self):
        for step in range(1, self.ny):
            self.arrival(self.z, step).wait_recv()

        @pl.when(self.z < ZS - 1)
        def _():
            self.right(0).start()

        @pl.when(self.z > 0)
        def _():
            self.left(0).start()

        self.twin(self.z).start()

    def hop(self, k):
        @pl.when(self.z >= k)
        def _():
            self.right(k - 1).wait_recv()
            if k < ZS - 1:
                @pl.when(self.z < ZS - 1)
                def _():
                    self.right(k).start()
            self.twin(self.z - k).start()

        @pl.when(self.z + k < ZS)
        def _():
            self.left(k - 1).wait_recv()
            if k < ZS - 1:
                @pl.when(self.z > 0)
                def _():
                    self.left(k).start()
            self.twin(self.z + k).start()

    def finish(self):
        for k in range(ZS - 1):
            @pl.when((self.z < ZS - 1) & (self.z >= k))
            def _():
                self.right(k).wait_send()

            @pl.when((self.z > 0) & (self.z + k < ZS))
            def _():
                self.left(k).wait_send()
        for step in range(1, self.ny):
            self.across(self.z, step).wait_send()
        mine, theirs = self.twins()
        mine.wait_send()
        theirs.wait_recv()


def gather_sems(ny):
    sem = pltpu.SemaphoreType.DMA
    return [sem((ZS - 1,)), sem((ZS - 1,)), sem((ZS - 1,)), sem((ZS - 1,)), sem((max(ny - 1, 1),)), sem((max(ny - 1, 1),)),
            sem((1,)), sem((1,))]


def greet_all(ny, heads):
    z, y, core = place(ny)
    head = lax.axis_index("head")
    barrier = pltpu.get_barrier_semaphore()

    def signal(device):
        pl.semaphore_signal(barrier, 1, device_id=device, device_id_type=MESH)

    for step in range(1, ZS):
        signal({"scene": (z + step) % ZS * ny + y})
    for step in range(1, ny):
        signal({"scene": z * ny + (y + step) % ny})
    for step in range(1, heads):
        signal({"head": (head + step) % heads})
    signal({"seq": 1 - core})
    pl.semaphore_wait(barrier, ZS + ny - 1 + heads - 1)


def split_cols(total, parts):
    size = total // parts
    return [pl.ds(i * size, size) for i in range(parts)]


def forward_kernel(dims, counts, gain_one, shift_one, gain_two, shift_two, w_qkv, shard_out, shard_up, shard_down, tokens,
                   n1_out, q_out, k_out, v_out, full_qkv, full_out, full_up, full_down, probs, context, context_all, inverse,
                   w0, hat, n1, q_s, k_s, v_s, bias, ctx_s, scores, tops, probs_v, probs_sem, local_sem, kv_send, kv_recv, xw_send, xw_recv, xt_send, xt_recv, xc_send, xc_recv, *sems):
    ny, heads, rows, width, size, block, pairs, steps_q, halves = dims
    pair, part = pl.program_id(0), pl.program_id(1)
    step = pair * steps_q + part
    z, y, core = place(ny)
    head = lax.axis_index("head")
    d_model = tokens.shape[1]
    per = 8
    own_cols = pl.ds(pl.multiple_of(head * width, width), width)

    def of(i):
        return sems[i * per:(i + 1) * per]

    group = 6 * size
    edges = [0] + [128 + (p + 1) * group for p in range(pairs)]
    firsts = []
    for p in range(pairs):
        cols = pl.ds(edges[p], edges[p + 1] - edges[p])
        firsts.append(Gather(ny, partial(lambda c: w0.at[z, y, core, :, c], cols), w0, cols, of(2 + 2 * halves + p)))
    outer = Gather(ny, lambda: shard_out, full_out, own_cols, of(1))
    thick = []
    for n, (shard, full) in enumerate(((shard_up, full_up), (shard_down, full_down))):
        for i, cols in enumerate(split_cols(full_up.shape[-1], halves)):
            kind = PairGather if n == 1 and i == halves - 1 else Gather
            thick.append(kind(ny, partial(lambda s, c: s.at[:, c], shard, cols), full, cols, of(2 + n * halves + i)))
    up_a, up_b, down_a, down_b = thick

    def local(src, dst, i):
        return pltpu.make_async_copy(src, dst, local_sem.at[i])

    def cols_of(step):
        return pl.ds(pl.multiple_of((head + heads - step) % heads * width, width), width)

    def out_copy(step):
        mine = full_out.at[:, :, core, :, own_cols]
        return remote(mine, mine, xw_send.at[step - 1], xw_recv.at[step - 1], {"head": (head + step) % heads})

    def out_twin(step):
        other = full_out.at[:, :, core, :, cols_of(step)]
        return remote(other, other, xt_send.at[step - 1], xt_recv.at[step - 1], {"seq": 1 - core})

    def kv_copy(p, i):
        src = (k_s, v_s)[i]
        cols = pl.ds(p * 2 * size, 2 * size)
        return remote(src.at[pl.ds(0, rows), cols], src.at[pl.ds(rows, rows), cols], kv_send.at[p, i], kv_recv.at[p, i],
                      {"seq": 1 - core})

    def project(p):
        tile = min(256, rows)

        @pl.loop(0, rows // tile)
        def _(i):
            at = pl.ds(pl.multiple_of(i * tile, tile), tile)
            w = w0[:, :, :, :, 128 + p * group:128 + (p + 1) * group].reshape(d_model, group)
            value = dot(n1[at], w, 1, 0).astype(LOW)
            cols = pl.ds(p * 2 * size, 2 * size)
            q_s[at, cols] = value[:, :2 * size] * LOW(size ** -0.5)
            k_s[at, cols] = value[:, 2 * size:4 * size]
            v_s[at, cols] = value[:, 4 * size:]

        for i in range(2):
            kv_copy(p, i).start()

    def ctx_copy(p, step):
        cols = pl.ds(pl.multiple_of(p * 2 * size, 2 * size), 2 * size)
        wide = pl.ds(pl.multiple_of(head * width + p * 2 * size, 2 * size), 2 * size)
        return remote(ctx_s.at[:, cols], context_all.at[:, wide], xc_send.at[p, step - 1], xc_recv.at[p, step - 1],
                      {"head": (head + step) % heads})

    own_blocks = [(shard_out, full_out.at[z, y, core, :, own_cols], 1),
                  (shard_up, full_up.at[z, y, core], 2), (shard_down, full_down.at[z, y, core], 3)]
    results = [(w0, full_qkv, 4), (n1, n1_out, 5), (q_s, q_out, 6), (k_s, k_out, 7), (v_s, v_out, 8)]
    ctx_local = (ctx_s, context_all.at[:, own_cols], 9)

    @pl.when(step == 0)
    def _():
        for item in own_blocks:
            local(*item).start()
        greet_all(ny, heads)
        columns = jnp.concatenate([a[...].astype(F32) for a in (gain_one, shift_one, gain_two, shift_two)]
                                  + [jnp.zeros((124, gain_one.shape[1]), F32)], axis=0)
        w0[z, y, core, :, :128] = columns.T.astype(LOW)
        for p in range(pairs):
            for c in range(3):
                w0[z, y, core, :, 128 * (3 * p + c + 1):128 * (3 * p + c + 2)] = w_qkv[c, :, 128 * p:128 * (p + 1)]
            if p < 2:
                firsts[p].begin()
        tile = min(128, rows)

        @pl.loop(0, rows // tile)
        def _(i):
            at = pl.ds(pl.multiple_of(i * tile, tile), tile)
            x = tokens[at].astype(F32)
            centre = x - jnp.mean(x, axis=1, keepdims=True)
            spread = jnp.mean(centre * centre, axis=1, keepdims=True)
            hat[at] = centre * lax.rsqrt(spread + 1e-05)

        low_rows = lax.broadcasted_iota(jnp.int32, bias.shape, 0)
        lane = lax.broadcasted_iota(jnp.int32, bias.shape, 1)
        limit = jnp.where(low_rows < rows, counts[0] - core * rows, counts[0] - (1 - core) * rows + rows)
        bias[...] = jnp.where((low_rows >= limit) & (lane == 0), -1e30, 0.0).astype(LOW)
        after = [
            (0, lambda g: g.hop(1)), (2, lambda g: g.begin()), (0, lambda g: g.hop(2)), (1, lambda g: g.hop(1)), (0, lambda g: g.hop(3)),
            (3, lambda g: g.begin()), (1, lambda g: g.hop(2)), (0, lambda g: g.spread()), (1, lambda g: g.hop(3)),
            (2, lambda g: g.hop(1)), (1, lambda g: g.spread()), (2, lambda g: g.hop(2))]
        for p, act in after[:9]:
            if p < pairs:
                act(firsts[p])
        firsts[0].finish()
        for item in own_blocks:
            local(*item).wait()
        norms = w0[:, :, :, :, :128].reshape(d_model, 128).astype(F32).T
        gain, shift = norms[0:1], norms[1:2]
        tile = min(256, rows)

        @pl.loop(0, rows // tile)
        def _(i):
            at = pl.ds(pl.multiple_of(i * tile, tile), tile)
            n1[at] = (hat[at] * gain + shift).astype(LOW)

        local(*results[1]).start()
        project(0)
        for p, act in after[9:]:
            if p < pairs:
                act(firsts[p])

    total = pairs * steps_q
    per_slot = 2
    in_step = 4 * rows // min(256, rows) // per_slot
    slots = in_step * total

    def send_out():
        for i in range(1, heads):
            out_copy(i).start()

    def pass_out():
        for i in range(1, heads):
            out_copy(i).wait_recv()
            out_twin(i).start()

    def on_pair(p, what, *given):
        if p < pairs:
            getattr(firsts[p], what)(*given)

    events = [
        (0.1, lambda: on_pair(2, "hop", 3)), (0.3, lambda: on_pair(3, "hop", 1)), (0.4, outer.begin),
        (1, lambda: on_pair(3, "hop", 2)), (1.2, lambda: on_pair(2, "spread")), (1.4, up_a.begin),
        (2, lambda: on_pair(3, "hop", 3)), (2.6, lambda: outer.hop(1)), (3.2, lambda: outer.hop(2)), (3.2, up_b.begin),
        (3.8, lambda: on_pair(3, "spread")), (3.9, lambda: outer.hop(3)), (5.2, lambda: up_a.hop(1)), (6, outer.spread), (6.1, send_out),
        (6.5, lambda: up_a.hop(2)), (7, down_a.begin), (7.2, down_b.begin),
        (7.8, lambda: up_a.hop(3)), (9.2, lambda: up_b.hop(1)), (10.5, lambda: up_b.hop(2)), (10.6, pass_out), (10.8, down_b.pair),
        (11.8, lambda: up_b.hop(3)), (12, up_a.spread), (13.2, lambda: down_a.hop(1)), (14.5, lambda: down_a.hop(2)),
        (15.2, lambda: down_b.hop(1)), (15.8, lambda: down_a.hop(3)), (16, lambda: down_b.hop(2)), (16, up_b.spread),
        (16, down_a.spread), (16, lambda: down_b.hop(3))]

    def run(slot_in_step):
        for when, act in events:
            slot = min(int(when * slots / 16), slots - 1)
            if when < 16 and slot % in_step == slot_in_step:
                pl.when(step == slot // in_step)(act)

    for p in range(pairs):
        @pl.when(step == p * steps_q)
        def _():
            if p == 0:
                for i in range(2):
                    kv_copy(0, i).wait()
            if p + 1 < pairs:
                firsts[p + 1].finish()
                project(p + 1)
            else:
                for item in (results[0], *results[2:]):
                    local(*item).start()

        if p + 1 < pairs:
            @pl.when(step == (p + 1) * steps_q - 1)
            def _():
                for i in range(2):
                    kv_copy(p + 1, i).wait()

    width2, chunk = 2 * size, min(256, rows)
    n_chunks = 2 * rows // chunk
    ones = (lax.broadcasted_iota(jnp.int32, (block, bias.shape[1]), 1) == 0).astype(LOW)

    def asked(at, h):
        rows_at = pl.ds(pl.multiple_of(at % steps_q * block, block), block)
        cols_at = pl.ds(pl.multiple_of(at // steps_q * width2, width2), width2)
        return jnp.concatenate([only_head(q_s[rows_at, cols_at], h, size), ones], axis=1)

    def score(at, query, slot, c, top):
        cols_at = pl.ds(pl.multiple_of(at // steps_q * width2, width2), width2)
        keys_at = pl.ds(c * chunk, chunk)
        value = dot(jnp.concatenate([k_s[keys_at, cols_at], bias[keys_at]], axis=1), query, 1, 1)
        scores[slot, keys_at] = value
        return jnp.maximum(top, jnp.max(value.reshape(chunk // 8, 8, block), axis=0))

    def weigh(h, c, top, total_e):
        keys_at = pl.ds(c * chunk, chunk)
        expo = jnp.exp(scores[h, keys_at] - top)
        probs_v[slot_now, h, keys_at] = expo.astype(LOW)
        return total_e + jnp.sum(expo.reshape(chunk // 8, 8, block), axis=0)

    slot_now = step % 2

    def probs_copy(at):
        there = pl.ds(pl.multiple_of(at % steps_q * block, block), block)
        return pltpu.make_async_copy(probs_v.at[at % 2], probs.at[pl.ds(at // steps_q * 2, 2), :, there], probs_sem.at[at % 2])

    @pl.when(step >= 2)
    def _():
        probs_copy(step - 2).wait()

    lowest = jnp.full((8, block), -3e38, F32)

    @pl.when(step == 0)
    def _():
        top, query = lowest, asked(0, 0)
        for c in range(n_chunks):
            top = score(0, query, 0, c, top)
        tops[...] = top

    cols = pl.ds(pl.multiple_of(pair * width2, width2), width2)
    following = jnp.minimum(step + 1, total - 1)
    values_t = v_s[:, cols].T
    pieces = []
    for h in range(2):
        top = jnp.max(tops[...], axis=0, keepdims=True)
        total_e, next_top = jnp.zeros((8, block), F32), lowest
        ahead = (step, 1) if h == 0 else (following, 0)
        query = asked(*ahead)
        for c in range(n_chunks):
            if c % per_slot == 0:
                run(h * (n_chunks // per_slot) + c // per_slot)
            next_top = score(ahead[0], query, 1 - h, c, next_top)
            total_e = weigh(h, c, top, total_e)
        tops[...] = next_top
        over = 1.0 / jnp.sum(total_e, axis=0, keepdims=True)
        pieces.append(dot(values_t, probs_v[slot_now, h], 1, 0)[h * size:(h + 1) * size] * over)
        inverse[0, h:h + 1] = over
    here = jnp.concatenate(pieces, axis=0).T.astype(LOW)
    probs_copy(step).start()
    context[...] = here
    ctx_s[pl.ds(pl.multiple_of(part * block, block), block), cols] = here

    @pl.when(part == steps_q - 1)
    def _():
        for i in range(1, heads):
            ctx_copy(pair, i).start()

    @pl.when(step == total - 1)
    def _():
        local(*ctx_local).start()
        for when, act in events:
            if when >= 16:
                act()
        for gather in (outer, *thick):
            gather.finish()
        for item in results:
            local(*item).wait()
        local(*ctx_local).wait()
        for at in range(max(total - 2, 0), total):
            probs_copy(at).wait()
        for i in range(1, heads):
            out_copy(i).wait_send()
            out_twin(i).wait()
            for p in range(pairs):
                ctx_copy(p, i).wait()


def forward(counts, norms, w_qkv, shard_out, shard_up, shard_down, tokens, scenes, heads, size):
    ny = scenes // ZS
    rows, d_model = tokens.shape
    rl, width = shard_out.shape
    hidden = shard_up.shape[1]
    pairs = width // (2 * size)
    block = min(512, rows)
    steps_q = rows // block
    halves = 2
    sem = pltpu.SemaphoreType.DMA
    any_space = pl.BlockSpec(memory_space=pl.ANY)
    shape = jax.ShapeDtypeStruct
    wide = 128 + 3 * width
    outs = [shape((rows, d_model), LOW), shape((rows, width), LOW), shape((2 * rows, width), LOW), shape((2 * rows, width), LOW),
            shape((ZS, ny, 2, rl, wide), LOW), shape((ZS, ny, 2, rl, d_model), LOW), shape((ZS, ny, 2, rl, hidden), LOW),
            shape((ZS, ny, 2, rl, hidden), LOW), shape((2 * pairs, 2 * rows, rows), LOW), shape((rows, width), LOW),
            shape((rows, d_model), LOW), shape((pairs, 8, rows), F32)]
    out_specs = [any_space] * 8 + [
        any_space, pl.BlockSpec((block, 2 * size), lambda p, i: (i, p)),
        any_space, pl.BlockSpec((1, 8, block), lambda p, i: (p, 0, i))]
    scratch = [pltpu.VMEM((ZS, ny, 2, rl, wide), LOW), pltpu.VMEM((rows, d_model), F32), pltpu.VMEM((rows, d_model), LOW),
               pltpu.VMEM((rows, width), LOW), pltpu.VMEM((2 * rows, width), LOW), pltpu.VMEM((2 * rows, width), LOW),
               pltpu.VMEM((2 * rows, 128), LOW), pltpu.VMEM((rows, width), LOW),
               pltpu.VMEM((2, 2 * rows, block), F32), pltpu.VMEM((8, block), F32),
               pltpu.VMEM((2, 2, 2 * rows, block), LOW), sem((2,)), sem((10,)), sem((pairs, 2)), sem((pairs, 2)),
               sem((max(heads - 1, 1),)), sem((max(heads - 1, 1),)), sem((max(heads - 1, 1),)), sem((max(heads - 1, 1),)), sem((pairs, max(heads - 1, 1))), sem((pairs, max(heads - 1, 1)))]
    for _ in range(2 + 2 * halves + pairs):
        scratch += gather_sems(ny)
    dims = (ny, heads, rows, width, size, block, pairs, steps_q, halves)
    flops = 2 * rows * d_model * 3 * width + 8 * rows * rows * width
    results = pl.pallas_call(
        partial(forward_kernel, dims),
        grid=(pairs, steps_q),
        out_shape=outs,
        in_specs=[pl.BlockSpec(memory_space=pltpu.SMEM)] + [pl.BlockSpec(memory_space=pltpu.VMEM)] * 8 + [pl.BlockSpec(memory_space=pltpu.VMEM)],
        out_specs=out_specs,
        scratch_shapes=scratch,
        compiler_params=pltpu.CompilerParams(collective_id=0, has_side_effects=True, vmem_limit_bytes=60 * 2**20),
        cost_estimate=pl.CostEstimate(flops=flops, bytes_accessed=60 * 2**20, transcendentals=0),
        name="forward_attention",
    )(counts, *[a.reshape(1, rl) for a in norms], w_qkv, shard_out, shard_up, shard_down, tokens)
    n1, q, k, v, full_qkv, full_out, full_up, full_down, probs, context, context_all, inverse = results
    flat = lambda a: a.reshape(d_model, a.shape[-1])
    return n1, q, k, v, flat(full_qkv), flat(full_out), flat(full_up), flat(full_down), probs, context, context_all, inverse


class Scatter:
    def __init__(self, ny, parts, cols, bufs, sems):
        self.ny, self.parts, self.cols = ny, parts, cols
        self.own, self.from_core, self.from_y, self.sum_two, self.from_z = bufs
        self.load_sem, self.csend, self.crecv, self.ysend, self.yrecv, self.zsend, self.zrecv = sems
        self.z, self.y, self.core = place(ny)

    def load(self):
        return pltpu.make_async_copy(self.parts.at[:, :, self.core, :, self.cols], self.own, self.load_sem.at[0])

    def to_core(self):
        return remote(self.parts.at[:, :, 1 - self.core, :, self.cols], self.from_core, self.csend.at[0], self.crecv.at[0],
                      {"seq": 1 - self.core})

    def to_y(self, step):
        yy = (self.y + step) % self.ny
        return remote(self.own.at[:, yy], self.from_y.at[step - 1], self.ysend.at[step - 1], self.yrecv.at[step - 1],
                      {"scene": self.z * self.ny + yy})

    def to_z(self, step):
        zz = (self.z + step) % ZS
        return remote(self.sum_two.at[zz], self.from_z.at[step - 1], self.zsend.at[step - 1], self.zrecv.at[step - 1],
                      {"scene": zz * self.ny + self.y})

    def begin(self):
        self.load().start()
        self.to_core().start()

    def one(self):
        self.load().wait()
        self.to_core().wait_recv()
        for zz in range(ZS):
            for yy in range(self.ny):
                self.own[zz, yy] = (self.own[zz, yy].astype(F32) + self.from_core[zz, yy].astype(F32)).astype(LOW)
        for step in range(1, self.ny):
            self.to_y(step).start()

    def two(self):
        for step in range(1, self.ny):
            self.to_y(step).wait_recv()
        for zz in range(ZS):
            total = self.own[zz, self.y].astype(F32)
            for step in range(1, self.ny):
                total += self.from_y[step - 1, zz].astype(F32)
            self.sum_two[zz] = total.astype(LOW)
        for step in range(1, ZS):
            self.to_z(step).start()

    def three(self, out, alone=False):
        for step in range(1, ZS):
            self.to_z(step).wait_recv()
        total = self.sum_two[self.z].astype(F32)
        for step in range(1, ZS):
            total += self.from_z[step - 1].astype(F32)
        if alone:
            out[...] = total
        else:
            out[:, self.cols] = total

    def finish(self):
        self.to_core().wait_send()
        for step in range(1, self.ny):
            self.to_y(step).wait_send()
        for step in range(1, ZS):
            self.to_z(step).wait_send()


SCATTER_BUFS, SCATTER_SEMS = 5, 7


def scatter_scratch(ny, rl, cols):
    sem = pltpu.SemaphoreType.DMA
    other = max(ny - 1, 1)
    return [pltpu.VMEM((ZS, ny, rl, cols), LOW), pltpu.VMEM((ZS, ny, rl, cols), LOW), pltpu.VMEM((other, ZS, rl, cols), LOW),
            pltpu.VMEM((ZS, rl, cols), LOW), pltpu.VMEM((ZS - 1, rl, cols), LOW),
            sem((1,)), sem((1,)), sem((1,)), sem((other,)), sem((other,)), sem((ZS - 1,)), sem((ZS - 1,))]


def make_scatters(ny, plan, scratch):
    n = SCATTER_BUFS + SCATTER_SEMS
    result = []
    for i, (parts, cols) in enumerate(plan):
        mine = scratch[i * n:(i + 1) * n]
        result.append(Scatter(ny, parts, cols, mine[:SCATTER_BUFS], mine[SCATTER_BUFS:]))
    return result

def middle_kernel(dims, tokens, context_all, cotangent, full_qkv, full_out, full_up, full_down,
                  resid_grad, base, mlp_low, grad_context, norm_two, parts_out, parts_up, parts_down, mine_down,
                  x_v, ctx_v, cot_v, norm_v, wo, wu, wd, n2, act, gu, resid, part, low, arrived, up_v, down_v, out_v, gctx_v,
                  base_v, mlp_v, in_sem, out_sem, slot_sem, x_send, x_recv, g_send, g_recv, *scratch):
    ny, heads, rows, d_model, width, hidden, tile, size_f, first_cols = dims
    head = lax.axis_index("head")
    chunks = rows // tile
    part_rows = rows // heads
    per_part = part_rows // tile
    (down,) = make_scatters(ny, [(down_v, pl.ds(0, first_cols))], scratch)
    own_rows = pl.ds(pl.multiple_of(head * part_rows, part_rows), part_rows)

    def load(src, dst, i):
        return pltpu.make_async_copy(src, dst, in_sem.at[i])

    loads = [load(context_all, ctx_v, 0), load(full_out, wo, 1), load(tokens, x_v, 2), load(full_qkv.at[:, pl.ds(0, 128)], norm_v, 3),
             load(full_up, wu, 4), load(cotangent, cot_v, 5), load(full_down, wd, 6)]
    for item in loads:
        item.start()
    half = tile // 2

    def place_of(i):
        whole_tile = not isinstance(i, int)
        number = 0 if not whole_tile and i == chunks else i
        step = number // per_part + 1
        within = number % per_part * tile
        size = tile if whole_tile or 0 < i < chunks else half
        within = within + (half if not whole_tile and i == 0 else 0)
        return step, within, size

    def rows_of(i):
        step, within, size = place_of(i)
        return pl.ds(pl.multiple_of((head + step) % heads * part_rows + within, half), size)

    def x_copy(i, step):
        _, within, size = place_of(i)
        return remote(low.at[rows_of(i)], arrived.at[step - 1, pl.ds(within, size)], x_send.at[i], x_recv.at[i],
                      {"head": (head + step) % heads})

    def g_copy(j, step):
        to = (head + step) % heads
        at = pl.ds(j * tile, tile)
        there = pl.ds(pl.multiple_of(head * part_rows + j * tile, tile), tile)
        return remote(gctx_v.at[at, pl.ds(pl.multiple_of(to * width, width), width)], grad_context.at[there],
                      g_send.at[j, step - 1], g_recv.at[j, step - 1], {"head": to})

    greet_all(ny, heads)
    for item in loads[:4]:
        item.wait()
    norms = norm_v[...].astype(F32).T
    gain, shift = norms[2:3], norms[3:4]

    def hat_of(value):
        centre = value - jnp.mean(value, axis=1, keepdims=True)
        spread = lax.rsqrt(jnp.mean(centre * centre, axis=1, keepdims=True) + 1e-05)
        return centre * spread, spread

    norm_two[...] = jnp.zeros_like(norm_two)

    def forward_and_back(i, early=False):
        at = rows_of(i)
        value = x_v[at].astype(F32) + dot(ctx_v[at], wo[...], 1, 1)
        resid[at] = value
        n2[at] = (hat_of(value)[0] * gain + shift).astype(LOW)
        if early:
            loads[4].wait()
        for f in range(hidden // size_f):
            cols = slice(f * size_f, (f + 1) * size_f)
            u = dot(n2[at], wu[:, cols], 1, 0)
            if early and f == 0:
                loads[5].wait()
                loads[6].wait()
            ga = dot(cot_v[at], wd[:, cols], 1, 0)
            phi = 0.5 + 0.5 * lax.erf(u * (0.5 ** 0.5))
            act[at, cols] = (u * phi).astype(LOW)
            gu[at, cols] = (ga * (phi + u * (jnp.exp(u * u * -0.5) * 0.3989422804014327))).astype(LOW)
        total = dot(gu[at], wu[...], 1, 1)
        part[at] = total
        low[at] = total.astype(LOW)

    def sums(i):
        at = rows_of(i)
        total = part[at]
        hat, _ = hat_of(resid[at])
        norm_two[0:1] += jnp.sum(total * hat, axis=0, keepdims=True)
        norm_two[1:2] += jnp.sum(total, axis=0, keepdims=True)

    if heads > 1:
        forward_and_back(chunks, True)
        x_copy(chunks, 1).start()
        forward_and_back(0)
        x_copy(0, 1).start()
        for step in range(1, heads):
            first = (step - 1) * per_part

            @pl.loop(max(first, 1), first + per_part)
            def _(i):
                forward_and_back(i)
                x_copy(i, step).start()

    else:
        forward_and_back(chunks, True)
        forward_and_back(0)

    @pl.loop(max(chunks - per_part, 1), chunks)
    def _(i):
        forward_and_back(i)

    def weight_grad(src, other, dst, count):
        per_z = d_model // ZS
        for f in range(count // size_f):
            cols = slice(f * size_f, (f + 1) * size_f)

            @pl.loop(0, ZS // 2)
            def _(j):
                at = pl.ds(pl.multiple_of(j * 2 * per_z, 2 * per_z), 2 * per_z)
                value = dot(src[:, at], other[:, cols], 0, 0).astype(LOW)
                dst[pl.ds(2 * j, 2), :, :, :, cols] = value.reshape(2, *dst.shape[1:4], size_f)

    weight_grad(cot_v, act, down_v, hidden)
    down.begin()

    def own_store(j):
        at = pl.ds(j * tile, tile)
        there = pl.ds(pl.multiple_of(head * part_rows + j * tile, tile), tile)
        return (pltpu.make_async_copy(part.at[there], resid_grad.at[at], out_sem.at[3 + 2 * j]),
                pltpu.make_async_copy(gctx_v.at[at, pl.ds(pl.multiple_of(head * width, width), width)], grad_context.at[there],
                                      out_sem.at[4 + 2 * j]))

    for j in range(per_part):
        at = pl.ds(pl.multiple_of(head * part_rows + j * tile, tile), tile)
        total = part[at]
        for step in range(1, heads):
            i = (step - 1) * per_part + j
            x_copy(i, step).wait_recv()
            if i == 0:
                x_copy(chunks, step).wait_recv()
            total += arrived[step - 1, j * tile:(j + 1) * tile].astype(F32)
        hat, spread = hat_of(resid[at])
        own_part = part[at]
        norm_two[0:1] += jnp.sum(own_part * hat, axis=0, keepdims=True)
        norm_two[1:2] += jnp.sum(own_part, axis=0, keepdims=True)
        scaled = total * gain
        inner = scaled - jnp.mean(scaled, axis=1, keepdims=True) - hat * jnp.mean(scaled * hat, axis=1, keepdims=True)
        total = cot_v[at].astype(F32) + inner * spread
        part[at] = total
        rounded = total.astype(LOW)
        low[at] = rounded
        gctx_v[j * tile:(j + 1) * tile] = dot(rounded, wo[...], 1, 0).astype(LOW)
        for step in range(1, heads):
            g_copy(j, step).start()
        for item in own_store(j):
            item.start()
    down.one()
    weight_grad(n2, gu, up_v, hidden)
    stores = [pltpu.make_async_copy(up_v, parts_up, out_sem.at[0]), pltpu.make_async_copy(down_v, parts_down, out_sem.at[1]),
              pltpu.make_async_copy(out_v, parts_out, out_sem.at[2])]
    for item in stores[:2]:
        item.start()
    down.two()
    weight_grad(low.at[own_rows], ctx_v.at[own_rows], out_v, d_model)
    stores[2].start()

    def slot_copies(i):
        at = pl.ds(pl.multiple_of(i * tile, tile), tile)
        slot = i % 2
        return (pltpu.make_async_copy(base_v.at[slot], base.at[at], slot_sem.at[0, slot]),
                pltpu.make_async_copy(mlp_v.at[slot], mlp_low.at[at], slot_sem.at[1, slot]))

    def slot_loop(i):
        at = pl.ds(pl.multiple_of(i * tile, tile), tile)
        value = dot(act[at], wd[...], 1, 1)

        @pl.when(i >= 2)
        def _():
            for item in slot_copies(i - 2):
                item.wait()

        base_v[i % 2] = (resid[at] + value).astype(LOW)
        mlp_v[i % 2] = value.astype(LOW)
        for item in slot_copies(i):
            item.start()

    pl.loop(0, chunks)(slot_loop)
    if heads > 1:
        sums(chunks)
        sums(0)
        pl.loop(1, chunks - per_part)(sums)
    for i in range(max(0, chunks - 2), chunks):
        for item in slot_copies(i):
            item.wait()
    down.three(mine_down)
    down.finish()
    for item in stores:
        item.wait()
    for j in range(per_part):
        for item in own_store(j):
            item.wait()
        for step in range(1, heads):
            g_copy(j, step).wait()
    for step in range(1, heads):
        for j in range(per_part):
            x_copy((step - 1) * per_part + j, step).wait_send()
    if heads > 1:
        x_copy(chunks, 1).wait_send()


def shares(hidden):
    n = hidden // 128
    first = max(n // 8, 1)
    return first * 128, (n - first) * 128


def middle(tokens, context_all, cotangent, full_qkv, full_out, full_up, full_down, scenes, heads):
    ny = scenes // ZS
    rows, d_model = tokens.shape
    rl = d_model // (2 * scenes)
    hidden, width = full_up.shape[1], d_model // heads
    tile, size_f = min(256, rows // heads), min(1024, hidden)
    part_rows = rows // heads
    per_part = part_rows // tile
    chunks = rows // tile
    first_cols = shares(hidden)[0]
    others = max(heads - 1, 1)
    sem = pltpu.SemaphoreType.DMA
    shape, vmem = jax.ShapeDtypeStruct, pltpu.VMEM
    any_space, whole = pl.BlockSpec(memory_space=pl.ANY), pl.BlockSpec(memory_space=pltpu.VMEM)
    big, wide, blocks = (rows, d_model), (rows, hidden), (ZS, ny, 2, rl, hidden)
    scratch = [vmem(big, LOW), vmem(big, LOW), vmem(big, LOW), vmem((d_model, 128), LOW), vmem((d_model, d_model), LOW),
               vmem((d_model, hidden), LOW), vmem((d_model, hidden), LOW), vmem(big, LOW), vmem(wide, LOW), vmem(wide, LOW),
               vmem(big, F32), vmem(big, F32), vmem(big, LOW), vmem((others, part_rows, d_model), LOW), vmem(blocks, LOW),
               vmem(blocks, LOW), vmem((ZS, ny, 2, rl, d_model), LOW), vmem((part_rows, d_model), LOW), vmem((2, tile, d_model), LOW),
               vmem((2, tile, d_model), LOW), sem((7,)), sem((3 + 2 * per_part,)), sem((2, 2)), sem((chunks + 1,)),
               sem((chunks + 1,)), sem((per_part, others)), sem((per_part, others))]
    scratch += scatter_scratch(ny, rl, first_cols)
    return pl.pallas_call(
        partial(middle_kernel, (ny, heads, rows, d_model, width, hidden, tile, size_f, first_cols)),
        out_shape=[shape((part_rows, d_model), F32), shape(big, LOW), shape(big, LOW), shape((rows, width), LOW), shape((8, d_model), F32),
                   shape((ZS, ny, 2, rl, d_model), LOW), shape(blocks, LOW), shape(blocks, LOW), shape((rl, first_cols), F32)],
        in_specs=[any_space] * 7,
        out_specs=[any_space] * 4 + [whole] + [any_space] * 3 + [whole],
        scratch_shapes=scratch,
        compiler_params=pltpu.CompilerParams(collective_id=3, has_side_effects=True, vmem_limit_bytes=63 * 2**20),
        cost_estimate=pl.CostEstimate(flops=14 * rows * d_model * hidden, bytes_accessed=50 * 2**20, transcendentals=0),
        name="middle_stage",
    )(tokens, context_all, cotangent, full_qkv, full_out, full_up, full_down)


def backward_kernel(dims, probs, queries, keys, values, grad, context, inverse, parts_out, parts_up, mlp_low,
                    grads_out, mine_out, mine_up, mlp_land,
                    grads, grads_sem,
                    dk_acc, dv_acc, kept, stage, landed, kv_send, kv_recv, m_send, m_recv, *scratch):
    ny, heads, rows, size, pairs, steps_q, halves = dims
    pair, part = pl.program_id(0), pl.program_id(1)
    step = pair * steps_q + part
    total = pairs * steps_q
    block = grad.shape[0]
    z, y, core = place(ny)
    width = parts_out.shape[-1]
    ends = split_cols(width, 2)
    plan = [(parts_out, ends[0])] + [(parts_up, cols) for cols in split_cols(parts_up.shape[-1], halves)] + [(parts_out, ends[1])]
    scatters = make_scatters(ny, plan, scratch)
    targets = [mine_out] + [mine_up] * halves + [mine_out]

    def kv_copy(p, i):
        return remote(stage.at[p, i], landed.at[p, i], kv_send.at[p, i], kv_recv.at[p, i], {"seq": 1 - core})

    head = lax.axis_index("head")

    def mlp_copy(i, step):
        return remote(mlp_low.at[pl.ds(i * (rows // 4), rows // 4)], mlp_land.at[step - 1, pl.ds(i * (rows // 4), rows // 4)],
                      m_send.at[i, step - 1], m_recv.at[i, step - 1], {"head": (head + step) % heads})

    @pl.when(step == 0)
    def _():
        greet_all(ny, heads)
        for i in range(4):
            for j in range(1, heads):
                mlp_copy(i, j).start()
        for item in scatters:
            item.begin()

    slots = 2 * total
    plan_at = [(0.3 + 0.3 * i, 3.5 + 2.3 * i, 7.0 + 2.3 * i) for i in range(len(scatters))]
    events = sorted((plan_at[i][j], i, j + 1) for i in range(len(scatters)) for j in range(3))

    def run(slot_in_step):
        for when, i, what in events:
            slot = min(int(when * min(1.0, slots / 16)), slots)
            if slot == slots or slot % 2 != slot_in_step:
                continue

            @pl.when(step == slot // 2)
            def _():
                if what == 1:
                    scatters[i].one()
                elif what == 2:
                    scatters[i].two()
                else:
                    scatters[i].three(targets[i])

    @pl.when(part == 0)
    def _():
        dk_acc[...] = jnp.zeros_like(dk_acc)
        dv_acc[...] = jnp.zeros_like(dv_acc)

    upper = grad[...].astype(F32)
    inner = (upper * context[...].astype(F32)).T
    upper_t = upper.T
    row = lax.broadcasted_iota(jnp.int32, upper_t.shape, 0)
    keys_t = keys[...].T
    pieces = []
    for h in range(2):
        run(h)
        over = inverse[0, h:h + 1]
        shift = jnp.sum(inner[h * size:(h + 1) * size], axis=0, keepdims=True) * over
        scaled = jnp.where(row // size == h, upper_t * over, 0.0)
        dp = dot(values[...], scaled.astype(LOW), 1, 0) - shift
        low = probs[h]
        ds = (low.astype(F32) * dp).astype(LOW)
        dv_acc[...] += dot(low, scaled.T.astype(LOW), 1, 0)
        dk_acc[...] += dot(ds, only_head(queries[...], h, size), 1, 0)
        pieces.append(dot(keys_t, ds, 1, 0)[h * size:(h + 1) * size])
    grads[pl.ds(pl.multiple_of(part * block, block), block), pl.ds(pl.multiple_of(pair * 6 * size, 2 * size), 2 * size)] = (
        (jnp.concatenate(pieces, axis=0) * size ** -0.5).T.astype(LOW))

    @pl.when(part == steps_q - 1)
    def _():
        for i, acc in enumerate((dk_acc, dv_acc)):
            stage[pair, i] = acc[rows:].astype(LOW)
            kv_copy(pair, i).start()
            kept[pair, i] = acc[:rows]

    @pl.when(step == total - 1)
    def _():
        for when, i, what in events:
            if min(int(when * min(1.0, slots / 16)), slots) == slots:
                if what == 1:
                    scatters[i].one()
                elif what == 2:
                    scatters[i].two()
                else:
                    scatters[i].three(targets[i])
        for item in scatters:
            item.finish()
        for p in range(pairs):
            for i in range(2):
                kv_copy(p, i).wait()
                grads[:, (3 * p + i + 1) * 2 * size:(3 * p + i + 2) * 2 * size] = (kept[p, i] + landed[p, i].astype(F32)).astype(LOW)
        store = pltpu.make_async_copy(grads, grads_out, grads_sem)
        store.start()
        for i in range(4):
            for j in range(1, heads):
                mlp_copy(i, j).wait()
        store.wait()


def backward(probs, q, k, v, grad, context, inverse, parts_out, parts_up, mlp_low, scenes, heads, size):
    ny = scenes // ZS
    rows, width = q.shape
    pairs = width // (2 * size)
    block = min(512, rows)
    d_model, hidden = parts_out.shape[-1], parts_up.shape[-1]
    rl = d_model // (2 * scenes)
    others = max(heads - 1, 1)
    halves = 4
    spec = pl.BlockSpec
    q_spec = spec((block, 2 * size), lambda p, i: (i, p))
    k_spec = spec((2 * rows, 2 * size), lambda p, i: (0, p))
    any_space = spec(memory_space=pl.ANY)
    whole = spec(memory_space=pltpu.VMEM)
    shape = jax.ShapeDtypeStruct
    sem = pltpu.SemaphoreType.DMA
    pair_buf = (pairs, 2, rows, 2 * size)
    scratch = [pltpu.VMEM((rows, 3 * width), LOW), sem, pltpu.VMEM((2 * rows, 2 * size), F32), pltpu.VMEM((2 * rows, 2 * size), F32), pltpu.VMEM(pair_buf, F32),
               pltpu.VMEM(pair_buf, LOW), pltpu.VMEM(pair_buf, LOW), sem((pairs, 2)), sem((pairs, 2)), sem((4, others)), sem((4, others))]
    for cols in [d_model // 2] + [hidden // halves] * halves + [d_model // 2]:
        scratch += scatter_scratch(ny, rl, cols)
    return pl.pallas_call(
        partial(backward_kernel, (ny, heads, rows, size, pairs, rows // block, halves)),
        grid=(pairs, rows // block),
        out_shape=[shape((rows, 3 * width), LOW), shape((rl, d_model), F32), shape((rl, hidden), F32), shape((others, rows, d_model), LOW)],
        in_specs=[spec((2, 2 * rows, block), lambda p, i: (p, 0, i)), q_spec, k_spec, k_spec, q_spec, q_spec,
                  spec((1, 8, block), lambda p, i: (p, 0, i)), any_space, any_space, any_space],
        out_specs=[any_space, whole, whole, any_space],
        scratch_shapes=scratch,
        compiler_params=pltpu.CompilerParams(collective_id=1, has_side_effects=True, vmem_limit_bytes=60 * 2**20),
        cost_estimate=pl.CostEstimate(flops=16 * rows * rows * width, bytes_accessed=50 * 2**20, transcendentals=0),
        name="backward_attention",
    )(probs, q, k, v, grad, context, inverse, parts_out, parts_up, mlp_low)


def thirds(start, count):
    n = count // 128
    edges = [start + n * i // 3 * 128 for i in range(4)]
    return [(a, b - a) for a, b in zip(edges, edges[1:])]


def last_kernel(dims, grads, n1, tokens, resid, full_qkv, norm_two, parts_down, down_a, out_all,
                own_grad, done_land, mine_w, mine_norm, mine_out, mine_down,
                g_v, n1_v, x_v, res_v, w_v, in_sem,
                part_one, part_low, arrived, parts_qkv, tiny_land, tiny_own, done_low, x_send, x_recv, t_send, t_recv,
                n_send, n_recv, o_send, o_recv, out_sem, mine_qkv, out_land, *scratch):
    ny, heads, rows, d_model, width, tile, down_at, qkv_at = dims
    z, y, core = place(ny)
    head = lax.axis_index("head")
    wide = full_qkv.shape[1]
    rl = mine_qkv.shape[0]
    plan = [(parts_down, pl.ds(*item)) for item in down_at] + [(parts_qkv, pl.ds(*item)) for item in qkv_at]
    scatters = make_scatters(ny, plan, scratch)
    downs, qkvs = scatters[:len(down_at)], scatters[len(down_at):]
    down_x, down_y, down_z = downs

    def down_done(i):
        downs[i].three(mine_down.at[:, pl.ds(*down_at[i])], True)

    chunks = rows // tile
    part_rows = rows // heads
    per_part = part_rows // tile
    loads = [pltpu.make_async_copy(src, dst, in_sem.at[i]) for i, (src, dst) in enumerate((
        (grads, g_v), (full_qkv, w_v), (n1, n1_v), (tokens, x_v), (resid, res_v)))]
    for item in loads:
        item.start()
    def rows_at(step, j):
        return pl.ds(pl.multiple_of((head + heads + step) % heads * part_rows + j * tile, tile), tile)

    def x_copy(step, j):
        return remote(part_low.at[rows_at(step, j)], arrived.at[step - 1, pl.ds(j * tile, tile)], x_send.at[step - 1, j],
                      x_recv.at[step - 1, j], {"head": (head + step) % heads})

    def t_copy(step, j):
        at = pl.ds(j * tile, tile)
        return remote(done_low.at[at], done_land.at[step - 1, at], t_send.at[step - 1, j], t_recv.at[step - 1, j],
                      {"head": (head + step) % heads})

    def n_copy(step):
        return remote(tiny_own, tiny_land.at[step - 1], n_send.at[step - 1], n_recv.at[step - 1], {"head": (head + step) % heads})

    def o_copy(step):
        to = (head + step) % heads
        return remote(out_all.at[:, pl.ds(pl.multiple_of(to * width, width), width)], out_land.at[step - 1], o_send.at[step - 1],
                      o_recv.at[step - 1], {"head": to})

    def out_copy(j):
        at = pl.ds(j * tile, tile)
        return pltpu.make_async_copy(done_low.at[at], own_grad.at[at], out_sem.at[j])

    greet_all(ny, heads)
    for item in downs:
        item.begin()
    for item in loads[:2]:
        item.wait()

    def partial_sum(step, j):
        at = rows_at(step, j)
        total = dot(g_v[at], w_v[:, 128:], 1, 1)
        part_one[at] = total
        part_low[at] = total.astype(LOW)

    for step in range(1, heads):
        for j in range(per_part):
            partial_sum(step, j)
            x_copy(step, j).start()
    for step in range(1, heads):
        o_copy(step).start()
    down_x.one()
    down_y.one()
    for j in range(per_part):
        partial_sum(0, j)
    for item in loads[2:]:
        item.wait()
    per_z = d_model // ZS
    for zz in range(0, ZS, 2):
        cols = n1_v[:, zz * per_z:(zz + 2) * per_z]
        value = dot(cols, g_v[...], 0, 0).astype(LOW)
        parts_qkv[zz:zz + 2, :, :, :, 128:] = value.reshape(2, ny, 2, rl, 3 * width)
    for item in qkvs[1:]:
        item.begin()
    gain = w_v[:, :128].astype(F32).T[0:1]

    def hat_of(at):
        x = x_v[at].astype(F32)
        centre = x - jnp.mean(x, axis=1, keepdims=True)
        spread = lax.rsqrt(jnp.mean(centre * centre, axis=1, keepdims=True) + 1e-05)
        return centre * spread, spread

    gain_sum = jnp.zeros((1, d_model), F32)
    shift_sum = jnp.zeros((1, d_model), F32)
    for i in range(chunks):
        at = pl.ds(i * tile, tile)
        hat, _ = hat_of(at)
        gain_sum += jnp.sum(part_one[at] * hat, axis=0, keepdims=True)
        shift_sum += jnp.sum(part_one[at], axis=0, keepdims=True)
        if i == chunks // 4:
            qkvs[1].one()
            down_x.two()
        if i == chunks // 2:
            qkvs[2].one()
    sums = jnp.concatenate([gain_sum, shift_sum, norm_two[0:2], jnp.zeros((124, d_model), F32)], axis=0).T.astype(LOW)
    parts_qkv[:, :, :, :, :128] = sums.reshape(ZS, ny, 2, rl, 128)
    qkvs[0].begin()

    def receive(j):
        at = rows_at(0, j)
        here = pl.ds(j * tile, tile)
        total = part_one[at]
        for step in range(1, heads):
            x_copy(step, j).wait_recv()
            total += arrived[step - 1, here].astype(F32)
        hat, spread = hat_of(at)
        scaled = total * gain
        inner = scaled - jnp.mean(scaled, axis=1, keepdims=True) - hat * jnp.mean(scaled * hat, axis=1, keepdims=True)
        total = res_v[here] + inner * spread
        done_low[here] = total.astype(LOW)
        out_copy(j).start()
        for step in range(1, heads):
            t_copy(step, j).start()

    first = pl.ds(pl.multiple_of(head * width, width), width)

    def share(items, i, n):
        return items[len(items) * i // n:len(items) * (i + 1) // n]

    def receive_some(i):
        for j in share(range(per_part), i, 4):
            receive(j)

    def send_norms():
        tiny_own[...] = mine_qkv[:, :128]
        for step in range(1, heads):
            n_copy(step).start()

    receive_some(0)
    qkvs[0].one()
    down_z.one()
    down_y.two()
    receive_some(1)
    mine_down[:, :down_a.shape[1]] = down_a[...]
    down_done(0)
    receive_some(2)
    qkvs[1].two()
    down_done(1)
    receive_some(3)
    qkvs[2].two()
    qkvs[1].three(mine_qkv)
    total = out_all[:, first]
    for step in range(1, heads):
        o_copy(step).wait()
        total += out_land[step - 1]
    mine_out[...] = total
    qkvs[0].two()
    qkvs[2].three(mine_qkv)
    down_z.two()
    qkvs[0].three(mine_qkv)
    send_norms()
    down_done(2)
    total = mine_qkv[:, :128]
    for step in range(1, heads):
        n_copy(step).wait()
        total += tiny_land[step - 1]
    mine_norm[...] = total.T[:8]
    for p in range(width // 128):
        for c in range(3):
            mine_w[c, :, p * 128:(p + 1) * 128] = mine_qkv[:, 128 * (3 * p + c + 1):128 * (3 * p + c + 2)]
    for item in scatters:
        item.finish()
    for j in range(per_part):
        out_copy(j).wait()
        for step in range(1, heads):
            x_copy(step, j).wait_send()
            t_copy(step, j).wait()


def last_stage(grads, n1, tokens, resid, full_qkv, norm_two, parts_down, down_a, out_all, scenes, heads):
    ny = scenes // ZS
    rows, d_model = tokens.shape
    width, hidden = grads.shape[1] // 3, parts_down.shape[-1]
    first, third = shares(hidden)
    rl = d_model // (2 * scenes)
    wide = full_qkv.shape[1]
    part_rows = rows // heads
    tile = min(128, part_rows)
    chunks, per_part = rows // tile, part_rows // tile
    down_at, qkv_at = thirds(first, third), thirds(0, wide)
    others = max(heads - 1, 1)
    sem = pltpu.SemaphoreType.DMA
    shape, vmem = jax.ShapeDtypeStruct, pltpu.VMEM
    any_space, whole = pl.BlockSpec(memory_space=pl.ANY), pl.BlockSpec(memory_space=pltpu.VMEM)
    big, own = (rows, d_model), (part_rows, d_model)
    scratch = [vmem((rows, 3 * width), LOW), vmem(big, LOW), vmem(big, LOW), vmem(own, F32), vmem((d_model, wide), LOW), sem((5,)),
               vmem(big, F32), vmem(big, LOW), vmem((others, *own), LOW), vmem((ZS, ny, 2, rl, wide), LOW), vmem((others, rl, 128), F32),
               vmem((rl, 128), F32), vmem(own, LOW), sem((others, per_part)),
               sem((others, per_part)), sem((others, per_part)), sem((others, per_part)), sem((others,)), sem((others,)),
               sem((others,)), sem((others,)), sem((per_part,)), vmem((rl, wide), F32), vmem((others, rl, width), F32)]
    for _, cols in down_at + qkv_at:
        scratch += scatter_scratch(ny, rl, cols)
    return pl.pallas_call(
        partial(last_kernel, (ny, heads, rows, d_model, width, tile, down_at, qkv_at)),
        out_shape=[shape(own, LOW), shape((others, *own), LOW), shape((3, rl, width), F32), shape((8, rl), F32), shape((rl, width), F32),
                   shape((rl, hidden), F32)],
        in_specs=[any_space] * 5 + [whole, any_space, whole, whole],
        out_specs=[any_space, any_space, whole, whole, whole, whole],
        scratch_shapes=scratch,
        compiler_params=pltpu.CompilerParams(collective_id=2, has_side_effects=True, vmem_limit_bytes=63 * 2**20),
        cost_estimate=pl.CostEstimate(flops=12 * rows * d_model * width, bytes_accessed=30 * 2**20, transcendentals=0),
        name="last_stage",
    )(grads, n1, tokens, resid, full_qkv, norm_two, parts_down, down_a, out_all)


def finish_kernel(heads, tile, base, mlp_land, own, land, w, out, up, down, norm,
                  output, tokens_grad, w_o, out_o, up_o, down_o, n_a, n_b, n_c, n_d,
                  sum_v, base_v, own_v, mlp_v, grad_v, land_v, w_v, out_v, up_v, down_v, base_sem, mlp_sem, own_sem, land_sem, small_sem,
                  out_sem, back_sem, far_sem, last_sem):
    rows = base.shape[0]
    part_rows = rows // heads
    chunks, per_part = rows // tile, part_rows // tile
    head = lax.axis_index("head")
    copy = pltpu.make_async_copy

    def rows_at(step, j):
        return pl.ds(pl.multiple_of((head + heads - step) % heads * part_rows + j * tile, tile), tile)

    def loads(i):
        at = pl.ds(i * tile, tile)
        return copy(base.at[at], base_v.at[at], base_sem.at[i]), copy(mlp_land.at[:, at], mlp_v.at[:, at], mlp_sem.at[i])

    def own_load(j):
        at = pl.ds(j * tile, tile)
        return copy(own.at[at], own_v.at[at], own_sem.at[j])

    land_load = copy(land, land_v, land_sem.at[0])
    smalls = ((w, w_v, w_o), (out, out_v, out_o), (up, up_v, up_o), (down, down_v, down_o))
    small_loads = [copy(src, mid, small_sem.at[i]) for i, (src, mid, _) in enumerate(smalls)]
    small_stores = [copy(mid, dst, last_sem.at[i]) for i, (_, mid, dst) in enumerate(smalls)]

    def out_store(i):
        at = pl.ds(i * tile, tile)
        return copy(sum_v.at[at], output.at[at], out_sem.at[i])

    def own_store(j):
        return copy(grad_v.at[rows_at(0, j)], tokens_grad.at[rows_at(0, j)], back_sem.at[j])

    def far_store(step, j):
        return copy(grad_v.at[rows_at(step, j)], tokens_grad.at[rows_at(step, j)], far_sem.at[step - 1, j])

    for j in range(per_part):
        own_load(j).start()
    if heads > 1:
        land_load.start()
    for i in range(chunks):
        for item in loads(i):
            item.start()
    for item in small_loads:
        item.start()
    for i, dst in enumerate((n_a, n_b, n_c, n_d)):
        dst[...] = norm[i:i + 1]
    for j in range(per_part):
        own_load(j).wait()
        grad_v[rows_at(0, j)] = own_v[j * tile:(j + 1) * tile].astype(F32)
        own_store(j).start()
    if heads > 1:
        land_load.wait()
        for step in range(1, heads):
            for j in range(per_part):
                grad_v[rows_at(step, j)] = land_v[step - 1, j * tile:(j + 1) * tile].astype(F32)
                far_store(step, j).start()
    for i in range(chunks):
        at = pl.ds(i * tile, tile)
        for item in loads(i):
            item.wait()
        total = base_v[at].astype(F32)
        for step in range(1, heads):
            total += mlp_v[step - 1, at].astype(F32)
        sum_v[at] = total
        out_store(i).start()
    for first, second in zip(small_loads, small_stores):
        first.wait()
        second.start()
    for j in range(per_part):
        own_store(j).wait()
        for step in range(1, heads):
            far_store(step, j).wait()
    for i in range(chunks):
        out_store(i).wait()
    for item in small_stores:
        item.wait()


def finish(base, mlp_land, own, land, w, out, up, down, norm, heads):
    rows, d_model = base.shape
    part_rows = rows // heads
    tile = min(128, part_rows)
    chunks, per_part = rows // tile, part_rows // tile
    rl, others = up.shape[0], max(heads - 1, 1)
    spec, shape, vmem, sem = pl.BlockSpec, jax.ShapeDtypeStruct, pltpu.VMEM, pltpu.SemaphoreType.DMA
    any_space, whole = spec(memory_space=pl.ANY), spec(memory_space=pltpu.VMEM)
    return pl.pallas_call(
        partial(finish_kernel, heads, tile),
        in_specs=[any_space] * 8 + [whole],
        out_specs=[any_space] * 6 + [whole] * 4,
        out_shape=[shape((rows, d_model), F32), shape((rows, d_model), F32)] + [shape(a.shape, F32) for a in (w, out, up, down)]
        + [shape((1, rl), F32)] * 4,
        scratch_shapes=[vmem(base.shape, F32), vmem(base.shape, LOW), vmem(own.shape, LOW), vmem(mlp_land.shape, LOW), vmem(base.shape, F32), vmem(land.shape, LOW)]
        + [vmem(a.shape, F32) for a in (w, out, up, down)]
        + [sem((chunks,)), sem((chunks,)), sem((per_part,)), sem((1,)), sem((4,)), sem((chunks,)), sem((per_part,)),
           sem((others, per_part)), sem((4,))],
        compiler_params=pltpu.CompilerParams(vmem_limit_bytes=63 * 2**20),
        name="finish",
    )(base, mlp_land, own, land, w, out, up, down, norm)


def on_device(n_scene, n_head, tokens, counts, w_qkv, w_out, w_up, w_down, gain_one, shift_one, gain_two, shift_two, cotangent):
    rows, d_model = tokens.shape
    width, hidden = w_qkv.shape[2], w_up.shape[1]
    size = 64
    n1, q, k, v, full_qkv, full_out, full_up, full_down, probs, context, context_all, inverse = forward(
        counts, (gain_one, shift_one, gain_two, shift_two), w_qkv, w_out.T, w_up, w_down.T, tokens, n_scene, n_head, size)
    grad_resid, base, mlp_low, grad_context, norm_two, grad_outproj, grad_up, grad_down, down_a = middle(
        tokens, context_all, cotangent, full_qkv, full_out, full_up, full_down, n_scene, n_head)
    grads, out_all, mine_up, mlp_land = backward(
        probs, q, k, v, grad_context, context, inverse, grad_outproj, grad_up, mlp_low, n_scene, n_head, size)
    own, land, mine_qkv, norms, mine_out, mine_down = last_stage(
        grads, n1, tokens, grad_resid, full_qkv, norm_two, grad_down, down_a, out_all, n_scene, n_head)
    output, tokens_grad, mine_qkv, mine_out, mine_up, mine_down, *norms = finish(
        base, mlp_land, own, land, mine_qkv, mine_out, mine_up, mine_down, norms, n_head)
    return (output, tokens_grad, mine_qkv, mine_out.T, mine_up, mine_down.T, *[a.reshape(-1) for a in norms])


def solution(mesh):
    rows, both = ("scene", "seq"), P(("scene", "seq"))
    weights = (P(None, rows, "head"), P("head", rows), P(rows, "head"), P("head", rows), both, both, both, both)
    return jax.shard_map(
        partial(on_device, mesh.shape["scene"], mesh.shape["head"]), mesh=mesh,
        in_specs=(P(rows, None), P("scene"), *weights, P(rows, None)),
        out_specs=(P(rows, None), P(rows, None), *weights),
        check_vma=False,
    )
```

```python
from functools import partial

import jax
import jax.numpy as jnp
from jax import lax
from jax.experimental import pallas as pl
from jax.experimental.pallas import tpu as pltpu
from jax.sharding import PartitionSpec as P

MESH = pl.DeviceIdType.MESH
ZS = 4


def place(ny):
    scene = lax.axis_index("scene")
    return scene // ny, scene % ny, lax.axis_index("seq")


def remote(src, dst, send_sem, recv_sem, device):
    return pltpu.make_async_remote_copy(
        src_ref=src, dst_ref=dst, send_sem=send_sem, recv_sem=recv_sem,
        device_id=device, device_id_type=MESH,
    )


F32 = jnp.float32
LOW = jnp.bfloat16


def dot(a, b, ca, cb):
    return lax.dot_general(a, b, (((ca,), (cb,)), ((), ())), preferred_element_type=F32)


def only_head(x, h, size):
    lane = lax.broadcasted_iota(jnp.int32, x.shape, 1)
    return jnp.where(lane // size == h, x, jnp.zeros_like(x))


class Gather:
    def __init__(self, ny, source, full, cols, sems):
        self.ny, self.source, self.full, self.cols = ny, source, full, cols
        self.rsend, self.rrecv, self.lsend, self.lrecv, self.ysend, self.yrecv, self.csend, self.crecv = sems
        self.z, self.y, self.core = place(ny)

    def at(self, zz, yy):
        return self.full.at[zz, yy, self.core, :, self.cols]

    def right(self, k):
        src = self.source() if k == 0 else self.at(self.z - k, self.y)
        dst = self.at(self.z - k, self.y)
        return remote(src, dst, self.rsend.at[k], self.rrecv.at[k], {"scene": (self.z + 1) * self.ny + self.y})

    def left(self, k):
        src = self.source() if k == 0 else self.at(self.z + k, self.y)
        dst = self.at(self.z + k, self.y)
        return remote(src, dst, self.lsend.at[k], self.lrecv.at[k], {"scene": (self.z - 1) * self.ny + self.y})

    def across(self, zz, step, own=False):
        src = self.source() if own else self.at(zz, self.y)
        peer = self.z * self.ny + (self.y + step) % self.ny
        return remote(src, self.at(zz, self.y), self.ysend.at[step - 1], self.yrecv.at[step - 1], {"scene": peer})

    def arrival(self, zz, step):
        yy = (self.y + self.ny - step) % self.ny
        return remote(self.at(zz, yy), self.at(zz, yy), self.ysend.at[step - 1], self.yrecv.at[step - 1],
                      {"scene": self.z * self.ny + yy})

    def twin(self, zz, step, own=False):
        src = self.source() if own else self.at(zz, (self.y + self.ny - step) % self.ny)
        dst = self.at(zz, (self.y + self.ny - step) % self.ny)
        return remote(src, dst, self.csend.at[0], self.crecv.at[0], {"seq": 1 - self.core})

    def column(self, step):
        yy = (self.y + self.ny - step) % self.ny
        all_z = self.full.at[:, yy, self.core, :, self.cols]
        return remote(all_z, all_z, self.ysend.at[step - 1], self.yrecv.at[step - 1], {"scene": self.z * self.ny + yy})

    def twins(self):
        mine, theirs = [self.full.at[:, :, c, :, self.cols] for c in (self.core, 1 - self.core)]
        return [remote(item, item, self.csend.at[0], self.crecv.at[0], {"seq": 1 - self.core}) for item in (mine, theirs)]

    def begin(self):
        @pl.when(self.z < ZS - 1)
        def _():
            self.right(0).start()

        @pl.when(self.z > 0)
        def _():
            self.left(0).start()

        for step in range(1, self.ny):
            self.across(self.z, step, True).start()
        self.twin(self.z, 0, True).start()

    def hop(self, k):
        @pl.when(self.z >= k)
        def _():
            self.right(k - 1).wait_recv()
            if k < ZS - 1:
                @pl.when(self.z < ZS - 1)
                def _():
                    self.right(k).start()
            for step in range(1, self.ny):
                self.across(self.z - k, step).start()
            self.twin(self.z - k, 0).start()

        @pl.when(self.z + k < ZS)
        def _():
            self.left(k - 1).wait_recv()
            if k < ZS - 1:
                @pl.when(self.z > 0)
                def _():
                    self.left(k).start()
            for step in range(1, self.ny):
                self.across(self.z + k, step).start()
            self.twin(self.z + k, 0).start()

    def spread(self):
        for step in range(1, self.ny):
            self.column(step).wait_recv()
            for zz in range(ZS):
                self.twin(zz, step).start()

    def finish(self):
        for k in range(ZS - 1):
            @pl.when((self.z < ZS - 1) & (self.z >= k))
            def _():
                self.right(k).wait_send()

            @pl.when((self.z > 0) & (self.z + k < ZS))
            def _():
                self.left(k).wait_send()
        for step in range(1, self.ny):
            self.column(step).wait_send()
        mine, theirs = self.twins()
        mine.wait_send()
        theirs.wait_recv()


class PairGather(Gather):
    def row(self, zz):
        return self.full.at[zz, :, self.core, :, self.cols]

    def right(self, k):
        return remote(self.row(self.z - k), self.row(self.z - k), self.rsend.at[k], self.rrecv.at[k],
                      {"scene": (self.z + 1) * self.ny + self.y})

    def left(self, k):
        return remote(self.row(self.z + k), self.row(self.z + k), self.lsend.at[k], self.lrecv.at[k],
                      {"scene": (self.z - 1) * self.ny + self.y})

    def twin(self, zz):
        return remote(self.row(zz), self.row(zz), self.csend.at[0], self.crecv.at[0], {"seq": 1 - self.core})

    def begin(self):
        for step in range(1, self.ny):
            self.across(self.z, step, True).start()

    def pair(self):
        for step in range(1, self.ny):
            self.arrival(self.z, step).wait_recv()

        @pl.when(self.z < ZS - 1)
        def _():
            self.right(0).start()

        @pl.when(self.z > 0)
        def _():
            self.left(0).start()

        self.twin(self.z).start()

    def hop(self, k):
        @pl.when(self.z >= k)
        def _():
            self.right(k - 1).wait_recv()
            if k < ZS - 1:
                @pl.when(self.z < ZS - 1)
                def _():
                    self.right(k).start()
            self.twin(self.z - k).start()

        @pl.when(self.z + k < ZS)
        def _():
            self.left(k - 1).wait_recv()
            if k < ZS - 1:
                @pl.when(self.z > 0)
                def _():
                    self.left(k).start()
            self.twin(self.z + k).start()

    def finish(self):
        for k in range(ZS - 1):
            @pl.when((self.z < ZS - 1) & (self.z >= k))
            def _():
                self.right(k).wait_send()

            @pl.when((self.z > 0) & (self.z + k < ZS))
            def _():
                self.left(k).wait_send()
        for step in range(1, self.ny):
            self.across(self.z, step).wait_send()
        mine, theirs = self.twins()
        mine.wait_send()
        theirs.wait_recv()


def gather_sems(ny):
    sem = pltpu.SemaphoreType.DMA
    return [sem((ZS - 1,)), sem((ZS - 1,)), sem((ZS - 1,)), sem((ZS - 1,)), sem((max(ny - 1, 1),)), sem((max(ny - 1, 1),)),
            sem((1,)), sem((1,))]


def greet_all(ny, heads):
    z, y, core = place(ny)
    head = lax.axis_index("head")
    barrier = pltpu.get_barrier_semaphore()

    def signal(device):
        pl.semaphore_signal(barrier, 1, device_id=device, device_id_type=MESH)

    for step in range(1, ZS):
        signal({"scene": (z + step) % ZS * ny + y})
    for step in range(1, ny):
        signal({"scene": z * ny + (y + step) % ny})
    for step in range(1, heads):
        signal({"head": (head + step) % heads})
    signal({"seq": 1 - core})
    pl.semaphore_wait(barrier, ZS + ny - 1 + heads - 1)


def split_cols(total, parts):
    size = total // parts
    return [pl.ds(i * size, size) for i in range(parts)]


def forward_kernel(dims, counts, gain_one, shift_one, gain_two, shift_two, w_qkv, shard_out, shard_up, shard_down, tokens,
                   n1_out, q_out, k_out, v_out, full_qkv, full_out, full_up, full_down, probs, context, context_all, inverse,
                   w0, hat, n1, q_s, k_s, v_s, bias, ctx_s, scores, tops, probs_v, probs_sem, local_sem, kv_send, kv_recv, xw_send, xw_recv, xt_send, xt_recv, xc_send, xc_recv, *sems):
    ny, heads, rows, width, size, block, pairs, steps_q, halves = dims
    pair, part = pl.program_id(0), pl.program_id(1)
    step = pair * steps_q + part
    z, y, core = place(ny)
    head = lax.axis_index("head")
    d_model = tokens.shape[1]
    per = 8
    own_cols = pl.ds(pl.multiple_of(head * width, width), width)

    def of(i):
        return sems[i * per:(i + 1) * per]

    group = 6 * size
    edges = [0] + [128 + (p + 1) * group for p in range(pairs)]
    firsts = []
    for p in range(pairs):
        cols = pl.ds(edges[p], edges[p + 1] - edges[p])
        firsts.append(Gather(ny, partial(lambda c: w0.at[z, y, core, :, c], cols), w0, cols, of(2 + 2 * halves + p)))
    outer = Gather(ny, lambda: shard_out, full_out, own_cols, of(1))
    thick = []
    for n, (shard, full) in enumerate(((shard_up, full_up), (shard_down, full_down))):
        for i, cols in enumerate(split_cols(full_up.shape[-1], halves)):
            kind = PairGather if n == 1 and i == halves - 1 else Gather
            thick.append(kind(ny, partial(lambda s, c: s.at[:, c], shard, cols), full, cols, of(2 + n * halves + i)))
    up_a, up_b, down_a, down_b = thick

    def local(src, dst, i):
        return pltpu.make_async_copy(src, dst, local_sem.at[i])

    def cols_of(step):
        return pl.ds(pl.multiple_of((head + heads - step) % heads * width, width), width)

    def out_copy(step):
        mine = full_out.at[:, :, core, :, own_cols]
        return remote(mine, mine, xw_send.at[step - 1], xw_recv.at[step - 1], {"head": (head + step) % heads})

    def out_twin(step):
        other = full_out.at[:, :, core, :, cols_of(step)]
        return remote(other, other, xt_send.at[step - 1], xt_recv.at[step - 1], {"seq": 1 - core})

    def kv_copy(p, i):
        src = (k_s, v_s)[i]
        cols = pl.ds(p * 2 * size, 2 * size)
        return remote(src.at[pl.ds(0, rows), cols], src.at[pl.ds(rows, rows), cols], kv_send.at[p, i], kv_recv.at[p, i],
                      {"seq": 1 - core})

    def project(p):
        tile = min(256, rows)

        @pl.loop(0, rows // tile)
        def _(i):
            at = pl.ds(pl.multiple_of(i * tile, tile), tile)
            w = w0[:, :, :, :, 128 + p * group:128 + (p + 1) * group].reshape(d_model, group)
            value = dot(n1[at], w, 1, 0).astype(LOW)
            cols = pl.ds(p * 2 * size, 2 * size)
            q_s[at, cols] = value[:, :2 * size] * LOW(size ** -0.5)
            k_s[at, cols] = value[:, 2 * size:4 * size]
            v_s[at, cols] = value[:, 4 * size:]

        for i in range(2):
            kv_copy(p, i).start()

    def ctx_copy(p, step):
        cols = pl.ds(pl.multiple_of(p * 2 * size, 2 * size), 2 * size)
        wide = pl.ds(pl.multiple_of(head * width + p * 2 * size, 2 * size), 2 * size)
        return remote(ctx_s.at[:, cols], context_all.at[:, wide], xc_send.at[p, step - 1], xc_recv.at[p, step - 1],
                      {"head": (head + step) % heads})

    own_blocks = [(shard_out, full_out.at[z, y, core, :, own_cols], 1),
                  (shard_up, full_up.at[z, y, core], 2), (shard_down, full_down.at[z, y, core], 3)]
    results = [(w0, full_qkv, 4), (n1, n1_out, 5), (q_s, q_out, 6), (k_s, k_out, 7), (v_s, v_out, 8)]
    ctx_local = (ctx_s, context_all.at[:, own_cols], 9)

    @pl.when(step == 0)
    def _():
        for item in own_blocks:
            local(*item).start()
        greet_all(ny, heads)
        columns = jnp.concatenate([a[...].astype(F32) for a in (gain_one, shift_one, gain_two, shift_two)]
                                  + [jnp.zeros((124, gain_one.shape[1]), F32)], axis=0)
        w0[z, y, core, :, :128] = columns.T.astype(LOW)
        for p in range(pairs):
            for c in range(3):
                w0[z, y, core, :, 128 * (3 * p + c + 1):128 * (3 * p + c + 2)] = w_qkv[c, :, 128 * p:128 * (p + 1)]
            if p < 2:
                firsts[p].begin()
        tile = min(128, rows)

        @pl.loop(0, rows // tile)
        def _(i):
            at = pl.ds(pl.multiple_of(i * tile, tile), tile)
            x = tokens[at].astype(F32)
            centre = x - jnp.mean(x, axis=1, keepdims=True)
            spread = jnp.mean(centre * centre, axis=1, keepdims=True)
            hat[at] = centre * lax.rsqrt(spread + 1e-05)

        low_rows = lax.broadcasted_iota(jnp.int32, bias.shape, 0)
        lane = lax.broadcasted_iota(jnp.int32, bias.shape, 1)
        limit = jnp.where(low_rows < rows, counts[0] - core * rows, counts[0] - (1 - core) * rows + rows)
        bias[...] = jnp.where((low_rows >= limit) & (lane == 0), -1e30, 0.0).astype(LOW)
        after = [
            (0, lambda g: g.hop(1)), (2, lambda g: g.begin()), (0, lambda g: g.hop(2)), (1, lambda g: g.hop(1)), (0, lambda g: g.hop(3)),
            (3, lambda g: g.begin()), (1, lambda g: g.hop(2)), (0, lambda g: g.spread()), (1, lambda g: g.hop(3)),
            (2, lambda g: g.hop(1)), (1, lambda g: g.spread()), (2, lambda g: g.hop(2))]
        for p, act in after[:9]:
            if p < pairs:
                act(firsts[p])
        firsts[0].finish()
        for item in own_blocks:
            local(*item).wait()
        norms = w0[:, :, :, :, :128].reshape(d_model, 128).astype(F32).T
        gain, shift = norms[0:1], norms[1:2]
        tile = min(256, rows)

        @pl.loop(0, rows // tile)
        def _(i):
            at = pl.ds(pl.multiple_of(i * tile, tile), tile)
            n1[at] = (hat[at] * gain + shift).astype(LOW)

        local(*results[1]).start()
        project(0)
        for p, act in after[9:]:
            if p < pairs:
                act(firsts[p])

    total = pairs * steps_q
    per_slot = 2
    in_step = 4 * rows // min(256, rows) // per_slot
    slots = in_step * total

    def send_out():
        for i in range(1, heads):
            out_copy(i).start()

    def pass_out():
        for i in range(1, heads):
            out_copy(i).wait_recv()
            out_twin(i).start()

    def on_pair(p, what, *given):
        if p < pairs:
            getattr(firsts[p], what)(*given)

    events = [
        (0.1, lambda: on_pair(2, "hop", 3)), (0.3, lambda: on_pair(3, "hop", 1)), (0.4, outer.begin),
        (1, lambda: on_pair(3, "hop", 2)), (1.2, lambda: on_pair(2, "spread")), (1.4, up_a.begin),
        (2, lambda: on_pair(3, "hop", 3)), (2.6, lambda: outer.hop(1)), (3.2, lambda: outer.hop(2)), (3.2, up_b.begin),
        (3.8, lambda: on_pair(3, "spread")), (3.9, lambda: outer.hop(3)), (5.2, lambda: up_a.hop(1)), (6, outer.spread), (6.1, send_out),
        (6.5, lambda: up_a.hop(2)), (7, down_a.begin), (7.2, down_b.begin),
        (7.8, lambda: up_a.hop(3)), (9.2, lambda: up_b.hop(1)), (10.5, lambda: up_b.hop(2)), (10.6, pass_out), (10.8, down_b.pair),
        (11.8, lambda: up_b.hop(3)), (12, up_a.spread), (13.2, lambda: down_a.hop(1)), (14.5, lambda: down_a.hop(2)),
        (15.2, lambda: down_b.hop(1)), (15.8, lambda: down_a.hop(3)), (16, lambda: down_b.hop(2)), (16, up_b.spread),
        (16, down_a.spread), (16, lambda: down_b.hop(3))]

    def run(slot_in_step):
        for when, act in events:
            slot = min(int(when * slots / 16), slots - 1)
            if when < 16 and slot % in_step == slot_in_step:
                pl.when(step == slot // in_step)(act)

    for p in range(pairs):
        @pl.when(step == p * steps_q)
        def _():
            if p == 0:
                for i in range(2):
                    kv_copy(0, i).wait()
            if p + 1 < pairs:
                firsts[p + 1].finish()
                project(p + 1)
            else:
                for item in (results[0], *results[2:]):
                    local(*item).start()

        if p + 1 < pairs:
            @pl.when(step == (p + 1) * steps_q - 1)
            def _():
                for i in range(2):
                    kv_copy(p + 1, i).wait()

    width2, chunk = 2 * size, min(256, rows)
    n_chunks = 2 * rows // chunk
    ones = (lax.broadcasted_iota(jnp.int32, (block, bias.shape[1]), 1) == 0).astype(LOW)

    def asked(at, h):
        rows_at = pl.ds(pl.multiple_of(at % steps_q * block, block), block)
        cols_at = pl.ds(pl.multiple_of(at // steps_q * width2, width2), width2)
        return jnp.concatenate([only_head(q_s[rows_at, cols_at], h, size), ones], axis=1)

    def score(at, query, slot, c, top):
        cols_at = pl.ds(pl.multiple_of(at // steps_q * width2, width2), width2)
        keys_at = pl.ds(c * chunk, chunk)
        value = dot(jnp.concatenate([k_s[keys_at, cols_at], bias[keys_at]], axis=1), query, 1, 1)
        scores[slot, keys_at] = value
        return jnp.maximum(top, jnp.max(value.reshape(chunk // 8, 8, block), axis=0))

    def weigh(h, c, top, total_e):
        keys_at = pl.ds(c * chunk, chunk)
        expo = jnp.exp(scores[h, keys_at] - top)
        probs_v[slot_now, h, keys_at] = expo.astype(LOW)
        return total_e + jnp.sum(expo.reshape(chunk // 8, 8, block), axis=0)

    slot_now = step % 2

    def probs_copy(at):
        there = pl.ds(pl.multiple_of(at % steps_q * block, block), block)
        return pltpu.make_async_copy(probs_v.at[at % 2], probs.at[pl.ds(at // steps_q * 2, 2), :, there], probs_sem.at[at % 2])

    @pl.when(step >= 2)
    def _():
        probs_copy(step - 2).wait()

    lowest = jnp.full((8, block), -3e38, F32)

    @pl.when(step == 0)
    def _():
        top, query = lowest, asked(0, 0)
        for c in range(n_chunks):
            top = score(0, query, 0, c, top)
        tops[...] = top

    cols = pl.ds(pl.multiple_of(pair * width2, width2), width2)
    following = jnp.minimum(step + 1, total - 1)
    values_t = v_s[:, cols].T
    pieces = []
    for h in range(2):
        top = jnp.max(tops[...], axis=0, keepdims=True)
        total_e, next_top = jnp.zeros((8, block), F32), lowest
        ahead = (step, 1) if h == 0 else (following, 0)
        query = asked(*ahead)
        for c in range(n_chunks):
            if c % per_slot == 0:
                run(h * (n_chunks // per_slot) + c // per_slot)
            next_top = score(ahead[0], query, 1 - h, c, next_top)
            total_e = weigh(h, c, top, total_e)
        tops[...] = next_top
        over = 1.0 / jnp.sum(total_e, axis=0, keepdims=True)
        pieces.append(dot(values_t, probs_v[slot_now, h], 1, 0)[h * size:(h + 1) * size] * over)
        inverse[0, h:h + 1] = over
    here = jnp.concatenate(pieces, axis=0).T.astype(LOW)
    probs_copy(step).start()
    context[...] = here
    ctx_s[pl.ds(pl.multiple_of(part * block, block), block), cols] = here

    @pl.when(part == steps_q - 1)
    def _():
        for i in range(1, heads):
            ctx_copy(pair, i).start()

    @pl.when(step == total - 1)
    def _():
        local(*ctx_local).start()
        for when, act in events:
            if when >= 16:
                act()
        for gather in (outer, *thick):
            gather.finish()
        for item in results:
            local(*item).wait()
        local(*ctx_local).wait()
        for at in range(max(total - 2, 0), total):
            probs_copy(at).wait()
        for i in range(1, heads):
            out_copy(i).wait_send()
            out_twin(i).wait()
            for p in range(pairs):
                ctx_copy(p, i).wait()


def forward(counts, norms, w_qkv, shard_out, shard_up, shard_down, tokens, scenes, heads, size):
    ny = scenes // ZS
    rows, d_model = tokens.shape
    rl, width = shard_out.shape
    hidden = shard_up.shape[1]
    pairs = width // (2 * size)
    block = min(512, rows)
    steps_q = rows // block
    halves = 2
    sem = pltpu.SemaphoreType.DMA
    any_space = pl.BlockSpec(memory_space=pl.ANY)
    shape = jax.ShapeDtypeStruct
    wide = 128 + 3 * width
    outs = [shape((rows, d_model), LOW), shape((rows, width), LOW), shape((2 * rows, width), LOW), shape((2 * rows, width), LOW),
            shape((ZS, ny, 2, rl, wide), LOW), shape((ZS, ny, 2, rl, d_model), LOW), shape((ZS, ny, 2, rl, hidden), LOW),
            shape((ZS, ny, 2, rl, hidden), LOW), shape((2 * pairs, 2 * rows, rows), LOW), shape((rows, width), LOW),
            shape((rows, d_model), LOW), shape((pairs, 8, rows), F32)]
    out_specs = [any_space] * 8 + [
        any_space, pl.BlockSpec((block, 2 * size), lambda p, i: (i, p)),
        any_space, pl.BlockSpec((1, 8, block), lambda p, i: (p, 0, i))]
    scratch = [pltpu.VMEM((ZS, ny, 2, rl, wide), LOW), pltpu.VMEM((rows, d_model), F32), pltpu.VMEM((rows, d_model), LOW),
               pltpu.VMEM((rows, width), LOW), pltpu.VMEM((2 * rows, width), LOW), pltpu.VMEM((2 * rows, width), LOW),
               pltpu.VMEM((2 * rows, 128), LOW), pltpu.VMEM((rows, width), LOW),
               pltpu.VMEM((2, 2 * rows, block), F32), pltpu.VMEM((8, block), F32),
               pltpu.VMEM((2, 2, 2 * rows, block), LOW), sem((2,)), sem((10,)), sem((pairs, 2)), sem((pairs, 2)),
               sem((max(heads - 1, 1),)), sem((max(heads - 1, 1),)), sem((max(heads - 1, 1),)), sem((max(heads - 1, 1),)), sem((pairs, max(heads - 1, 1))), sem((pairs, max(heads - 1, 1)))]
    for _ in range(2 + 2 * halves + pairs):
        scratch += gather_sems(ny)
    dims = (ny, heads, rows, width, size, block, pairs, steps_q, halves)
    flops = 2 * rows * d_model * 3 * width + 8 * rows * rows * width
    results = pl.pallas_call(
        partial(forward_kernel, dims),
        grid=(pairs, steps_q),
        out_shape=outs,
        in_specs=[pl.BlockSpec(memory_space=pltpu.SMEM)] + [pl.BlockSpec(memory_space=pltpu.VMEM)] * 8 + [pl.BlockSpec(memory_space=pltpu.VMEM)],
        out_specs=out_specs,
        scratch_shapes=scratch,
        compiler_params=pltpu.CompilerParams(collective_id=0, has_side_effects=True, vmem_limit_bytes=60 * 2**20),
        cost_estimate=pl.CostEstimate(flops=flops, bytes_accessed=60 * 2**20, transcendentals=0),
        name="forward_attention",
    )(counts, *[a.reshape(1, rl) for a in norms], w_qkv, shard_out, shard_up, shard_down, tokens)
    n1, q, k, v, full_qkv, full_out, full_up, full_down, probs, context, context_all, inverse = results
    flat = lambda a: a.reshape(d_model, a.shape[-1])
    return n1, q, k, v, flat(full_qkv), flat(full_out), flat(full_up), flat(full_down), probs, context, context_all, inverse


class Scatter:
    def __init__(self, ny, parts, cols, bufs, sems):
        self.ny, self.parts, self.cols = ny, parts, cols
        self.own, self.from_core, self.from_y, self.sum_two, self.from_z = bufs
        self.load_sem, self.csend, self.crecv, self.ysend, self.yrecv, self.zsend, self.zrecv = sems
        self.z, self.y, self.core = place(ny)

    def load(self):
        return pltpu.make_async_copy(self.parts.at[:, :, self.core, :, self.cols], self.own, self.load_sem.at[0])

    def to_core(self):
        return remote(self.parts.at[:, :, 1 - self.core, :, self.cols], self.from_core, self.csend.at[0], self.crecv.at[0],
                      {"seq": 1 - self.core})

    def to_y(self, step):
        yy = (self.y + step) % self.ny
        return remote(self.own.at[:, yy], self.from_y.at[step - 1], self.ysend.at[step - 1], self.yrecv.at[step - 1],
                      {"scene": self.z * self.ny + yy})

    def to_z(self, step):
        zz = (self.z + step) % ZS
        return remote(self.sum_two.at[zz], self.from_z.at[step - 1], self.zsend.at[step - 1], self.zrecv.at[step - 1],
                      {"scene": zz * self.ny + self.y})

    def begin(self):
        self.load().start()
        self.to_core().start()

    def one(self):
        self.load().wait()
        self.to_core().wait_recv()
        for zz in range(ZS):
            for yy in range(self.ny):
                self.own[zz, yy] = (self.own[zz, yy].astype(F32) + self.from_core[zz, yy].astype(F32)).astype(LOW)
        for step in range(1, self.ny):
            self.to_y(step).start()

    def two(self):
        for step in range(1, self.ny):
            self.to_y(step).wait_recv()
        for zz in range(ZS):
            total = self.own[zz, self.y].astype(F32)
            for step in range(1, self.ny):
                total += self.from_y[step - 1, zz].astype(F32)
            self.sum_two[zz] = total.astype(LOW)
        for step in range(1, ZS):
            self.to_z(step).start()

    def three(self, out, alone=False):
        for step in range(1, ZS):
            self.to_z(step).wait_recv()
        total = self.sum_two[self.z].astype(F32)
        for step in range(1, ZS):
            total += self.from_z[step - 1].astype(F32)
        if alone:
            out[...] = total
        else:
            out[:, self.cols] = total

    def finish(self):
        self.to_core().wait_send()
        for step in range(1, self.ny):
            self.to_y(step).wait_send()
        for step in range(1, ZS):
            self.to_z(step).wait_send()


SCATTER_BUFS, SCATTER_SEMS = 5, 7


def scatter_scratch(ny, rl, cols):
    sem = pltpu.SemaphoreType.DMA
    other = max(ny - 1, 1)
    return [pltpu.VMEM((ZS, ny, rl, cols), LOW), pltpu.VMEM((ZS, ny, rl, cols), LOW), pltpu.VMEM((other, ZS, rl, cols), LOW),
            pltpu.VMEM((ZS, rl, cols), LOW), pltpu.VMEM((ZS - 1, rl, cols), LOW),
            sem((1,)), sem((1,)), sem((1,)), sem((other,)), sem((other,)), sem((ZS - 1,)), sem((ZS - 1,))]


def make_scatters(ny, plan, scratch):
    n = SCATTER_BUFS + SCATTER_SEMS
    result = []
    for i, (parts, cols) in enumerate(plan):
        mine = scratch[i * n:(i + 1) * n]
        result.append(Scatter(ny, parts, cols, mine[:SCATTER_BUFS], mine[SCATTER_BUFS:]))
    return result

def middle_kernel(dims, tokens, context_all, cotangent, full_qkv, full_out, full_up, full_down,
                  resid_grad, base, mlp_low, grad_context, norm_two, parts_out, parts_up, parts_down, mine_down,
                  x_v, ctx_v, cot_v, norm_v, wo, wu, wd, n2, act, gu, resid, part, low, arrived, up_v, down_v, out_v, gctx_v,
                  base_v, mlp_v, in_sem, out_sem, slot_sem, x_send, x_recv, g_send, g_recv, *scratch):
    ny, heads, rows, d_model, width, hidden, tile, size_f, first_cols = dims
    head = lax.axis_index("head")
    chunks = rows // tile
    part_rows = rows // heads
    per_part = part_rows // tile
    (down,) = make_scatters(ny, [(down_v, pl.ds(0, first_cols))], scratch)
    own_rows = pl.ds(pl.multiple_of(head * part_rows, part_rows), part_rows)

    def load(src, dst, i):
        return pltpu.make_async_copy(src, dst, in_sem.at[i])

    loads = [load(context_all, ctx_v, 0), load(full_out, wo, 1), load(tokens, x_v, 2), load(full_qkv.at[:, pl.ds(0, 128)], norm_v, 3),
             load(full_up, wu, 4), load(cotangent, cot_v, 5), load(full_down, wd, 6)]
    for item in loads:
        item.start()
    half = tile // 2

    def place_of(i):
        whole_tile = not isinstance(i, int)
        number = 0 if not whole_tile and i == chunks else i
        step = number // per_part + 1
        within = number % per_part * tile
        size = tile if whole_tile or 0 < i < chunks else half
        within = within + (half if not whole_tile and i == 0 else 0)
        return step, within, size

    def rows_of(i):
        step, within, size = place_of(i)
        return pl.ds(pl.multiple_of((head + step) % heads * part_rows + within, half), size)

    def x_copy(i, step):
        _, within, size = place_of(i)
        return remote(low.at[rows_of(i)], arrived.at[step - 1, pl.ds(within, size)], x_send.at[i], x_recv.at[i],
                      {"head": (head + step) % heads})

    def g_copy(j, step):
        to = (head + step) % heads
        at = pl.ds(j * tile, tile)
        there = pl.ds(pl.multiple_of(head * part_rows + j * tile, tile), tile)
        return remote(gctx_v.at[at, pl.ds(pl.multiple_of(to * width, width), width)], grad_context.at[there],
                      g_send.at[j, step - 1], g_recv.at[j, step - 1], {"head": to})

    greet_all(ny, heads)
    for item in loads[:4]:
        item.wait()
    norms = norm_v[...].astype(F32).T
    gain, shift = norms[2:3], norms[3:4]

    def hat_of(value):
        centre = value - jnp.mean(value, axis=1, keepdims=True)
        spread = lax.rsqrt(jnp.mean(centre * centre, axis=1, keepdims=True) + 1e-05)
        return centre * spread, spread

    norm_two[...] = jnp.zeros_like(norm_two)

    def forward_and_back(i, early=False):
        at = rows_of(i)
        value = x_v[at].astype(F32) + dot(ctx_v[at], wo[...], 1, 1)
        resid[at] = value
        n2[at] = (hat_of(value)[0] * gain + shift).astype(LOW)
        if early:
            loads[4].wait()
        for f in range(hidden // size_f):
            cols = slice(f * size_f, (f + 1) * size_f)
            u = dot(n2[at], wu[:, cols], 1, 0)
            if early and f == 0:
                loads[5].wait()
                loads[6].wait()
            ga = dot(cot_v[at], wd[:, cols], 1, 0)
            phi = 0.5 + 0.5 * lax.erf(u * (0.5 ** 0.5))
            act[at, cols] = (u * phi).astype(LOW)
            gu[at, cols] = (ga * (phi + u * (jnp.exp(u * u * -0.5) * 0.3989422804014327))).astype(LOW)
        total = dot(gu[at], wu[...], 1, 1)
        part[at] = total
        low[at] = total.astype(LOW)

    def sums(i):
        at = rows_of(i)
        total = part[at]
        hat, _ = hat_of(resid[at])
        norm_two[0:1] += jnp.sum(total * hat, axis=0, keepdims=True)
        norm_two[1:2] += jnp.sum(total, axis=0, keepdims=True)

    if heads > 1:
        forward_and_back(chunks, True)
        x_copy(chunks, 1).start()
        forward_and_back(0)
        x_copy(0, 1).start()
        for step in range(1, heads):
            first = (step - 1) * per_part

            @pl.loop(max(first, 1), first + per_part)
            def _(i):
                forward_and_back(i)
                x_copy(i, step).start()

    else:
        forward_and_back(chunks, True)
        forward_and_back(0)

    @pl.loop(max(chunks - per_part, 1), chunks)
    def _(i):
        forward_and_back(i)

    def weight_grad(src, other, dst, count):
        per_z = d_model // ZS
        for f in range(count // size_f):
            cols = slice(f * size_f, (f + 1) * size_f)

            @pl.loop(0, ZS // 2)
            def _(j):
                at = pl.ds(pl.multiple_of(j * 2 * per_z, 2 * per_z), 2 * per_z)
                value = dot(src[:, at], other[:, cols], 0, 0).astype(LOW)
                dst[pl.ds(2 * j, 2), :, :, :, cols] = value.reshape(2, *dst.shape[1:4], size_f)

    weight_grad(cot_v, act, down_v, hidden)
    down.begin()

    def own_store(j):
        at = pl.ds(j * tile, tile)
        there = pl.ds(pl.multiple_of(head * part_rows + j * tile, tile), tile)
        return (pltpu.make_async_copy(part.at[there], resid_grad.at[at], out_sem.at[3 + 2 * j]),
                pltpu.make_async_copy(gctx_v.at[at, pl.ds(pl.multiple_of(head * width, width), width)], grad_context.at[there],
                                      out_sem.at[4 + 2 * j]))

    for j in range(per_part):
        at = pl.ds(pl.multiple_of(head * part_rows + j * tile, tile), tile)
        total = part[at]
        for step in range(1, heads):
            i = (step - 1) * per_part + j
            x_copy(i, step).wait_recv()
            if i == 0:
                x_copy(chunks, step).wait_recv()
            total += arrived[step - 1, j * tile:(j + 1) * tile].astype(F32)
        hat, spread = hat_of(resid[at])
        own_part = part[at]
        norm_two[0:1] += jnp.sum(own_part * hat, axis=0, keepdims=True)
        norm_two[1:2] += jnp.sum(own_part, axis=0, keepdims=True)
        scaled = total * gain
        inner = scaled - jnp.mean(scaled, axis=1, keepdims=True) - hat * jnp.mean(scaled * hat, axis=1, keepdims=True)
        total = cot_v[at].astype(F32) + inner * spread
        part[at] = total
        rounded = total.astype(LOW)
        low[at] = rounded
        gctx_v[j * tile:(j + 1) * tile] = dot(rounded, wo[...], 1, 0).astype(LOW)
        for step in range(1, heads):
            g_copy(j, step).start()
        for item in own_store(j):
            item.start()
    down.one()
    weight_grad(n2, gu, up_v, hidden)
    stores = [pltpu.make_async_copy(up_v, parts_up, out_sem.at[0]), pltpu.make_async_copy(down_v, parts_down, out_sem.at[1]),
              pltpu.make_async_copy(out_v, parts_out, out_sem.at[2])]
    for item in stores[:2]:
        item.start()
    down.two()
    weight_grad(low.at[own_rows], ctx_v.at[own_rows], out_v, d_model)
    stores[2].start()

    def slot_copies(i):
        at = pl.ds(pl.multiple_of(i * tile, tile), tile)
        slot = i % 2
        return (pltpu.make_async_copy(base_v.at[slot], base.at[at], slot_sem.at[0, slot]),
                pltpu.make_async_copy(mlp_v.at[slot], mlp_low.at[at], slot_sem.at[1, slot]))

    def slot_loop(i):
        at = pl.ds(pl.multiple_of(i * tile, tile), tile)
        value = dot(act[at], wd[...], 1, 1)

        @pl.when(i >= 2)
        def _():
            for item in slot_copies(i - 2):
                item.wait()

        base_v[i % 2] = (resid[at] + value).astype(LOW)
        mlp_v[i % 2] = value.astype(LOW)
        for item in slot_copies(i):
            item.start()

    pl.loop(0, chunks)(slot_loop)
    if heads > 1:
        sums(chunks)
        sums(0)
        pl.loop(1, chunks - per_part)(sums)
    for i in range(max(0, chunks - 2), chunks):
        for item in slot_copies(i):
            item.wait()
    down.three(mine_down)
    down.finish()
    for item in stores:
        item.wait()
    for j in range(per_part):
        for item in own_store(j):
            item.wait()
        for step in range(1, heads):
            g_copy(j, step).wait()
    for step in range(1, heads):
        for j in range(per_part):
            x_copy((step - 1) * per_part + j, step).wait_send()
    if heads > 1:
        x_copy(chunks, 1).wait_send()


def shares(hidden):
    n = hidden // 128
    first = max(n // 8, 1)
    return first * 128, (n - first) * 128


def middle(tokens, context_all, cotangent, full_qkv, full_out, full_up, full_down, scenes, heads):
    ny = scenes // ZS
    rows, d_model = tokens.shape
    rl = d_model // (2 * scenes)
    hidden, width = full_up.shape[1], d_model // heads
    tile, size_f = min(256, rows // heads), min(1024, hidden)
    part_rows = rows // heads
    per_part = part_rows // tile
    chunks = rows // tile
    first_cols = shares(hidden)[0]
    others = max(heads - 1, 1)
    sem = pltpu.SemaphoreType.DMA
    shape, vmem = jax.ShapeDtypeStruct, pltpu.VMEM
    any_space, whole = pl.BlockSpec(memory_space=pl.ANY), pl.BlockSpec(memory_space=pltpu.VMEM)
    big, wide, blocks = (rows, d_model), (rows, hidden), (ZS, ny, 2, rl, hidden)
    scratch = [vmem(big, LOW), vmem(big, LOW), vmem(big, LOW), vmem((d_model, 128), LOW), vmem((d_model, d_model), LOW),
               vmem((d_model, hidden), LOW), vmem((d_model, hidden), LOW), vmem(big, LOW), vmem(wide, LOW), vmem(wide, LOW),
               vmem(big, F32), vmem(big, F32), vmem(big, LOW), vmem((others, part_rows, d_model), LOW), vmem(blocks, LOW),
               vmem(blocks, LOW), vmem((ZS, ny, 2, rl, d_model), LOW), vmem((part_rows, d_model), LOW), vmem((2, tile, d_model), LOW),
               vmem((2, tile, d_model), LOW), sem((7,)), sem((3 + 2 * per_part,)), sem((2, 2)), sem((chunks + 1,)),
               sem((chunks + 1,)), sem((per_part, others)), sem((per_part, others))]
    scratch += scatter_scratch(ny, rl, first_cols)
    return pl.pallas_call(
        partial(middle_kernel, (ny, heads, rows, d_model, width, hidden, tile, size_f, first_cols)),
        out_shape=[shape((part_rows, d_model), F32), shape(big, LOW), shape(big, LOW), shape((rows, width), LOW), shape((8, d_model), F32),
                   shape((ZS, ny, 2, rl, d_model), LOW), shape(blocks, LOW), shape(blocks, LOW), shape((rl, first_cols), F32)],
        in_specs=[any_space] * 7,
        out_specs=[any_space] * 4 + [whole] + [any_space] * 3 + [whole],
        scratch_shapes=scratch,
        compiler_params=pltpu.CompilerParams(collective_id=3, has_side_effects=True, vmem_limit_bytes=63 * 2**20),
        cost_estimate=pl.CostEstimate(flops=14 * rows * d_model * hidden, bytes_accessed=50 * 2**20, transcendentals=0),
        name="middle_stage",
    )(tokens, context_all, cotangent, full_qkv, full_out, full_up, full_down)


def backward_kernel(dims, probs, queries, keys, values, grad, context, inverse, parts_out, parts_up, mlp_low,
                    grads_out, mine_out, mine_up, mlp_land,
                    grads, grads_sem,
                    dk_acc, dv_acc, kept, stage, landed, kv_send, kv_recv, m_send, m_recv, *scratch):
    ny, heads, rows, size, pairs, steps_q, halves = dims
    pair, part = pl.program_id(0), pl.program_id(1)
    step = pair * steps_q + part
    total = pairs * steps_q
    block = grad.shape[0]
    z, y, core = place(ny)
    width = parts_out.shape[-1]
    ends = split_cols(width, 2)
    plan = [(parts_out, ends[0])] + [(parts_up, cols) for cols in split_cols(parts_up.shape[-1], halves)] + [(parts_out, ends[1])]
    scatters = make_scatters(ny, plan, scratch)
    targets = [mine_out] + [mine_up] * halves + [mine_out]

    def kv_copy(p, i):
        return remote(stage.at[p, i], landed.at[p, i], kv_send.at[p, i], kv_recv.at[p, i], {"seq": 1 - core})

    head = lax.axis_index("head")

    def mlp_copy(i, step):
        return remote(mlp_low.at[pl.ds(i * (rows // 4), rows // 4)], mlp_land.at[step - 1, pl.ds(i * (rows // 4), rows // 4)],
                      m_send.at[i, step - 1], m_recv.at[i, step - 1], {"head": (head + step) % heads})

    @pl.when(step == 0)
    def _():
        greet_all(ny, heads)
        for i in range(4):
            for j in range(1, heads):
                mlp_copy(i, j).start()
        for item in scatters:
            item.begin()

    slots = 2 * total
    plan_at = [(0.2 + 0.2 * i, 3.4 + 2.2 * i, 7.0 + 2.2 * i) for i in range(len(scatters))]
    events = sorted((plan_at[i][j], i, j + 1) for i in range(len(scatters)) for j in range(3))

    def run(slot_in_step):
        for when, i, what in events:
            slot = min(int(when * min(1.0, slots / 16)), slots)
            if slot == slots or slot % 2 != slot_in_step:
                continue

            @pl.when(step == slot // 2)
            def _():
                if what == 1:
                    scatters[i].one()
                elif what == 2:
                    scatters[i].two()
                else:
                    scatters[i].three(targets[i])

    @pl.when(part == 0)
    def _():
        dk_acc[...] = jnp.zeros_like(dk_acc)
        dv_acc[...] = jnp.zeros_like(dv_acc)

    upper = grad[...].astype(F32)
    inner = (upper * context[...].astype(F32)).T
    upper_t = upper.T
    row = lax.broadcasted_iota(jnp.int32, upper_t.shape, 0)
    keys_t = keys[...].T
    pieces = []
    for h in range(2):
        run(h)
        over = inverse[0, h:h + 1]
        shift = jnp.sum(inner[h * size:(h + 1) * size], axis=0, keepdims=True) * over
        scaled = jnp.where(row // size == h, upper_t * over, 0.0)
        dp = dot(values[...], scaled.astype(LOW), 1, 0) - shift
        low = probs[h]
        ds = (low.astype(F32) * dp).astype(LOW)
        dv_acc[...] += dot(low, scaled.T.astype(LOW), 1, 0)
        dk_acc[...] += dot(ds, only_head(queries[...], h, size), 1, 0)
        pieces.append(dot(keys_t, ds, 1, 0)[h * size:(h + 1) * size])
    grads[pl.ds(pl.multiple_of(part * block, block), block), pl.ds(pl.multiple_of(pair * 6 * size, 2 * size), 2 * size)] = (
        (jnp.concatenate(pieces, axis=0) * size ** -0.5).T.astype(LOW))

    @pl.when(part == steps_q - 1)
    def _():
        for i, acc in enumerate((dk_acc, dv_acc)):
            stage[pair, i] = acc[rows:].astype(LOW)
            kv_copy(pair, i).start()
            kept[pair, i] = acc[:rows]

    @pl.when(step == total - 1)
    def _():
        for when, i, what in events:
            if min(int(when * min(1.0, slots / 16)), slots) == slots:
                if what == 1:
                    scatters[i].one()
                elif what == 2:
                    scatters[i].two()
                else:
                    scatters[i].three(targets[i])
        for item in scatters:
            item.finish()
        for p in range(pairs):
            for i in range(2):
                kv_copy(p, i).wait()
                grads[:, (3 * p + i + 1) * 2 * size:(3 * p + i + 2) * 2 * size] = (kept[p, i] + landed[p, i].astype(F32)).astype(LOW)
        store = pltpu.make_async_copy(grads, grads_out, grads_sem)
        store.start()
        for i in range(4):
            for j in range(1, heads):
                mlp_copy(i, j).wait()
        store.wait()


def backward(probs, q, k, v, grad, context, inverse, parts_out, parts_up, mlp_low, scenes, heads, size):
    ny = scenes // ZS
    rows, width = q.shape
    pairs = width // (2 * size)
    block = min(512, rows)
    d_model, hidden = parts_out.shape[-1], parts_up.shape[-1]
    rl = d_model // (2 * scenes)
    others = max(heads - 1, 1)
    halves = 4
    spec = pl.BlockSpec
    q_spec = spec((block, 2 * size), lambda p, i: (i, p))
    k_spec = spec((2 * rows, 2 * size), lambda p, i: (0, p))
    any_space = spec(memory_space=pl.ANY)
    whole = spec(memory_space=pltpu.VMEM)
    shape = jax.ShapeDtypeStruct
    sem = pltpu.SemaphoreType.DMA
    pair_buf = (pairs, 2, rows, 2 * size)
    scratch = [pltpu.VMEM((rows, 3 * width), LOW), sem, pltpu.VMEM((2 * rows, 2 * size), F32), pltpu.VMEM((2 * rows, 2 * size), F32), pltpu.VMEM(pair_buf, F32),
               pltpu.VMEM(pair_buf, LOW), pltpu.VMEM(pair_buf, LOW), sem((pairs, 2)), sem((pairs, 2)), sem((4, others)), sem((4, others))]
    for cols in [d_model // 2] + [hidden // halves] * halves + [d_model // 2]:
        scratch += scatter_scratch(ny, rl, cols)
    return pl.pallas_call(
        partial(backward_kernel, (ny, heads, rows, size, pairs, rows // block, halves)),
        grid=(pairs, rows // block),
        out_shape=[shape((rows, 3 * width), LOW), shape((rl, d_model), F32), shape((rl, hidden), F32), shape((others, rows, d_model), LOW)],
        in_specs=[spec((2, 2 * rows, block), lambda p, i: (p, 0, i)), q_spec, k_spec, k_spec, q_spec, q_spec,
                  spec((1, 8, block), lambda p, i: (p, 0, i)), any_space, any_space, any_space],
        out_specs=[any_space, whole, whole, any_space],
        scratch_shapes=scratch,
        compiler_params=pltpu.CompilerParams(collective_id=1, has_side_effects=True, vmem_limit_bytes=60 * 2**20),
        cost_estimate=pl.CostEstimate(flops=16 * rows * rows * width, bytes_accessed=50 * 2**20, transcendentals=0),
        name="backward_attention",
    )(probs, q, k, v, grad, context, inverse, parts_out, parts_up, mlp_low)


def thirds(start, count):
    n = count // 128
    edges = [start + n * i // 3 * 128 for i in range(4)]
    return [(a, b - a) for a, b in zip(edges, edges[1:])]


def last_kernel(dims, grads, n1, tokens, resid, full_qkv, norm_two, parts_down, down_a, out_all,
                own_grad, done_land, mine_w, mine_norm, mine_out, mine_down,
                g_v, n1_v, x_v, res_v, w_v, in_sem,
                part_one, part_low, arrived, parts_qkv, tiny_land, tiny_own, done_low, x_send, x_recv, t_send, t_recv,
                n_send, n_recv, o_send, o_recv, out_sem, mine_qkv, out_land, *scratch):
    ny, heads, rows, d_model, width, tile, down_at, qkv_at = dims
    z, y, core = place(ny)
    head = lax.axis_index("head")
    wide = full_qkv.shape[1]
    rl = mine_qkv.shape[0]
    plan = [(parts_down, pl.ds(*item)) for item in down_at] + [(parts_qkv, pl.ds(*item)) for item in qkv_at]
    scatters = make_scatters(ny, plan, scratch)
    downs, qkvs = scatters[:len(down_at)], scatters[len(down_at):]
    down_x, down_y, down_z = downs

    def down_done(i):
        downs[i].three(mine_down.at[:, pl.ds(*down_at[i])], True)

    chunks = rows // tile
    part_rows = rows // heads
    per_part = part_rows // tile
    loads = [pltpu.make_async_copy(src, dst, in_sem.at[i]) for i, (src, dst) in enumerate((
        (grads, g_v), (full_qkv, w_v), (n1, n1_v), (tokens, x_v), (resid, res_v)))]
    for item in loads:
        item.start()
    def rows_at(step, j):
        return pl.ds(pl.multiple_of((head + heads + step) % heads * part_rows + j * tile, tile), tile)

    def x_copy(step, j):
        return remote(part_low.at[rows_at(step, j)], arrived.at[step - 1, pl.ds(j * tile, tile)], x_send.at[step - 1, j],
                      x_recv.at[step - 1, j], {"head": (head + step) % heads})

    def t_copy(step, j):
        at = pl.ds(j * tile, tile)
        return remote(done_low.at[at], done_land.at[step - 1, at], t_send.at[step - 1, j], t_recv.at[step - 1, j],
                      {"head": (head + step) % heads})

    def n_copy(step):
        return remote(tiny_own, tiny_land.at[step - 1], n_send.at[step - 1], n_recv.at[step - 1], {"head": (head + step) % heads})

    def o_copy(step):
        to = (head + step) % heads
        return remote(out_all.at[:, pl.ds(pl.multiple_of(to * width, width), width)], out_land.at[step - 1], o_send.at[step - 1],
                      o_recv.at[step - 1], {"head": to})

    def out_copy(j):
        at = pl.ds(j * tile, tile)
        return pltpu.make_async_copy(done_low.at[at], own_grad.at[at], out_sem.at[j])

    greet_all(ny, heads)
    for item in downs:
        item.begin()
    for item in loads[:2]:
        item.wait()

    def partial_sum(step, j):
        at = rows_at(step, j)
        total = dot(g_v[at], w_v[:, 128:], 1, 1)
        part_one[at] = total
        part_low[at] = total.astype(LOW)

    for step in range(1, heads):
        for j in range(per_part):
            partial_sum(step, j)
            x_copy(step, j).start()
    for step in range(1, heads):
        o_copy(step).start()
    down_x.one()
    down_y.one()
    for j in range(per_part):
        partial_sum(0, j)
    for item in loads[2:]:
        item.wait()
    per_z = d_model // ZS
    for zz in range(0, ZS, 2):
        cols = n1_v[:, zz * per_z:(zz + 2) * per_z]
        value = dot(cols, g_v[...], 0, 0).astype(LOW)
        parts_qkv[zz:zz + 2, :, :, :, 128:] = value.reshape(2, ny, 2, rl, 3 * width)
    for item in qkvs[1:]:
        item.begin()
    gain = w_v[:, :128].astype(F32).T[0:1]

    def hat_of(at):
        x = x_v[at].astype(F32)
        centre = x - jnp.mean(x, axis=1, keepdims=True)
        spread = lax.rsqrt(jnp.mean(centre * centre, axis=1, keepdims=True) + 1e-05)
        return centre * spread, spread

    gain_sum = jnp.zeros((1, d_model), F32)
    shift_sum = jnp.zeros((1, d_model), F32)
    for i in range(chunks):
        at = pl.ds(i * tile, tile)
        hat, _ = hat_of(at)
        gain_sum += jnp.sum(part_one[at] * hat, axis=0, keepdims=True)
        shift_sum += jnp.sum(part_one[at], axis=0, keepdims=True)
        if i == chunks // 4:
            qkvs[1].one()
            down_x.two()
        if i == chunks // 2:
            qkvs[2].one()
    sums = jnp.concatenate([gain_sum, shift_sum, norm_two[0:2], jnp.zeros((124, d_model), F32)], axis=0).T.astype(LOW)
    parts_qkv[:, :, :, :, :128] = sums.reshape(ZS, ny, 2, rl, 128)
    qkvs[0].begin()

    def receive(j):
        at = rows_at(0, j)
        here = pl.ds(j * tile, tile)
        total = part_one[at]
        for step in range(1, heads):
            x_copy(step, j).wait_recv()
            total += arrived[step - 1, here].astype(F32)
        hat, spread = hat_of(at)
        scaled = total * gain
        inner = scaled - jnp.mean(scaled, axis=1, keepdims=True) - hat * jnp.mean(scaled * hat, axis=1, keepdims=True)
        total = res_v[here] + inner * spread
        done_low[here] = total.astype(LOW)
        out_copy(j).start()
        for step in range(1, heads):
            t_copy(step, j).start()

    first = pl.ds(pl.multiple_of(head * width, width), width)

    def share(items, i, n):
        return items[len(items) * i // n:len(items) * (i + 1) // n]

    def receive_some(i):
        for j in share(range(per_part), i, 4):
            receive(j)

    def send_norms():
        tiny_own[...] = mine_qkv[:, :128]
        for step in range(1, heads):
            n_copy(step).start()

    receive_some(0)
    qkvs[0].one()
    down_z.one()
    down_y.two()
    receive_some(1)
    mine_down[:, :down_a.shape[1]] = down_a[...]
    down_done(0)
    receive_some(2)
    qkvs[1].two()
    down_done(1)
    receive_some(3)
    qkvs[2].two()
    qkvs[1].three(mine_qkv)
    total = out_all[:, first]
    for step in range(1, heads):
        o_copy(step).wait()
        total += out_land[step - 1]
    mine_out[...] = total
    qkvs[0].two()
    qkvs[2].three(mine_qkv)
    down_z.two()
    qkvs[0].three(mine_qkv)
    send_norms()
    down_done(2)
    total = mine_qkv[:, :128]
    for step in range(1, heads):
        n_copy(step).wait()
        total += tiny_land[step - 1]
    mine_norm[...] = total.T[:8]
    for p in range(width // 128):
        for c in range(3):
            mine_w[c, :, p * 128:(p + 1) * 128] = mine_qkv[:, 128 * (3 * p + c + 1):128 * (3 * p + c + 2)]
    for item in scatters:
        item.finish()
    for j in range(per_part):
        out_copy(j).wait()
        for step in range(1, heads):
            x_copy(step, j).wait_send()
            t_copy(step, j).wait()


def last_stage(grads, n1, tokens, resid, full_qkv, norm_two, parts_down, down_a, out_all, scenes, heads):
    ny = scenes // ZS
    rows, d_model = tokens.shape
    width, hidden = grads.shape[1] // 3, parts_down.shape[-1]
    first, third = shares(hidden)
    rl = d_model // (2 * scenes)
    wide = full_qkv.shape[1]
    part_rows = rows // heads
    tile = min(128, part_rows)
    chunks, per_part = rows // tile, part_rows // tile
    down_at, qkv_at = thirds(first, third), thirds(0, wide)
    others = max(heads - 1, 1)
    sem = pltpu.SemaphoreType.DMA
    shape, vmem = jax.ShapeDtypeStruct, pltpu.VMEM
    any_space, whole = pl.BlockSpec(memory_space=pl.ANY), pl.BlockSpec(memory_space=pltpu.VMEM)
    big, own = (rows, d_model), (part_rows, d_model)
    scratch = [vmem((rows, 3 * width), LOW), vmem(big, LOW), vmem(big, LOW), vmem(own, F32), vmem((d_model, wide), LOW), sem((5,)),
               vmem(big, F32), vmem(big, LOW), vmem((others, *own), LOW), vmem((ZS, ny, 2, rl, wide), LOW), vmem((others, rl, 128), F32),
               vmem((rl, 128), F32), vmem(own, LOW), sem((others, per_part)),
               sem((others, per_part)), sem((others, per_part)), sem((others, per_part)), sem((others,)), sem((others,)),
               sem((others,)), sem((others,)), sem((per_part,)), vmem((rl, wide), F32), vmem((others, rl, width), F32)]
    for _, cols in down_at + qkv_at:
        scratch += scatter_scratch(ny, rl, cols)
    return pl.pallas_call(
        partial(last_kernel, (ny, heads, rows, d_model, width, tile, down_at, qkv_at)),
        out_shape=[shape(own, LOW), shape((others, *own), LOW), shape((3, rl, width), F32), shape((8, rl), F32), shape((rl, width), F32),
                   shape((rl, hidden), F32)],
        in_specs=[any_space] * 5 + [whole, any_space, whole, whole],
        out_specs=[any_space, any_space, whole, whole, whole, whole],
        scratch_shapes=scratch,
        compiler_params=pltpu.CompilerParams(collective_id=2, has_side_effects=True, vmem_limit_bytes=63 * 2**20),
        cost_estimate=pl.CostEstimate(flops=12 * rows * d_model * width, bytes_accessed=30 * 2**20, transcendentals=0),
        name="last_stage",
    )(grads, n1, tokens, resid, full_qkv, norm_two, parts_down, down_a, out_all)


def finish_kernel(heads, tile, base, mlp_land, own, land, w, out, up, down, norm,
                  output, tokens_grad, w_o, out_o, up_o, down_o, n_a, n_b, n_c, n_d,
                  sum_v, base_v, own_v, mlp_v, grad_v, land_v, w_v, out_v, up_v, down_v, base_sem, mlp_sem, own_sem, land_sem, small_sem,
                  out_sem, back_sem, far_sem, last_sem):
    rows = base.shape[0]
    part_rows = rows // heads
    chunks, per_part = rows // tile, part_rows // tile
    head = lax.axis_index("head")
    copy = pltpu.make_async_copy

    def rows_at(step, j):
        return pl.ds(pl.multiple_of((head + heads - step) % heads * part_rows + j * tile, tile), tile)

    def loads(i):
        at = pl.ds(i * tile, tile)
        return copy(base.at[at], base_v.at[at], base_sem.at[i]), copy(mlp_land.at[:, at], mlp_v.at[:, at], mlp_sem.at[i])

    def own_load(j):
        at = pl.ds(j * tile, tile)
        return copy(own.at[at], own_v.at[at], own_sem.at[j])

    land_load = copy(land, land_v, land_sem.at[0])
    smalls = ((w, w_v, w_o), (out, out_v, out_o), (up, up_v, up_o), (down, down_v, down_o))
    small_loads = [copy(src, mid, small_sem.at[i]) for i, (src, mid, _) in enumerate(smalls)]
    small_stores = [copy(mid, dst, last_sem.at[i]) for i, (_, mid, dst) in enumerate(smalls)]

    def out_store(i):
        at = pl.ds(i * tile, tile)
        return copy(sum_v.at[at], output.at[at], out_sem.at[i])

    def own_store(j):
        return copy(grad_v.at[rows_at(0, j)], tokens_grad.at[rows_at(0, j)], back_sem.at[j])

    def far_store(step, j):
        return copy(grad_v.at[rows_at(step, j)], tokens_grad.at[rows_at(step, j)], far_sem.at[step - 1, j])

    for j in range(per_part):
        own_load(j).start()
    if heads > 1:
        land_load.start()
    for i in range(chunks):
        for item in loads(i):
            item.start()
    for item in small_loads:
        item.start()
    for i, dst in enumerate((n_a, n_b, n_c, n_d)):
        dst[...] = norm[i:i + 1]
    for j in range(per_part):
        own_load(j).wait()
        grad_v[rows_at(0, j)] = own_v[j * tile:(j + 1) * tile].astype(F32)
        own_store(j).start()
    if heads > 1:
        land_load.wait()
        for step in range(1, heads):
            for j in range(per_part):
                grad_v[rows_at(step, j)] = land_v[step - 1, j * tile:(j + 1) * tile].astype(F32)
                far_store(step, j).start()
    for i in range(chunks):
        at = pl.ds(i * tile, tile)
        for item in loads(i):
            item.wait()
        total = base_v[at].astype(F32)
        for step in range(1, heads):
            total += mlp_v[step - 1, at].astype(F32)
        sum_v[at] = total
        out_store(i).start()
    for first, second in zip(small_loads, small_stores):
        first.wait()
        second.start()
    for j in range(per_part):
        own_store(j).wait()
        for step in range(1, heads):
            far_store(step, j).wait()
    for i in range(chunks):
        out_store(i).wait()
    for item in small_stores:
        item.wait()


def finish(base, mlp_land, own, land, w, out, up, down, norm, heads):
    rows, d_model = base.shape
    part_rows = rows // heads
    tile = min(128, part_rows)
    chunks, per_part = rows // tile, part_rows // tile
    rl, others = up.shape[0], max(heads - 1, 1)
    spec, shape, vmem, sem = pl.BlockSpec, jax.ShapeDtypeStruct, pltpu.VMEM, pltpu.SemaphoreType.DMA
    any_space, whole = spec(memory_space=pl.ANY), spec(memory_space=pltpu.VMEM)
    return pl.pallas_call(
        partial(finish_kernel, heads, tile),
        in_specs=[any_space] * 8 + [whole],
        out_specs=[any_space] * 6 + [whole] * 4,
        out_shape=[shape((rows, d_model), F32), shape((rows, d_model), F32)] + [shape(a.shape, F32) for a in (w, out, up, down)]
        + [shape((1, rl), F32)] * 4,
        scratch_shapes=[vmem(base.shape, F32), vmem(base.shape, LOW), vmem(own.shape, LOW), vmem(mlp_land.shape, LOW), vmem(base.shape, F32), vmem(land.shape, LOW)]
        + [vmem(a.shape, F32) for a in (w, out, up, down)]
        + [sem((chunks,)), sem((chunks,)), sem((per_part,)), sem((1,)), sem((4,)), sem((chunks,)), sem((per_part,)),
           sem((others, per_part)), sem((4,))],
        compiler_params=pltpu.CompilerParams(vmem_limit_bytes=63 * 2**20),
        name="finish",
    )(base, mlp_land, own, land, w, out, up, down, norm)


def on_device(n_scene, n_head, tokens, counts, w_qkv, w_out, w_up, w_down, gain_one, shift_one, gain_two, shift_two, cotangent):
    rows, d_model = tokens.shape
    width, hidden = w_qkv.shape[2], w_up.shape[1]
    size = 64
    n1, q, k, v, full_qkv, full_out, full_up, full_down, probs, context, context_all, inverse = forward(
        counts, (gain_one, shift_one, gain_two, shift_two), w_qkv, w_out.T, w_up, w_down.T, tokens, n_scene, n_head, size)
    grad_resid, base, mlp_low, grad_context, norm_two, grad_outproj, grad_up, grad_down, down_a = middle(
        tokens, context_all, cotangent, full_qkv, full_out, full_up, full_down, n_scene, n_head)
    grads, out_all, mine_up, mlp_land = backward(
        probs, q, k, v, grad_context, context, inverse, grad_outproj, grad_up, mlp_low, n_scene, n_head, size)
    own, land, mine_qkv, norms, mine_out, mine_down = last_stage(
        grads, n1, tokens, grad_resid, full_qkv, norm_two, grad_down, down_a, out_all, n_scene, n_head)
    output, tokens_grad, mine_qkv, mine_out, mine_up, mine_down, *norms = finish(
        base, mlp_land, own, land, mine_qkv, mine_out, mine_up, mine_down, norms, n_head)
    return (output, tokens_grad, mine_qkv, mine_out.T, mine_up, mine_down.T, *[a.reshape(-1) for a in norms])


def solution(mesh):
    rows, both = ("scene", "seq"), P(("scene", "seq"))
    weights = (P(None, rows, "head"), P("head", rows), P(rows, "head"), P("head", rows), both, both, both, both)
    return jax.shard_map(
        partial(on_device, mesh.shape["scene"], mesh.shape["head"]), mesh=mesh,
        in_specs=(P(rows, None), P("scene"), *weights, P(rows, None)),
        out_specs=(P(rows, None), P(rows, None), *weights),
        check_vma=False,
    )
```
